32 devices in a mesh: batch: 2 (over x), ctx: 16 (over z, y, core).
Axes of the slice: x: 2, y: 2, z: 4, core: 2. Of those that a mesh axis runs over, the one named last changes fastest.
Arguments:
- inputs: float32 [4, 1024, 768], P('batch', 'ctx'), may hold values from -6 to 6
- teacher: float32 [4, 1024, 768], P('batch', 'ctx'), may hold values from -6 to 6
- segments: int32 [4, 1024], P('batch'), may hold values from 0 to 15, never falling along the last dimension, each value on 1 to 768 neighbouring positions
- w_query: bfloat16 [768, 768], P('batch'), may hold values from -0.21875 to 0.21875
- b_query: bfloat16 [768], P('batch'), may hold values from -4 to 4
- w_key: bfloat16 [768, 768], P('batch'), may hold values from -0.21875 to 0.21875
- w_value: bfloat16 [768, 768], P('batch'), may hold values from -0.21875 to 0.21875
- b_value: bfloat16 [768], P('batch'), may hold values from -0.75 to 0.75
- w_out: bfloat16 [768, 768], P('batch'), may hold values from -1.25 to 1.25
- b_out: bfloat16 [768], P('batch'), may hold values from -4 to 4
- gain_one: bfloat16 [768], P('batch'), may hold values from 0.25 to 1.75
- shift_one: bfloat16 [768], P('batch'), may hold values from -4 to 4
- w_inner: bfloat16 [768, 3072], P('batch'), may hold values from -0.21875 to 0.21875
- b_inner: bfloat16 [3072], P('batch'), may hold values from -4 to 4
- w_outer: bfloat16 [3072, 768], P('batch'), may hold values from -0.109375 to 0.109375
- b_outer: bfloat16 [768], P('batch'), may hold values from -4 to 4
- gain_two: bfloat16 [768], P('batch'), may hold values from 0.25 to 1.75
- shift_two: bfloat16 [768], P('batch'), may hold values from -4 to 4
Outputs:
- output: float32 [4, 1024, 768], P('batch', 'ctx')
- loss: float32 [], replicated
- grad_inputs: float32 [4, 1024, 768], P('batch', 'ctx')
- grad_w_query: float32 [768, 768], P('batch')
- grad_b_query: float32 [768], P('batch')
- grad_w_key: float32 [768, 768], P('batch')
- grad_w_value: float32 [768, 768], P('batch')
- grad_b_value: float32 [768], P('batch')
- grad_w_out: float32 [768, 768], P('batch')
- grad_b_out: float32 [768], P('batch')
- grad_gain_one: float32 [768], P('batch')
- grad_shift_one: float32 [768], P('batch')
- grad_w_inner: float32 [768, 3072], P('batch')
- grad_b_inner: float32 [3072], P('batch')
- grad_w_outer: float32 [3072, 768], P('batch')
- grad_b_outer: float32 [768], P('batch')
- grad_gain_two: float32 [768], P('batch')
- grad_shift_two: float32 [768], P('batch')
The draws below stay inside these ranges and needn't reach their ends.
Inputs may be any that keep to these rules, and one draw needn't show every extreme that they name: `segments`: segment ids never fall along a sequence, every id of 0 to 15 occurs in each sequence, each segment covers 1 to 768 positions and one covers exactly 768.
All inputs are finite; a program needn't handle non-finite values.
Results may differ from the reference program's by a relative error of at most 0.014.
The reference program's roundings to bfloat16 on the way count: a program that leaves them out, or rounds other values in their place, can miss the bound.
Values may be sent and summed in bfloat16 or wider, within the bound.
No kernel may reach another device: no remote copies, remote signals or barrier semaphores. Data moves between devices by JAX's collectives and lax.ppermute only.
A program may use at most 320 MiB of HBM per device.

```python
import math
import jax
import jax.numpy as jnp
import numpy as np
from jax import lax

D = 768
H = 12
HD = 64
FF = 3072
LEN = 1024
SEQUENCES = 4
TOKENS = 4096


def levels(key, dims, cuts, smallest, high):
    def one(axis_at, shards_of):
        heights = jax.random.uniform(jax.random.fold_in(jax.random.fold_in(key, 6), axis_at), (shards_of,), jnp.float32, smallest / len(cuts), high / len(cuts))
        return jnp.repeat(jnp.exp(heights), dims[axis_at] // shards_of).reshape((-1,) + (1,) * (len(dims) - axis_at - 1))

    level = one(*cuts[0])
    for cut in cuts[1:]:
        level = level * one(*cut)
    return level


def profile(count, total, most, lean):
    weights = [(1 << 20) // math.isqrt(rank ** lean) + 1 for rank in range(2, count + 1)]
    spare, holding = total - most - (count - 1), [1] * (count - 1)
    while spare > 0:
        free = [i for i in range(count - 1) if holding[i] < most]
        mass, remaining = sum([weights[i] for i in free]), spare
        for i in free:
            more = min(most - holding[i], max(1, remaining * weights[i] // mass), spare)
            holding[i] = holding[i] + more
            spare = spare - more
    return np.array([most] + holding)


def uneven_parts(stream_key, number_of, total, most, slope):
    if number_of == 2:
        one = jax.random.randint(stream_key, (), max(1, total - most), min(most, total - 1) + 1)
        return jnp.stack([one, total - one])
    tallies = jnp.asarray(profile(number_of, total, most, slope), jnp.int32)
    twos = (number_of - 1) // 2
    giver, sink = tallies[1:1 + 2 * twos:2], tallies[2:2 + 2 * twos:2]
    margin = jnp.minimum(giver - 1, most - sink)
    passed = jax.random.randint(jax.random.fold_in(stream_key, 1), (twos,), 0, 1 << 20) % (margin + 1)
    tallies = tallies.at[1:1 + 2 * twos:2].set(giver - passed).at[2:2 + 2 * twos:2].set(sink + passed)
    return tallies[jax.random.permutation(jax.random.fold_in(stream_key, 2), number_of)]


def noise(key, dims, scale, limit, split=(), kind=jnp.bfloat16):
    level = levels(key, dims, split, -0.22, 0.18) if split else 1.0
    values = jax.random.normal(key, dims, jnp.float32) * scale * level
    return jnp.minimum(jnp.maximum(values, -limit), limit).astype(kind)


def setup_inputs(seed: int = 0) -> dict:
    splits = jax.random.split(jax.random.key(seed), 19)
    inputs = noise(splits[0], (SEQUENCES, LEN, D), 1.0, 6.0, ((0, 2), (1, 16)), jnp.float32)
    teacher = noise(splits[1], (SEQUENCES, LEN, D), 1.0, 6.0, ((0, 2), (1, 16)), jnp.float32)
    segments = jax.vmap(lambda own: jnp.searchsorted(jnp.cumsum(uneven_parts(own, 16, LEN, 3 * LEN // 4, 2)), jnp.arange(LEN), side="right"))(jax.random.split(splits[2], SEQUENCES)).reshape((SEQUENCES, LEN)).astype(jnp.int32)
    w_query = noise(splits[3], (D, D), D ** -0.5, 0.21875, ((0, 2),))
    b_query = noise(splits[4], (D,), 0.3, 4.0, ((0, 2),))
    w_key = noise(splits[5], (D, D), D ** -0.5, 0.21875, ((0, 2),))
    w_value = noise(splits[6], (D, D), D ** -0.5, 0.21875, ((0, 2),))
    b_value = noise(splits[7], (D,), 0.05, 0.75, ((0, 2),))
    w_out = noise(splits[8], (D, D), (D // 32) ** -0.5, 1.25, ((0, 2),))
    b_out = noise(splits[9], (D,), 0.3, 4.0, ((0, 2),))
    gain_one = jnp.clip(1.0 + 0.15 * jax.random.normal(splits[10], (D,), jnp.float32), 0.25, 1.75).astype(jnp.bfloat16)
    shift_one = noise(splits[11], (D,), 0.3, 4.0, ((0, 2),))
    w_inner = noise(splits[12], (D, FF), D ** -0.5, 0.21875, ((0, 2),))
    b_inner = noise(splits[13], (FF,), 0.3, 4.0, ((0, 2),))
    w_outer = noise(splits[14], (FF, D), FF ** -0.5, 0.109375, ((0, 2),))
    b_outer = noise(splits[15], (D,), 0.3, 4.0, ((0, 2),))
    gain_two = jnp.clip(1.0 + 0.15 * jax.random.normal(splits[16], (D,), jnp.float32), 0.25, 1.75).astype(jnp.bfloat16)
    shift_two = noise(splits[17], (D,), 0.3, 4.0, ((0, 2),))
    return dict(inputs=inputs, teacher=teacher, segments=segments, w_query=w_query, b_query=b_query, w_key=w_key, w_value=w_value, b_value=b_value, w_out=w_out, b_out=b_out, gain_one=gain_one, shift_one=shift_one, w_inner=w_inner, b_inner=b_inner, w_outer=w_outer, b_outer=b_outer, gain_two=gain_two, shift_two=shift_two)


@jax.custom_vjp
def low(v):
    return lax.optimization_barrier(v.astype(jnp.bfloat16)).astype(jnp.float32)

@jax.custom_vjp
def low_back(v):
    return v

def low_keep(v):
    return (low(v), None)

def low_pass(kept, grad):
    return (grad,)

def back_keep(v):
    return (v, None)

def back_low(kept, grad):
    return (low(grad),)
low.defvjp(low_keep, low_pass)
low_back.defvjp(back_keep, back_low)
NEGATIVE = -1e+30
EPSILON = 1e-12

def rounded(values):
    return low(low_back(values))

def matmul(left, right):
    return jnp.dot(left, right, precision=lax.Precision.HIGHEST)

def norm_rows(hidden, gain, shift):
    center = hidden - lax.optimization_barrier(jnp.mean(hidden, -1, keepdims=True))
    spread = lax.optimization_barrier(jnp.mean(center * center, -1, keepdims=True))
    return center * lax.rsqrt(spread + EPSILON) * gain + shift

def attention(query, key, value, segments):
    block = math.gcd(LEN, 512)

    def one_sequence(items):
        query_one, key_one, value_one, seg_one = items
        query_blocks = query_one.reshape(LEN // block, block, H, HD)
        seg_blocks = seg_one.reshape(LEN // block, block)

        def one_block(parts):
            query_part, seg_part = parts
            raw = jnp.einsum('qhd,khd->hqk', query_part, key_one, precision=lax.Precision.HIGHEST) * HD ** (-0.5)
            scores = low_back(raw)
            allowed = seg_part[None, :, None] == seg_one[None, None, :]
            probs = low(jax.nn.softmax(jnp.where(allowed, scores, NEGATIVE), axis=-1))
            return jnp.einsum('hqk,khd->qhd', probs, value_one, precision=lax.Precision.HIGHEST)
        mixed = lax.map(jax.checkpoint(one_block), (query_blocks, seg_blocks))
        return mixed.reshape(LEN, H, HD)
    return lax.map(one_sequence, (query, key, value, segments))

def layer(inputs, w_query, b_query, w_key, w_value, b_value, w_out, b_out, gain_one, shift_one, w_inner, b_inner, w_outer, b_outer, gain_two, shift_two, teacher, segments):
    count_seq = inputs.shape[0]
    flat = inputs.reshape(count_seq * LEN, D)
    flat_low = low(flat)
    query = rounded(matmul(flat_low, w_query) + b_query).reshape(count_seq, LEN, H, HD)
    key = rounded(matmul(flat_low, w_key)).reshape(count_seq, LEN, H, HD)
    value = rounded(matmul(flat_low, w_value) + b_value).reshape(count_seq, LEN, H, HD)
    attended = rounded(attention(query, key, value, segments).reshape(count_seq * LEN, D))
    branch_one = low_back(matmul(attended, w_out) + b_out)
    hidden_one = flat + branch_one
    normed_one = norm_rows(hidden_one, gain_one, shift_one)
    inner_pre = low_back(matmul(low(normed_one), w_inner) + b_inner)
    active = low(jax.nn.gelu(inner_pre, approximate=False))
    branch_two = low_back(matmul(active, w_outer) + b_outer)
    output = norm_rows(normed_one + branch_two, gain_two, shift_two)
    valid = (segments.reshape(count_seq * LEN) != 0).astype(jnp.float32)[:, None]
    error = output - teacher.reshape(count_seq * LEN, D)
    valid_count = jnp.sum(valid)
    loss = jnp.sum(valid * error * error) / (2.0 * valid_count)
    return (TOKENS * loss, (output.reshape(inputs.shape), loss))

def reference(inputs, teacher, segments, w_query, b_query, w_key, w_value, b_value, w_out, b_out, gain_one, shift_one, w_inner, b_inner, w_outer, b_outer, gain_two, shift_two):
    params = (w_query, b_query, w_key, w_value, b_value, w_out, b_out, gain_one, shift_one, w_inner, b_inner, w_outer, b_outer, gain_two, shift_two)
    params = tuple((entry.astype(jnp.float32) for entry in params))

    def objective(states, *weights):
        return layer(states, *weights, teacher, segments)
    total, backward, extra = jax.vjp(objective, inputs, *params, has_aux=True)
    grads = backward(jnp.ones_like(total))
    output, loss = extra
    return (output, loss, grads[0], grads[1], grads[2], grads[3], grads[4], grads[5], grads[6], grads[7], grads[8], grads[9], grads[10], grads[11], grads[12], grads[13], grads[14], grads[15])
```

```python
import jax
import jax.numpy as jnp
from jax import lax
from jax.sharding import PartitionSpec as P

H = 12
HD = 64


NEGATIVE = -1e30
EPSILON = 1e-12


def norm_rows(hidden, gain, shift):
    center = hidden - jnp.mean(hidden, -1, keepdims=True)
    spread = jnp.mean(center * center, -1, keepdims=True)
    return center * lax.rsqrt(spread + EPSILON) * gain + shift


def gelu_exact(values):
    return jax.nn.gelu(values, approximate=False)


def linear(rows_in, weight):
    return jnp.dot(rows_in, weight, preferred_element_type=jnp.float32)


def contract_rows(left, right):
    return lax.dot_general(
        left, right, (((0,), (0,)), ((), ())), preferred_element_type=jnp.float32
    )


def times_transpose(rows_in, weight):
    return lax.dot_general(
        rows_in, weight, (((1,), (1,)), ((), ())), preferred_element_type=jnp.float32
    )


def score_rows(query_one, keys_all, seg_mine, seg_all):
    heads_query = query_one.reshape(query_one.shape[0], H, HD)
    heads_key = keys_all.reshape(keys_all.shape[0], H, HD)
    raw = jnp.einsum(
        "chd,khd->hck", heads_query, heads_key, preferred_element_type=jnp.float32
    ) * HD ** (-0.5)
    allowed = seg_mine[None, :, None] == seg_all[None, None, :]
    return jnp.where(allowed, raw, NEGATIVE)


def per_device_any(
    inputs,
    teacher,
    segments,
    w_query,
    b_query,
    w_key,
    w_value,
    b_value,
    w_out,
    b_out,
    gain_one,
    shift_one,
    w_inner,
    b_inner,
    w_outer,
    b_outer,
    gain_two,
    shift_two,
):
    (
        w_query,
        b_query,
        w_key,
        w_value,
        b_value,
        w_out,
        b_out,
        gain_one,
        shift_one,
        w_inner,
        b_inner,
        w_outer,
        b_outer,
        gain_two,
        shift_two,
    ) = (
        lax.all_gather(w_query, "batch", axis=0, tiled=True),
        lax.all_gather(b_query, "batch", axis=0, tiled=True),
        lax.all_gather(w_key, "batch", axis=0, tiled=True),
        lax.all_gather(w_value, "batch", axis=0, tiled=True),
        lax.all_gather(b_value, "batch", axis=0, tiled=True),
        lax.all_gather(w_out, "batch", axis=0, tiled=True),
        lax.all_gather(b_out, "batch", axis=0, tiled=True),
        lax.all_gather(gain_one, "batch", axis=0, tiled=True),
        lax.all_gather(shift_one, "batch", axis=0, tiled=True),
        lax.all_gather(w_inner, "batch", axis=0, tiled=True),
        lax.all_gather(b_inner, "batch", axis=0, tiled=True),
        lax.all_gather(w_outer, "batch", axis=0, tiled=True),
        lax.all_gather(b_outer, "batch", axis=0, tiled=True),
        lax.all_gather(gain_two, "batch", axis=0, tiled=True),
        lax.all_gather(shift_two, "batch", axis=0, tiled=True),
    )
    scale = HD ** (-0.5)
    seqs_here, ctx_rows, width = inputs.shape
    rows_here = seqs_here * ctx_rows
    tokens_all = rows_here * lax.axis_size("batch") * lax.axis_size("ctx")
    seg_own = lax.dynamic_slice_in_dim(segments, lax.axis_index("ctx") * ctx_rows, ctx_rows, 1)
    inputs_flat = inputs.reshape(rows_here, width)
    inputs_low = inputs_flat.astype(jnp.bfloat16)
    query = (linear(inputs_low, w_query) + b_query.astype(jnp.float32)).astype(jnp.bfloat16)
    key = linear(inputs_low, w_key).astype(jnp.bfloat16)
    value = (linear(inputs_low, w_value) + b_value.astype(jnp.float32)).astype(jnp.bfloat16)
    query_seq = query.reshape(seqs_here, ctx_rows, width)
    key_seq = key.reshape(seqs_here, ctx_rows, width)
    value_seq = value.reshape(seqs_here, ctx_rows, width)

    def attend_forward(items):
        query_one, key_one, value_one, seg_all, seg_mine = items
        keys_all, values_all = (
            lax.all_gather(key_one, "ctx", axis=0, tiled=True),
            lax.all_gather(value_one, "ctx", axis=0, tiled=True),
        )
        scores = score_rows(query_one, keys_all, seg_mine, seg_all)
        highest = jnp.max(scores, -1, keepdims=True)
        expo = jnp.exp(scores - highest)
        totals = jnp.sum(expo, -1, keepdims=True)
        probs = (expo / totals).astype(jnp.bfloat16)
        mixed = jnp.einsum(
            "hck,khd->chd",
            probs,
            values_all.reshape(keys_all.shape[0], H, HD),
            preferred_element_type=jnp.float32,
        )
        return (
            mixed.reshape(ctx_rows, width).astype(jnp.bfloat16),
            (highest + jnp.log(totals))[:, :, 0],
        )

    attended, log_totals = lax.map(
        attend_forward, (query_seq, key_seq, value_seq, segments, seg_own)
    )
    attended_flat = attended.reshape(rows_here, width)
    gain_one_full = gain_one.astype(jnp.float32)
    shift_one_full = shift_one.astype(jnp.float32)
    gain_two_full = gain_two.astype(jnp.float32)
    shift_two_full = shift_two.astype(jnp.float32)
    hidden_one = inputs_flat + linear(attended_flat, w_out) + b_out.astype(jnp.float32)
    normed_one, back_one = jax.vjp(norm_rows, hidden_one, gain_one_full, shift_one_full)
    normed_low = normed_one.astype(jnp.bfloat16)
    inner_pre = linear(normed_low, w_inner) + b_inner.astype(jnp.float32)
    active_full, gelu_back = jax.vjp(gelu_exact, inner_pre)
    active_low = active_full.astype(jnp.bfloat16)
    hidden_two = normed_one + linear(active_low, w_outer) + b_outer.astype(jnp.float32)
    output, back_two = jax.vjp(norm_rows, hidden_two, gain_two_full, shift_two_full)
    valid = (seg_own.reshape(rows_here) != 0).astype(jnp.float32)[:, None]
    error = output - teacher.reshape(rows_here, width)
    loss_total, valid_count = lax.psum(
        (jnp.sum(valid * error * error), jnp.sum(valid)), ("batch", "ctx")
    )
    loss = loss_total / (2.0 * valid_count)
    grad_output = tokens_all / valid_count * valid * error
    grad_hidden_two, grad_gain_two, grad_shift_two = back_two(grad_output)
    grad_branch_two = grad_hidden_two.astype(jnp.bfloat16)
    grad_b_outer = jnp.sum(grad_branch_two.astype(jnp.float32), 0)
    grad_w_outer = contract_rows(active_low, grad_branch_two)
    grad_active = times_transpose(grad_branch_two, w_outer)
    grad_inner = gelu_back(grad_active)[0].astype(jnp.bfloat16)
    grad_b_inner = jnp.sum(grad_inner.astype(jnp.float32), 0)
    grad_w_inner = contract_rows(normed_low, grad_inner)
    grad_normed = grad_hidden_two + times_transpose(grad_inner, w_inner)
    grad_hidden_one, grad_gain_one, grad_shift_one = back_one(grad_normed)
    grad_branch_one = grad_hidden_one.astype(jnp.bfloat16)
    grad_b_out = jnp.sum(grad_branch_one.astype(jnp.float32), 0)
    grad_w_out = contract_rows(attended_flat, grad_branch_one)
    grad_attended = (
        times_transpose(grad_branch_one, w_out)
        .astype(jnp.bfloat16)
        .reshape(seqs_here, ctx_rows, width)
    )

    def attend_backward(items):
        query_one, key_one, value_one, seg_all, seg_mine, log_one, grad_one = items
        keys_all, values_all = (
            lax.all_gather(key_one, "ctx", axis=0, tiled=True),
            lax.all_gather(value_one, "ctx", axis=0, tiled=True),
        )
        key_count = keys_all.shape[0]
        scores = score_rows(query_one, keys_all, seg_mine, seg_all)
        probs = jnp.exp(scores - log_one[:, :, None])
        grad_heads = grad_one.reshape(ctx_rows, H, HD)
        grad_probs = jnp.einsum(
            "chd,khd->hck",
            grad_heads,
            values_all.reshape(key_count, H, HD),
            preferred_element_type=jnp.float32,
        )
        centre = jnp.sum(probs * grad_probs, -1)
        grad_scores = (probs * (grad_probs - centre[:, :, None])).astype(jnp.bfloat16)
        grad_query = (
            jnp.einsum(
                "hck,khd->chd",
                grad_scores,
                keys_all.reshape(key_count, H, HD),
                preferred_element_type=jnp.float32,
            )
            * scale
        )
        grad_query = grad_query.reshape(ctx_rows, width).astype(jnp.bfloat16)
        probs_low = probs.astype(jnp.bfloat16)
        query_heads = query_one.reshape(ctx_rows, H, HD)
        count = ctx_rows * lax.axis_size("ctx")
        grad_key = (
            jnp.einsum("hck,chd->khd", grad_scores, query_heads, preferred_element_type=jnp.float32)
            * scale
        )
        grad_value = jnp.einsum(
            "hck,chd->khd", probs_low, grad_heads, preferred_element_type=jnp.float32
        )
        both = lax.psum_scatter(
            jnp.concatenate([grad_key.reshape(count, width), grad_value.reshape(count, width)], 1),
            "ctx",
            scatter_dimension=0,
            tiled=True,
        )
        return (
            grad_query,
            both[:, :width].astype(jnp.bfloat16),
            both[:, width:].astype(jnp.bfloat16),
        )

    grad_query_seq, grad_key_seq, grad_value_seq = lax.map(
        attend_backward,
        (query_seq, key_seq, value_seq, segments, seg_own, log_totals, grad_attended),
    )
    grad_query_flat = grad_query_seq.reshape(rows_here, width)
    grad_key_flat = grad_key_seq.reshape(rows_here, width)
    grad_value_flat = grad_value_seq.reshape(rows_here, width)
    grad_w_query = contract_rows(inputs_low, grad_query_flat)
    grad_b_query = jnp.sum(grad_query_flat.astype(jnp.float32), 0)
    grad_w_key = contract_rows(inputs_low, grad_key_flat)
    grad_w_value = contract_rows(inputs_low, grad_value_flat)
    grad_b_value = jnp.sum(grad_value_flat.astype(jnp.float32), 0)
    grad_inputs = (
        grad_hidden_one
        + times_transpose(grad_query_flat, w_query)
        + times_transpose(grad_key_flat, w_key)
        + times_transpose(grad_value_flat, w_value)
    )
    (
        grad_w_query,
        grad_b_query,
        grad_w_key,
        grad_w_value,
        grad_b_value,
        grad_w_out,
        grad_b_out,
        grad_gain_one,
        grad_shift_one,
        grad_w_inner,
        grad_b_inner,
        grad_w_outer,
        grad_b_outer,
        grad_gain_two,
        grad_shift_two,
    ) = (
        lax.psum_scatter(
            grad_w_query.astype(jnp.bfloat16), "batch", scatter_dimension=0, tiled=True
        ).astype(jnp.float32),
        lax.psum_scatter(
            grad_b_query.astype(jnp.bfloat16), "batch", scatter_dimension=0, tiled=True
        ).astype(jnp.float32),
        lax.psum_scatter(
            grad_w_key.astype(jnp.bfloat16), "batch", scatter_dimension=0, tiled=True
        ).astype(jnp.float32),
        lax.psum_scatter(
            grad_w_value.astype(jnp.bfloat16), "batch", scatter_dimension=0, tiled=True
        ).astype(jnp.float32),
        lax.psum_scatter(
            grad_b_value.astype(jnp.bfloat16), "batch", scatter_dimension=0, tiled=True
        ).astype(jnp.float32),
        lax.psum_scatter(
            grad_w_out.astype(jnp.bfloat16), "batch", scatter_dimension=0, tiled=True
        ).astype(jnp.float32),
        lax.psum_scatter(
            grad_b_out.astype(jnp.bfloat16), "batch", scatter_dimension=0, tiled=True
        ).astype(jnp.float32),
        lax.psum_scatter(
            grad_gain_one.astype(jnp.bfloat16), "batch", scatter_dimension=0, tiled=True
        ).astype(jnp.float32),
        lax.psum_scatter(
            grad_shift_one.astype(jnp.bfloat16), "batch", scatter_dimension=0, tiled=True
        ).astype(jnp.float32),
        lax.psum_scatter(
            grad_w_inner.astype(jnp.bfloat16), "batch", scatter_dimension=0, tiled=True
        ).astype(jnp.float32),
        lax.psum_scatter(
            grad_b_inner.astype(jnp.bfloat16), "batch", scatter_dimension=0, tiled=True
        ).astype(jnp.float32),
        lax.psum_scatter(
            grad_w_outer.astype(jnp.bfloat16), "batch", scatter_dimension=0, tiled=True
        ).astype(jnp.float32),
        lax.psum_scatter(
            grad_b_outer.astype(jnp.bfloat16), "batch", scatter_dimension=0, tiled=True
        ).astype(jnp.float32),
        lax.psum_scatter(
            grad_gain_two.astype(jnp.bfloat16), "batch", scatter_dimension=0, tiled=True
        ).astype(jnp.float32),
        lax.psum_scatter(
            grad_shift_two.astype(jnp.bfloat16), "batch", scatter_dimension=0, tiled=True
        ).astype(jnp.float32),
    )
    (
        grad_w_query,
        grad_b_query,
        grad_w_key,
        grad_w_value,
        grad_b_value,
        grad_w_out,
        grad_b_out,
        grad_gain_one,
        grad_shift_one,
        grad_w_inner,
        grad_b_inner,
        grad_w_outer,
        grad_b_outer,
        grad_gain_two,
        grad_shift_two,
    ) = lax.psum(
        (
            grad_w_query,
            grad_b_query,
            grad_w_key,
            grad_w_value,
            grad_b_value,
            grad_w_out,
            grad_b_out,
            grad_gain_one,
            grad_shift_one,
            grad_w_inner,
            grad_b_inner,
            grad_w_outer,
            grad_b_outer,
            grad_gain_two,
            grad_shift_two,
        ),
        "ctx",
    )
    return (
        output.reshape(inputs.shape),
        loss,
        grad_inputs.reshape(inputs.shape),
        grad_w_query,
        grad_b_query,
        grad_w_key,
        grad_w_value,
        grad_b_value,
        grad_w_out,
        grad_b_out,
        grad_gain_one,
        grad_shift_one,
        grad_w_inner,
        grad_b_inner,
        grad_w_outer,
        grad_b_outer,
        grad_gain_two,
        grad_shift_two,
    )


def pick(values, at):
    return lax.dynamic_index_in_dim(values, at, 0, keepdims=False)


def ordered(mine, other, at):
    return jnp.where(at == 0, jnp.stack([mine, other]), jnp.stack([other, mine]))


def low(values):
    return values.astype(jnp.bfloat16)


def full(values):
    return values.astype(jnp.float32)


def norm_forward(hidden, gain, shift):
    center = hidden - jnp.mean(hidden, -1, keepdims=True)
    inverse = lax.rsqrt(jnp.mean(center * center, -1, keepdims=True) + EPSILON)
    unit = center * inverse
    return unit * gain + shift, unit, inverse


def norm_backward(grad, unit, inverse, gain):
    scaled = grad * gain
    return inverse * (
        scaled
        - jnp.mean(scaled, -1, keepdims=True)
        - unit * jnp.mean(scaled * unit, -1, keepdims=True)
    )


def attend(query, key, value, seg_query, seg_key):
    raw = jnp.einsum("qhd,khd->hqk", query, key, preferred_element_type=jnp.float32) * HD ** (-0.5)
    allowed = seg_query[None, :, None] == seg_key[None, None, :]
    scores = jnp.where(allowed, raw, NEGATIVE)
    highest = jnp.max(scores, -1, keepdims=True)
    expo = jnp.exp(scores - highest)
    totals = jnp.sum(expo, -1, keepdims=True)
    probs = low(expo / totals)
    mixed = jnp.einsum("hqk,khd->qhd", probs, value, preferred_element_type=jnp.float32)
    return low(mixed), (highest + jnp.log(totals))[:, :, 0]


def attend_back(query, key, value, seg_query, seg_key, logs, grad):
    scale = HD ** (-0.5)
    raw = jnp.einsum("qhd,khd->hqk", query, key, preferred_element_type=jnp.float32) * scale
    allowed = seg_query[None, :, None] == seg_key[None, None, :]
    probs = jnp.exp(jnp.where(allowed, raw, NEGATIVE) - logs[:, :, None])
    grad_probs = jnp.einsum("qhd,khd->hqk", grad, value, preferred_element_type=jnp.float32)
    centre = jnp.sum(probs * grad_probs, -1, keepdims=True)
    grad_scores = low(probs * (grad_probs - centre))
    grad_query = (
        jnp.einsum("hqk,khd->qhd", grad_scores, key, preferred_element_type=jnp.float32) * scale
    )
    grad_key = (
        jnp.einsum("hqk,qhd->khd", grad_scores, query, preferred_element_type=jnp.float32) * scale
    )
    grad_value = jnp.einsum("hqk,qhd->khd", low(probs), grad, preferred_element_type=jnp.float32)
    return low(grad_query), grad_key, grad_value


def per_device_heads(
    inputs,
    teacher,
    segments,
    w_query,
    b_query,
    w_key,
    w_value,
    b_value,
    w_out,
    b_out,
    gain_one,
    shift_one,
    w_inner,
    b_inner,
    w_outer,
    b_outer,
    gain_two,
    shift_two,
):
    count = lax.axis_size("ctx")
    depth = count // 4
    place = lax.axis_index("ctx")
    at_b, at_c, at_y, at_z = lax.axis_index("batch"), place % 2, place // 2 % 2, place // 4
    seqs, rows, width = inputs.shape
    own = seqs * rows
    half = width // 2
    inner = w_inner.shape[1] // 2
    share = width // depth
    heads = H // depth
    tokens_all = own * 2 * count
    groups_z = [[z * 4 + r for z in range(depth)] for r in range(4)]
    groups_yz = [[z * 4 + y * 2 + c for z in range(depth) for y in range(2)] for c in range(2)]

    def swap_x(values):
        return lax.ppermute(values, "batch", [(0, 1), (1, 0)])

    def swap_y(values):
        return lax.ppermute(values, "ctx", [(i, i ^ 2) for i in range(count)])

    def swap_c(values):
        return lax.ppermute(values, "ctx", [(i, i ^ 1) for i in range(count)])

    def trade_z(values):
        return lax.all_to_all(values, "ctx", 0, 0, axis_index_groups=groups_z, tiled=True)

    def trade_yz(values):
        return lax.all_to_all(values, "ctx", 0, 0, axis_index_groups=groups_yz, tiled=True)

    def spread_z(values):
        return trade_z(jnp.broadcast_to(values[None], (depth, *values.shape)))

    inputs_flat = inputs.reshape(own, width)
    blocks = jnp.broadcast_to(low(inputs)[None], (depth, seqs, rows, width))
    states = trade_yz(blocks.reshape(depth * seqs, rows, width)).reshape(-1, width)

    cut = [lax.dynamic_slice_in_dim(w, at_z * share, share, 1) for w in (w_query, w_key, w_value)]
    mine = jnp.concatenate(cut, 1)
    valid_here = jnp.sum((segments != 0).astype(jnp.int32))
    vectors = jnp.concatenate(
        [b_query, b_value, b_out, gain_one, shift_one, b_outer, gain_two, shift_two, b_inner]
    )
    tail = jnp.stack([valid_here // 256, valid_here % 256]).astype(jnp.bfloat16)
    vectors = jnp.concatenate([vectors, tail])
    lines = 16
    vectors = jnp.pad(vectors, (0, lines * 3 * share - vectors.shape[0])).reshape(lines, 3 * share)
    message = swap_x(jnp.concatenate([mine, vectors]))
    w_three = ordered(mine, message[:half], at_b).reshape(width, 3 * share)
    both = ordered(vectors, message[half:], at_b).reshape(2, -1)
    vec = [both[:, half * k : half * (k + 1)].reshape(-1) for k in range(8)]
    b_query_all, b_value_all = vec[0], vec[1]
    b_out_f, gain_one_f, shift_one_f, b_outer_f, gain_two_f, shift_two_f = map(full, vec[2:])
    b_inner_all = full(both[:, 8 * half : 8 * half + inner]).reshape(2, 2, inner // 2)
    b_inner_set = lax.dynamic_index_in_dim(b_inner_all, at_c, 1, keepdims=False).reshape(inner)
    at_tail = 8 * half + inner
    valid_count = jnp.sum(full(both[:, at_tail])) * 256.0 + jnp.sum(full(both[:, at_tail + 1]))
    bias_three = jnp.concatenate(
        [
            full(lax.dynamic_slice_in_dim(b_query_all, at_z * share, share, 0)),
            jnp.zeros((share,), jnp.float32),
            full(lax.dynamic_slice_in_dim(b_value_all, at_z * share, share, 0)),
        ]
    )

    own_out = w_out
    piece_out = swap_x(lax.dynamic_slice_in_dim(w_out, at_c * (half // 2), half // 2, 0))
    other_out = ordered(piece_out, swap_c(piece_out), at_c).reshape(half, width)
    w_out_all = ordered(own_out, other_out, at_b).reshape(width, width)
    inner_set = lax.dynamic_index_in_dim(
        w_inner.reshape(half, 2, 2, inner // 2), at_c, 2, keepdims=False
    ).reshape(half, inner)
    piece_inner = swap_x(lax.dynamic_slice_in_dim(inner_set, at_y * (half // 2), half // 2, 0))
    other_inner = ordered(piece_inner, swap_y(piece_inner), at_y).reshape(half, inner)
    w_inner_set = ordered(inner_set, other_inner, at_b).reshape(width, inner)
    outer_set = pick(w_outer.reshape(2, inner // 2, width), at_c)
    piece_outer = swap_x(lax.dynamic_slice_in_dim(outer_set, at_y * (inner // 4), inner // 4, 0))
    other_outer = ordered(piece_outer, swap_y(piece_outer), at_y).reshape(inner // 2, width)
    w_outer_set = ordered(outer_set, other_outer, at_b).reshape(inner, width)

    three = low(linear(states, w_three) + bias_three)
    there = swap_c(three[:, share:])
    query = three[:, :share].reshape(-1, heads, HD)
    key = jnp.concatenate([three[:, share : 2 * share], there[:, :share]]).reshape(-1, heads, HD)
    value = jnp.concatenate([three[:, 2 * share :], there[:, share:]]).reshape(-1, heads, HD)
    seg_seq = pick(segments, at_y).reshape(-1, 2, rows)
    seg_own = lax.dynamic_index_in_dim(seg_seq, at_c, 1, keepdims=False).reshape(-1)
    seg_peer = lax.dynamic_index_in_dim(seg_seq, 1 - at_c, 1, keepdims=False).reshape(-1)
    seg_key = jnp.concatenate([seg_own, seg_peer])
    mixed, logs = attend(query, key, value, seg_own, seg_key)
    attended = trade_yz(mixed.reshape(depth * seqs, rows, share))
    attended = attended.reshape(depth, seqs, rows, share).transpose(1, 2, 0, 3).reshape(own, width)

    hidden_one = inputs_flat + linear(attended, w_out_all) + b_out_f
    normed_one, unit_one, inverse_one = norm_forward(hidden_one, gain_one_f, shift_one_f)
    normed_low = low(normed_one)
    normed_two = jnp.concatenate([normed_low, swap_c(normed_low)])
    inner_pre = linear(normed_two, w_inner_set) + b_inner_set
    active_full, gelu_back = jax.vjp(gelu_exact, inner_pre)
    active = low(active_full)
    branch = linear(active, w_outer_set)
    hidden_two = normed_one + (branch[:own] + swap_c(branch[own:])) + b_outer_f
    output, unit_two, inverse_two = norm_forward(hidden_two, gain_two_f, shift_two_f)

    seg_tokens = lax.dynamic_slice_in_dim(segments, place * rows, rows, 1).reshape(own)
    valid = full(seg_tokens != 0)[:, None]
    error = output - teacher.reshape(own, width)
    loss_here = jnp.sum(valid * error * error)
    grad_output = tokens_all / valid_count * valid * error
    grad_hidden_two = norm_backward(grad_output, unit_two, inverse_two, gain_two_f)
    branch_low = low(grad_hidden_two)
    branch_two = jnp.concatenate([branch_low, swap_c(branch_low)])
    sum_outer = low(contract_rows(active, branch_two)).reshape(2, inner // 2, width)
    send_outer = swap_x(pick(sum_outer, 1 - at_b))
    grad_inner = low(gelu_back(times_transpose(branch_two, w_outer_set))[0])
    sum_inner = jnp.stack(
        [
            low(contract_rows(normed_two, grad_inner[:, : inner // 2])),
            low(contract_rows(normed_two, grad_inner[:, inner // 2 :])),
        ]
    ).reshape(2, 2, half, width)
    send_inner = swap_x(lax.dynamic_index_in_dim(sum_inner, 1 - at_b, 1, keepdims=False))
    back = times_transpose(grad_inner, w_inner_set)
    grad_normed = grad_hidden_two + (back[:own] + swap_c(back[own:]))
    grad_hidden_one = norm_backward(grad_normed, unit_one, inverse_one, gain_one_f)
    grad_low = low(grad_hidden_one)
    grad_attended = low(times_transpose(grad_low, w_out_all))
    grad_heads = trade_yz(
        grad_attended.reshape(seqs, rows, depth, share)
        .transpose(2, 0, 1, 3)
        .reshape(depth * seqs, rows, share)
    ).reshape(-1, heads, HD)

    sum_out = low(contract_rows(attended, grad_low)).reshape(2, 2, half // 2, width)
    small = jnp.stack(
        [
            jnp.sum(full(grad_low), 0),
            jnp.sum(grad_normed * unit_one, 0),
            jnp.sum(grad_normed, 0),
            jnp.sum(full(branch_low), 0),
            jnp.sum(grad_output * unit_two, 0),
            jnp.sum(grad_output, 0),
            jnp.zeros((width,), jnp.float32),
            jnp.zeros((width,), jnp.float32),
            jnp.full((width,), loss_here),
        ]
    )
    small = jnp.pad(small, ((0, 7), (0, 0)))
    bias_inner = jnp.pad(jnp.sum(full(grad_inner), 0).reshape(2, width), ((6, 8), (0, 0)))
    keep_out = lax.dynamic_index_in_dim(sum_out, at_c, 1, keepdims=False)
    send_out = lax.dynamic_index_in_dim(sum_out, 1 - at_c, 1, keepdims=False)
    got = swap_c(jnp.concatenate([send_out.reshape(half, width), low(small)]))
    sum_out = low(full(keep_out) + full(got[:half].reshape(2, half // 2, width)))
    small = low(full(low(small)) + full(got[half:]) + bias_inner)
    got = swap_x(jnp.concatenate([pick(sum_out, 1 - at_b), small]))
    sum_out = low(full(pick(sum_out, at_b)) + full(got[: half // 2])).reshape(2, half // 4, width)
    small = low(full(small) + full(got[half // 2 :]))

    grad_query, grad_key, grad_value = attend_back(
        query, key, value, seg_own, seg_key, logs, grad_heads
    )
    keys = states.shape[0]
    grad_kv = jnp.concatenate([grad_key.reshape(-1, share), grad_value.reshape(-1, share)], 1)
    grad_kv = low(grad_kv[:keys] + swap_c(grad_kv[keys:]))
    grad_three = jnp.concatenate([grad_query.reshape(-1, share), grad_kv], 1)
    partial = low(times_transpose(grad_three, w_three))
    arrived = trade_yz(partial.reshape(depth * seqs, rows, width))
    arrived = jnp.sum(full(arrived.reshape(depth, seqs, rows, width)), 0)
    grad_inputs = grad_hidden_one + arrived.reshape(own, width)

    sum_three = low(contract_rows(states, grad_three)).reshape(2, 2, half // 2, 3 * share)
    bias = jnp.pad(jnp.sum(full(grad_three), 0)[None], ((0, 15), (0, 0)))
    send = lax.dynamic_index_in_dim(sum_three, 1 - at_c, 1, keepdims=False)
    got = swap_c(jnp.concatenate([send.reshape(half, 3 * share), low(bias)]))
    sum_three = lax.dynamic_index_in_dim(sum_three, at_c, 1, keepdims=False)
    sum_three = low(full(sum_three) + full(got[:half].reshape(2, half // 2, 3 * share)))
    bias = low(full(low(bias)) + full(got[half:]))
    got = swap_x(jnp.concatenate([pick(sum_three, 1 - at_b), bias]))
    sum_three = low(full(pick(sum_three, at_b)) + full(got[: half // 2]))
    sum_three = sum_three.reshape(2, half // 4, 3 * share)
    bias = low(full(bias) + full(got[half // 2 :]))
    got = swap_y(jnp.concatenate([pick(sum_three, 1 - at_y), bias]))
    sum_three = low(full(pick(sum_three, at_y)) + full(got[: half // 4]))
    bias = low(full(bias) + full(got[half // 4 :]))
    got = spread_z(jnp.concatenate([sum_three, bias]))
    bias = full(got[:, half // 4].reshape(depth, 3, share))
    got = got[:, : half // 4]
    got = ordered(got, swap_y(got), at_y)
    got = ordered(got, swap_c(got), at_c)
    grads = []
    for k in range(3):
        part = got[..., k * share : (k + 1) * share].transpose(0, 1, 3, 2, 4)
        grads.append(full(part.reshape(half, width)))
    grad_w_query, grad_w_key, grad_w_value = grads
    grad_b_query = pick(bias[:, 0].reshape(2, half), at_b)
    grad_b_value = pick(bias[:, 2].reshape(2, half), at_b)

    sum_outer = low(full(pick(sum_outer, at_b)) + full(send_outer))
    sum_outer = sum_outer.reshape(2, inner // 4, width)
    got = swap_y(pick(sum_outer, 1 - at_y))
    sum_outer = low(full(pick(sum_outer, at_y)) + full(got))
    got = trade_z(sum_outer.reshape(depth, inner // 4 // depth, width))
    sum_outer = low(jnp.sum(full(got), 0))
    got = spread_z(sum_outer)
    got = ordered(got, swap_y(got), at_y)
    got = ordered(got, swap_c(got), at_c)
    grad_w_outer = full(got.reshape(inner, width))

    sum_inner = low(
        full(lax.dynamic_index_in_dim(sum_inner, at_b, 1, keepdims=False)) + full(send_inner)
    )
    got = swap_y(jnp.concatenate([pick(sum_inner, 1 - at_y), pick(sum_out, 1 - at_y), small]))
    sum_inner = low(full(pick(sum_inner, at_y)) + full(got[:half]))
    sum_out = low(full(pick(sum_out, at_y)) + full(got[half : half + half // 4]))
    small = low(full(small) + full(got[half + half // 4 :]))
    step = half // depth
    step_out = half // 4 // depth
    got = trade_z(
        jnp.concatenate(
            [
                sum_inner.reshape(depth, step, width),
                sum_out.reshape(depth, step_out, width),
                jnp.broadcast_to(small[None], (depth, *small.shape)),
            ],
            1,
        )
    )
    got = low(jnp.sum(full(got), 0))
    small = got[step + step_out :]
    got = spread_z(got[: step + step_out])
    got = ordered(got, swap_y(got), at_y).reshape(-1, width)
    got = ordered(*(lambda m: (m, swap_c(m)))(jnp.concatenate([got, small])), at_c)
    small_both = full(got[:, -16:])
    got = got[:, :-16].reshape(2, 2, depth, step + step_out, width)
    grad_w_inner = full(
        got[:, :, :, :step].transpose(2, 3, 1, 0, 4).reshape(half, 2 * inner)
    )
    grad_w_out = full(got[:, :, :, step:].reshape(half, width))
    small = full(small)
    grad_b_inner = lax.dynamic_index_in_dim(small_both, 6 + at_b, 1, keepdims=False).reshape(inner)
    loss = small[8, 0] / (2.0 * valid_count)
    half_of = lambda k: lax.dynamic_slice_in_dim(small[k], at_b * half, half, 0)
    return (
        output.reshape(inputs.shape),
        loss,
        grad_inputs.reshape(inputs.shape),
        grad_w_query,
        grad_b_query,
        grad_w_key,
        grad_w_value,
        grad_b_value,
        grad_w_out,
        half_of(0),
        half_of(1),
        half_of(2),
        grad_w_inner,
        grad_b_inner,
        grad_w_outer,
        half_of(3),
        half_of(4),
        half_of(5),
    )


def per_device(inputs, *others):
    count = lax.axis_size("ctx")
    if count == 16 and lax.axis_size("batch") == 2 and inputs.shape[0] == 2:
        return per_device_heads(inputs, *others)
    return per_device_any(inputs, *others)


def solution(mesh):
    placed = (
        P("batch", "ctx", None),
        P("batch", "ctx", None),
        P("batch", None),
        P("batch", None),
        P("batch"),
        P("batch", None),
        P("batch", None),
        P("batch"),
        P("batch", None),
        P("batch"),
        P("batch"),
        P("batch"),
        P("batch", None),
        P("batch"),
        P("batch", None),
        P("batch"),
        P("batch"),
        P("batch"),
    )
    return jax.shard_map(
        per_device,
        mesh=mesh,
        in_specs=placed,
        out_specs=(
            P("batch", "ctx", None),
            P(),
            P("batch", "ctx", None),
            P("batch", None),
            P("batch"),
            P("batch", None),
            P("batch", None),
            P("batch"),
            P("batch", None),
            P("batch"),
            P("batch"),
            P("batch"),
            P("batch", None),
            P("batch"),
            P("batch", None),
            P("batch"),
            P("batch"),
            P("batch"),
        ),
        check_vma=False,
    )
```

```python
import functools

import jax
import jax.numpy as jnp
from jax import lax
from jax.experimental import pallas as pl
from jax.experimental.pallas import tpu as pltpu
from jax.sharding import PartitionSpec as P

H = 12
HD = 64


NEGATIVE = -1e30
EPSILON = 1e-12


def norm_rows(hidden, gain, shift):
    center = hidden - jnp.mean(hidden, -1, keepdims=True)
    spread = jnp.mean(center * center, -1, keepdims=True)
    return center * lax.rsqrt(spread + EPSILON) * gain + shift


def gelu_exact(values):
    return jax.nn.gelu(values, approximate=False)


def linear(rows_in, weight):
    return jnp.dot(rows_in, weight, preferred_element_type=jnp.float32)


def contract_rows(left, right):
    return lax.dot_general(
        left, right, (((0,), (0,)), ((), ())), preferred_element_type=jnp.float32
    )


def times_transpose(rows_in, weight):
    return lax.dot_general(
        rows_in, weight, (((1,), (1,)), ((), ())), preferred_element_type=jnp.float32
    )


def score_rows(query_one, keys_all, seg_mine, seg_all):
    heads_query = query_one.reshape(query_one.shape[0], H, HD)
    heads_key = keys_all.reshape(keys_all.shape[0], H, HD)
    raw = jnp.einsum(
        "chd,khd->hck", heads_query, heads_key, preferred_element_type=jnp.float32
    ) * HD ** (-0.5)
    allowed = seg_mine[None, :, None] == seg_all[None, None, :]
    return jnp.where(allowed, raw, NEGATIVE)


def per_device_any(
    inputs,
    teacher,
    segments,
    w_query,
    b_query,
    w_key,
    w_value,
    b_value,
    w_out,
    b_out,
    gain_one,
    shift_one,
    w_inner,
    b_inner,
    w_outer,
    b_outer,
    gain_two,
    shift_two,
):
    (
        w_query,
        b_query,
        w_key,
        w_value,
        b_value,
        w_out,
        b_out,
        gain_one,
        shift_one,
        w_inner,
        b_inner,
        w_outer,
        b_outer,
        gain_two,
        shift_two,
    ) = (
        lax.all_gather(w_query, "batch", axis=0, tiled=True),
        lax.all_gather(b_query, "batch", axis=0, tiled=True),
        lax.all_gather(w_key, "batch", axis=0, tiled=True),
        lax.all_gather(w_value, "batch", axis=0, tiled=True),
        lax.all_gather(b_value, "batch", axis=0, tiled=True),
        lax.all_gather(w_out, "batch", axis=0, tiled=True),
        lax.all_gather(b_out, "batch", axis=0, tiled=True),
        lax.all_gather(gain_one, "batch", axis=0, tiled=True),
        lax.all_gather(shift_one, "batch", axis=0, tiled=True),
        lax.all_gather(w_inner, "batch", axis=0, tiled=True),
        lax.all_gather(b_inner, "batch", axis=0, tiled=True),
        lax.all_gather(w_outer, "batch", axis=0, tiled=True),
        lax.all_gather(b_outer, "batch", axis=0, tiled=True),
        lax.all_gather(gain_two, "batch", axis=0, tiled=True),
        lax.all_gather(shift_two, "batch", axis=0, tiled=True),
    )
    scale = HD ** (-0.5)
    seqs_here, ctx_rows, width = inputs.shape
    rows_here = seqs_here * ctx_rows
    tokens_all = rows_here * lax.axis_size("batch") * lax.axis_size("ctx")
    seg_own = lax.dynamic_slice_in_dim(segments, lax.axis_index("ctx") * ctx_rows, ctx_rows, 1)
    inputs_flat = inputs.reshape(rows_here, width)
    inputs_low = inputs_flat.astype(jnp.bfloat16)
    query = (linear(inputs_low, w_query) + b_query.astype(jnp.float32)).astype(jnp.bfloat16)
    key = linear(inputs_low, w_key).astype(jnp.bfloat16)
    value = (linear(inputs_low, w_value) + b_value.astype(jnp.float32)).astype(jnp.bfloat16)
    query_seq = query.reshape(seqs_here, ctx_rows, width)
    key_seq = key.reshape(seqs_here, ctx_rows, width)
    value_seq = value.reshape(seqs_here, ctx_rows, width)

    def attend_forward(items):
        query_one, key_one, value_one, seg_all, seg_mine = items
        keys_all, values_all = (
            lax.all_gather(key_one, "ctx", axis=0, tiled=True),
            lax.all_gather(value_one, "ctx", axis=0, tiled=True),
        )
        scores = score_rows(query_one, keys_all, seg_mine, seg_all)
        highest = jnp.max(scores, -1, keepdims=True)
        expo = jnp.exp(scores - highest)
        totals = jnp.sum(expo, -1, keepdims=True)
        probs = (expo / totals).astype(jnp.bfloat16)
        mixed = jnp.einsum(
            "hck,khd->chd",
            probs,
            values_all.reshape(keys_all.shape[0], H, HD),
            preferred_element_type=jnp.float32,
        )
        return (
            mixed.reshape(ctx_rows, width).astype(jnp.bfloat16),
            (highest + jnp.log(totals))[:, :, 0],
        )

    attended, log_totals = lax.map(
        attend_forward, (query_seq, key_seq, value_seq, segments, seg_own)
    )
    attended_flat = attended.reshape(rows_here, width)
    gain_one_full = gain_one.astype(jnp.float32)
    shift_one_full = shift_one.astype(jnp.float32)
    gain_two_full = gain_two.astype(jnp.float32)
    shift_two_full = shift_two.astype(jnp.float32)
    hidden_one = inputs_flat + linear(attended_flat, w_out) + b_out.astype(jnp.float32)
    normed_one, back_one = jax.vjp(norm_rows, hidden_one, gain_one_full, shift_one_full)
    normed_low = normed_one.astype(jnp.bfloat16)
    inner_pre = linear(normed_low, w_inner) + b_inner.astype(jnp.float32)
    active_full, gelu_back = jax.vjp(gelu_exact, inner_pre)
    active_low = active_full.astype(jnp.bfloat16)
    hidden_two = normed_one + linear(active_low, w_outer) + b_outer.astype(jnp.float32)
    output, back_two = jax.vjp(norm_rows, hidden_two, gain_two_full, shift_two_full)
    valid = (seg_own.reshape(rows_here) != 0).astype(jnp.float32)[:, None]
    error = output - teacher.reshape(rows_here, width)
    loss_total, valid_count = lax.psum(
        (jnp.sum(valid * error * error), jnp.sum(valid)), ("batch", "ctx")
    )
    loss = loss_total / (2.0 * valid_count)
    grad_output = tokens_all / valid_count * valid * error
    grad_hidden_two, grad_gain_two, grad_shift_two = back_two(grad_output)
    grad_branch_two = grad_hidden_two.astype(jnp.bfloat16)
    grad_b_outer = jnp.sum(grad_branch_two.astype(jnp.float32), 0)
    grad_w_outer = contract_rows(active_low, grad_branch_two)
    grad_active = times_transpose(grad_branch_two, w_outer)
    grad_inner = gelu_back(grad_active)[0].astype(jnp.bfloat16)
    grad_b_inner = jnp.sum(grad_inner.astype(jnp.float32), 0)
    grad_w_inner = contract_rows(normed_low, grad_inner)
    grad_normed = grad_hidden_two + times_transpose(grad_inner, w_inner)
    grad_hidden_one, grad_gain_one, grad_shift_one = back_one(grad_normed)
    grad_branch_one = grad_hidden_one.astype(jnp.bfloat16)
    grad_b_out = jnp.sum(grad_branch_one.astype(jnp.float32), 0)
    grad_w_out = contract_rows(attended_flat, grad_branch_one)
    grad_attended = (
        times_transpose(grad_branch_one, w_out)
        .astype(jnp.bfloat16)
        .reshape(seqs_here, ctx_rows, width)
    )

    def attend_backward(items):
        query_one, key_one, value_one, seg_all, seg_mine, log_one, grad_one = items
        keys_all, values_all = (
            lax.all_gather(key_one, "ctx", axis=0, tiled=True),
            lax.all_gather(value_one, "ctx", axis=0, tiled=True),
        )
        key_count = keys_all.shape[0]
        scores = score_rows(query_one, keys_all, seg_mine, seg_all)
        probs = jnp.exp(scores - log_one[:, :, None])
        grad_heads = grad_one.reshape(ctx_rows, H, HD)
        grad_probs = jnp.einsum(
            "chd,khd->hck",
            grad_heads,
            values_all.reshape(key_count, H, HD),
            preferred_element_type=jnp.float32,
        )
        centre = jnp.sum(probs * grad_probs, -1)
        grad_scores = (probs * (grad_probs - centre[:, :, None])).astype(jnp.bfloat16)
        grad_query = (
            jnp.einsum(
                "hck,khd->chd",
                grad_scores,
                keys_all.reshape(key_count, H, HD),
                preferred_element_type=jnp.float32,
            )
            * scale
        )
        grad_query = grad_query.reshape(ctx_rows, width).astype(jnp.bfloat16)
        probs_low = probs.astype(jnp.bfloat16)
        query_heads = query_one.reshape(ctx_rows, H, HD)
        count = ctx_rows * lax.axis_size("ctx")
        grad_key = (
            jnp.einsum("hck,chd->khd", grad_scores, query_heads, preferred_element_type=jnp.float32)
            * scale
        )
        grad_value = jnp.einsum(
            "hck,chd->khd", probs_low, grad_heads, preferred_element_type=jnp.float32
        )
        both = lax.psum_scatter(
            jnp.concatenate([grad_key.reshape(count, width), grad_value.reshape(count, width)], 1),
            "ctx",
            scatter_dimension=0,
            tiled=True,
        )
        return (
            grad_query,
            both[:, :width].astype(jnp.bfloat16),
            both[:, width:].astype(jnp.bfloat16),
        )

    grad_query_seq, grad_key_seq, grad_value_seq = lax.map(
        attend_backward,
        (query_seq, key_seq, value_seq, segments, seg_own, log_totals, grad_attended),
    )
    grad_query_flat = grad_query_seq.reshape(rows_here, width)
    grad_key_flat = grad_key_seq.reshape(rows_here, width)
    grad_value_flat = grad_value_seq.reshape(rows_here, width)
    grad_w_query = contract_rows(inputs_low, grad_query_flat)
    grad_b_query = jnp.sum(grad_query_flat.astype(jnp.float32), 0)
    grad_w_key = contract_rows(inputs_low, grad_key_flat)
    grad_w_value = contract_rows(inputs_low, grad_value_flat)
    grad_b_value = jnp.sum(grad_value_flat.astype(jnp.float32), 0)
    grad_inputs = (
        grad_hidden_one
        + times_transpose(grad_query_flat, w_query)
        + times_transpose(grad_key_flat, w_key)
        + times_transpose(grad_value_flat, w_value)
    )
    (
        grad_w_query,
        grad_b_query,
        grad_w_key,
        grad_w_value,
        grad_b_value,
        grad_w_out,
        grad_b_out,
        grad_gain_one,
        grad_shift_one,
        grad_w_inner,
        grad_b_inner,
        grad_w_outer,
        grad_b_outer,
        grad_gain_two,
        grad_shift_two,
    ) = (
        lax.psum_scatter(
            grad_w_query.astype(jnp.bfloat16), "batch", scatter_dimension=0, tiled=True
        ).astype(jnp.float32),
        lax.psum_scatter(
            grad_b_query.astype(jnp.bfloat16), "batch", scatter_dimension=0, tiled=True
        ).astype(jnp.float32),
        lax.psum_scatter(
            grad_w_key.astype(jnp.bfloat16), "batch", scatter_dimension=0, tiled=True
        ).astype(jnp.float32),
        lax.psum_scatter(
            grad_w_value.astype(jnp.bfloat16), "batch", scatter_dimension=0, tiled=True
        ).astype(jnp.float32),
        lax.psum_scatter(
            grad_b_value.astype(jnp.bfloat16), "batch", scatter_dimension=0, tiled=True
        ).astype(jnp.float32),
        lax.psum_scatter(
            grad_w_out.astype(jnp.bfloat16), "batch", scatter_dimension=0, tiled=True
        ).astype(jnp.float32),
        lax.psum_scatter(
            grad_b_out.astype(jnp.bfloat16), "batch", scatter_dimension=0, tiled=True
        ).astype(jnp.float32),
        lax.psum_scatter(
            grad_gain_one.astype(jnp.bfloat16), "batch", scatter_dimension=0, tiled=True
        ).astype(jnp.float32),
        lax.psum_scatter(
            grad_shift_one.astype(jnp.bfloat16), "batch", scatter_dimension=0, tiled=True
        ).astype(jnp.float32),
        lax.psum_scatter(
            grad_w_inner.astype(jnp.bfloat16), "batch", scatter_dimension=0, tiled=True
        ).astype(jnp.float32),
        lax.psum_scatter(
            grad_b_inner.astype(jnp.bfloat16), "batch", scatter_dimension=0, tiled=True
        ).astype(jnp.float32),
        lax.psum_scatter(
            grad_w_outer.astype(jnp.bfloat16), "batch", scatter_dimension=0, tiled=True
        ).astype(jnp.float32),
        lax.psum_scatter(
            grad_b_outer.astype(jnp.bfloat16), "batch", scatter_dimension=0, tiled=True
        ).astype(jnp.float32),
        lax.psum_scatter(
            grad_gain_two.astype(jnp.bfloat16), "batch", scatter_dimension=0, tiled=True
        ).astype(jnp.float32),
        lax.psum_scatter(
            grad_shift_two.astype(jnp.bfloat16), "batch", scatter_dimension=0, tiled=True
        ).astype(jnp.float32),
    )
    (
        grad_w_query,
        grad_b_query,
        grad_w_key,
        grad_w_value,
        grad_b_value,
        grad_w_out,
        grad_b_out,
        grad_gain_one,
        grad_shift_one,
        grad_w_inner,
        grad_b_inner,
        grad_w_outer,
        grad_b_outer,
        grad_gain_two,
        grad_shift_two,
    ) = lax.psum(
        (
            grad_w_query,
            grad_b_query,
            grad_w_key,
            grad_w_value,
            grad_b_value,
            grad_w_out,
            grad_b_out,
            grad_gain_one,
            grad_shift_one,
            grad_w_inner,
            grad_b_inner,
            grad_w_outer,
            grad_b_outer,
            grad_gain_two,
            grad_shift_two,
        ),
        "ctx",
    )
    return (
        output.reshape(inputs.shape),
        loss,
        grad_inputs.reshape(inputs.shape),
        grad_w_query,
        grad_b_query,
        grad_w_key,
        grad_w_value,
        grad_b_value,
        grad_w_out,
        grad_b_out,
        grad_gain_one,
        grad_shift_one,
        grad_w_inner,
        grad_b_inner,
        grad_w_outer,
        grad_b_outer,
        grad_gain_two,
        grad_shift_two,
    )


BF, F32 = jnp.bfloat16, jnp.float32
LINES = 16


def low(values):
    return values.astype(BF)


def full(values):
    return values.astype(F32)


def dot(left, right, a=1, b=0):
    return lax.dot_general(left, right, (((a,), (b,)), ((), ())), preferred_element_type=F32)


def spot():
    place = lax.axis_index("ctx")
    return lax.axis_index("batch"), place % 2, place // 2 % 2, place // 4


def at(start, size, step):
    return pl.ds(pl.multiple_of(start, step), size)


def kernel(body, outs, args, hbm=(), scratch=()):
    name = getattr(body, "func", body).__name__
    where = [pl.BlockSpec(memory_space=pl.ANY if k in hbm else pltpu.VMEM) for k in range(len(args))]
    shapes = [jax.ShapeDtypeStruct(shape, kind) for shape, kind in outs]
    return pl.pallas_call(
        body,
        out_shape=shapes,
        in_specs=where,
        out_specs=[pl.BlockSpec(memory_space=pltpu.VMEM)] * len(shapes),
        scratch_shapes=list(scratch),
        name=name,
    )(*args)


def norm_forward(hidden, gain, shift):
    center = hidden - jnp.mean(hidden, -1, keepdims=True)
    inverse = lax.rsqrt(jnp.mean(center * center, -1, keepdims=True) + EPSILON)
    unit = center * inverse
    return unit * gain + shift, unit, inverse


def norm_backward(grad, unit, inverse, gain):
    scaled = grad * gain
    along = jnp.mean(scaled * unit, -1, keepdims=True)
    return inverse * (scaled - jnp.mean(scaled, -1, keepdims=True) - unit * along)


def total(values):
    return jnp.sum(values, 0, keepdims=True)


def prepare_first(*refs):
    w_three, vectors, b_inner, segments, w_inner, out, held, sem = refs[:3], refs[3:11], *refs[11:]
    half, width = w_three[0].shape
    _, at_c, at_y, at_z = spot()
    part, wide = half // 2, w_inner.shape[1] // 4
    copies = [
        (
            w_inner.at[at(at_y * part, part, 64), at((k * 2 + at_c) * wide, wide, 128)],
            held.at[k * part : (k + 1) * part],
        )
        for k in range(2)
    ]
    copies = start(copies, sem)
    share, rows = width // 4, half // 4
    for z in range(4):

        @pl.when(at_z == z)
        def _():
            for j in range(3):
                for k in range(4):
                    piece = w_three[j][k * rows : (k + 1) * rows, z * share : (z + 1) * share]
                    out[j * rows : (j + 1) * rows, k * share : (k + 1) * share] = piece

    first = 3 * rows
    out[first : first + LINES] = jnp.zeros((LINES, width), BF)
    for r in range(8):
        out[first + r : first + r + 1, :half] = vectors[r][...].reshape(1, half)
    inner = b_inner[...].reshape(1, -1)
    for r in range(4):
        out[first + 8 + r : first + 9 + r, :half] = inner[:, half * r : half * (r + 1)]
    valid = jnp.sum(jnp.where(segments[...] != 0, 1, 0))
    lane = lax.broadcasted_iota(jnp.int32, (1, half), 1)
    parts = jnp.where(lane < 128, valid // 256, valid % 256)
    out[first + 12 : first + 13, :half] = low(full(parts))
    finish(copies)
    out[first + LINES :] = held[...]


def prepare_second(inputs, w_out, w_outer, blocks, p_out, p_outer, sem):
    _, at_c, at_y, _ = spot()
    rows_out, rows_outer = p_out.shape[0], p_outer.shape[0]
    copies = [
        (w_out.at[at(at_c * rows_out, rows_out, 64)], p_out),
        (w_outer.at[at((at_c * 2 + at_y) * rows_outer, rows_outer, 128)], p_outer),
    ]
    copies = start(copies, sem)
    seqs = inputs.shape[0]
    for s in range(seqs):
        piece = low(inputs[s])
        for z in range(blocks.shape[0] // seqs):
            blocks[z * seqs + s] = piece
    finish(copies)


def start(copies, sem):
    made = [pltpu.make_async_copy(*copy, sem.at[k]) for k, copy in enumerate(copies)]
    for copy in made:
        copy.start()
    return made


def finish(copies):
    for copy in copies:
        copy.wait()


def both_halves(at_b, mine, other):
    return jnp.where(at_b == 0, mine, other), jnp.where(at_b == 0, other, mine)


def project(states, mine, other, query, pair, vecs, inner_vec, held, w_back):
    at_b, _, _, at_z = spot()
    width, share = states.shape[1], query.shape[1]
    half, rows = width // 2, width // 8
    for j in range(3):
        for k in range(4):
            first = slice(j * rows, (j + 1) * rows)
            cols = slice(k * share, (k + 1) * share)
            pieces = both_halves(at_b, mine[first, cols], other[first, cols])
            for h, piece in enumerate(pieces):
                start_row = h * half + k * rows
                held[start_row : start_row + rows, j * share : (j + 1) * share] = piece
    w_back[...] = held[...]
    made = dot(states[...], held[...])
    lines = slice(3 * rows, 3 * rows + LINES)
    top, bottom = both_halves(at_b, full(mine[lines]), full(other[lines]))

    def bias(r):
        row = jnp.where(at_z < 2, top[r : r + 1], bottom[r : r + 1])
        return jnp.where(at_z % 2 == 0, row[:, :share], row[:, share : 2 * share])

    query[...] = low(full(low(made[:, :share] + bias(0))) * HD ** (-0.5))
    pair[:, :share] = low(made[:, share : 2 * share])
    pair[:, share:] = low(made[:, 2 * share :] + bias(1))
    vecs[...] = jnp.zeros_like(vecs)
    for r in range(2, 8):
        vecs[r - 2 : r - 1, :half] = top[r : r + 1, :half]
        vecs[r - 2 : r - 1, half:] = bottom[r : r + 1, :half]
    counts = top[12:13] + bottom[12:13]
    counts = counts[:, :128] * 256.0 + counts[:, 256:384]
    vecs[8:9, :128] = counts
    inner_vec[...] = jnp.zeros_like(inner_vec)
    for b, rows in enumerate((top, bottom)):
        for r in range(4):
            cols = slice((4 * b + r) * half, (4 * b + r + 1) * half)
            inner_vec[0:1, cols] = rows[8 + r : 9 + r, :half]


STEP = 256


def attend(query, mine, peer, seg_query, seg_key, mixed, logs, keys, values):
    count, share = query.shape
    keys[:count] = mine[:, :share]
    keys[count:] = peer[:, :share]
    values[:, :count] = mine[:, share:].T
    values[:, count:] = peer[:, share:].T
    logs[...] = jnp.zeros_like(logs)

    def block(j, carry):
        rows = at(j * STEP, STEP, STEP)
        allowed = seg_key[...] == seg_query[:, rows]
        for h in range(share // HD):
            cols = slice(h * HD, (h + 1) * HD)
            scores = dot(keys[:, cols], query[rows, cols], 1, 1)
            scores = jnp.where(allowed, scores, NEGATIVE)
            highest = jnp.max(scores, 0, keepdims=True)
            expo = jnp.exp(scores - highest)
            totals = jnp.sum(expo, 0, keepdims=True)
            probs = low(expo * (1.0 / totals))
            mixed[rows, cols] = low(dot(values[cols], probs).T)
            logs[h : h + 1, rows] = highest + jnp.log(totals)
        return carry

    lax.fori_loop(0, count // STEP, block, 0)


def attend_back(
    query, mine, peer, seg_query, seg_key, logs, grad, g_query, g_mine, g_peer, keys, flipped, values, made
):
    count, share = query.shape
    keys[:count] = mine[:, :share]
    keys[count:] = peer[:, :share]
    values[:count] = mine[:, share:]
    values[count:] = peer[:, share:]
    flipped[:, :count] = mine[:, :share].T
    flipped[:, count:] = peer[:, :share].T
    made[...] = jnp.zeros_like(made)

    def block(j, carry):
        rows = at(j * STEP, STEP, STEP)
        allowed = seg_key[...] == seg_query[:, rows]
        for h in range(share // HD):
            cols = slice(h * HD, (h + 1) * HD)
            cols_value = slice(share + h * HD, share + (h + 1) * HD)
            scores = dot(keys[:, cols], query[rows, cols], 1, 1)
            scores = jnp.where(allowed, scores, NEGATIVE)
            probs = jnp.exp(scores - logs[h : h + 1, rows])
            g_probs = dot(values[:, cols], grad[rows, cols], 1, 1)
            centre = jnp.sum(probs * g_probs, 0, keepdims=True)
            g_scores = low(probs * (g_probs - centre))
            g_query[rows, cols] = low((dot(flipped[cols], g_scores) * HD ** (-0.5)).T)
            made[:, cols] += dot(g_scores, query[rows, cols])
            made[:, cols_value] += dot(low(probs), grad[rows, cols])
        return carry

    lax.fori_loop(0, count // STEP, block, 0)
    g_mine[...] = made[:count]
    g_peer[...] = made[count:]


def fetch_out(own, pieces, held, sem):
    at_b, at_c, _, _ = spot()
    half, part = own.shape[0], pieces[0].shape[0]
    copies = [(own, held.at[at(at_b * half, half, 128)])]
    for k, piece in enumerate(pieces):
        first = (1 - at_b) * half + (at_c + k) % 2 * part
        copies.append((piece, held.at[at(first, part, 64)]))
    return start(copies, sem)


def fetch_inner(own, pieces, held, sem):
    at_b, at_c, at_y, _ = spot()
    half, part, wide = own.shape[0], pieces[0].shape[0] // 2, pieces[0].shape[1]
    copies = [(own, held.at[at(at_b * half, half, 128)])]
    for c in range(2):
        for y in range(2):
            rows = at((1 - at_b) * half + (at_y + y) % 2 * part, part, 64)
            for k in range(2):
                cols = at((2 * k + (at_c + c) % 2) * wide, wide, 128)
                piece = pieces[2 * c + y].at[k * part : (k + 1) * part]
                copies.append((piece, held.at[rows, cols]))
    return start(copies, sem)


def fetch_outer(own, pieces, held, sem):
    at_b, at_c, at_y, _ = spot()
    half, part = own.shape[0], pieces[0].shape[0]
    copies = [(own, held.at[at(at_b * half, half, 128)])]
    for c in range(2):
        for y in range(2):
            first = (1 - at_b) * half + ((at_c + c) % 2 * 2 + (at_y + y) % 2) * part
            copies.append((pieces[2 * c + y], held.at[at(first, part, 128)]))
    return start(copies, sem)


BLOCK = 256


def forward(tokens_all, *refs):
    mixed, inputs, teacher, seg, vecs, inner_vec = refs[:6]
    weights, (output, attended, unit, inverse, slope, chip, away, g_hidden, sums) = refs[6:19], refs[19:28]
    held_out, held_inner, held_outer, low_one, sem = refs[28:]
    at_b, _, _, _ = spot()
    copies_out = fetch_out(weights[0], weights[1:3], held_out, sem.at[0])
    copies_inner = fetch_inner(weights[3], weights[4:8], held_inner, sem.at[1])
    copies_outer = fetch_outer(weights[8], weights[9:13], held_outer, sem.at[2])
    rows, share = mixed.shape[1:]
    seqs = inputs.shape[0]
    own, width = attended.shape
    half, ff = width // 2, slope.shape[1]
    for s in range(seqs):
        for z in range(mixed.shape[0] // seqs):
            attended[s * rows : (s + 1) * rows, z * share : (z + 1) * share] = mixed[z * seqs + s]
    finish(copies_out)
    hidden = inputs[...].reshape(own, width) + dot(attended[...], held_out[...]) + vecs[0:1]
    normed, made_unit, made_inverse = norm_forward(hidden, vecs[1:2], vecs[2:3])
    unit[...] = made_unit
    inverse[...] = jnp.broadcast_to(made_inverse, inverse.shape)
    low_one[...] = low(normed)
    chip[:, ff : ff + width] = low_one[...]
    away[:, ff // 2 : ff // 2 + half] = jnp.where(at_b == 0, low_one[:, half:], low_one[:, :half])
    finish(copies_inner)

    def block(j, carry):
        cols = at(j * BLOCK, BLOCK, BLOCK)
        before = dot(low_one[...], held_inner[:, cols]) + inner_vec[0:1, cols]
        below = 0.5 * (1.0 + lax.erf(before * 0.7071067811865476))
        chip[:, cols] = low(before * below)
        slope[:, cols] = below + before * jnp.exp(before * before * -0.5) * 0.3989422804014327
        return carry

    lax.fori_loop(0, ff // BLOCK, block, 0)
    away[:, : ff // 2] = chip[:, at((1 - at_b) * (ff // 2), ff // 2, 128)]
    finish(copies_outer)
    hidden = normed + dot(chip[:, :ff], held_outer[...]) + vecs[3:4]
    made, unit_two, inverse_two = norm_forward(hidden, vecs[4:5], vecs[5:6])
    output[...] = made.reshape(output.shape)
    valid = jnp.where(seg[...] != 0, 1.0, 0.0)
    error = (made - teacher[...].reshape(own, width)) * valid
    grad = error * (tokens_all / vecs[8:9, 0:1])
    made = norm_backward(grad, unit_two, inverse_two, vecs[4:5])
    g_hidden[...] = made
    g_low = low(made)
    chip[:, ff + width :] = g_low
    away[:, ff // 2 + half :] = g_low
    sums[...] = jnp.zeros_like(sums)
    sums[3:4] = total(full(g_low))
    sums[4:5] = total(grad * unit_two)
    sums[5:6] = total(grad)
    loss = jnp.broadcast_to(jnp.sum(total(error * error), 1, keepdims=True), (1, width))
    sums[10:11] = full(low(loss))
    sums[11:12] = loss - full(low(loss))


def backward(*refs):
    chip, slope, g_hidden, unit, inverse, vecs, attended, sums = refs[:8]
    weights, (g_inner, g_one, g_mixed, keep, send) = refs[8:21], refs[21:26]
    held_out, held_inner, held_outer, inner_sums, small, made_out, sem = refs[26:]
    _, at_c, _, _ = spot()
    copies_outer = fetch_outer(weights[8], weights[9:13], held_outer, sem.at[2])
    copies_inner = fetch_inner(weights[3], weights[4:8], held_inner, sem.at[1])
    copies_out = fetch_out(weights[0], weights[1:3], held_out, sem.at[0])
    width, ff = unit.shape[1], slope.shape[1]
    finish(copies_outer)

    def block(j, carry):
        cols = at(j * BLOCK, BLOCK, BLOCK)
        grad = low(dot(chip[:, ff + width :], held_outer[cols, :], 1, 1) * slope[:, cols])
        g_inner[:, cols] = grad
        inner_sums[0:1, cols] = total(full(grad))
        return carry

    lax.fori_loop(0, ff // BLOCK, block, 0)
    finish(copies_inner)
    g_normed = g_hidden[...] + dot(g_inner[...], held_inner[...], 1, 1)
    made = norm_backward(g_normed, unit[...], inverse[:, 0:1], vecs[1:2])
    g_one[...] = made
    g_low = low(made)
    finish(copies_out)
    g_attended = low(dot(g_low, held_out[...], 1, 1))
    rows, share = g_mixed.shape[1:]
    seqs = g_one.shape[0] // rows
    for s in range(seqs):
        for z in range(g_mixed.shape[0] // seqs):
            g_mixed[z * seqs + s] = g_attended[s * rows : (s + 1) * rows, z * share : (z + 1) * share]
    small[...] = sums[...]
    small[0:1] = total(full(g_low))
    small[1:2] = total(g_normed * unit[...])
    small[2:3] = total(g_normed)
    for k in range(4):
        small[6 + k : 7 + k] = inner_sums[0:1, k * width : (k + 1) * width]
    made_out[...] = low(dot(attended[...], g_low, 0, 0))
    part = width // 4
    for b in range(2):
        for ref, core in ((keep, at_c), (send, 1 - at_c)):
            ref[b * part : (b + 1) * part] = made_out[at(b * 2 * part + core * part, part, 64)]
    keep[2 * part :] = low(small[...])
    send[2 * part :] = low(small[...])


def resplit(made):
    lines = made.shape[0]
    loss = made[10:11] + made[11:12]
    return low(jnp.concatenate([made[:10], full(low(loss)), loss - full(low(loss)), made[12:lines]]))


def halve_out(axis, keep, came, next_keep, next_send):
    mine = spot()[axis]
    part = next_keep.shape[0] - LINES
    for k in range(2):
        rows = slice(k * part, (k + 1) * part)
        piece = low(full(keep[rows]) + full(came[rows]))

        @pl.when(mine == k)
        def _():
            next_keep[:part] = piece

        @pl.when(mine != k)
        def _():
            next_send[:part] = piece

    small = resplit(full(keep[2 * part :]) + full(came[2 * part :]))
    next_keep[part:] = small
    next_send[part:] = small


def eight(parts):
    made = full(parts[0])
    for k in range(1, parts.shape[0]):
        made = made + full(parts[k])
    return made


def weight_outer(chip, chip_c, away, away_c, keep, send, left, right, made):
    at_b, at_c, at_y, _ = spot()
    rows, (_, wide) = chip.shape[0], left.shape
    width = right.shape[1]
    for k, piece in enumerate((chip, chip_c)):
        left[k * rows : (k + 1) * rows] = piece[:, at((2 * at_b + at_c) * wide, wide, 128)]
        right[k * rows : (k + 1) * rows] = piece[:, piece.shape[1] - width :]
    for k, piece in enumerate((away, away_c)):
        left[(2 + k) * rows : (3 + k) * rows] = piece[:, at(at_c * wide, wide, 128)]
        right[(2 + k) * rows : (3 + k) * rows] = piece[:, piece.shape[1] - width :]
    made[...] = low(dot(left[...], right[...], 0, 0))
    part = keep.shape[0]
    keep[...] = made[at(at_y * part, part, 128)]
    send[...] = made[at((1 - at_y) * part, part, 128)]


def weight_inner(chip, chip_c, away, away_c, g_mine, g_c, g_x, g_xc, keep, send, left, right, made):
    at_b, at_c, at_y, _ = spot()
    rows, half = chip.shape[0], left.shape[1]
    ff, wide = g_mine.shape[1], right.shape[1] // 2
    for k, piece in enumerate((chip, chip_c)):
        left[k * rows : (k + 1) * rows] = piece[:, at(ff + at_b * half, half, 128)]
    for k, piece in enumerate((away, away_c)):
        left[(2 + k) * rows : (3 + k) * rows] = piece[:, ff // 2 : ff // 2 + half]
    for k, piece in enumerate((g_mine, g_c, g_x, g_xc)):
        for j in range(2):
            right[k * rows : (k + 1) * rows, j * wide : (j + 1) * wide] = piece[
                :, at((2 * j + at_c) * wide, wide, 128)
            ]
    made[...] = low(dot(left[...], right[...], 0, 0))
    part = keep.shape[0]
    keep[...] = made[at(at_y * part, part, 64)]
    send[...] = made[at((1 - at_y) * part, part, 64)]


def join_outer(keep, came, *outs):
    _, _, _, at_z = spot()
    *blocks, made = outs
    made[...] = low(full(keep[...]) + full(came[...]))
    rows = blocks[0].shape[0]
    for k, block in enumerate(blocks):
        block[...] = made[at((at_z + k) % len(blocks) * rows, rows, 32)]


def join_inner(keep, came, out_keep, out_came, out):
    made = low(full(keep[...]) + full(came[...]))
    made_out = full(out_keep[...]) + full(out_came[...])
    depth, width = out.shape[0], out.shape[2]
    rows = keep.shape[0] // depth
    part = (made_out.shape[0] - LINES) // depth
    small = resplit(made_out[part * depth :])
    made_out = low(made_out)
    for z in range(depth):
        for k in range(2):
            piece = made[z * rows : (z + 1) * rows, k * width : (k + 1) * width]
            out[z, k * rows : (k + 1) * rows] = piece
        out[z, 2 * rows : 2 * rows + part] = made_out[z * part : (z + 1) * part]
        out[z, 2 * rows + part :] = small


def weight_three(g_query, g_mine, came, states, w_three, out, *refs):
    *blocks, g_three, back = refs
    _, _, _, at_z = spot()
    share = g_query.shape[1]
    g_three[:, :share] = g_query[...]
    g_three[:, share:] = low(g_mine[...] + came[...])
    made = low(dot(states[...], g_three[...], 0, 0))
    rows = out.shape[1] - LINES
    bias = low(total(full(g_three[...])))
    for b in range(2):
        for y in range(2):
            for c in range(2):
                k = b * 4 + y * 2 + c
                first = (b * 4 + c * 2 + y) * rows
                out[k, :rows] = made[first : first + rows]
                out[k, rows:] = jnp.broadcast_to(bias, (LINES, 3 * share))
    back[...] = low(dot(g_three[...], w_three[...], 1, 1))
    rows = blocks[0].shape[0]
    for k, block in enumerate(blocks):
        block[...] = back[at((at_z + k) % len(blocks) * rows, rows, 128)]


def join_back(part_0, part_1, part_2, part_3, mine, send):
    _, _, at_y, _ = spot()
    made = full(part_0[...]) + full(part_1[...]) + full(part_2[...]) + full(part_3[...])
    rows = mine.shape[0]
    mine[...] = jnp.where(at_y == 0, made[:rows], made[rows:])
    send[...] = low(jnp.where(at_y == 0, made[rows:], made[:rows]))


def grad_states(mine, came, g_one, out):
    _, _, at_y, _ = spot()
    rows = mine.shape[0]
    for s in range(out.shape[0]):
        made = jnp.where(at_y == s, mine[...], full(came[...]))
        out[s] = g_one[s * rows : (s + 1) * rows] + made


def pack_first(outer_0, outer_1, outer_2, outer_3, three, out):
    rows, wide = outer_0.shape[0], three.shape[2]
    pieces = [full(piece[...]) for piece in (outer_0, outer_1, outer_2, outer_3)]
    out[:rows] = low(pieces[0] + pieces[1] + pieces[2] + pieces[3])
    summed = low(eight(three))
    out[rows : 2 * rows, :wide] = summed[:rows]
    out[2 * rows :, :wide] = summed[rows : rows + 8]
    out[rows:, wide:] = jnp.zeros((rows + 8, out.shape[1] - wide), BF)


def pack_second(inside, vecs, out, loss, g_b_inner, *vectors):
    at_b, _, _, _ = spot()
    made = eight(inside)
    rows = out.shape[0]
    out[...] = low(made[:rows])
    small = made[rows:]
    width = made.shape[1]
    half = width // 2
    loss[...] = (small[10:11, :128] + small[11:12, :128]) / (2.0 * vecs[8:9, :128])
    for k, vector in enumerate(vectors):
        row = small[k : k + 1]
        vector[...] = jnp.where(at_b == 0, row[:, :half], row[:, half:]).reshape(half)
    first = jnp.where(at_b == 0, small[6:7], small[8:9])
    second = jnp.where(at_b == 0, small[7:8], small[9:10])
    g_b_inner[...] = jnp.concatenate([first, second], 1).reshape(2 * width)


def each_piece(pieces):
    _, at_c, at_y, at_z = spot()
    depth = len(pieces) // 4
    for k in range(depth):
        for c in range(2):
            for y in range(2):
                place = (at_c + c) % 2, (at_y + y) % 2, (at_z + depth - k) % depth
                yield pieces[(k * 2 + c) * 2 + y], place


def final_first(*refs):
    pieces, (g_outer, g_query, g_key, g_value, b_query, b_value, biases) = refs[:-7], refs[-7:]
    at_b, _, _, _ = spot()
    depth = len(pieces) // 4
    width = g_query.shape[1]
    rows, share, half = width // 8, width // depth, width // 2
    for piece, (c, y, z) in each_piece(pieces):
        g_outer[at(((c * 2 + y) * depth + z) * rows, rows, 32)] = full(piece[:rows])
        there = at((c * 2 + y) * rows, rows, 32)
        for k in range(depth):

            @pl.when(z == k)
            def _():
                cols = slice(k * share, (k + 1) * share)
                for j, out in enumerate((g_query, g_key, g_value)):
                    out[there, cols] = full(piece[rows : 2 * rows, j * share : (j + 1) * share])
                for j in (0, 2):
                    bias = full(piece[2 * rows :, j * share : (j + 1) * share])
                    biases[j : j + 1, cols] = bias[0:1]

    for j, out in ((0, b_query), (2, b_value)):
        row = biases[j : j + 1]
        out[...] = jnp.where(at_b == 0, row[:, :half], row[:, half:]).reshape(half)


def final_second(*refs):
    pieces, (g_inner, g_out) = refs[:-2], refs[-2:]
    depth = len(pieces) // 4
    half, width = g_out.shape
    rows, part = half // 2 // depth, half // 4 // depth
    for piece, (c, y, z) in each_piece(pieces):
        for k in range(2):
            cols = at((2 * k + c) * width, width, 128)
            g_inner[at((y * depth + z) * rows, rows, 16), cols] = full(piece[k * rows : (k + 1) * rows])
        g_out[at(((c * 2 + y) * depth + z) * part, part, 8)] = full(piece[2 * rows :])


def per_device_heads(
    inputs,
    teacher,
    segments,
    w_query,
    b_query,
    w_key,
    w_value,
    b_value,
    w_out,
    b_out,
    gain_one,
    shift_one,
    w_inner,
    b_inner,
    w_outer,
    b_outer,
    gain_two,
    shift_two,
):
    count = lax.axis_size("ctx")
    depth = count // 4
    place = lax.axis_index("ctx")
    at_c, at_y = place % 2, place // 2 % 2
    seqs, rows, width = inputs.shape
    own = seqs * rows
    half = width // 2
    ff = w_inner.shape[1]
    share = width // depth
    keys = count // 2 * rows
    joint = ("batch", "ctx")
    pairs = [(y, c) for y in range(2) for c in range(2)]
    groups_z = [[z * 4 + r for z in range(depth)] for r in range(4)]
    groups_yz = [[z * 4 + y * 2 + c for z in range(depth) for y in range(2)] for c in range(2)]
    groups_xyc = [[b * count + z * 4 + y * 2 + c for b in range(2) for y, c in pairs] for z in range(depth)]

    def swap_x(values):
        return lax.ppermute(values, "batch", [(0, 1), (1, 0)])

    def swap_y(values):
        return lax.ppermute(values, "ctx", [(i, i ^ 2) for i in range(count)])

    def swap_c(values):
        return lax.ppermute(values, "ctx", [(i, i ^ 1) for i in range(count)])

    def shift_z(values, step):
        return lax.ppermute(values, "ctx", [(i, (i + 4 * step) % count) for i in range(count)])

    def trade(values, groups, axes="ctx"):
        return lax.all_to_all(values, axes, 0, 0, axis_index_groups=groups, tiled=True)

    tie = lax.optimization_barrier
    dma = pltpu.SemaphoreType.DMA

    def spread(block):
        held = [block]
        for _ in range(depth - 1):
            held.append(shift_z(held[-1], 1))
        pieces = []
        for piece in held:
            by_y = swap_y(piece)
            pieces += [piece, by_y, swap_c(piece), swap_c(by_y)]
        return pieces

    rows_first = 3 * half // 4
    (first,) = kernel(
        prepare_first,
        [((rows_first + LINES + half, width), BF)],
        [w_query, w_key, w_value, b_query, b_value, b_out, gain_one, shift_one]
        + [b_outer, gain_two, shift_two, b_inner, segments, w_inner],
        hbm=(13,),
        scratch=[pltpu.VMEM((half, width), BF), dma((2,))],
    )
    other = swap_x(first)
    blocks, p_out, p_outer = kernel(
        prepare_second,
        [((depth * seqs, rows, width), BF), ((half // 2, width), BF), ((ff // 8, width), BF)],
        [inputs, w_out, w_outer],
        hbm=(1, 2),
        scratch=[dma((2,))],
    )
    states = trade(blocks, groups_yz).reshape(keys, width)
    states, other, p_out, p_outer = tie((states, other, p_out, p_outer))
    x_inner = other[rows_first + LINES :]

    seg_seq = lax.dynamic_index_in_dim(segments, at_y, 0, keepdims=False).reshape(-1, 2, rows)
    seg_own = lax.dynamic_index_in_dim(seg_seq, at_c, 1, keepdims=False).reshape(-1)
    seg_peer = lax.dynamic_index_in_dim(seg_seq, 1 - at_c, 1, keepdims=False).reshape(-1)
    seg_key = jnp.concatenate([seg_own, seg_peer])[:, None]
    seg_query = seg_own[None, :]
    seg_tokens = lax.dynamic_slice_in_dim(segments, place * rows, rows, 1).reshape(own, 1)

    x_outer = swap_x(p_outer)
    x_out = swap_x(p_out)
    y_inner = swap_y(x_inner)
    query, pair, vecs, inner_vec, w_three = kernel(
        project,
        [
            ((keys, share), BF),
            ((keys, 2 * share), BF),
            ((LINES, width), F32),
            ((8, ff), F32),
            ((width, 3 * share), BF),
        ],
        [states, first, other],
        scratch=[pltpu.VMEM((width, 3 * share), BF)],
    )
    peer = swap_c(pair)
    mixed, logs = kernel(
        attend,
        [((keys, share), BF), ((8, keys), F32)],
        [query, pair, peer, seg_query, seg_key],
        scratch=[pltpu.VMEM((2 * keys, share), BF), pltpu.VMEM((share, 2 * keys), BF)],
    )
    x_outer, y_inner, mixed, x_out = tie((x_outer, y_inner, mixed, x_out))
    mixed = trade(mixed.reshape(depth * seqs, rows, share), groups_yz)
    y_outer = swap_y(x_outer)
    c_out, c_inner, yc_inner, c_outer = map(swap_c, (x_out, x_inner, y_inner, x_outer))
    mixed, y_outer, c_out, c_inner, yc_inner, c_outer = tie(
        (mixed, y_outer, c_out, c_inner, yc_inner, c_outer)
    )
    weights = [w_out, x_out, c_out]
    weights += [w_inner, x_inner, y_inner, c_inner, yc_inner]
    weights += [w_outer, x_outer, y_outer, c_outer, swap_c(y_outer)]
    held = [pltpu.VMEM((width, width), BF), pltpu.VMEM((width, ff), BF), pltpu.VMEM((ff, width), BF)]
    output, attended, unit, inverse, slope, chip, away, g_hidden, sums = kernel(
        functools.partial(forward, float(own * 2 * count)),
        [
            (inputs.shape, F32),
            ((own, width), BF),
            ((own, width), F32),
            ((own, 128), F32),
            ((own, ff), F32),
            ((own, ff + 2 * width), BF),
            ((own, ff // 2 + half + width), BF),
            ((own, width), F32),
            ((LINES, width), F32),
        ],
        [mixed, inputs, teacher, seg_tokens, vecs, inner_vec, *weights],
        hbm=range(6, 19),
        scratch=[*held, pltpu.VMEM((own, width), BF), dma((3, 9))],
    )
    away = swap_x(away)
    chip_c = swap_c(chip)
    g_inner, g_one, g_mixed, out_keep, out_send = kernel(
        backward,
        [
            ((own, ff), BF),
            ((own, width), F32),
            ((depth * seqs, rows, share), BF),
            ((half + LINES, width), BF),
            ((half + LINES, width), BF),
        ],
        [chip, slope, g_hidden, unit, inverse, vecs, attended, sums, *weights],
        hbm=range(8, 21),
        scratch=[
            *held,
            pltpu.VMEM((8, ff), F32),
            pltpu.VMEM((LINES, width), F32),
            pltpu.VMEM((width, width), BF),
            dma((3, 9)),
        ],
    )
    away, chip_c, g_inner, g_mixed, out_send = tie((away, chip_c, g_inner, g_mixed, out_send))

    g_inner_x = swap_x(g_inner)
    g_mixed = trade(g_mixed, groups_yz).reshape(keys, share)
    away_c = swap_c(away)
    g_inner_c = swap_c(g_inner)
    out_came = swap_c(out_send)
    outer_keep, outer_send = kernel(
        weight_outer,
        [((ff // 8, width), BF)] * 2,
        [chip, chip_c, away, away_c],
        scratch=[
            pltpu.VMEM((4 * own, ff // 4), BF),
            pltpu.VMEM((4 * own, width), BF),
            pltpu.VMEM((ff // 4, width), BF),
        ],
    )
    out_keep, out_send = kernel(
        functools.partial(halve_out, 0),
        [((half // 2 + LINES, width), BF)] * 2,
        [out_keep, out_came],
    )
    g_mixed, outer_send, out_send = tie((g_mixed, outer_send, out_send))

    outer_came = swap_y(outer_send)
    out_came = swap_x(out_send)
    g_query, g_mine, g_theirs = kernel(
        attend_back,
        [((keys, share), BF), ((keys, 2 * share), F32), ((keys, 2 * share), F32)],
        [query, pair, peer, seg_query, seg_key, logs, g_mixed],
        scratch=[
            pltpu.VMEM((2 * keys, share), BF),
            pltpu.VMEM((share, 2 * keys), BF),
            pltpu.VMEM((2 * keys, share), BF),
            pltpu.VMEM((2 * keys, 2 * share), F32),
        ],
    )
    outer_came, g_theirs, g_inner_x, out_came = tie((outer_came, g_theirs, g_inner_x, out_came))

    came = swap_c(g_theirs)
    g_inner_xc = swap_c(g_inner_x)
    outer_rows = ff // 8 // depth
    *outer, _ = kernel(
        join_outer,
        [((outer_rows, width), BF)] * depth + [((ff // 8, width), BF)],
        [outer_keep, outer_came],
    )
    outer = [outer[0]] + [shift_z(outer[k], k) for k in range(1, depth)]
    three, *back = kernel(
        weight_three,
        [((8, half // 4 + LINES, 3 * share), BF)] + [((own, width), BF)] * depth,
        [g_query, g_mine, came, states, w_three],
        scratch=[pltpu.VMEM((keys, 3 * share), BF), pltpu.VMEM((keys, width), BF)],
    )
    three = trade(three, groups_xyc, joint)
    back = [back[0]] + [shift_z(back[k], k) for k in range(1, depth)]
    inner_keep, inner_send = kernel(
        weight_inner,
        [((half // 2, ff // 2), BF)] * 2,
        [chip, chip_c, away, away_c, g_inner, g_inner_c, g_inner_x, g_inner_xc],
        scratch=[
            pltpu.VMEM((4 * own, half), BF),
            pltpu.VMEM((4 * own, ff // 2), BF),
            pltpu.VMEM((half, ff // 2), BF),
        ],
    )
    inner_came = swap_y(inner_send)
    out_keep, out_send = kernel(
        functools.partial(halve_out, 2),
        [((half // 4 + LINES, width), BF)] * 2,
        [out_keep, out_came],
    )
    out_came = swap_y(out_send)
    outer, three, inner_came, out_came, back = tie((outer, three, inner_came, out_came, back))

    inner_rows = (half + half // 4) // depth
    (inside,) = kernel(
        join_inner,
        [((depth, inner_rows + LINES, width), BF)],
        [inner_keep, inner_came, out_keep, out_came],
    )
    inside = trade(inside, groups_z)
    (packed,) = kernel(pack_first, [((2 * outer_rows + 8, width), BF)], [*outer, three])
    pieces = spread(packed)
    back_mine, back_send = kernel(join_back, [((rows, width), F32), ((rows, width), BF)], back)
    back_came = swap_y(back_send)
    (g_inputs,) = kernel(grad_states, [(inputs.shape, F32)], [back_mine, back_came, g_one])

    packed, loss, g_b_inner, *vectors = kernel(
        pack_second,
        [((inner_rows, width), BF), ((1, 128), F32), ((ff // 2,), F32)] + [((half,), F32)] * 6,
        [inside, vecs],
    )
    g_w_outer, g_w_query, g_w_key, g_w_value, g_b_query, g_b_value = kernel(
        final_first,
        [((ff // 2, width), F32)] + [((half, width), F32)] * 3 + [((half,), F32)] * 2,
        pieces,
        scratch=[pltpu.VMEM((8, width), F32)],
    )
    g_w_inner, g_w_out = kernel(
        final_second, [((half, ff), F32), ((half, width), F32)], spread(packed)
    )
    g_b_out, g_gain_one, g_shift_one, g_b_outer, g_gain_two, g_shift_two = vectors
    return (
        output,
        loss[0, 0],
        g_inputs,
        g_w_query,
        g_b_query,
        g_w_key,
        g_w_value,
        g_b_value,
        g_w_out,
        g_b_out,
        g_gain_one,
        g_shift_one,
        g_w_inner,
        g_b_inner,
        g_w_outer,
        g_b_outer,
        g_gain_two,
        g_shift_two,
    )


def per_device(inputs, *others):
    sizes = (lax.axis_size("batch"), lax.axis_size("ctx"), inputs.shape[0])
    if sizes == (2, 16, 2):
        return per_device_heads(inputs, *others)
    return per_device_any(inputs, *others)


def solution(mesh):
    placed = (
        P("batch", "ctx", None),
        P("batch", "ctx", None),
        P("batch", None),
        P("batch", None),
        P("batch"),
        P("batch", None),
        P("batch", None),
        P("batch"),
        P("batch", None),
        P("batch"),
        P("batch"),
        P("batch"),
        P("batch", None),
        P("batch"),
        P("batch", None),
        P("batch"),
        P("batch"),
        P("batch"),
    )
    return jax.shard_map(
        per_device,
        mesh=mesh,
        in_specs=placed,
        out_specs=(
            P("batch", "ctx", None),
            P(),
            P("batch", "ctx", None),
            P("batch", None),
            P("batch"),
            P("batch", None),
            P("batch", None),
            P("batch"),
            P("batch", None),
            P("batch"),
            P("batch"),
            P("batch"),
            P("batch", None),
            P("batch"),
            P("batch", None),
            P("batch"),
            P("batch"),
            P("batch"),
        ),
        check_vma=False,
    )
```

```python
import functools
import math

import jax
import jax.numpy as jnp
from jax import lax
from jax.experimental import pallas as pl
from jax.experimental.pallas import tpu as pltpu
from jax.sharding import PartitionSpec as P

H = 12
HD = 64


NEGATIVE = -1e30
EPSILON = 1e-12


def norm_rows(hidden, gain, shift):
    center = hidden - jnp.mean(hidden, -1, keepdims=True)
    spread = jnp.mean(center * center, -1, keepdims=True)
    return center * lax.rsqrt(spread + EPSILON) * gain + shift


def gelu_exact(values):
    return jax.nn.gelu(values, approximate=False)


def linear(rows_in, weight):
    return jnp.dot(rows_in, weight, preferred_element_type=jnp.float32)


def contract_rows(left, right):
    return lax.dot_general(
        left, right, (((0,), (0,)), ((), ())), preferred_element_type=jnp.float32
    )


def times_transpose(rows_in, weight):
    return lax.dot_general(
        rows_in, weight, (((1,), (1,)), ((), ())), preferred_element_type=jnp.float32
    )


def score_rows(query_one, keys_all, seg_mine, seg_all):
    heads_query = query_one.reshape(query_one.shape[0], H, HD)
    heads_key = keys_all.reshape(keys_all.shape[0], H, HD)
    raw = jnp.einsum(
        "chd,khd->hck", heads_query, heads_key, preferred_element_type=jnp.float32
    ) * HD ** (-0.5)
    allowed = seg_mine[None, :, None] == seg_all[None, None, :]
    return jnp.where(allowed, raw, NEGATIVE)


def per_device_any(
    inputs,
    teacher,
    segments,
    w_query,
    b_query,
    w_key,
    w_value,
    b_value,
    w_out,
    b_out,
    gain_one,
    shift_one,
    w_inner,
    b_inner,
    w_outer,
    b_outer,
    gain_two,
    shift_two,
):
    (
        w_query,
        b_query,
        w_key,
        w_value,
        b_value,
        w_out,
        b_out,
        gain_one,
        shift_one,
        w_inner,
        b_inner,
        w_outer,
        b_outer,
        gain_two,
        shift_two,
    ) = (
        lax.all_gather(w_query, "batch", axis=0, tiled=True),
        lax.all_gather(b_query, "batch", axis=0, tiled=True),
        lax.all_gather(w_key, "batch", axis=0, tiled=True),
        lax.all_gather(w_value, "batch", axis=0, tiled=True),
        lax.all_gather(b_value, "batch", axis=0, tiled=True),
        lax.all_gather(w_out, "batch", axis=0, tiled=True),
        lax.all_gather(b_out, "batch", axis=0, tiled=True),
        lax.all_gather(gain_one, "batch", axis=0, tiled=True),
        lax.all_gather(shift_one, "batch", axis=0, tiled=True),
        lax.all_gather(w_inner, "batch", axis=0, tiled=True),
        lax.all_gather(b_inner, "batch", axis=0, tiled=True),
        lax.all_gather(w_outer, "batch", axis=0, tiled=True),
        lax.all_gather(b_outer, "batch", axis=0, tiled=True),
        lax.all_gather(gain_two, "batch", axis=0, tiled=True),
        lax.all_gather(shift_two, "batch", axis=0, tiled=True),
    )
    scale = HD ** (-0.5)
    seqs_here, ctx_rows, width = inputs.shape
    rows_here = seqs_here * ctx_rows
    tokens_all = rows_here * lax.axis_size("batch") * lax.axis_size("ctx")
    seg_own = lax.dynamic_slice_in_dim(segments, lax.axis_index("ctx") * ctx_rows, ctx_rows, 1)
    inputs_flat = inputs.reshape(rows_here, width)
    inputs_low = inputs_flat.astype(jnp.bfloat16)
    query = (linear(inputs_low, w_query) + b_query.astype(jnp.float32)).astype(jnp.bfloat16)
    key = linear(inputs_low, w_key).astype(jnp.bfloat16)
    value = (linear(inputs_low, w_value) + b_value.astype(jnp.float32)).astype(jnp.bfloat16)
    query_seq = query.reshape(seqs_here, ctx_rows, width)
    key_seq = key.reshape(seqs_here, ctx_rows, width)
    value_seq = value.reshape(seqs_here, ctx_rows, width)

    def attend_forward(items):
        query_one, key_one, value_one, seg_all, seg_mine = items
        keys_all, values_all = (
            lax.all_gather(key_one, "ctx", axis=0, tiled=True),
            lax.all_gather(value_one, "ctx", axis=0, tiled=True),
        )
        scores = score_rows(query_one, keys_all, seg_mine, seg_all)
        highest = jnp.max(scores, -1, keepdims=True)
        expo = jnp.exp(scores - highest)
        totals = jnp.sum(expo, -1, keepdims=True)
        probs = (expo / totals).astype(jnp.bfloat16)
        mixed = jnp.einsum(
            "hck,khd->chd",
            probs,
            values_all.reshape(keys_all.shape[0], H, HD),
            preferred_element_type=jnp.float32,
        )
        return (
            mixed.reshape(ctx_rows, width).astype(jnp.bfloat16),
            (highest + jnp.log(totals))[:, :, 0],
        )

    attended, log_totals = lax.map(
        attend_forward, (query_seq, key_seq, value_seq, segments, seg_own)
    )
    attended_flat = attended.reshape(rows_here, width)
    gain_one_full = gain_one.astype(jnp.float32)
    shift_one_full = shift_one.astype(jnp.float32)
    gain_two_full = gain_two.astype(jnp.float32)
    shift_two_full = shift_two.astype(jnp.float32)
    hidden_one = inputs_flat + linear(attended_flat, w_out) + b_out.astype(jnp.float32)
    normed_one, back_one = jax.vjp(norm_rows, hidden_one, gain_one_full, shift_one_full)
    normed_low = normed_one.astype(jnp.bfloat16)
    inner_pre = linear(normed_low, w_inner) + b_inner.astype(jnp.float32)
    active_full, gelu_back = jax.vjp(gelu_exact, inner_pre)
    active_low = active_full.astype(jnp.bfloat16)
    hidden_two = normed_one + linear(active_low, w_outer) + b_outer.astype(jnp.float32)
    output, back_two = jax.vjp(norm_rows, hidden_two, gain_two_full, shift_two_full)
    valid = (seg_own.reshape(rows_here) != 0).astype(jnp.float32)[:, None]
    error = output - teacher.reshape(rows_here, width)
    loss_total, valid_count = lax.psum(
        (jnp.sum(valid * error * error), jnp.sum(valid)), ("batch", "ctx")
    )
    loss = loss_total / (2.0 * valid_count)
    grad_output = tokens_all / valid_count * valid * error
    grad_hidden_two, grad_gain_two, grad_shift_two = back_two(grad_output)
    grad_branch_two = grad_hidden_two.astype(jnp.bfloat16)
    grad_b_outer = jnp.sum(grad_branch_two.astype(jnp.float32), 0)
    grad_w_outer = contract_rows(active_low, grad_branch_two)
    grad_active = times_transpose(grad_branch_two, w_outer)
    grad_inner = gelu_back(grad_active)[0].astype(jnp.bfloat16)
    grad_b_inner = jnp.sum(grad_inner.astype(jnp.float32), 0)
    grad_w_inner = contract_rows(normed_low, grad_inner)
    grad_normed = grad_hidden_two + times_transpose(grad_inner, w_inner)
    grad_hidden_one, grad_gain_one, grad_shift_one = back_one(grad_normed)
    grad_branch_one = grad_hidden_one.astype(jnp.bfloat16)
    grad_b_out = jnp.sum(grad_branch_one.astype(jnp.float32), 0)
    grad_w_out = contract_rows(attended_flat, grad_branch_one)
    grad_attended = (
        times_transpose(grad_branch_one, w_out)
        .astype(jnp.bfloat16)
        .reshape(seqs_here, ctx_rows, width)
    )

    def attend_backward(items):
        query_one, key_one, value_one, seg_all, seg_mine, log_one, grad_one = items
        keys_all, values_all = (
            lax.all_gather(key_one, "ctx", axis=0, tiled=True),
            lax.all_gather(value_one, "ctx", axis=0, tiled=True),
        )
        key_count = keys_all.shape[0]
        scores = score_rows(query_one, keys_all, seg_mine, seg_all)
        probs = jnp.exp(scores - log_one[:, :, None])
        grad_heads = grad_one.reshape(ctx_rows, H, HD)
        grad_probs = jnp.einsum(
            "chd,khd->hck",
            grad_heads,
            values_all.reshape(key_count, H, HD),
            preferred_element_type=jnp.float32,
        )
        centre = jnp.sum(probs * grad_probs, -1)
        grad_scores = (probs * (grad_probs - centre[:, :, None])).astype(jnp.bfloat16)
        grad_query = (
            jnp.einsum(
                "hck,khd->chd",
                grad_scores,
                keys_all.reshape(key_count, H, HD),
                preferred_element_type=jnp.float32,
            )
            * scale
        )
        grad_query = grad_query.reshape(ctx_rows, width).astype(jnp.bfloat16)
        probs_low = probs.astype(jnp.bfloat16)
        query_heads = query_one.reshape(ctx_rows, H, HD)
        count = ctx_rows * lax.axis_size("ctx")
        grad_key = (
            jnp.einsum("hck,chd->khd", grad_scores, query_heads, preferred_element_type=jnp.float32)
            * scale
        )
        grad_value = jnp.einsum(
            "hck,chd->khd", probs_low, grad_heads, preferred_element_type=jnp.float32
        )
        both = lax.psum_scatter(
            jnp.concatenate([grad_key.reshape(count, width), grad_value.reshape(count, width)], 1),
            "ctx",
            scatter_dimension=0,
            tiled=True,
        )
        return (
            grad_query,
            both[:, :width].astype(jnp.bfloat16),
            both[:, width:].astype(jnp.bfloat16),
        )

    grad_query_seq, grad_key_seq, grad_value_seq = lax.map(
        attend_backward,
        (query_seq, key_seq, value_seq, segments, seg_own, log_totals, grad_attended),
    )
    grad_query_flat = grad_query_seq.reshape(rows_here, width)
    grad_key_flat = grad_key_seq.reshape(rows_here, width)
    grad_value_flat = grad_value_seq.reshape(rows_here, width)
    grad_w_query = contract_rows(inputs_low, grad_query_flat)
    grad_b_query = jnp.sum(grad_query_flat.astype(jnp.float32), 0)
    grad_w_key = contract_rows(inputs_low, grad_key_flat)
    grad_w_value = contract_rows(inputs_low, grad_value_flat)
    grad_b_value = jnp.sum(grad_value_flat.astype(jnp.float32), 0)
    grad_inputs = (
        grad_hidden_one
        + times_transpose(grad_query_flat, w_query)
        + times_transpose(grad_key_flat, w_key)
        + times_transpose(grad_value_flat, w_value)
    )
    (
        grad_w_query,
        grad_b_query,
        grad_w_key,
        grad_w_value,
        grad_b_value,
        grad_w_out,
        grad_b_out,
        grad_gain_one,
        grad_shift_one,
        grad_w_inner,
        grad_b_inner,
        grad_w_outer,
        grad_b_outer,
        grad_gain_two,
        grad_shift_two,
    ) = (
        lax.psum_scatter(
            grad_w_query.astype(jnp.bfloat16), "batch", scatter_dimension=0, tiled=True
        ).astype(jnp.float32),
        lax.psum_scatter(
            grad_b_query.astype(jnp.bfloat16), "batch", scatter_dimension=0, tiled=True
        ).astype(jnp.float32),
        lax.psum_scatter(
            grad_w_key.astype(jnp.bfloat16), "batch", scatter_dimension=0, tiled=True
        ).astype(jnp.float32),
        lax.psum_scatter(
            grad_w_value.astype(jnp.bfloat16), "batch", scatter_dimension=0, tiled=True
        ).astype(jnp.float32),
        lax.psum_scatter(
            grad_b_value.astype(jnp.bfloat16), "batch", scatter_dimension=0, tiled=True
        ).astype(jnp.float32),
        lax.psum_scatter(
            grad_w_out.astype(jnp.bfloat16), "batch", scatter_dimension=0, tiled=True
        ).astype(jnp.float32),
        lax.psum_scatter(
            grad_b_out.astype(jnp.bfloat16), "batch", scatter_dimension=0, tiled=True
        ).astype(jnp.float32),
        lax.psum_scatter(
            grad_gain_one.astype(jnp.bfloat16), "batch", scatter_dimension=0, tiled=True
        ).astype(jnp.float32),
        lax.psum_scatter(
            grad_shift_one.astype(jnp.bfloat16), "batch", scatter_dimension=0, tiled=True
        ).astype(jnp.float32),
        lax.psum_scatter(
            grad_w_inner.astype(jnp.bfloat16), "batch", scatter_dimension=0, tiled=True
        ).astype(jnp.float32),
        lax.psum_scatter(
            grad_b_inner.astype(jnp.bfloat16), "batch", scatter_dimension=0, tiled=True
        ).astype(jnp.float32),
        lax.psum_scatter(
            grad_w_outer.astype(jnp.bfloat16), "batch", scatter_dimension=0, tiled=True
        ).astype(jnp.float32),
        lax.psum_scatter(
            grad_b_outer.astype(jnp.bfloat16), "batch", scatter_dimension=0, tiled=True
        ).astype(jnp.float32),
        lax.psum_scatter(
            grad_gain_two.astype(jnp.bfloat16), "batch", scatter_dimension=0, tiled=True
        ).astype(jnp.float32),
        lax.psum_scatter(
            grad_shift_two.astype(jnp.bfloat16), "batch", scatter_dimension=0, tiled=True
        ).astype(jnp.float32),
    )
    (
        grad_w_query,
        grad_b_query,
        grad_w_key,
        grad_w_value,
        grad_b_value,
        grad_w_out,
        grad_b_out,
        grad_gain_one,
        grad_shift_one,
        grad_w_inner,
        grad_b_inner,
        grad_w_outer,
        grad_b_outer,
        grad_gain_two,
        grad_shift_two,
    ) = lax.psum(
        (
            grad_w_query,
            grad_b_query,
            grad_w_key,
            grad_w_value,
            grad_b_value,
            grad_w_out,
            grad_b_out,
            grad_gain_one,
            grad_shift_one,
            grad_w_inner,
            grad_b_inner,
            grad_w_outer,
            grad_b_outer,
            grad_gain_two,
            grad_shift_two,
        ),
        "ctx",
    )
    return (
        output.reshape(inputs.shape),
        loss,
        grad_inputs.reshape(inputs.shape),
        grad_w_query,
        grad_b_query,
        grad_w_key,
        grad_w_value,
        grad_b_value,
        grad_w_out,
        grad_b_out,
        grad_gain_one,
        grad_shift_one,
        grad_w_inner,
        grad_b_inner,
        grad_w_outer,
        grad_b_outer,
        grad_gain_two,
        grad_shift_two,
    )


BF, F32 = jnp.bfloat16, jnp.float32
LINES = 16
ROOM = 6 << 20


def low(values):
    return values.astype(BF)


def full(values):
    return values.astype(F32)


def dot(left, right, a=1, b=0):
    return lax.dot_general(left, right, (((a,), (b,)), ((), ())), preferred_element_type=F32)


def spot():
    place = lax.axis_index("ctx")
    return lax.axis_index("batch"), place % 2, place // 2 % 2, place // 4


def at(start, size, step):
    return pl.ds(pl.multiple_of(start, step), size)


def kernel(body, outs, args, hbm=(), scratch=(), pin=()):
    name = getattr(body, "func", body).__name__
    where = [pl.BlockSpec(memory_space=pl.ANY if k in hbm else pltpu.VMEM) for k in range(len(args))]
    shapes = [jax.ShapeDtypeStruct(shape, kind) for shape, kind in outs]
    held = [a for k, a in enumerate(args) if k not in hbm] + shapes
    held += [a for a in scratch if a.memory_space == pltpu.VMEM]
    room = sum(math.prod(a.shape) * jnp.dtype(a.dtype).itemsize for a in held) + ROOM
    args = [
        pltpu.with_memory_space_constraint(a, pltpu.HBM) if k in hbm or k in pin else a
        for k, a in enumerate(args)
    ]
    return pl.pallas_call(
        body,
        out_shape=shapes,
        in_specs=where,
        out_specs=[pl.BlockSpec(memory_space=pltpu.VMEM)] * len(shapes),
        scratch_shapes=list(scratch),
        compiler_params=pltpu.CompilerParams(vmem_limit_bytes=room),
        name=name,
    )(*args)


def norm_forward(hidden, gain, shift):
    center = hidden - jnp.mean(hidden, -1, keepdims=True)
    inverse = lax.rsqrt(jnp.mean(center * center, -1, keepdims=True) + EPSILON)
    unit = center * inverse
    return unit * gain + shift, unit, inverse


def norm_backward(grad, unit, inverse, gain):
    scaled = grad * gain
    along = jnp.mean(scaled * unit, -1, keepdims=True)
    return inverse * (scaled - jnp.mean(scaled, -1, keepdims=True) - unit * along)


def total(values):
    return jnp.sum(values, 0, keepdims=True)


def prepare(*refs):
    inputs, w_three, vectors, b_inner, segments = refs[0], refs[1:4], refs[4:12], refs[12], refs[13]
    w_inner, w_outer, w_out, blocks, out, p_inner, p_outer, p_out, sem = refs[14:]
    half, width = w_three[0].shape
    _, at_c, at_y, at_z = spot()
    part, wide = half // 2, w_inner.shape[1] // 4
    rows_out, rows_outer = p_out.shape[0], p_outer.shape[0]
    copies = [
        (
            w_inner.at[at(at_y * part, part, 64), at((k * 2 + at_c) * wide, wide, 128)],
            p_inner.at[k * part : (k + 1) * part],
        )
        for k in range(2)
    ]
    copies.append((w_outer.at[at((at_c * 2 + at_y) * rows_outer, rows_outer, 128)], p_outer))
    copies.append((w_out.at[at(at_c * rows_out, rows_out, 64)], p_out))
    copies = start(copies, sem)
    seqs = inputs.shape[0]
    for s in range(seqs):
        piece = low(inputs[s])
        for z in range(blocks.shape[0] // seqs):
            blocks[z * seqs + s] = piece
    share, rows = width // 4, half // 4
    for z in range(4):

        @pl.when(at_z == z)
        def _():
            for j in range(3):
                for k in range(4):
                    piece = w_three[j][k * rows : (k + 1) * rows, z * share : (z + 1) * share]
                    out[j * rows : (j + 1) * rows, k * share : (k + 1) * share] = piece

    first = 3 * rows
    out[first : first + LINES] = jnp.zeros((LINES, width), BF)
    for r in range(8):
        out[first + r : first + r + 1, :half] = vectors[r][...].reshape(1, half)
    inner = b_inner[...].reshape(1, -1)
    for r in range(4):
        out[first + 8 + r : first + 9 + r, :half] = inner[:, half * r : half * (r + 1)]
    valid = jnp.sum(jnp.where(segments[...] != 0, 1, 0))
    lane = lax.broadcasted_iota(jnp.int32, (1, half), 1)
    parts = jnp.where(lane < 128, valid // 256, valid % 256)
    out[first + 12 : first + 13, :half] = low(full(parts))
    finish(copies)


def start(copies, sem):
    made = [pltpu.make_async_copy(*copy, sem.at[k]) for k, copy in enumerate(copies)]
    for copy in made:
        copy.start()
    return made


def finish(copies):
    for copy in copies:
        copy.wait()


def both_halves(at_b, mine, other):
    return jnp.where(at_b == 0, mine, other), jnp.where(at_b == 0, other, mine)


def project(states, mine, other, query, pair, vecs, inner_vec, held, w_back):
    at_b, _, _, at_z = spot()
    width, share = states.shape[1], query.shape[1]
    half, rows = width // 2, width // 8
    for j in range(3):
        for k in range(4):
            first = slice(j * rows, (j + 1) * rows)
            cols = slice(k * share, (k + 1) * share)
            pieces = both_halves(at_b, mine[first, cols], other[first, cols])
            for h, piece in enumerate(pieces):
                start_row = h * half + k * rows
                held[start_row : start_row + rows, j * share : (j + 1) * share] = piece
    w_back[...] = held[...]
    made = dot(states[...], held[...])
    lines = slice(3 * rows, 3 * rows + LINES)
    top, bottom = both_halves(at_b, full(mine[lines]), full(other[lines]))

    def bias(r):
        row = jnp.where(at_z < 2, top[r : r + 1], bottom[r : r + 1])
        return jnp.where(at_z % 2 == 0, row[:, :share], row[:, share : 2 * share])

    query[...] = low(full(low(made[:, :share] + bias(0))) * HD ** (-0.5))
    pair[:, :share] = low(made[:, share : 2 * share])
    pair[:, share:] = low(made[:, 2 * share :] + bias(1))
    vecs[...] = jnp.zeros_like(vecs)
    for r in range(2, 8):
        vecs[r - 2 : r - 1, :half] = top[r : r + 1, :half]
        vecs[r - 2 : r - 1, half:] = bottom[r : r + 1, :half]
    counts = top[12:13] + bottom[12:13]
    counts = counts[:, :128] * 256.0 + counts[:, 256:384]
    vecs[8:9, :128] = counts
    inner_vec[...] = jnp.zeros_like(inner_vec)
    for b, rows in enumerate((top, bottom)):
        for r in range(4):
            cols = slice((4 * b + r) * half, (4 * b + r + 1) * half)
            inner_vec[0:1, cols] = rows[8 + r : 9 + r, :half]


STEP = 256


def attend(query, mine, peer, seg_query, seg_key, mixed, logs, keys, values):
    count, share = query.shape
    keys[:count] = mine[:, :share]
    keys[count:] = peer[:, :share]
    values[:, :count] = mine[:, share:].T
    values[:, count:] = peer[:, share:].T
    logs[...] = jnp.zeros_like(logs)

    def block(j, carry):
        rows = at(j * STEP, STEP, STEP)
        allowed = seg_key[...] == seg_query[:, rows]
        for h in range(share // HD):
            cols = slice(h * HD, (h + 1) * HD)
            scores = dot(keys[:, cols], query[rows, cols], 1, 1)
            scores = jnp.where(allowed, scores, NEGATIVE)
            highest = jnp.max(scores, 0, keepdims=True)
            expo = jnp.exp(scores - highest)
            totals = jnp.sum(expo, 0, keepdims=True)
            probs = low(expo * (1.0 / totals))
            mixed[rows, cols] = low(dot(values[cols], probs).T)
            logs[h : h + 1, rows] = highest + jnp.log(totals)
        return carry

    lax.fori_loop(0, count // STEP, block, 0)


def attend_back(
    query, mine, peer, seg_query, seg_key, logs, grad, g_query, g_mine, g_peer, keys, flipped, values, made
):
    count, share = query.shape
    keys[:count] = mine[:, :share]
    keys[count:] = peer[:, :share]
    values[:count] = mine[:, share:]
    values[count:] = peer[:, share:]
    flipped[:, :count] = mine[:, :share].T
    flipped[:, count:] = peer[:, :share].T
    made[...] = jnp.zeros_like(made)

    def block(j, carry):
        rows = at(j * STEP, STEP, STEP)
        allowed = seg_key[...] == seg_query[:, rows]
        for h in range(share // HD):
            cols = slice(h * HD, (h + 1) * HD)
            cols_value = slice(share + h * HD, share + (h + 1) * HD)
            scores = dot(keys[:, cols], query[rows, cols], 1, 1)
            scores = jnp.where(allowed, scores, NEGATIVE)
            probs = jnp.exp(scores - logs[h : h + 1, rows])
            g_probs = dot(values[:, cols], grad[rows, cols], 1, 1)
            centre = jnp.sum(probs * g_probs, 0, keepdims=True)
            g_scores = low(probs * (g_probs - centre))
            g_query[rows, cols] = low((dot(flipped[cols], g_scores) * HD ** (-0.5)).T)
            made[:, cols] += dot(g_scores, query[rows, cols])
            made[:, cols_value] += dot(low(probs), grad[rows, cols])
        return carry

    lax.fori_loop(0, count // STEP, block, 0)
    g_mine[...] = made[:count]
    g_peer[...] = made[count:]


def fetch_out(own, pieces, held, sem):
    at_b, at_c, _, _ = spot()
    half, part = own.shape[0], pieces[0].shape[0]
    copies = [(own, held.at[at(at_b * half, half, 128)])]
    for k, piece in enumerate(pieces):
        first = (1 - at_b) * half + (at_c + k) % 2 * part
        copies.append((piece, held.at[at(first, part, 64)]))
    return start(copies, sem)


def fetch_inner(own, pieces, held, sem):
    at_b, at_c, at_y, _ = spot()
    half, part, wide = own.shape[0], pieces[0].shape[0] // 2, pieces[0].shape[1]
    copies = [(own, held.at[at(at_b * half, half, 128)])]
    for c in range(2):
        for y in range(2):
            rows = at((1 - at_b) * half + (at_y + y) % 2 * part, part, 64)
            for k in range(2):
                cols = at((2 * k + (at_c + c) % 2) * wide, wide, 128)
                piece = pieces[2 * c + y].at[k * part : (k + 1) * part]
                copies.append((piece, held.at[rows, cols]))
    return start(copies, sem)


def fetch_outer(own, pieces, held, sem):
    at_b, at_c, at_y, _ = spot()
    half, part = own.shape[0], pieces[0].shape[0]
    copies = [(own, held.at[at(at_b * half, half, 128)])]
    for c in range(2):
        for y in range(2):
            first = (1 - at_b) * half + ((at_c + c) % 2 * 2 + (at_y + y) % 2) * part
            copies.append((pieces[2 * c + y], held.at[at(first, part, 128)]))
    return start(copies, sem)


BLOCK = 256


def forward(tokens_all, *refs):
    mixed, inputs, teacher, seg, vecs, inner_vec = refs[:6]
    weights, (output, attended, unit, inverse, slope, chip, away, g_hidden, sums) = refs[6:19], refs[19:28]
    held_out, held_inner, held_outer, low_one, sem = refs[28:]
    at_b, _, _, _ = spot()
    copies_out = fetch_out(weights[0], weights[1:3], held_out, sem.at[0])
    copies_inner = fetch_inner(weights[3], weights[4:8], held_inner, sem.at[1])
    copies_outer = fetch_outer(weights[8], weights[9:13], held_outer, sem.at[2])
    rows, share = mixed.shape[1:]
    seqs = inputs.shape[0]
    own, width = attended.shape
    half, ff = width // 2, slope.shape[1]
    for s in range(seqs):
        for z in range(mixed.shape[0] // seqs):
            attended[s * rows : (s + 1) * rows, z * share : (z + 1) * share] = mixed[z * seqs + s]
    finish(copies_out)
    hidden = inputs[...].reshape(own, width) + dot(attended[...], held_out[...]) + vecs[0:1]
    normed, made_unit, made_inverse = norm_forward(hidden, vecs[1:2], vecs[2:3])
    unit[...] = made_unit
    inverse[...] = jnp.broadcast_to(made_inverse, inverse.shape)
    low_one[...] = low(normed)
    chip[:, ff : ff + width] = low_one[...]
    away[:, ff // 2 : ff // 2 + half] = jnp.where(at_b == 0, low_one[:, half:], low_one[:, :half])
    finish(copies_inner)

    def block(j, carry):
        cols = at(j * BLOCK, BLOCK, BLOCK)
        before = dot(low_one[...], held_inner[:, cols]) + inner_vec[0:1, cols]
        below = 0.5 * (1.0 + lax.erf(before * 0.7071067811865476))
        chip[:, cols] = low(before * below)
        slope[:, cols] = below + before * jnp.exp(before * before * -0.5) * 0.3989422804014327
        return carry

    lax.fori_loop(0, ff // BLOCK, block, 0)
    away[:, : ff // 2] = chip[:, at((1 - at_b) * (ff // 2), ff // 2, 128)]
    finish(copies_outer)
    hidden = normed + dot(chip[:, :ff], held_outer[...]) + vecs[3:4]
    made, unit_two, inverse_two = norm_forward(hidden, vecs[4:5], vecs[5:6])
    output[...] = made.reshape(output.shape)
    valid = jnp.where(seg[...] != 0, 1.0, 0.0)
    error = (made - teacher[...].reshape(own, width)) * valid
    grad = error * (tokens_all / vecs[8:9, 0:1])
    made = norm_backward(grad, unit_two, inverse_two, vecs[4:5])
    g_hidden[...] = made
    g_low = low(made)
    chip[:, ff + width :] = g_low
    away[:, ff // 2 + half :] = g_low
    sums[...] = jnp.zeros_like(sums)
    sums[3:4] = total(full(g_low))
    sums[4:5] = total(grad * unit_two)
    sums[5:6] = total(grad)
    loss = jnp.broadcast_to(jnp.sum(total(error * error), 1, keepdims=True), (1, width))
    sums[10:11] = full(low(loss))
    sums[11:12] = loss - full(low(loss))


def backward(*refs):
    chip, slope, g_hidden, unit, inverse, vecs, attended, sums = refs[:8]
    weights, (chip_two, away_two, g_one, g_mixed) = refs[8:21], refs[21:25]
    held_out, held_inner, held_outer, inner_sums, small, sem = refs[25:]
    at_b, _, _, _ = spot()
    copies_outer = fetch_outer(weights[8], weights[9:13], held_outer, sem.at[2])
    copies_inner = fetch_inner(weights[3], weights[4:8], held_inner, sem.at[1])
    copies_out = fetch_out(weights[0], weights[1:3], held_out, sem.at[0])
    (own, width), ff = unit.shape, slope.shape[1]
    half = width // 2
    chip_two[:own, ff + width :] = attended[...]
    away_two[:own, ff + width :] = jnp.where(at_b == 0, attended[:, half:], attended[:, :half])
    finish(copies_outer)

    def block(j, carry):
        cols = at(j * BLOCK, BLOCK, BLOCK)
        grad = low(dot(chip[:, ff + width :], held_outer[cols, :], 1, 1) * slope[:, cols])
        chip_two[:own, cols] = grad
        away_two[:own, cols] = grad
        inner_sums[0:1, cols] = total(full(grad))
        return carry

    lax.fori_loop(0, ff // BLOCK, block, 0)
    finish(copies_inner)
    g_normed = g_hidden[...] + dot(chip_two[:own, :ff], held_inner[...], 1, 1)
    made = norm_backward(g_normed, unit[...], inverse[:, 0:1], vecs[1:2])
    g_one[...] = made
    g_low = low(made)
    chip_two[:own, ff : ff + width] = g_low
    away_two[:own, ff : ff + width] = g_low
    finish(copies_out)
    g_attended = low(dot(g_low, held_out[...], 1, 1))
    rows, share = g_mixed.shape[1:]
    seqs = own // rows
    for s in range(seqs):
        for z in range(g_mixed.shape[0] // seqs):
            g_mixed[z * seqs + s] = g_attended[s * rows : (s + 1) * rows, z * share : (z + 1) * share]
    small[...] = sums[...]
    small[0:1] = total(full(g_low))
    small[1:2] = total(g_normed * unit[...])
    small[2:3] = total(g_normed)
    for k in range(4):
        small[6 + k : 7 + k] = inner_sums[0:1, k * width : (k + 1) * width]
    for out in (chip_two, away_two):
        out[own:, :width] = low(small[...])
        out[own:, width:] = jnp.zeros((LINES, out.shape[1] - width), BF)


def resplit(made):
    lines = made.shape[0]
    loss = made[10:11] + made[11:12]
    return low(jnp.concatenate([made[:10], full(low(loss)), loss - full(low(loss)), made[12:lines]]))


def halve_out(axis, keep, came, next_keep, next_send):
    mine = spot()[axis]
    part = next_keep.shape[0] - LINES
    for k in range(2):
        rows = slice(k * part, (k + 1) * part)
        piece = low(full(keep[rows]) + full(came[rows]))

        @pl.when(mine == k)
        def _():
            next_keep[:part] = piece

        @pl.when(mine != k)
        def _():
            next_send[:part] = piece

    small = resplit(full(keep[2 * part :]) + full(came[2 * part :]))
    next_keep[part:] = small
    next_send[part:] = small


def eight(parts):
    made = full(parts[0])
    for k in range(1, parts.shape[0]):
        made = made + full(parts[k])
    return made


def weight_outer(chip, chip_c, away, away_c, keep, send, left, right, made):
    at_b, at_c, at_y, _ = spot()
    rows, (_, wide) = chip.shape[0], left.shape
    width = right.shape[1]
    for k, piece in enumerate((chip, chip_c)):
        left[k * rows : (k + 1) * rows] = piece[:, at((2 * at_b + at_c) * wide, wide, 128)]
        right[k * rows : (k + 1) * rows] = piece[:, piece.shape[1] - width :]
    for k, piece in enumerate((away, away_c)):
        left[(2 + k) * rows : (3 + k) * rows] = piece[:, at(at_c * wide, wide, 128)]
        right[(2 + k) * rows : (3 + k) * rows] = piece[:, piece.shape[1] - width :]
    made[...] = low(dot(left[...], right[...], 0, 0))
    part = keep.shape[0]
    keep[...] = made[at(at_y * part, part, 128)]
    send[...] = made[at((1 - at_y) * part, part, 128)]


def weight_inner(chip, chip_c, away, away_c, two, two_c, two_x, two_xc, keep, send, *refs):
    left, right, made, left_out, right_out, made_out = refs
    at_b, at_c, at_y, _ = spot()
    rows, (_, half) = chip.shape[0], left.shape
    wide, width = right.shape[1] // 2, right_out.shape[1]
    ff, quarter = 4 * wide, half // 2
    for k, piece in enumerate((chip, chip_c)):
        left[k * rows : (k + 1) * rows] = piece[:, at(ff + at_b * half, half, 128)]
    for k, piece in enumerate((away, away_c)):
        left[(2 + k) * rows : (3 + k) * rows] = piece[:, ff // 2 : ff // 2 + half]
    for k, piece in enumerate((two, two_c, two_x, two_xc)):
        there = slice(k * rows, (k + 1) * rows)
        for j in range(2):
            right[there, j * wide : (j + 1) * wide] = piece[:rows, at((2 * j + at_c) * wide, wide, 128)]
        right_out[there] = piece[:rows, ff : ff + width]
        if k < 2:
            mixed = piece[:rows, at(ff + width + at_b * half, half, 128)]
        else:
            mixed = piece[:rows, ff + width : ff + width + half]
        left_out[there] = jnp.where(at_c == 0, mixed[:, :quarter], mixed[:, quarter:])
    made[...] = low(dot(left[...], right[...], 0, 0))
    made_out[...] = low(dot(left_out[...], right_out[...], 0, 0))
    small = resplit(sum(full(piece[rows:, :width]) for piece in (two, two_c, two_x, two_xc)))
    for out, y in ((keep, at_y), (send, 1 - at_y)):
        for k in range(2):
            piece = made[at(y * quarter, quarter, 64), k * wide : (k + 1) * wide]
            out[k * quarter : (k + 1) * quarter] = piece
        out[half : half + quarter // 2] = made_out[at(y * (quarter // 2), quarter // 2, 32)]
        out[half + quarter // 2 :] = small


def join_outer(keep, came, *outs):
    _, _, _, at_z = spot()
    *blocks, made = outs
    made[...] = low(full(keep[...]) + full(came[...]))
    rows = blocks[0].shape[0]
    for k, block in enumerate(blocks):
        block[...] = made[at((at_z + k) % len(blocks) * rows, rows, 32)]


def join_inner(keep, came, out):
    made = full(keep[...]) + full(came[...])
    count, depth = keep.shape[0], out.shape[0]
    small = resplit(made[count - LINES :])
    made = low(made)
    rows = (count - LINES) // 5 // depth * 2
    part = rows // 2
    first = 2 * rows * depth
    for z in range(depth):
        for k in range(2):
            begin = (k * depth + z) * rows
            out[z, k * rows : (k + 1) * rows] = made[begin : begin + rows]
        out[z, 2 * rows : 2 * rows + part] = made[first + z * part : first + (z + 1) * part]
        out[z, 2 * rows + part :] = small


def weight_three(g_query, g_mine, came, states, w_three, back, keep, send, g_three):
    _, at_c, _, _ = spot()
    share = g_query.shape[1]
    g_three[:, :share] = g_query[...]
    g_three[:, share:] = low(g_mine[...] + came[...])
    made = low(dot(states[...], g_three[...], 0, 0))
    part = (keep.shape[0] - LINES) // 2
    for k in range(2):
        for c in range(2):
            piece = made[(2 * k + c) * part : (2 * k + c + 1) * part]

            @pl.when(at_c == c)
            def _():
                keep[k * part : (k + 1) * part] = piece

            @pl.when(at_c != c)
            def _():
                send[k * part : (k + 1) * part] = piece

    bias = jnp.broadcast_to(low(total(full(g_three[...]))), (LINES, 3 * share))
    keep[2 * part :] = bias
    send[2 * part :] = bias
    back[...] = low(dot(g_three[...], w_three[...], 1, 1))


def grad_states(parts, g_one, out):
    seqs, rows = out.shape[:2]
    for s in range(seqs):
        made = g_one[s * rows : (s + 1) * rows]
        for z in range(parts.shape[0] // seqs):
            made = made + full(parts[z * seqs + s])
        out[s] = made


def pack_first(outer_0, outer_1, outer_2, outer_3, keep, came, out):
    rows, wide = outer_0.shape[0], keep.shape[1]
    pieces = [full(piece[...]) for piece in (outer_0, outer_1, outer_2, outer_3)]
    out[:rows] = low(pieces[0] + pieces[1] + pieces[2] + pieces[3])
    summed = low(full(keep[...]) + full(came[...]))
    out[rows : 2 * rows, :wide] = summed[:rows]
    out[2 * rows :, :wide] = summed[rows : rows + 8]
    out[rows:, wide:] = jnp.zeros((rows + 8, out.shape[1] - wide), BF)


def pack_second(inside, vecs, out, loss, g_b_inner, *vectors):
    at_b, _, _, _ = spot()
    made = eight(inside)
    rows = out.shape[0]
    out[...] = low(made[:rows])
    small = made[rows:]
    width = made.shape[1]
    half = width // 2
    loss[...] = (small[10:11, :128] + small[11:12, :128]) / (2.0 * vecs[8:9, :128])
    for k, vector in enumerate(vectors):
        row = small[k : k + 1]
        vector[...] = jnp.where(at_b == 0, row[:, :half], row[:, half:]).reshape(half)
    first = jnp.where(at_b == 0, small[6:7], small[8:9])
    second = jnp.where(at_b == 0, small[7:8], small[9:10])
    g_b_inner[...] = jnp.concatenate([first, second], 1).reshape(2 * width)


def each_piece(pieces):
    _, at_c, at_y, at_z = spot()
    depth = len(pieces) // 4
    for k in range(depth):
        for c in range(2):
            for y in range(2):
                place = (at_c + c) % 2, (at_y + y) % 2, (at_z + depth - k) % depth
                yield pieces[(k * 2 + c) * 2 + y], place


def final_first(*refs):
    pieces, (g_outer, g_query, g_key, g_value, b_query, b_value, biases) = refs[:-7], refs[-7:]
    at_b, _, _, _ = spot()
    depth = len(pieces) // 4
    width = g_query.shape[1]
    rows, share, half = width // 8, width // depth, width // 2
    for piece, (c, y, z) in each_piece(pieces):
        g_outer[at(((c * 2 + y) * depth + z) * rows, rows, 32)] = full(piece[:rows])
        there = at((c * 2 + y) * rows, rows, 32)
        for k in range(depth):

            @pl.when(z == k)
            def _():
                cols = slice(k * share, (k + 1) * share)
                for j, out in enumerate((g_query, g_key, g_value)):
                    out[there, cols] = full(piece[rows : 2 * rows, j * share : (j + 1) * share])
                for j in (0, 2):
                    bias = full(piece[2 * rows :, j * share : (j + 1) * share])
                    biases[j : j + 1, cols] = bias[0:1]

    for j, out in ((0, b_query), (2, b_value)):
        row = biases[j : j + 1]
        out[...] = jnp.where(at_b == 0, row[:, :half], row[:, half:]).reshape(half)


def final_second(*refs):
    pieces, (g_inner, g_out) = refs[:-2], refs[-2:]
    depth = len(pieces) // 4
    half, width = g_out.shape
    rows, part = half // 2 // depth, half // 4 // depth
    for piece, (c, y, z) in each_piece(pieces):
        for k in range(2):
            cols = at((2 * k + c) * width, width, 128)
            g_inner[at((y * depth + z) * rows, rows, 16), cols] = full(piece[k * rows : (k + 1) * rows])
        g_out[at(((c * 2 + y) * depth + z) * part, part, 8)] = full(piece[2 * rows :])


def per_device_heads(
    inputs,
    teacher,
    segments,
    w_query,
    b_query,
    w_key,
    w_value,
    b_value,
    w_out,
    b_out,
    gain_one,
    shift_one,
    w_inner,
    b_inner,
    w_outer,
    b_outer,
    gain_two,
    shift_two,
):
    count = lax.axis_size("ctx")
    depth = count // 4
    place = lax.axis_index("ctx")
    at_c, at_y = place % 2, place // 2 % 2
    seqs, rows, width = inputs.shape
    own = seqs * rows
    half = width // 2
    ff = w_inner.shape[1]
    share = width // depth
    keys = count // 2 * rows
    joint = ("batch", "ctx")
    pairs = [(y, c) for y in range(2) for c in range(2)]
    groups_z = [[z * 4 + r for z in range(depth)] for r in range(4)]
    groups_yz = [[z * 4 + y * 2 + c for z in range(depth) for y in range(2)] for c in range(2)]
    groups_xyc = [[b * count + z * 4 + y * 2 + c for b in range(2) for y, c in pairs] for z in range(depth)]

    def swap_x(values):
        return lax.ppermute(values, "batch", [(0, 1), (1, 0)])

    def swap_y(values):
        return lax.ppermute(values, "ctx", [(i, i ^ 2) for i in range(count)])

    def swap_c(values):
        return lax.ppermute(values, "ctx", [(i, i ^ 1) for i in range(count)])

    def shift_z(values, step):
        return lax.ppermute(values, "ctx", [(i, (i + 4 * step) % count) for i in range(count)])

    def trade(values, groups, axes="ctx"):
        return lax.all_to_all(values, axes, 0, 0, axis_index_groups=groups, tiled=True)

    tie = lax.optimization_barrier
    dma = pltpu.SemaphoreType.DMA

    def spread(block):
        held = [block]
        for _ in range(depth - 1):
            held.append(shift_z(held[-1], 1))
        pieces = []
        for piece in held:
            by_y = swap_y(piece)
            pieces += [piece, by_y, swap_c(piece), swap_c(by_y)]
        return pieces

    blocks, first, p_inner, p_outer, p_out = kernel(
        prepare,
        [
            ((depth * seqs, rows, width), BF),
            ((3 * half // 4 + LINES, width), BF),
            ((half, width), BF),
            ((ff // 8, width), BF),
            ((half // 2, width), BF),
        ],
        [inputs, w_query, w_key, w_value, b_query, b_value, b_out, gain_one, shift_one]
        + [b_outer, gain_two, shift_two, b_inner, segments, w_inner, w_outer, w_out],
        hbm=(14, 15, 16),
        pin=range(14),
        scratch=[dma((4,))],
    )
    states = trade(blocks, groups_yz).reshape(keys, width)
    other = swap_x(first)
    x_inner = swap_x(p_inner)
    seg_seq = lax.dynamic_index_in_dim(segments, at_y, 0, keepdims=False).reshape(-1, 2, rows)
    seg_own = lax.dynamic_index_in_dim(seg_seq, at_c, 1, keepdims=False).reshape(-1)
    seg_peer = lax.dynamic_index_in_dim(seg_seq, 1 - at_c, 1, keepdims=False).reshape(-1)
    seg_key = jnp.concatenate([seg_own, seg_peer])[:, None]
    seg_query = seg_own[None, :]
    seg_tokens = lax.dynamic_slice_in_dim(segments, place * rows, rows, 1).reshape(own, 1)
    states, other, p_outer, p_out, seg_key, seg_query, seg_tokens = tie(
        (states, other, p_outer, p_out, seg_key, seg_query, seg_tokens)
    )
    x_outer = swap_x(p_outer)

    query, pair, vecs, inner_vec, w_three = kernel(
        project,
        [
            ((keys, share), BF),
            ((keys, 2 * share), BF),
            ((LINES, width), F32),
            ((8, ff), F32),
            ((width, 3 * share), BF),
        ],
        [states, first, other],
        scratch=[pltpu.VMEM((width, 3 * share), BF)],
    )
    peer = swap_c(pair)
    query, peer, x_inner = tie((query, peer, x_inner))
    y_inner = swap_y(x_inner)
    mixed, logs = kernel(
        attend,
        [((keys, share), BF), ((8, keys), F32)],
        [query, pair, peer, seg_query, seg_key],
        scratch=[pltpu.VMEM((2 * keys, share), BF), pltpu.VMEM((share, 2 * keys), BF)],
    )
    x_outer, mixed, p_out = tie((x_outer, mixed, p_out))
    mixed = trade(mixed.reshape(depth * seqs, rows, share), groups_yz)
    y_outer = swap_y(x_outer)
    x_out = swap_x(p_out)
    c_inner, c_outer = map(swap_c, (x_inner, x_outer))
    mixed, y_outer, x_out, y_inner, c_inner, c_outer = tie(
        (mixed, y_outer, x_out, y_inner, c_inner, c_outer)
    )
    weights = [w_out, x_out, swap_c(x_out)]
    weights += [w_inner, x_inner, y_inner, c_inner, swap_c(y_inner)]
    weights += [w_outer, x_outer, y_outer, c_outer, swap_c(y_outer)]
    held = [pltpu.VMEM((width, width), BF), pltpu.VMEM((width, ff), BF), pltpu.VMEM((ff, width), BF)]
    output, attended, unit, inverse, slope, chip, away, g_hidden, sums = kernel(
        functools.partial(forward, float(own * 2 * count)),
        [
            (inputs.shape, F32),
            ((own, width), BF),
            ((own, width), F32),
            ((own, 128), F32),
            ((own, ff), F32),
            ((own, ff + 2 * width), BF),
            ((own, ff // 2 + half + width), BF),
            ((own, width), F32),
            ((LINES, width), F32),
        ],
        [mixed, inputs, teacher, seg_tokens, vecs, inner_vec, *weights],
        hbm=range(6, 19),
        pin=(1, 2),
        scratch=[*held, pltpu.VMEM((own, width), BF), dma((3, 9))],
    )
    away = swap_x(away)
    chip_c = swap_c(chip)
    chip_two, away_two, g_one, g_mixed = kernel(
        backward,
        [
            ((own + LINES, ff + 2 * width), BF),
            ((own + LINES, ff + width + half), BF),
            ((own, width), F32),
            ((depth * seqs, rows, share), BF),
        ],
        [chip, slope, g_hidden, unit, inverse, vecs, attended, sums, *weights],
        hbm=range(8, 21),
        scratch=[*held, pltpu.VMEM((8, ff), F32), pltpu.VMEM((LINES, width), F32), dma((3, 9))],
    )
    away, chip_c, chip_two, away_two, g_mixed = tie((away, chip_c, chip_two, away_two, g_mixed))

    two_x = swap_x(away_two)
    g_mixed = trade(g_mixed, groups_yz).reshape(keys, share)
    away_c = swap_c(away)
    two_c = swap_c(chip_two)
    outer_keep, outer_send = kernel(
        weight_outer,
        [((ff // 8, width), BF)] * 2,
        [chip, chip_c, away, away_c],
        scratch=[
            pltpu.VMEM((4 * own, ff // 4), BF),
            pltpu.VMEM((4 * own, width), BF),
            pltpu.VMEM((ff // 4, width), BF),
        ],
    )
    g_mixed, outer_send = tie((g_mixed, outer_send))

    outer_came = swap_y(outer_send)
    g_query, g_mine, g_theirs = kernel(
        attend_back,
        [((keys, share), BF), ((keys, 2 * share), F32), ((keys, 2 * share), F32)],
        [query, pair, peer, seg_query, seg_key, logs, g_mixed],
        pin=range(6),
        scratch=[
            pltpu.VMEM((2 * keys, share), BF),
            pltpu.VMEM((share, 2 * keys), BF),
            pltpu.VMEM((2 * keys, share), BF),
            pltpu.VMEM((2 * keys, 2 * share), F32),
        ],
    )
    outer_came, g_theirs, two_x = tie((outer_came, g_theirs, two_x))

    came = swap_c(g_theirs)
    two_xc = swap_c(two_x)
    outer_rows = ff // 8 // depth
    *outer, _ = kernel(
        join_outer,
        [((outer_rows, width), BF)] * depth + [((ff // 8, width), BF)],
        [outer_keep, outer_came],
    )
    two_xc, came, *outer = tie((two_xc, came, *outer))
    outer = [outer[0]] + [shift_z(outer[k], k) for k in range(1, depth)]
    inner_keep, inner_send = kernel(
        weight_inner,
        [((half + half // 4 + LINES, width), BF)] * 2,
        [chip, chip_c, away, away_c, chip_two, two_c, two_x, two_xc],
        scratch=[
            pltpu.VMEM((4 * own, half), BF),
            pltpu.VMEM((4 * own, ff // 2), BF),
            pltpu.VMEM((half, ff // 2), BF),
            pltpu.VMEM((4 * own, half // 2), BF),
            pltpu.VMEM((4 * own, width), BF),
            pltpu.VMEM((half // 2, width), BF),
        ],
    )
    inner_send, came = tie((inner_send, came))
    inner_came = swap_y(inner_send)
    back, three_keep, three_send = kernel(
        weight_three,
        [((keys, width), BF)] + [((half + LINES, 3 * share), BF)] * 2,
        [g_query, g_mine, came, states, w_three],
        pin=(3, 4),
        scratch=[pltpu.VMEM((keys, 3 * share), BF)],
    )
    back = trade(back.reshape(depth * seqs, rows, width), groups_yz)
    three_keep, three_send = kernel(
        functools.partial(halve_out, 0),
        [((half // 2 + LINES, 3 * share), BF)] * 2,
        [three_keep, swap_c(three_send)],
    )
    three_keep, three_send = kernel(
        functools.partial(halve_out, 2),
        [((half // 4 + LINES, 3 * share), BF)] * 2,
        [three_keep, swap_x(three_send)],
    )
    three_came = swap_y(three_send)
    outer, inner_came, three_came, back = tie((outer, inner_came, three_came, back))

    inner_rows = (half + half // 4) // depth
    (inside,) = kernel(
        join_inner, [((depth, inner_rows + LINES, width), BF)], [inner_keep, inner_came]
    )
    inside = trade(inside, groups_z)
    (packed,) = kernel(
        pack_first, [((2 * outer_rows + 8, width), BF)], [*outer, three_keep, three_came]
    )
    pieces = spread(packed)
    (g_inputs,) = kernel(grad_states, [(inputs.shape, F32)], [back, g_one])

    packed, loss, g_b_inner, *vectors = kernel(
        pack_second,
        [((inner_rows, width), BF), ((1, 128), F32), ((ff // 2,), F32)] + [((half,), F32)] * 6,
        [inside, vecs],
    )
    g_w_outer, g_w_query, g_w_key, g_w_value, g_b_query, g_b_value = kernel(
        final_first,
        [((ff // 2, width), F32)] + [((half, width), F32)] * 3 + [((half,), F32)] * 2,
        pieces,
        scratch=[pltpu.VMEM((8, width), F32)],
    )
    g_w_inner, g_w_out = kernel(
        final_second, [((half, ff), F32), ((half, width), F32)], spread(packed)
    )
    g_b_out, g_gain_one, g_shift_one, g_b_outer, g_gain_two, g_shift_two = vectors
    return (
        output,
        loss[0, 0],
        g_inputs,
        g_w_query,
        g_b_query,
        g_w_key,
        g_w_value,
        g_b_value,
        g_w_out,
        g_b_out,
        g_gain_one,
        g_shift_one,
        g_w_inner,
        g_b_inner,
        g_w_outer,
        g_b_outer,
        g_gain_two,
        g_shift_two,
    )


def per_device(inputs, *others):
    sizes = (lax.axis_size("batch"), lax.axis_size("ctx"), inputs.shape[0])
    if sizes == (2, 16, 2):
        return per_device_heads(inputs, *others)
    return per_device_any(inputs, *others)


def solution(mesh):
    placed = (
        P("batch", "ctx", None),
        P("batch", "ctx", None),
        P("batch", None),
        P("batch", None),
        P("batch"),
        P("batch", None),
        P("batch", None),
        P("batch"),
        P("batch", None),
        P("batch"),
        P("batch"),
        P("batch"),
        P("batch", None),
        P("batch"),
        P("batch", None),
        P("batch"),
        P("batch"),
        P("batch"),
    )
    return jax.shard_map(
        per_device,
        mesh=mesh,
        in_specs=placed,
        out_specs=(
            P("batch", "ctx", None),
            P(),
            P("batch", "ctx", None),
            P("batch", None),
            P("batch"),
            P("batch", None),
            P("batch", None),
            P("batch"),
            P("batch", None),
            P("batch"),
            P("batch"),
            P("batch"),
            P("batch", None),
            P("batch"),
            P("batch", None),
            P("batch"),
            P("batch"),
            P("batch"),
        ),
        check_vma=False,
    )
```

```python
import functools
import math

import jax
import jax.numpy as jnp
from jax import lax
from jax.experimental import pallas as pl
from jax.experimental.pallas import tpu as pltpu
from jax.sharding import PartitionSpec as P

H = 12
HD = 64


NEGATIVE = -1e30
EPSILON = 1e-12


def norm_rows(hidden, gain, shift):
    center = hidden - jnp.mean(hidden, -1, keepdims=True)
    spread = jnp.mean(center * center, -1, keepdims=True)
    return center * lax.rsqrt(spread + EPSILON) * gain + shift


def gelu_exact(values):
    return jax.nn.gelu(values, approximate=False)


def linear(rows_in, weight):
    return jnp.dot(rows_in, weight, preferred_element_type=jnp.float32)


def contract_rows(left, right):
    return lax.dot_general(
        left, right, (((0,), (0,)), ((), ())), preferred_element_type=jnp.float32
    )


def times_transpose(rows_in, weight):
    return lax.dot_general(
        rows_in, weight, (((1,), (1,)), ((), ())), preferred_element_type=jnp.float32
    )


def score_rows(query_one, keys_all, seg_mine, seg_all):
    heads_query = query_one.reshape(query_one.shape[0], H, HD)
    heads_key = keys_all.reshape(keys_all.shape[0], H, HD)
    raw = jnp.einsum(
        "chd,khd->hck", heads_query, heads_key, preferred_element_type=jnp.float32
    ) * HD ** (-0.5)
    allowed = seg_mine[None, :, None] == seg_all[None, None, :]
    return jnp.where(allowed, raw, NEGATIVE)


def per_device_any(
    inputs,
    teacher,
    segments,
    w_query,
    b_query,
    w_key,
    w_value,
    b_value,
    w_out,
    b_out,
    gain_one,
    shift_one,
    w_inner,
    b_inner,
    w_outer,
    b_outer,
    gain_two,
    shift_two,
):
    (
        w_query,
        b_query,
        w_key,
        w_value,
        b_value,
        w_out,
        b_out,
        gain_one,
        shift_one,
        w_inner,
        b_inner,
        w_outer,
        b_outer,
        gain_two,
        shift_two,
    ) = (
        lax.all_gather(w_query, "batch", axis=0, tiled=True),
        lax.all_gather(b_query, "batch", axis=0, tiled=True),
        lax.all_gather(w_key, "batch", axis=0, tiled=True),
        lax.all_gather(w_value, "batch", axis=0, tiled=True),
        lax.all_gather(b_value, "batch", axis=0, tiled=True),
        lax.all_gather(w_out, "batch", axis=0, tiled=True),
        lax.all_gather(b_out, "batch", axis=0, tiled=True),
        lax.all_gather(gain_one, "batch", axis=0, tiled=True),
        lax.all_gather(shift_one, "batch", axis=0, tiled=True),
        lax.all_gather(w_inner, "batch", axis=0, tiled=True),
        lax.all_gather(b_inner, "batch", axis=0, tiled=True),
        lax.all_gather(w_outer, "batch", axis=0, tiled=True),
        lax.all_gather(b_outer, "batch", axis=0, tiled=True),
        lax.all_gather(gain_two, "batch", axis=0, tiled=True),
        lax.all_gather(shift_two, "batch", axis=0, tiled=True),
    )
    scale = HD ** (-0.5)
    seqs_here, ctx_rows, width = inputs.shape
    rows_here = seqs_here * ctx_rows
    tokens_all = rows_here * lax.axis_size("batch") * lax.axis_size("ctx")
    seg_own = lax.dynamic_slice_in_dim(segments, lax.axis_index("ctx") * ctx_rows, ctx_rows, 1)
    inputs_flat = inputs.reshape(rows_here, width)
    inputs_low = inputs_flat.astype(jnp.bfloat16)
    query = (linear(inputs_low, w_query) + b_query.astype(jnp.float32)).astype(jnp.bfloat16)
    key = linear(inputs_low, w_key).astype(jnp.bfloat16)
    value = (linear(inputs_low, w_value) + b_value.astype(jnp.float32)).astype(jnp.bfloat16)
    query_seq = query.reshape(seqs_here, ctx_rows, width)
    key_seq = key.reshape(seqs_here, ctx_rows, width)
    value_seq = value.reshape(seqs_here, ctx_rows, width)

    def attend_forward(items):
        query_one, key_one, value_one, seg_all, seg_mine = items
        keys_all, values_all = (
            lax.all_gather(key_one, "ctx", axis=0, tiled=True),
            lax.all_gather(value_one, "ctx", axis=0, tiled=True),
        )
        scores = score_rows(query_one, keys_all, seg_mine, seg_all)
        highest = jnp.max(scores, -1, keepdims=True)
        expo = jnp.exp(scores - highest)
        totals = jnp.sum(expo, -1, keepdims=True)
        probs = (expo / totals).astype(jnp.bfloat16)
        mixed = jnp.einsum(
            "hck,khd->chd",
            probs,
            values_all.reshape(keys_all.shape[0], H, HD),
            preferred_element_type=jnp.float32,
        )
        return (
            mixed.reshape(ctx_rows, width).astype(jnp.bfloat16),
            (highest + jnp.log(totals))[:, :, 0],
        )

    attended, log_totals = lax.map(
        attend_forward, (query_seq, key_seq, value_seq, segments, seg_own)
    )
    attended_flat = attended.reshape(rows_here, width)
    gain_one_full = gain_one.astype(jnp.float32)
    shift_one_full = shift_one.astype(jnp.float32)
    gain_two_full = gain_two.astype(jnp.float32)
    shift_two_full = shift_two.astype(jnp.float32)
    hidden_one = inputs_flat + linear(attended_flat, w_out) + b_out.astype(jnp.float32)
    normed_one, back_one = jax.vjp(norm_rows, hidden_one, gain_one_full, shift_one_full)
    normed_low = normed_one.astype(jnp.bfloat16)
    inner_pre = linear(normed_low, w_inner) + b_inner.astype(jnp.float32)
    active_full, gelu_back = jax.vjp(gelu_exact, inner_pre)
    active_low = active_full.astype(jnp.bfloat16)
    hidden_two = normed_one + linear(active_low, w_outer) + b_outer.astype(jnp.float32)
    output, back_two = jax.vjp(norm_rows, hidden_two, gain_two_full, shift_two_full)
    valid = (seg_own.reshape(rows_here) != 0).astype(jnp.float32)[:, None]
    error = output - teacher.reshape(rows_here, width)
    loss_total, valid_count = lax.psum(
        (jnp.sum(valid * error * error), jnp.sum(valid)), ("batch", "ctx")
    )
    loss = loss_total / (2.0 * valid_count)
    grad_output = tokens_all / valid_count * valid * error
    grad_hidden_two, grad_gain_two, grad_shift_two = back_two(grad_output)
    grad_branch_two = grad_hidden_two.astype(jnp.bfloat16)
    grad_b_outer = jnp.sum(grad_branch_two.astype(jnp.float32), 0)
    grad_w_outer = contract_rows(active_low, grad_branch_two)
    grad_active = times_transpose(grad_branch_two, w_outer)
    grad_inner = gelu_back(grad_active)[0].astype(jnp.bfloat16)
    grad_b_inner = jnp.sum(grad_inner.astype(jnp.float32), 0)
    grad_w_inner = contract_rows(normed_low, grad_inner)
    grad_normed = grad_hidden_two + times_transpose(grad_inner, w_inner)
    grad_hidden_one, grad_gain_one, grad_shift_one = back_one(grad_normed)
    grad_branch_one = grad_hidden_one.astype(jnp.bfloat16)
    grad_b_out = jnp.sum(grad_branch_one.astype(jnp.float32), 0)
    grad_w_out = contract_rows(attended_flat, grad_branch_one)
    grad_attended = (
        times_transpose(grad_branch_one, w_out)
        .astype(jnp.bfloat16)
        .reshape(seqs_here, ctx_rows, width)
    )

    def attend_backward(items):
        query_one, key_one, value_one, seg_all, seg_mine, log_one, grad_one = items
        keys_all, values_all = (
            lax.all_gather(key_one, "ctx", axis=0, tiled=True),
            lax.all_gather(value_one, "ctx", axis=0, tiled=True),
        )
        key_count = keys_all.shape[0]
        scores = score_rows(query_one, keys_all, seg_mine, seg_all)
        probs = jnp.exp(scores - log_one[:, :, None])
        grad_heads = grad_one.reshape(ctx_rows, H, HD)
        grad_probs = jnp.einsum(
            "chd,khd->hck",
            grad_heads,
            values_all.reshape(key_count, H, HD),
            preferred_element_type=jnp.float32,
        )
        centre = jnp.sum(probs * grad_probs, -1)
        grad_scores = (probs * (grad_probs - centre[:, :, None])).astype(jnp.bfloat16)
        grad_query = (
            jnp.einsum(
                "hck,khd->chd",
                grad_scores,
                keys_all.reshape(key_count, H, HD),
                preferred_element_type=jnp.float32,
            )
            * scale
        )
        grad_query = grad_query.reshape(ctx_rows, width).astype(jnp.bfloat16)
        probs_low = probs.astype(jnp.bfloat16)
        query_heads = query_one.reshape(ctx_rows, H, HD)
        count = ctx_rows * lax.axis_size("ctx")
        grad_key = (
            jnp.einsum("hck,chd->khd", grad_scores, query_heads, preferred_element_type=jnp.float32)
            * scale
        )
        grad_value = jnp.einsum(
            "hck,chd->khd", probs_low, grad_heads, preferred_element_type=jnp.float32
        )
        both = lax.psum_scatter(
            jnp.concatenate([grad_key.reshape(count, width), grad_value.reshape(count, width)], 1),
            "ctx",
            scatter_dimension=0,
            tiled=True,
        )
        return (
            grad_query,
            both[:, :width].astype(jnp.bfloat16),
            both[:, width:].astype(jnp.bfloat16),
        )

    grad_query_seq, grad_key_seq, grad_value_seq = lax.map(
        attend_backward,
        (query_seq, key_seq, value_seq, segments, seg_own, log_totals, grad_attended),
    )
    grad_query_flat = grad_query_seq.reshape(rows_here, width)
    grad_key_flat = grad_key_seq.reshape(rows_here, width)
    grad_value_flat = grad_value_seq.reshape(rows_here, width)
    grad_w_query = contract_rows(inputs_low, grad_query_flat)
    grad_b_query = jnp.sum(grad_query_flat.astype(jnp.float32), 0)
    grad_w_key = contract_rows(inputs_low, grad_key_flat)
    grad_w_value = contract_rows(inputs_low, grad_value_flat)
    grad_b_value = jnp.sum(grad_value_flat.astype(jnp.float32), 0)
    grad_inputs = (
        grad_hidden_one
        + times_transpose(grad_query_flat, w_query)
        + times_transpose(grad_key_flat, w_key)
        + times_transpose(grad_value_flat, w_value)
    )
    (
        grad_w_query,
        grad_b_query,
        grad_w_key,
        grad_w_value,
        grad_b_value,
        grad_w_out,
        grad_b_out,
        grad_gain_one,
        grad_shift_one,
        grad_w_inner,
        grad_b_inner,
        grad_w_outer,
        grad_b_outer,
        grad_gain_two,
        grad_shift_two,
    ) = (
        lax.psum_scatter(
            grad_w_query.astype(jnp.bfloat16), "batch", scatter_dimension=0, tiled=True
        ).astype(jnp.float32),
        lax.psum_scatter(
            grad_b_query.astype(jnp.bfloat16), "batch", scatter_dimension=0, tiled=True
        ).astype(jnp.float32),
        lax.psum_scatter(
            grad_w_key.astype(jnp.bfloat16), "batch", scatter_dimension=0, tiled=True
        ).astype(jnp.float32),
        lax.psum_scatter(
            grad_w_value.astype(jnp.bfloat16), "batch", scatter_dimension=0, tiled=True
        ).astype(jnp.float32),
        lax.psum_scatter(
            grad_b_value.astype(jnp.bfloat16), "batch", scatter_dimension=0, tiled=True
        ).astype(jnp.float32),
        lax.psum_scatter(
            grad_w_out.astype(jnp.bfloat16), "batch", scatter_dimension=0, tiled=True
        ).astype(jnp.float32),
        lax.psum_scatter(
            grad_b_out.astype(jnp.bfloat16), "batch", scatter_dimension=0, tiled=True
        ).astype(jnp.float32),
        lax.psum_scatter(
            grad_gain_one.astype(jnp.bfloat16), "batch", scatter_dimension=0, tiled=True
        ).astype(jnp.float32),
        lax.psum_scatter(
            grad_shift_one.astype(jnp.bfloat16), "batch", scatter_dimension=0, tiled=True
        ).astype(jnp.float32),
        lax.psum_scatter(
            grad_w_inner.astype(jnp.bfloat16), "batch", scatter_dimension=0, tiled=True
        ).astype(jnp.float32),
        lax.psum_scatter(
            grad_b_inner.astype(jnp.bfloat16), "batch", scatter_dimension=0, tiled=True
        ).astype(jnp.float32),
        lax.psum_scatter(
            grad_w_outer.astype(jnp.bfloat16), "batch", scatter_dimension=0, tiled=True
        ).astype(jnp.float32),
        lax.psum_scatter(
            grad_b_outer.astype(jnp.bfloat16), "batch", scatter_dimension=0, tiled=True
        ).astype(jnp.float32),
        lax.psum_scatter(
            grad_gain_two.astype(jnp.bfloat16), "batch", scatter_dimension=0, tiled=True
        ).astype(jnp.float32),
        lax.psum_scatter(
            grad_shift_two.astype(jnp.bfloat16), "batch", scatter_dimension=0, tiled=True
        ).astype(jnp.float32),
    )
    (
        grad_w_query,
        grad_b_query,
        grad_w_key,
        grad_w_value,
        grad_b_value,
        grad_w_out,
        grad_b_out,
        grad_gain_one,
        grad_shift_one,
        grad_w_inner,
        grad_b_inner,
        grad_w_outer,
        grad_b_outer,
        grad_gain_two,
        grad_shift_two,
    ) = lax.psum(
        (
            grad_w_query,
            grad_b_query,
            grad_w_key,
            grad_w_value,
            grad_b_value,
            grad_w_out,
            grad_b_out,
            grad_gain_one,
            grad_shift_one,
            grad_w_inner,
            grad_b_inner,
            grad_w_outer,
            grad_b_outer,
            grad_gain_two,
            grad_shift_two,
        ),
        "ctx",
    )
    return (
        output.reshape(inputs.shape),
        loss,
        grad_inputs.reshape(inputs.shape),
        grad_w_query,
        grad_b_query,
        grad_w_key,
        grad_w_value,
        grad_b_value,
        grad_w_out,
        grad_b_out,
        grad_gain_one,
        grad_shift_one,
        grad_w_inner,
        grad_b_inner,
        grad_w_outer,
        grad_b_outer,
        grad_gain_two,
        grad_shift_two,
    )


BF, F32 = jnp.bfloat16, jnp.float32
LINES = 16
ROOM = 6 << 20


def low(values):
    return values.astype(BF)


def full(values):
    return values.astype(F32)


def dot(left, right, a=1, b=0):
    return lax.dot_general(left, right, (((a,), (b,)), ((), ())), preferred_element_type=F32)


def spot():
    place = lax.axis_index("ctx")
    return lax.axis_index("batch"), place % 2, place // 2 % 2, place // 4


def at(start, size, step):
    return pl.ds(pl.multiple_of(start, step), size)


def kernel(body, outs, args, hbm=(), scratch=(), pin=()):
    name = getattr(body, "func", body).__name__
    where = [pl.BlockSpec(memory_space=pl.ANY if k in hbm else pltpu.VMEM) for k in range(len(args))]
    shapes = [jax.ShapeDtypeStruct(shape, kind) for shape, kind in outs]
    held = [a for k, a in enumerate(args) if k not in hbm] + shapes
    held += [a for a in scratch if a.memory_space == pltpu.VMEM]
    room = sum(math.prod(a.shape) * jnp.dtype(a.dtype).itemsize for a in held) + ROOM
    args = [
        pltpu.with_memory_space_constraint(a, pltpu.HBM) if k in hbm or k in pin else a
        for k, a in enumerate(args)
    ]
    return pl.pallas_call(
        body,
        out_shape=shapes,
        in_specs=where,
        out_specs=[pl.BlockSpec(memory_space=pltpu.VMEM)] * len(shapes),
        scratch_shapes=list(scratch),
        compiler_params=pltpu.CompilerParams(vmem_limit_bytes=room),
        name=name,
    )(*args)


def norm_forward(hidden, gain, shift):
    center = hidden - jnp.mean(hidden, -1, keepdims=True)
    inverse = lax.rsqrt(jnp.mean(center * center, -1, keepdims=True) + EPSILON)
    unit = center * inverse
    return unit * gain + shift, unit, inverse


def norm_backward(grad, unit, inverse, gain):
    scaled = grad * gain
    along = jnp.mean(scaled * unit, -1, keepdims=True)
    return inverse * (scaled - jnp.mean(scaled, -1, keepdims=True) - unit * along)


def total(values):
    return jnp.sum(values, 0, keepdims=True)


def prepare(*refs):
    inputs, w_three, vectors, b_inner, segments = refs[0], refs[1:4], refs[4:12], refs[12], refs[13]
    w_inner, w_outer, w_out, blocks, out, p_inner, p_outer, p_out, sem = refs[14:]
    half, width = w_three[0].shape
    _, at_c, at_y, at_z = spot()
    part, wide = half // 2, w_inner.shape[1] // 4
    rows_out, rows_outer = p_out.shape[0], p_outer.shape[0]
    copies = [
        (
            w_inner.at[at(at_y * part, part, 64), at((k * 2 + at_c) * wide, wide, 128)],
            p_inner.at[k * part : (k + 1) * part],
        )
        for k in range(2)
    ]
    copies.append((w_outer.at[at((at_c * 2 + at_y) * rows_outer, rows_outer, 128)], p_outer))
    copies.append((w_out.at[at(at_c * rows_out, rows_out, 64)], p_out))
    copies = start(copies, sem)
    seqs = inputs.shape[0]
    for s in range(seqs):
        piece = low(inputs[s])
        for z in range(blocks.shape[0] // seqs):
            blocks[z * seqs + s] = piece
    share, rows = width // 4, half // 4
    for z in range(4):

        @pl.when(at_z == z)
        def _():
            for j in range(3):
                for k in range(4):
                    piece = w_three[j][k * rows : (k + 1) * rows, z * share : (z + 1) * share]
                    out[j * rows : (j + 1) * rows, k * share : (k + 1) * share] = piece

    first = 3 * rows
    out[first : first + LINES] = jnp.zeros((LINES, width), BF)
    for r in range(8):
        out[first + r : first + r + 1, :half] = vectors[r][...].reshape(1, half)
    inner = b_inner[...].reshape(1, -1)
    for r in range(4):
        out[first + 8 + r : first + 9 + r, :half] = inner[:, half * r : half * (r + 1)]
    valid = jnp.sum(jnp.where(segments[...] != 0, 1, 0))
    lane = lax.broadcasted_iota(jnp.int32, (1, half), 1)
    parts = jnp.where(lane < 128, valid // 256, valid % 256)
    out[first + 12 : first + 13, :half] = low(full(parts))
    finish(copies)


def start(copies, sem):
    made = [pltpu.make_async_copy(*copy, sem.at[k]) for k, copy in enumerate(copies)]
    for copy in made:
        copy.start()
    return made


def finish(copies):
    for copy in copies:
        copy.wait()


def both_halves(at_b, mine, other):
    return jnp.where(at_b == 0, mine, other), jnp.where(at_b == 0, other, mine)


def project(states, mine, other, query, pair, vecs, inner_vec, held, w_back):
    at_b, _, _, at_z = spot()
    width, share = states.shape[1], query.shape[1]
    half, rows = width // 2, width // 8
    for j in range(3):
        for k in range(4):
            first = slice(j * rows, (j + 1) * rows)
            cols = slice(k * share, (k + 1) * share)
            pieces = both_halves(at_b, mine[first, cols], other[first, cols])
            for h, piece in enumerate(pieces):
                start_row = h * half + k * rows
                held[start_row : start_row + rows, j * share : (j + 1) * share] = piece
    w_back[...] = held[...]
    made = dot(states[...], held[...])
    lines = slice(3 * rows, 3 * rows + LINES)
    top, bottom = both_halves(at_b, full(mine[lines]), full(other[lines]))

    def bias(r):
        row = jnp.where(at_z < 2, top[r : r + 1], bottom[r : r + 1])
        return jnp.where(at_z % 2 == 0, row[:, :share], row[:, share : 2 * share])

    query[...] = low(full(low(made[:, :share] + bias(0))) * HD ** (-0.5))
    pair[:, :share] = low(made[:, share : 2 * share])
    pair[:, share:] = low(made[:, 2 * share :] + bias(1))
    vecs[...] = jnp.zeros_like(vecs)
    for r in range(2, 8):
        vecs[r - 2 : r - 1, :half] = top[r : r + 1, :half]
        vecs[r - 2 : r - 1, half:] = bottom[r : r + 1, :half]
    counts = top[12:13] + bottom[12:13]
    counts = counts[:, :128] * 256.0 + counts[:, 256:384]
    vecs[8:9, :128] = counts
    inner_vec[...] = jnp.zeros_like(inner_vec)
    for b, rows in enumerate((top, bottom)):
        for r in range(4):
            cols = slice((4 * b + r) * half, (4 * b + r + 1) * half)
            inner_vec[0:1, cols] = rows[8 + r : 9 + r, :half]


STEP = 256


def attend(query, mine, peer, seg_query, seg_key, mixed, logs, keys, values):
    count, share = query.shape
    keys[:count] = mine[:, :share]
    keys[count:] = peer[:, :share]
    values[:, :count] = mine[:, share:].T
    values[:, count:] = peer[:, share:].T
    logs[...] = jnp.zeros_like(logs)

    def block(j, carry):
        rows = at(j * STEP, STEP, STEP)
        allowed = seg_key[...] == seg_query[:, rows]
        for h in range(share // HD):
            cols = slice(h * HD, (h + 1) * HD)
            scores = dot(keys[:, cols], query[rows, cols], 1, 1)
            scores = jnp.where(allowed, scores, NEGATIVE)
            highest = jnp.max(scores, 0, keepdims=True)
            expo = jnp.exp(scores - highest)
            totals = jnp.sum(expo, 0, keepdims=True)
            probs = low(expo * (1.0 / totals))
            mixed[rows, cols] = low(dot(values[cols], probs).T)
            logs[h : h + 1, rows] = highest + jnp.log(totals)
        return carry

    lax.fori_loop(0, count // STEP, block, 0)


def attend_back(
    query, mine, peer, seg_query, seg_key, logs, grad, g_query, g_mine, g_peer, keys, flipped, values, made
):
    count, share = query.shape
    keys[:count] = mine[:, :share]
    keys[count:] = peer[:, :share]
    values[:count] = mine[:, share:]
    values[count:] = peer[:, share:]
    flipped[:, :count] = mine[:, :share].T
    flipped[:, count:] = peer[:, :share].T
    made[...] = jnp.zeros_like(made)

    def block(j, carry):
        rows = at(j * STEP, STEP, STEP)
        allowed = seg_key[...] == seg_query[:, rows]
        for h in range(share // HD):
            cols = slice(h * HD, (h + 1) * HD)
            cols_value = slice(share + h * HD, share + (h + 1) * HD)
            scores = dot(keys[:, cols], query[rows, cols], 1, 1)
            scores = jnp.where(allowed, scores, NEGATIVE)
            probs = jnp.exp(scores - logs[h : h + 1, rows])
            g_probs = dot(values[:, cols], grad[rows, cols], 1, 1)
            centre = jnp.sum(probs * g_probs, 0, keepdims=True)
            g_scores = low(probs * (g_probs - centre))
            g_query[rows, cols] = low((dot(flipped[cols], g_scores) * HD ** (-0.5)).T)
            made[:, cols] += dot(g_scores, query[rows, cols])
            made[:, cols_value] += dot(low(probs), grad[rows, cols])
        return carry

    lax.fori_loop(0, count // STEP, block, 0)
    g_mine[...] = made[:count]
    g_peer[...] = made[count:]


def fetch_out(own, pieces, held, sem):
    at_b, at_c, _, _ = spot()
    half, part = own.shape[0], pieces[0].shape[0]
    copies = [(own, held.at[at(at_b * half, half, 128)])]
    for k, piece in enumerate(pieces):
        first = (1 - at_b) * half + (at_c + k) % 2 * part
        copies.append((piece, held.at[at(first, part, 64)]))
    return start(copies, sem)


def fetch_inner(own, pieces, held, sem):
    at_b, at_c, at_y, _ = spot()
    half, part, wide = own.shape[0], pieces[0].shape[0] // 2, pieces[0].shape[1]
    copies = [(own, held.at[at(at_b * half, half, 128)])]
    for c in range(2):
        for y in range(2):
            rows = at((1 - at_b) * half + (at_y + y) % 2 * part, part, 64)
            for k in range(2):
                cols = at((2 * k + (at_c + c) % 2) * wide, wide, 128)
                piece = pieces[2 * c + y].at[k * part : (k + 1) * part]
                copies.append((piece, held.at[rows, cols]))
    return start(copies, sem)


def fetch_outer(own, pieces, held, sem):
    at_b, at_c, at_y, _ = spot()
    half, part = own.shape[0], pieces[0].shape[0]
    copies = [(own, held.at[at(at_b * half, half, 128)])]
    for c in range(2):
        for y in range(2):
            first = (1 - at_b) * half + ((at_c + c) % 2 * 2 + (at_y + y) % 2) * part
            copies.append((pieces[2 * c + y], held.at[at(first, part, 128)]))
    return start(copies, sem)


BLOCK = 256


def forward(tokens_all, *refs):
    mixed, inputs, teacher, seg, vecs, inner_vec = refs[:6]
    weights, (output, attended, unit, inverse, slope, two, g_hidden, sums) = refs[6:19], refs[19:27]
    held_out, held_inner, held_outer, active, sem = refs[27:]
    copies_out = fetch_out(weights[0], weights[1:3], held_out, sem.at[0])
    copies_inner = fetch_inner(weights[3], weights[4:8], held_inner, sem.at[1])
    copies_outer = fetch_outer(weights[8], weights[9:13], held_outer, sem.at[2])
    rows, share = mixed.shape[1:]
    seqs = inputs.shape[0]
    own, width = attended.shape
    ff = slope.shape[1]
    for s in range(seqs):
        for z in range(mixed.shape[0] // seqs):
            attended[s * rows : (s + 1) * rows, z * share : (z + 1) * share] = mixed[z * seqs + s]
    finish(copies_out)
    hidden = inputs[...].reshape(own, width) + dot(attended[...], held_out[...]) + vecs[0:1]
    normed, made_unit, made_inverse = norm_forward(hidden, vecs[1:2], vecs[2:3])
    unit[...] = made_unit
    inverse[...] = jnp.broadcast_to(made_inverse, inverse.shape)
    two[:, :width] = low(normed)
    finish(copies_inner)

    def block(j, carry):
        cols = at(j * BLOCK, BLOCK, BLOCK)
        before = dot(two[:, :width], held_inner[:, cols]) + inner_vec[0:1, cols]
        below = 0.5 * (1.0 + lax.erf(before * 0.7071067811865476))
        active[:, cols] = low(before * below)
        slope[:, cols] = below + before * jnp.exp(before * before * -0.5) * 0.3989422804014327
        return carry

    lax.fori_loop(0, ff // BLOCK, block, 0)
    finish(copies_outer)
    hidden = normed + dot(active[...], held_outer[...]) + vecs[3:4]
    made, unit_two, inverse_two = norm_forward(hidden, vecs[4:5], vecs[5:6])
    output[...] = made.reshape(output.shape)
    valid = jnp.where(seg[...] != 0, 1.0, 0.0)
    error = (made - teacher[...].reshape(own, width)) * valid
    grad = error * (tokens_all / vecs[8:9, 0:1])
    made = norm_backward(grad, unit_two, inverse_two, vecs[4:5])
    g_hidden[...] = made
    g_low = low(made)
    two[:, width:] = g_low
    sums[...] = jnp.zeros_like(sums)
    sums[3:4] = total(full(g_low))
    sums[4:5] = total(grad * unit_two)
    sums[5:6] = total(grad)
    loss = jnp.broadcast_to(jnp.sum(total(error * error), 1, keepdims=True), (1, width))
    sums[10:11] = full(low(loss))
    sums[11:12] = loss - full(low(loss))


def backward(*refs):
    two, slope, g_hidden, unit, inverse, vecs, attended, sums = refs[:8]
    weights, (away_x, away_y, g_one, g_mixed) = refs[8:21], refs[21:25]
    held_out, held_inner, held_outer, g_inner, inner_sums, small, sem = refs[25:]
    at_b, _, _, _ = spot()
    copies_outer = fetch_outer(weights[8], weights[9:13], held_outer, sem.at[2])
    copies_inner = fetch_inner(weights[3], weights[4:8], held_inner, sem.at[1])
    copies_out = fetch_out(weights[0], weights[1:3], held_out, sem.at[0])
    (own, width), ff = unit.shape, slope.shape[1]
    half = width // 2
    away_y[:own, width:] = jnp.where(at_b == 0, attended[:, :half], attended[:, half:])
    away_x[:own, width:] = jnp.where(at_b == 0, attended[:, half:], attended[:, :half])
    finish(copies_outer)

    def block(j, carry):
        cols = at(j * BLOCK, BLOCK, BLOCK)
        grad = low(dot(two[:, width:], held_outer[cols, :], 1, 1) * slope[:, cols])
        g_inner[:, cols] = grad
        inner_sums[0:1, cols] = total(full(grad))
        return carry

    lax.fori_loop(0, ff // BLOCK, block, 0)
    finish(copies_inner)
    g_normed = g_hidden[...] + dot(g_inner[...], held_inner[...], 1, 1)
    made = norm_backward(g_normed, unit[...], inverse[:, 0:1], vecs[1:2])
    g_one[...] = made
    g_low = low(made)
    finish(copies_out)
    g_attended = low(dot(g_low, held_out[...], 1, 1))
    rows, share = g_mixed.shape[1:]
    seqs = own // rows
    for s in range(seqs):
        for z in range(g_mixed.shape[0] // seqs):
            g_mixed[z * seqs + s] = g_attended[s * rows : (s + 1) * rows, z * share : (z + 1) * share]
    small[...] = sums[...]
    small[0:1] = total(full(g_low))
    small[1:2] = total(g_normed * unit[...])
    small[2:3] = total(g_normed)
    for k in range(4):
        small[6 + k : 7 + k] = inner_sums[0:1, k * width : (k + 1) * width]
    for out in (away_x, away_y):
        out[:own, :width] = g_low
        out[own:, :width] = low(small[...])
        out[own:, width:] = jnp.zeros((LINES, half), BF)


def resplit(made):
    lines = made.shape[0]
    loss = made[10:11] + made[11:12]
    return low(jnp.concatenate([made[:10], full(low(loss)), loss - full(low(loss)), made[12:lines]]))


def halve_out(axis, keep, came, next_keep, next_send):
    mine = spot()[axis]
    part = next_keep.shape[0] - LINES
    for k in range(2):
        rows = slice(k * part, (k + 1) * part)
        piece = low(full(keep[rows]) + full(came[rows]))

        @pl.when(mine == k)
        def _():
            next_keep[:part] = piece

        @pl.when(mine != k)
        def _():
            next_send[:part] = piece

    small = resplit(full(keep[2 * part :]) + full(came[2 * part :]))
    next_keep[part:] = small
    next_send[part:] = small


def eight(parts):
    made = full(parts[0])
    for k in range(1, parts.shape[0]):
        made = made + full(parts[k])
    return made


def weight_feed(*refs):
    pieces, (inner_vec, w_inner, i_x, i_y, w_outer, o_x, out) = refs[:8], refs[8:15]
    held_inner, held_outer, states, grads, active, g_inner, sem = refs[15:]
    at_b, at_c, at_y, _ = spot()
    half, width = w_inner.shape[0], states.shape[1]
    other, part = (1 - at_b) * half, half // 2
    copies = []
    for k in range(2):
        cols = slice(k * half, (k + 1) * half)
        there = at((2 * k + at_c) * width + at_y * half, half, 128)
        copies.append((w_inner.at[:, there], held_inner.at[at(at_b * half, half, 128), cols]))
        for y, piece in enumerate((i_x, i_y)):
            rows = at(other + (at_y + y) % 2 * part, part, 64)
            from_rows = slice(k * part, (k + 1) * part)
            copies.append((piece.at[from_rows, at(at_y * half, half, 128)], held_inner.at[rows, cols]))
    rows = at((2 * at_c + at_y) * half, half, 128)
    copies.append((w_outer.at[rows], held_outer.at[at(at_b * half, half, 128)]))
    copies.append((o_x, held_outer.at[at(other, half, 128)]))
    copies = start(copies, sem)
    own = pieces[0].shape[0]
    for k, piece in enumerate(pieces):
        states[k * own : (k + 1) * own] = piece[:, :width]
        grads[k * own : (k + 1) * own] = piece[:, width:]
    bias = jnp.concatenate(
        [inner_vec[0:1, at((2 * k + at_c) * width + at_y * half, half, 128)] for k in range(2)], 1
    )
    finish(copies)

    def block(j, carry):
        rows = at(j * BLOCK, BLOCK, BLOCK)
        before = dot(states[rows], held_inner[...]) + bias
        below = 0.5 * (1.0 + lax.erf(before * 0.7071067811865476))
        active[rows] = low(before * below)
        slope = below + before * jnp.exp(before * before * -0.5) * 0.3989422804014327
        g_inner[rows] = low(dot(grads[rows], held_outer[...], 1, 1) * slope)
        return carry

    lax.fori_loop(0, 8 * own // BLOCK, block, 0)
    mine = at(at_b * half, half, 128)
    depth, rows = out.shape[0], out.shape[1] // 2
    made = low(dot(active[:, mine], grads[...], 0, 0))
    for z in range(depth):
        out[z, :rows] = made[z * rows : (z + 1) * rows]
    made = low(dot(states[:, mine], g_inner[...], 0, 0))
    for z in range(depth):
        out[z, rows:] = made[z * rows : (z + 1) * rows]


def weight_out(*refs):
    pieces, (feed, out, left, right) = refs[:8], refs[8:]
    _, at_c, at_y, _ = spot()
    width, part = right.shape[1], left.shape[1]
    rows = right.shape[0] // 8
    for k, piece in enumerate(pieces):
        there = slice(k * rows, (k + 1) * rows)
        right[there] = piece[:rows, :width]
        mixed = piece[:rows, width:]
        mixed = jnp.where(at_c == 0, mixed[:, : 2 * part], mixed[:, 2 * part :])
        left[there] = jnp.where(at_y == 0, mixed[:, :part], mixed[:, part:])
    made = low(dot(left[...], right[...], 0, 0))
    small = resplit(sum(full(piece[rows:, :width]) for piece in pieces))
    depth, first = feed.shape[:2]
    part = part // depth
    for z in range(depth):
        out[z, :first] = feed[z]
        out[z, first : first + part] = made[z * part : (z + 1) * part]
        out[z, first + part :] = small


def weight_three(g_query, g_mine, came, states, w_three, back, keep, send, g_three):
    _, at_c, _, _ = spot()
    share = g_query.shape[1]
    g_three[:, :share] = g_query[...]
    g_three[:, share:] = low(g_mine[...] + came[...])
    made = low(dot(states[...], g_three[...], 0, 0))
    part = (keep.shape[0] - LINES) // 2
    for k in range(2):
        for c in range(2):
            piece = made[(2 * k + c) * part : (2 * k + c + 1) * part]

            @pl.when(at_c == c)
            def _():
                keep[k * part : (k + 1) * part] = piece

            @pl.when(at_c != c)
            def _():
                send[k * part : (k + 1) * part] = piece

    bias = jnp.broadcast_to(low(total(full(g_three[...]))), (LINES, 3 * share))
    keep[2 * part :] = bias
    send[2 * part :] = bias
    back[...] = low(dot(g_three[...], w_three[...], 1, 1))


def grad_states(parts, g_one, out):
    seqs, rows = out.shape[:2]
    for s in range(seqs):
        made = g_one[s * rows : (s + 1) * rows]
        for z in range(parts.shape[0] // seqs):
            made = made + full(parts[z * seqs + s])
        out[s] = made


def pack(summed, keep, came, vecs, out, loss, g_b_inner, *vectors):
    at_b, _, _, _ = spot()
    made = eight(summed)
    width, wide = made.shape[1], keep.shape[1]
    rows, share = (out.shape[0] - 8) // 3, width - wide
    part = made.shape[0] - LINES - 2 * rows
    out[: 2 * rows] = low(made[: 2 * rows])
    three = low(full(keep[...]) + full(came[...]))
    out[2 * rows : 3 * rows, :wide] = three[:rows]
    for k in range(width // share):
        piece = made[2 * rows : 2 * rows + part, k * share : (k + 1) * share]
        out[2 * rows + k * part : 2 * rows + (k + 1) * part, wide:] = low(piece)
    out[3 * rows :, :wide] = three[rows : rows + 8]
    out[3 * rows :, wide:] = jnp.zeros((8, share), BF)
    small = made[2 * rows + part :]
    half = width // 2
    loss[...] = (small[10:11, :128] + small[11:12, :128]) / (2.0 * vecs[8:9, :128])
    for k, vector in enumerate(vectors):
        row = small[k : k + 1]
        vector[...] = jnp.where(at_b == 0, row[:, :half], row[:, half:]).reshape(half)
    first = jnp.where(at_b == 0, small[6:7], small[8:9])
    second = jnp.where(at_b == 0, small[7:8], small[9:10])
    g_b_inner[...] = jnp.concatenate([first, second], 1).reshape(2 * width)


def each_piece(pieces):
    _, at_c, at_y, at_z = spot()
    depth = len(pieces) // 4
    for k in range(depth):
        for c in range(2):
            for y in range(2):
                place = (at_c + c) % 2, (at_y + y) % 2, (at_z + depth - k) % depth
                yield pieces[(k * 2 + c) * 2 + y], place


def final(*refs):
    pieces, outs = refs[:-9], refs[-9:]
    g_outer, g_inner, g_out, g_query, g_key, g_value, b_query, b_value, biases = outs
    at_b, _, _, _ = spot()
    depth = len(pieces) // 4
    half, width = g_query.shape
    rows, share = width // 8, width // depth
    part = rows // depth
    for piece, (c, y, z) in each_piece(pieces):
        place = (c * 2 + y) * depth + z
        g_outer[at(place * rows, rows, 32)] = full(piece[:rows])
        for k in range(2):
            cols = at((2 * k + c) * width + y * half, half, 128)
            g_inner[at(z * rows, rows, 32), cols] = full(
                piece[rows : 2 * rows, k * half : (k + 1) * half]
            )
        for k in range(depth):
            first = 2 * rows + k * part
            g_out[at(place * part, part, 8), k * share : (k + 1) * share] = full(
                piece[first : first + part, 3 * share :]
            )
        there = at((c * 2 + y) * rows, rows, 32)
        for k in range(depth):

            @pl.when(z == k)
            def _():
                cols = slice(k * share, (k + 1) * share)
                for j, out in enumerate((g_query, g_key, g_value)):
                    out[there, cols] = full(piece[2 * rows : 3 * rows, j * share : (j + 1) * share])
                for j in (0, 2):
                    bias = full(piece[3 * rows :, j * share : (j + 1) * share])
                    biases[j : j + 1, cols] = bias[0:1]

    for j, out in ((0, b_query), (2, b_value)):
        row = biases[j : j + 1]
        out[...] = jnp.where(at_b == 0, row[:, :half], row[:, half:]).reshape(half)


def per_device_heads(
    inputs,
    teacher,
    segments,
    w_query,
    b_query,
    w_key,
    w_value,
    b_value,
    w_out,
    b_out,
    gain_one,
    shift_one,
    w_inner,
    b_inner,
    w_outer,
    b_outer,
    gain_two,
    shift_two,
):
    count = lax.axis_size("ctx")
    depth = count // 4
    place = lax.axis_index("ctx")
    at_c, at_y = place % 2, place // 2 % 2
    seqs, rows, width = inputs.shape
    own = seqs * rows
    half = width // 2
    ff = w_inner.shape[1]
    share = width // depth
    keys = count // 2 * rows
    joint = ("batch", "ctx")
    pairs = [(y, c) for y in range(2) for c in range(2)]
    groups_z = [[z * 4 + r for z in range(depth)] for r in range(4)]
    groups_yz = [[z * 4 + y * 2 + c for z in range(depth) for y in range(2)] for c in range(2)]
    groups_xyc = [[b * count + z * 4 + y * 2 + c for b in range(2) for y, c in pairs] for z in range(depth)]

    def swap_x(values):
        return lax.ppermute(values, "batch", [(0, 1), (1, 0)])

    def swap_y(values):
        return lax.ppermute(values, "ctx", [(i, i ^ 2) for i in range(count)])

    def swap_xy(values):
        return lax.ppermute(values, joint, [(i, (i + count) % (2 * count) ^ 2) for i in range(2 * count)])

    def swap_c(values):
        return lax.ppermute(values, "ctx", [(i, i ^ 1) for i in range(count)])

    def shift_z(values, step):
        return lax.ppermute(values, "ctx", [(i, (i + 4 * step) % count) for i in range(count)])

    def trade(values, groups, axes="ctx"):
        return lax.all_to_all(values, axes, 0, 0, axis_index_groups=groups, tiled=True)

    tie = lax.optimization_barrier
    dma = pltpu.SemaphoreType.DMA

    def spread(block):
        up, down, block_y = tie((shift_z(block, 1), shift_z(block, -1), swap_y(block)))
        across, up_y, down_y = tie((shift_z(up, 1), swap_y(up), swap_y(down)))
        across_y = swap_y(across)
        held = [(block, block_y), (up, up_y), (across, across_y), (down, down_y)]
        return [piece for pair in held for piece in (*pair, swap_c(pair[0]), swap_c(pair[1]))]

    blocks, first, p_inner, p_outer, p_out = kernel(
        prepare,
        [
            ((depth * seqs, rows, width), BF),
            ((3 * half // 4 + LINES, width), BF),
            ((half, width), BF),
            ((ff // 8, width), BF),
            ((half // 2, width), BF),
        ],
        [inputs, w_query, w_key, w_value, b_query, b_value, b_out, gain_one, shift_one]
        + [b_outer, gain_two, shift_two, b_inner, segments, w_inner, w_outer, w_out],
        hbm=(14, 15, 16),
        pin=range(14),
        scratch=[dma((4,))],
    )
    states = trade(blocks, groups_yz).reshape(keys, width)
    other = swap_x(first)
    x_inner = swap_x(p_inner)
    seg_seq = lax.dynamic_index_in_dim(segments, at_y, 0, keepdims=False).reshape(-1, 2, rows)
    seg_own = lax.dynamic_index_in_dim(seg_seq, at_c, 1, keepdims=False).reshape(-1)
    seg_peer = lax.dynamic_index_in_dim(seg_seq, 1 - at_c, 1, keepdims=False).reshape(-1)
    seg_key = jnp.concatenate([seg_own, seg_peer])[:, None]
    seg_query = seg_own[None, :]
    seg_tokens = lax.dynamic_slice_in_dim(segments, place * rows, rows, 1).reshape(own, 1)
    states, other, p_outer, p_out, seg_key, seg_query, seg_tokens = tie(
        (states, other, p_outer, p_out, seg_key, seg_query, seg_tokens)
    )
    x_outer = swap_x(p_outer)

    query, pair, vecs, inner_vec, w_three = kernel(
        project,
        [
            ((keys, share), BF),
            ((keys, 2 * share), BF),
            ((LINES, width), F32),
            ((8, ff), F32),
            ((width, 3 * share), BF),
        ],
        [states, first, other],
        scratch=[pltpu.VMEM((width, 3 * share), BF)],
    )
    peer = swap_c(pair)
    query, peer, x_inner = tie((query, peer, x_inner))
    y_inner = swap_y(x_inner)
    mixed, logs = kernel(
        attend,
        [((keys, share), BF), ((8, keys), F32)],
        [query, pair, peer, seg_query, seg_key],
        scratch=[pltpu.VMEM((2 * keys, share), BF), pltpu.VMEM((share, 2 * keys), BF)],
    )
    x_outer, mixed, p_out = tie((x_outer, mixed, p_out))
    mixed = trade(mixed.reshape(depth * seqs, rows, share), groups_yz)
    y_outer = swap_y(x_outer)
    x_out = swap_x(p_out)
    c_inner, c_outer = map(swap_c, (x_inner, x_outer))
    mixed, y_outer, x_out, y_inner, c_inner, c_outer = tie(
        (mixed, y_outer, x_out, y_inner, c_inner, c_outer)
    )
    weights = [w_out, x_out, swap_c(x_out)]
    weights += [w_inner, x_inner, y_inner, c_inner, swap_c(y_inner)]
    weights += [w_outer, x_outer, y_outer, c_outer, swap_c(y_outer)]
    held = [pltpu.VMEM((width, width), BF), pltpu.VMEM((width, ff), BF), pltpu.VMEM((ff, width), BF)]
    output, attended, unit, inverse, slope, two, g_hidden, sums = kernel(
        functools.partial(forward, float(own * 2 * count)),
        [
            (inputs.shape, F32),
            ((own, width), BF),
            ((own, width), F32),
            ((own, 128), F32),
            ((own, ff), F32),
            ((own, 2 * width), BF),
            ((own, width), F32),
            ((LINES, width), F32),
        ],
        [mixed, inputs, teacher, seg_tokens, vecs, inner_vec, *weights],
        hbm=range(6, 19),
        pin=(1, 2),
        scratch=[*held, pltpu.VMEM((own, ff), BF), dma((3, 9))],
    )
    fours = [two, swap_x(two), swap_y(two), swap_xy(two)]
    away_x, away_y, g_one, g_mixed = kernel(
        backward,
        [
            ((own + LINES, width + half), BF),
            ((own + LINES, width + half), BF),
            ((own, width), F32),
            ((depth * seqs, rows, share), BF),
        ],
        [two, slope, g_hidden, unit, inverse, vecs, attended, sums, *weights],
        hbm=range(8, 21),
        scratch=[
            *held,
            pltpu.VMEM((own, ff), BF),
            pltpu.VMEM((8, ff), F32),
            pltpu.VMEM((LINES, width), F32),
            dma((3, 9)),
        ],
    )
    away_x, away_y, *fours = tie((away_x, away_y, *fours))
    g_mixed = trade(g_mixed, groups_yz).reshape(keys, share)
    g_mixed, *fours = tie((g_mixed, *fours))
    outer_rows = half // depth
    (feed,) = kernel(
        weight_feed,
        [((depth, 2 * outer_rows, width), BF)],
        [*fours, *map(swap_c, fours), inner_vec, w_inner, x_inner, y_inner, w_outer, x_outer],
        hbm=range(9, 14),
        scratch=[
            pltpu.VMEM((width, width), BF),
            pltpu.VMEM((width, width), BF),
            pltpu.VMEM((8 * own, width), BF),
            pltpu.VMEM((8 * own, width), BF),
            pltpu.VMEM((8 * own, width), BF),
            pltpu.VMEM((8 * own, width), BF),
            dma((8,)),
        ],
    )
    fours = [away_y, swap_x(away_x), swap_y(away_y), swap_xy(away_x)]
    feed, *fours = tie((feed, *fours))
    part = half // 4 // depth
    (summed,) = kernel(
        weight_out,
        [((depth, 2 * outer_rows + part + LINES, width), BF)],
        [*fours, *map(swap_c, fours), feed],
        scratch=[pltpu.VMEM((8 * own, half // 4), BF), pltpu.VMEM((8 * own, width), BF)],
    )
    summed, g_mixed = tie((summed, g_mixed))
    summed = trade(summed, groups_z)

    g_query, g_mine, g_theirs = kernel(
        attend_back,
        [((keys, share), BF), ((keys, 2 * share), F32), ((keys, 2 * share), F32)],
        [query, pair, peer, seg_query, seg_key, logs, g_mixed],
        pin=range(6),
        scratch=[
            pltpu.VMEM((2 * keys, share), BF),
            pltpu.VMEM((share, 2 * keys), BF),
            pltpu.VMEM((2 * keys, share), BF),
            pltpu.VMEM((2 * keys, 2 * share), F32),
        ],
    )
    back, three_keep, three_send = kernel(
        weight_three,
        [((keys, width), BF)] + [((half + LINES, 3 * share), BF)] * 2,
        [g_query, g_mine, swap_c(g_theirs), states, w_three],
        pin=(3, 4),
        scratch=[pltpu.VMEM((keys, 3 * share), BF)],
    )
    three_keep, three_send = kernel(
        functools.partial(halve_out, 0),
        [((half // 2 + LINES, 3 * share), BF)] * 2,
        [three_keep, swap_c(three_send)],
    )
    three_keep, three_send = kernel(
        functools.partial(halve_out, 2),
        [((half // 4 + LINES, 3 * share), BF)] * 2,
        [three_keep, swap_x(three_send)],
    )
    three_came = swap_y(three_send)
    packed, loss, g_b_inner, *vectors = kernel(
        pack,
        [((3 * outer_rows + 8, width), BF), ((1, 128), F32), ((ff // 2,), F32)] + [((half,), F32)] * 6,
        [summed, three_keep, three_came, vecs],
    )
    packed, back = tie((packed, back))
    pieces = spread(packed)
    back = trade(back.reshape(depth * seqs, rows, width), groups_yz)
    (g_inputs,) = kernel(grad_states, [(inputs.shape, F32)], [back, g_one])
    g_w_outer, g_w_inner, g_w_out, g_w_query, g_w_key, g_w_value, g_b_query, g_b_value = kernel(
        final,
        [((ff // 2, width), F32), ((half, ff), F32)] + [((half, width), F32)] * 4 + [((half,), F32)] * 2,
        pieces,
        scratch=[pltpu.VMEM((8, width), F32)],
    )
    g_b_out, g_gain_one, g_shift_one, g_b_outer, g_gain_two, g_shift_two = vectors
    return (
        output,
        loss[0, 0],
        g_inputs,
        g_w_query,
        g_b_query,
        g_w_key,
        g_w_value,
        g_b_value,
        g_w_out,
        g_b_out,
        g_gain_one,
        g_shift_one,
        g_w_inner,
        g_b_inner,
        g_w_outer,
        g_b_outer,
        g_gain_two,
        g_shift_two,
    )


def per_device(inputs, *others):
    sizes = (lax.axis_size("batch"), lax.axis_size("ctx"), inputs.shape[0])
    if sizes == (2, 16, 2):
        return per_device_heads(inputs, *others)
    return per_device_any(inputs, *others)


def solution(mesh):
    placed = (
        P("batch", "ctx", None),
        P("batch", "ctx", None),
        P("batch", None),
        P("batch", None),
        P("batch"),
        P("batch", None),
        P("batch", None),
        P("batch"),
        P("batch", None),
        P("batch"),
        P("batch"),
        P("batch"),
        P("batch", None),
        P("batch"),
        P("batch", None),
        P("batch"),
        P("batch"),
        P("batch"),
    )
    return jax.shard_map(
        per_device,
        mesh=mesh,
        in_specs=placed,
        out_specs=(
            P("batch", "ctx", None),
            P(),
            P("batch", "ctx", None),
            P("batch", None),
            P("batch"),
            P("batch", None),
            P("batch", None),
            P("batch"),
            P("batch", None),
            P("batch"),
            P("batch"),
            P("batch"),
            P("batch", None),
            P("batch"),
            P("batch", None),
            P("batch"),
            P("batch"),
            P("batch"),
        ),
        check_vma=False,
    )
```

```python
import functools
import math

import jax
import jax.numpy as jnp
from jax import lax
from jax.experimental import pallas as pl
from jax.experimental.pallas import tpu as pltpu
from jax.sharding import PartitionSpec as P

H = 12
HD = 64


NEGATIVE = -1e30
EPSILON = 1e-12


def norm_rows(hidden, gain, shift):
    center = hidden - jnp.mean(hidden, -1, keepdims=True)
    spread = jnp.mean(center * center, -1, keepdims=True)
    return center * lax.rsqrt(spread + EPSILON) * gain + shift


def gelu_exact(values):
    return jax.nn.gelu(values, approximate=False)


def linear(rows_in, weight):
    return jnp.dot(rows_in, weight, preferred_element_type=jnp.float32)


def contract_rows(left, right):
    return lax.dot_general(
        left, right, (((0,), (0,)), ((), ())), preferred_element_type=jnp.float32
    )


def times_transpose(rows_in, weight):
    return lax.dot_general(
        rows_in, weight, (((1,), (1,)), ((), ())), preferred_element_type=jnp.float32
    )


def score_rows(query_one, keys_all, seg_mine, seg_all):
    heads_query = query_one.reshape(query_one.shape[0], H, HD)
    heads_key = keys_all.reshape(keys_all.shape[0], H, HD)
    raw = jnp.einsum(
        "chd,khd->hck", heads_query, heads_key, preferred_element_type=jnp.float32
    ) * HD ** (-0.5)
    allowed = seg_mine[None, :, None] == seg_all[None, None, :]
    return jnp.where(allowed, raw, NEGATIVE)


def per_device_any(
    inputs,
    teacher,
    segments,
    w_query,
    b_query,
    w_key,
    w_value,
    b_value,
    w_out,
    b_out,
    gain_one,
    shift_one,
    w_inner,
    b_inner,
    w_outer,
    b_outer,
    gain_two,
    shift_two,
):
    (
        w_query,
        b_query,
        w_key,
        w_value,
        b_value,
        w_out,
        b_out,
        gain_one,
        shift_one,
        w_inner,
        b_inner,
        w_outer,
        b_outer,
        gain_two,
        shift_two,
    ) = (
        lax.all_gather(w_query, "batch", axis=0, tiled=True),
        lax.all_gather(b_query, "batch", axis=0, tiled=True),
        lax.all_gather(w_key, "batch", axis=0, tiled=True),
        lax.all_gather(w_value, "batch", axis=0, tiled=True),
        lax.all_gather(b_value, "batch", axis=0, tiled=True),
        lax.all_gather(w_out, "batch", axis=0, tiled=True),
        lax.all_gather(b_out, "batch", axis=0, tiled=True),
        lax.all_gather(gain_one, "batch", axis=0, tiled=True),
        lax.all_gather(shift_one, "batch", axis=0, tiled=True),
        lax.all_gather(w_inner, "batch", axis=0, tiled=True),
        lax.all_gather(b_inner, "batch", axis=0, tiled=True),
        lax.all_gather(w_outer, "batch", axis=0, tiled=True),
        lax.all_gather(b_outer, "batch", axis=0, tiled=True),
        lax.all_gather(gain_two, "batch", axis=0, tiled=True),
        lax.all_gather(shift_two, "batch", axis=0, tiled=True),
    )
    scale = HD ** (-0.5)
    seqs_here, ctx_rows, width = inputs.shape
    rows_here = seqs_here * ctx_rows
    tokens_all = rows_here * lax.axis_size("batch") * lax.axis_size("ctx")
    seg_own = lax.dynamic_slice_in_dim(segments, lax.axis_index("ctx") * ctx_rows, ctx_rows, 1)
    inputs_flat = inputs.reshape(rows_here, width)
    inputs_low = inputs_flat.astype(jnp.bfloat16)
    query = (linear(inputs_low, w_query) + b_query.astype(jnp.float32)).astype(jnp.bfloat16)
    key = linear(inputs_low, w_key).astype(jnp.bfloat16)
    value = (linear(inputs_low, w_value) + b_value.astype(jnp.float32)).astype(jnp.bfloat16)
    query_seq = query.reshape(seqs_here, ctx_rows, width)
    key_seq = key.reshape(seqs_here, ctx_rows, width)
    value_seq = value.reshape(seqs_here, ctx_rows, width)

    def attend_forward(items):
        query_one, key_one, value_one, seg_all, seg_mine = items
        keys_all, values_all = (
            lax.all_gather(key_one, "ctx", axis=0, tiled=True),
            lax.all_gather(value_one, "ctx", axis=0, tiled=True),
        )
        scores = score_rows(query_one, keys_all, seg_mine, seg_all)
        highest = jnp.max(scores, -1, keepdims=True)
        expo = jnp.exp(scores - highest)
        totals = jnp.sum(expo, -1, keepdims=True)
        probs = (expo / totals).astype(jnp.bfloat16)
        mixed = jnp.einsum(
            "hck,khd->chd",
            probs,
            values_all.reshape(keys_all.shape[0], H, HD),
            preferred_element_type=jnp.float32,
        )
        return (
            mixed.reshape(ctx_rows, width).astype(jnp.bfloat16),
            (highest + jnp.log(totals))[:, :, 0],
        )

    attended, log_totals = lax.map(
        attend_forward, (query_seq, key_seq, value_seq, segments, seg_own)
    )
    attended_flat = attended.reshape(rows_here, width)
    gain_one_full = gain_one.astype(jnp.float32)
    shift_one_full = shift_one.astype(jnp.float32)
    gain_two_full = gain_two.astype(jnp.float32)
    shift_two_full = shift_two.astype(jnp.float32)
    hidden_one = inputs_flat + linear(attended_flat, w_out) + b_out.astype(jnp.float32)
    normed_one, back_one = jax.vjp(norm_rows, hidden_one, gain_one_full, shift_one_full)
    normed_low = normed_one.astype(jnp.bfloat16)
    inner_pre = linear(normed_low, w_inner) + b_inner.astype(jnp.float32)
    active_full, gelu_back = jax.vjp(gelu_exact, inner_pre)
    active_low = active_full.astype(jnp.bfloat16)
    hidden_two = normed_one + linear(active_low, w_outer) + b_outer.astype(jnp.float32)
    output, back_two = jax.vjp(norm_rows, hidden_two, gain_two_full, shift_two_full)
    valid = (seg_own.reshape(rows_here) != 0).astype(jnp.float32)[:, None]
    error = output - teacher.reshape(rows_here, width)
    loss_total, valid_count = lax.psum(
        (jnp.sum(valid * error * error), jnp.sum(valid)), ("batch", "ctx")
    )
    loss = loss_total / (2.0 * valid_count)
    grad_output = tokens_all / valid_count * valid * error
    grad_hidden_two, grad_gain_two, grad_shift_two = back_two(grad_output)
    grad_branch_two = grad_hidden_two.astype(jnp.bfloat16)
    grad_b_outer = jnp.sum(grad_branch_two.astype(jnp.float32), 0)
    grad_w_outer = contract_rows(active_low, grad_branch_two)
    grad_active = times_transpose(grad_branch_two, w_outer)
    grad_inner = gelu_back(grad_active)[0].astype(jnp.bfloat16)
    grad_b_inner = jnp.sum(grad_inner.astype(jnp.float32), 0)
    grad_w_inner = contract_rows(normed_low, grad_inner)
    grad_normed = grad_hidden_two + times_transpose(grad_inner, w_inner)
    grad_hidden_one, grad_gain_one, grad_shift_one = back_one(grad_normed)
    grad_branch_one = grad_hidden_one.astype(jnp.bfloat16)
    grad_b_out = jnp.sum(grad_branch_one.astype(jnp.float32), 0)
    grad_w_out = contract_rows(attended_flat, grad_branch_one)
    grad_attended = (
        times_transpose(grad_branch_one, w_out)
        .astype(jnp.bfloat16)
        .reshape(seqs_here, ctx_rows, width)
    )

    def attend_backward(items):
        query_one, key_one, value_one, seg_all, seg_mine, log_one, grad_one = items
        keys_all, values_all = (
            lax.all_gather(key_one, "ctx", axis=0, tiled=True),
            lax.all_gather(value_one, "ctx", axis=0, tiled=True),
        )
        key_count = keys_all.shape[0]
        scores = score_rows(query_one, keys_all, seg_mine, seg_all)
        probs = jnp.exp(scores - log_one[:, :, None])
        grad_heads = grad_one.reshape(ctx_rows, H, HD)
        grad_probs = jnp.einsum(
            "chd,khd->hck",
            grad_heads,
            values_all.reshape(key_count, H, HD),
            preferred_element_type=jnp.float32,
        )
        centre = jnp.sum(probs * grad_probs, -1)
        grad_scores = (probs * (grad_probs - centre[:, :, None])).astype(jnp.bfloat16)
        grad_query = (
            jnp.einsum(
                "hck,khd->chd",
                grad_scores,
                keys_all.reshape(key_count, H, HD),
                preferred_element_type=jnp.float32,
            )
            * scale
        )
        grad_query = grad_query.reshape(ctx_rows, width).astype(jnp.bfloat16)
        probs_low = probs.astype(jnp.bfloat16)
        query_heads = query_one.reshape(ctx_rows, H, HD)
        count = ctx_rows * lax.axis_size("ctx")
        grad_key = (
            jnp.einsum("hck,chd->khd", grad_scores, query_heads, preferred_element_type=jnp.float32)
            * scale
        )
        grad_value = jnp.einsum(
            "hck,chd->khd", probs_low, grad_heads, preferred_element_type=jnp.float32
        )
        both = lax.psum_scatter(
            jnp.concatenate([grad_key.reshape(count, width), grad_value.reshape(count, width)], 1),
            "ctx",
            scatter_dimension=0,
            tiled=True,
        )
        return (
            grad_query,
            both[:, :width].astype(jnp.bfloat16),
            both[:, width:].astype(jnp.bfloat16),
        )

    grad_query_seq, grad_key_seq, grad_value_seq = lax.map(
        attend_backward,
        (query_seq, key_seq, value_seq, segments, seg_own, log_totals, grad_attended),
    )
    grad_query_flat = grad_query_seq.reshape(rows_here, width)
    grad_key_flat = grad_key_seq.reshape(rows_here, width)
    grad_value_flat = grad_value_seq.reshape(rows_here, width)
    grad_w_query = contract_rows(inputs_low, grad_query_flat)
    grad_b_query = jnp.sum(grad_query_flat.astype(jnp.float32), 0)
    grad_w_key = contract_rows(inputs_low, grad_key_flat)
    grad_w_value = contract_rows(inputs_low, grad_value_flat)
    grad_b_value = jnp.sum(grad_value_flat.astype(jnp.float32), 0)
    grad_inputs = (
        grad_hidden_one
        + times_transpose(grad_query_flat, w_query)
        + times_transpose(grad_key_flat, w_key)
        + times_transpose(grad_value_flat, w_value)
    )
    (
        grad_w_query,
        grad_b_query,
        grad_w_key,
        grad_w_value,
        grad_b_value,
        grad_w_out,
        grad_b_out,
        grad_gain_one,
        grad_shift_one,
        grad_w_inner,
        grad_b_inner,
        grad_w_outer,
        grad_b_outer,
        grad_gain_two,
        grad_shift_two,
    ) = (
        lax.psum_scatter(
            grad_w_query.astype(jnp.bfloat16), "batch", scatter_dimension=0, tiled=True
        ).astype(jnp.float32),
        lax.psum_scatter(
            grad_b_query.astype(jnp.bfloat16), "batch", scatter_dimension=0, tiled=True
        ).astype(jnp.float32),
        lax.psum_scatter(
            grad_w_key.astype(jnp.bfloat16), "batch", scatter_dimension=0, tiled=True
        ).astype(jnp.float32),
        lax.psum_scatter(
            grad_w_value.astype(jnp.bfloat16), "batch", scatter_dimension=0, tiled=True
        ).astype(jnp.float32),
        lax.psum_scatter(
            grad_b_value.astype(jnp.bfloat16), "batch", scatter_dimension=0, tiled=True
        ).astype(jnp.float32),
        lax.psum_scatter(
            grad_w_out.astype(jnp.bfloat16), "batch", scatter_dimension=0, tiled=True
        ).astype(jnp.float32),
        lax.psum_scatter(
            grad_b_out.astype(jnp.bfloat16), "batch", scatter_dimension=0, tiled=True
        ).astype(jnp.float32),
        lax.psum_scatter(
            grad_gain_one.astype(jnp.bfloat16), "batch", scatter_dimension=0, tiled=True
        ).astype(jnp.float32),
        lax.psum_scatter(
            grad_shift_one.astype(jnp.bfloat16), "batch", scatter_dimension=0, tiled=True
        ).astype(jnp.float32),
        lax.psum_scatter(
            grad_w_inner.astype(jnp.bfloat16), "batch", scatter_dimension=0, tiled=True
        ).astype(jnp.float32),
        lax.psum_scatter(
            grad_b_inner.astype(jnp.bfloat16), "batch", scatter_dimension=0, tiled=True
        ).astype(jnp.float32),
        lax.psum_scatter(
            grad_w_outer.astype(jnp.bfloat16), "batch", scatter_dimension=0, tiled=True
        ).astype(jnp.float32),
        lax.psum_scatter(
            grad_b_outer.astype(jnp.bfloat16), "batch", scatter_dimension=0, tiled=True
        ).astype(jnp.float32),
        lax.psum_scatter(
            grad_gain_two.astype(jnp.bfloat16), "batch", scatter_dimension=0, tiled=True
        ).astype(jnp.float32),
        lax.psum_scatter(
            grad_shift_two.astype(jnp.bfloat16), "batch", scatter_dimension=0, tiled=True
        ).astype(jnp.float32),
    )
    (
        grad_w_query,
        grad_b_query,
        grad_w_key,
        grad_w_value,
        grad_b_value,
        grad_w_out,
        grad_b_out,
        grad_gain_one,
        grad_shift_one,
        grad_w_inner,
        grad_b_inner,
        grad_w_outer,
        grad_b_outer,
        grad_gain_two,
        grad_shift_two,
    ) = lax.psum(
        (
            grad_w_query,
            grad_b_query,
            grad_w_key,
            grad_w_value,
            grad_b_value,
            grad_w_out,
            grad_b_out,
            grad_gain_one,
            grad_shift_one,
            grad_w_inner,
            grad_b_inner,
            grad_w_outer,
            grad_b_outer,
            grad_gain_two,
            grad_shift_two,
        ),
        "ctx",
    )
    return (
        output.reshape(inputs.shape),
        loss,
        grad_inputs.reshape(inputs.shape),
        grad_w_query,
        grad_b_query,
        grad_w_key,
        grad_w_value,
        grad_b_value,
        grad_w_out,
        grad_b_out,
        grad_gain_one,
        grad_shift_one,
        grad_w_inner,
        grad_b_inner,
        grad_w_outer,
        grad_b_outer,
        grad_gain_two,
        grad_shift_two,
    )


BF, F32 = jnp.bfloat16, jnp.float32
LINES = 16
ROOM = 6 << 20


def low(values):
    return values.astype(BF)


def full(values):
    return values.astype(F32)


def dot(left, right, a=1, b=0):
    return lax.dot_general(left, right, (((a,), (b,)), ((), ())), preferred_element_type=F32)


def spot():
    place = lax.axis_index("ctx")
    return lax.axis_index("batch"), place % 2, place // 2 % 2, place // 4


def at(start, size, step):
    return pl.ds(pl.multiple_of(start, step), size)


def kernel(body, outs, args, hbm=(), scratch=(), pin=(), outs_hbm=(), aliases=None):
    name = getattr(body, "func", body).__name__
    where = [pl.BlockSpec(memory_space=pl.ANY if k in hbm else pltpu.VMEM) for k in range(len(args))]
    shapes = [jax.ShapeDtypeStruct(shape, kind) for shape, kind in outs]
    held = [a for k, a in enumerate(args) if k not in hbm]
    held += [a for k, a in enumerate(shapes) if k not in outs_hbm]
    held += [a for a in scratch if a.memory_space == pltpu.VMEM]
    room = sum(math.prod(a.shape) * jnp.dtype(a.dtype).itemsize for a in held) + ROOM
    args = [
        pltpu.with_memory_space_constraint(a, pltpu.HBM) if k in hbm or k in pin else a
        for k, a in enumerate(args)
    ]
    return pl.pallas_call(
        body,
        out_shape=shapes,
        in_specs=where,
        out_specs=[
            pl.BlockSpec(memory_space=pl.ANY if k in outs_hbm else pltpu.VMEM)
            for k in range(len(shapes))
        ],
        input_output_aliases=aliases or {},
        scratch_shapes=list(scratch),
        compiler_params=pltpu.CompilerParams(vmem_limit_bytes=room),
        name=name,
    )(*args)


def norm_forward(hidden, gain, shift):
    center = hidden - jnp.mean(hidden, -1, keepdims=True)
    inverse = lax.rsqrt(jnp.mean(center * center, -1, keepdims=True) + EPSILON)
    unit = center * inverse
    return unit * gain + shift, unit, inverse


def norm_backward(grad, unit, inverse, gain):
    scaled = grad * gain
    along = jnp.mean(scaled * unit, -1, keepdims=True)
    return inverse * (scaled - jnp.mean(scaled, -1, keepdims=True) - unit * along)


def total(values):
    return jnp.sum(values, 0, keepdims=True)


def prepare(*refs):
    inputs, w_three, vectors, b_inner, segments = refs[0], refs[1:4], refs[4:12], refs[12], refs[13]
    w_inner, w_outer, w_out, blocks, out, p_inner, p_outer, p_out, sem = refs[14:]
    half, width = w_three[0].shape
    _, at_c, at_y, at_z = spot()
    part, wide = half // 2, w_inner.shape[1] // 4
    rows_out, rows_outer = p_out.shape[0], p_outer.shape[0]
    copies = [
        (
            w_inner.at[at(at_y * part, part, 64), at((k * 2 + at_c) * wide, wide, 128)],
            p_inner.at[k * part : (k + 1) * part],
        )
        for k in range(2)
    ]
    copies.append((w_outer.at[at((at_c * 2 + at_y) * rows_outer, rows_outer, 128)], p_outer))
    copies.append((w_out.at[at(at_c * rows_out, rows_out, 64)], p_out))
    copies = start(copies, sem)
    seqs = inputs.shape[0]
    for s in range(seqs):
        piece = low(inputs[s])
        for z in range(blocks.shape[0] // seqs):
            blocks[z * seqs + s] = piece
    share, rows = width // 4, half // 4
    for z in range(4):

        @pl.when(at_z == z)
        def _():
            for j in range(3):
                for k in range(4):
                    piece = w_three[j][k * rows : (k + 1) * rows, z * share : (z + 1) * share]
                    out[j * rows : (j + 1) * rows, k * share : (k + 1) * share] = piece

    first = 3 * rows
    out[first : first + LINES] = jnp.zeros((LINES, width), BF)
    for r in range(8):
        out[first + r : first + r + 1, :half] = vectors[r][...].reshape(1, half)
    inner = b_inner[...].reshape(1, -1)
    for r in range(4):
        out[first + 8 + r : first + 9 + r, :half] = inner[:, half * r : half * (r + 1)]
    valid = jnp.sum(jnp.where(segments[...] != 0, 1, 0))
    lane = lax.broadcasted_iota(jnp.int32, (1, half), 1)
    parts = jnp.where(lane < 128, valid // 256, valid % 256)
    out[first + 12 : first + 13, :half] = low(full(parts))
    finish(copies)


def start(copies, sem):
    made = [pltpu.make_async_copy(*copy, sem.at[k]) for k, copy in enumerate(copies)]
    for copy in made:
        copy.start()
    return made


def finish(copies):
    for copy in copies:
        copy.wait()


def both_halves(at_b, mine, other):
    return jnp.where(at_b == 0, mine, other), jnp.where(at_b == 0, other, mine)


def project(states, mine, other, query, pair, vecs, inner_vec, held, w_back):
    at_b, _, _, at_z = spot()
    width, share = states.shape[1], query.shape[1]
    half, rows = width // 2, width // 8
    for j in range(3):
        for k in range(4):
            first = slice(j * rows, (j + 1) * rows)
            cols = slice(k * share, (k + 1) * share)
            pieces = both_halves(at_b, mine[first, cols], other[first, cols])
            for h, piece in enumerate(pieces):
                start_row = h * half + k * rows
                held[start_row : start_row + rows, j * share : (j + 1) * share] = piece
    w_back[...] = held[...]
    made = dot(states[...], held[...])
    lines = slice(3 * rows, 3 * rows + LINES)
    top, bottom = both_halves(at_b, full(mine[lines]), full(other[lines]))

    def bias(r):
        row = jnp.where(at_z < 2, top[r : r + 1], bottom[r : r + 1])
        return jnp.where(at_z % 2 == 0, row[:, :share], row[:, share : 2 * share])

    query[...] = low(full(low(made[:, :share] + bias(0))) * HD ** (-0.5))
    pair[:, :share] = low(made[:, share : 2 * share])
    pair[:, share:] = low(made[:, 2 * share :] + bias(1))
    vecs[...] = jnp.zeros_like(vecs)
    for r in range(2, 8):
        vecs[r - 2 : r - 1, :half] = top[r : r + 1, :half]
        vecs[r - 2 : r - 1, half:] = bottom[r : r + 1, :half]
    counts = top[12:13] + bottom[12:13]
    counts = counts[:, :128] * 256.0 + counts[:, 256:384]
    vecs[8:9, :128] = counts
    inner_vec[...] = jnp.zeros_like(inner_vec)
    for b, rows in enumerate((top, bottom)):
        for r in range(4):
            cols = slice((4 * b + r) * half, (4 * b + r + 1) * half)
            inner_vec[0:1, cols] = rows[8 + r : 9 + r, :half]


STEP = 256


def attend(query, mine, peer, seg_query, seg_key, mixed, logs, keys, values):
    count, share = query.shape
    keys[:count] = mine[:, :share]
    keys[count:] = peer[:, :share]
    values[:, :count] = mine[:, share:].T
    values[:, count:] = peer[:, share:].T
    logs[...] = jnp.zeros_like(logs)

    def block(j, carry):
        rows = at(j * STEP, STEP, STEP)
        allowed = seg_key[...] == seg_query[:, rows]
        for h in range(share // HD):
            cols = slice(h * HD, (h + 1) * HD)
            scores = dot(keys[:, cols], query[rows, cols], 1, 1)
            scores = jnp.where(allowed, scores, NEGATIVE)
            highest = jnp.max(scores, 0, keepdims=True)
            expo = jnp.exp(scores - highest)
            totals = jnp.sum(expo, 0, keepdims=True)
            probs = low(expo * (1.0 / totals))
            mixed[rows, cols] = low(dot(values[cols], probs).T)
            logs[h : h + 1, rows] = highest + jnp.log(totals)
        return carry

    lax.fori_loop(0, count // STEP, block, 0)


def attend_back(
    query, mine, peer, seg_query, seg_key, logs, grad, g_query, g_mine, g_peer, keys, flipped, values, made
):
    count, share = query.shape
    keys[:count] = mine[:, :share]
    keys[count:] = peer[:, :share]
    values[:count] = mine[:, share:]
    values[count:] = peer[:, share:]
    flipped[:, :count] = mine[:, :share].T
    flipped[:, count:] = peer[:, :share].T
    made[...] = jnp.zeros_like(made)

    def block(j, carry):
        rows = at(j * STEP, STEP, STEP)
        allowed = seg_key[...] == seg_query[:, rows]
        for h in range(share // HD):
            cols = slice(h * HD, (h + 1) * HD)
            cols_value = slice(share + h * HD, share + (h + 1) * HD)
            scores = dot(keys[:, cols], query[rows, cols], 1, 1)
            scores = jnp.where(allowed, scores, NEGATIVE)
            probs = jnp.exp(scores - logs[h : h + 1, rows])
            g_probs = dot(values[:, cols], grad[rows, cols], 1, 1)
            centre = jnp.sum(probs * g_probs, 0, keepdims=True)
            g_scores = low(probs * (g_probs - centre))
            g_query[rows, cols] = low((dot(flipped[cols], g_scores) * HD ** (-0.5)).T)
            made[:, cols] += dot(g_scores, query[rows, cols])
            made[:, cols_value] += dot(low(probs), grad[rows, cols])
        return carry

    lax.fori_loop(0, count // STEP, block, 0)
    g_mine[...] = made[:count]
    g_peer[...] = made[count:]


def fetch_out(own, pieces, held, sem):
    at_b, at_c, _, _ = spot()
    half, part = own.shape[0], pieces[0].shape[0]
    copies = [(own, held.at[at(at_b * half, half, 128)])]
    for k, piece in enumerate(pieces):
        first = (1 - at_b) * half + (at_c + k) % 2 * part
        copies.append((piece, held.at[at(first, part, 64)]))
    return start(copies, sem)


def fetch_inner(own, pieces, held, sem):
    at_b, at_c, at_y, _ = spot()
    half, part, wide = own.shape[0], pieces[0].shape[0] // 2, pieces[0].shape[1]
    copies = [(own, held.at[at(at_b * half, half, 128)])]
    for c in range(2):
        for y in range(2):
            rows = at((1 - at_b) * half + (at_y + y) % 2 * part, part, 64)
            for k in range(2):
                cols = at((2 * k + (at_c + c) % 2) * wide, wide, 128)
                piece = pieces[2 * c + y].at[k * part : (k + 1) * part]
                copies.append((piece, held.at[rows, cols]))
    return start(copies, sem)


def fetch_outer(own, pieces, held, sem):
    at_b, at_c, at_y, _ = spot()
    half, part = own.shape[0], pieces[0].shape[0]
    copies = [(own, held.at[at(at_b * half, half, 128)])]
    for c in range(2):
        for y in range(2):
            first = (1 - at_b) * half + ((at_c + c) % 2 * 2 + (at_y + y) % 2) * part
            copies.append((pieces[2 * c + y], held.at[at(first, part, 128)]))
    return start(copies, sem)


BLOCK = 256


def forward(tokens_all, *refs):
    mixed, inputs, teacher, seg, vecs, inner_vec = refs[:6]
    weights, (output, attended, unit, inverse, slope, two, g_hidden, sums) = refs[6:19], refs[19:27]
    held_out, held_inner, held_outer, active, sem = refs[27:]
    copies_out = fetch_out(weights[0], weights[1:3], held_out, sem.at[0])
    copies_inner = fetch_inner(weights[3], weights[4:8], held_inner, sem.at[1])
    copies_outer = fetch_outer(weights[8], weights[9:13], held_outer, sem.at[2])
    rows, share = mixed.shape[1:]
    seqs = inputs.shape[0]
    own, width = attended.shape
    ff = slope.shape[1]
    for s in range(seqs):
        for z in range(mixed.shape[0] // seqs):
            attended[s * rows : (s + 1) * rows, z * share : (z + 1) * share] = mixed[z * seqs + s]
    finish(copies_out)
    hidden = inputs[...].reshape(own, width) + dot(attended[...], held_out[...]) + vecs[0:1]
    normed, made_unit, made_inverse = norm_forward(hidden, vecs[1:2], vecs[2:3])
    unit[...] = made_unit
    inverse[...] = jnp.broadcast_to(made_inverse, inverse.shape)
    two[:, :width] = low(normed)
    finish(copies_inner)

    def block(j, carry):
        cols = at(j * BLOCK, BLOCK, BLOCK)
        before = dot(two[:, :width], held_inner[:, cols]) + inner_vec[0:1, cols]
        below = 0.5 * (1.0 + lax.erf(before * 0.7071067811865476))
        active[:, cols] = low(before * below)
        slope[:, cols] = below + before * jnp.exp(before * before * -0.5) * 0.3989422804014327
        return carry

    lax.fori_loop(0, ff // BLOCK, block, 0)
    finish(copies_outer)
    hidden = normed + dot(active[...], held_outer[...]) + vecs[3:4]
    made, unit_two, inverse_two = norm_forward(hidden, vecs[4:5], vecs[5:6])
    output[...] = made.reshape(output.shape)
    valid = jnp.where(seg[...] != 0, 1.0, 0.0)
    error = (made - teacher[...].reshape(own, width)) * valid
    grad = error * (tokens_all / vecs[8:9, 0:1])
    made = norm_backward(grad, unit_two, inverse_two, vecs[4:5])
    g_hidden[...] = made
    g_low = low(made)
    two[:, width:] = g_low
    sums[...] = jnp.zeros_like(sums)
    sums[3:4] = total(full(g_low))
    sums[4:5] = total(grad * unit_two)
    sums[5:6] = total(grad)
    loss = jnp.broadcast_to(jnp.sum(total(error * error), 1, keepdims=True), (1, width))
    sums[10:11] = full(low(loss))
    sums[11:12] = loss - full(low(loss))


def backward(*refs):
    two, slope, g_hidden, unit, inverse, vecs, attended, sums = refs[:8]
    weights, (away_x, away_y, g_one, g_mixed) = refs[8:21], refs[21:25]
    held_out, held_inner, held_outer, g_inner, inner_sums, small, sem = refs[25:]
    at_b, _, _, _ = spot()
    copies_outer = fetch_outer(weights[8], weights[9:13], held_outer, sem.at[2])
    copies_inner = fetch_inner(weights[3], weights[4:8], held_inner, sem.at[1])
    copies_out = fetch_out(weights[0], weights[1:3], held_out, sem.at[0])
    (own, width), ff = unit.shape, slope.shape[1]
    half = width // 2
    away_y[:own, width:] = jnp.where(at_b == 0, attended[:, :half], attended[:, half:])
    away_x[:own, width:] = jnp.where(at_b == 0, attended[:, half:], attended[:, :half])
    finish(copies_outer)

    def block(j, carry):
        cols = at(j * BLOCK, BLOCK, BLOCK)
        grad = low(dot(two[:, width:], held_outer[cols, :], 1, 1) * slope[:, cols])
        g_inner[:, cols] = grad
        inner_sums[0:1, cols] = total(full(grad))
        return carry

    lax.fori_loop(0, ff // BLOCK, block, 0)
    finish(copies_inner)
    g_normed = g_hidden[...] + dot(g_inner[...], held_inner[...], 1, 1)
    made = norm_backward(g_normed, unit[...], inverse[:, 0:1], vecs[1:2])
    g_one[...] = made
    g_low = low(made)
    finish(copies_out)
    g_attended = low(dot(g_low, held_out[...], 1, 1))
    rows, share = g_mixed.shape[1:]
    seqs = own // rows
    for s in range(seqs):
        for z in range(g_mixed.shape[0] // seqs):
            g_mixed[z * seqs + s] = g_attended[s * rows : (s + 1) * rows, z * share : (z + 1) * share]
    small[...] = sums[...]
    small[0:1] = total(full(g_low))
    small[1:2] = total(g_normed * unit[...])
    small[2:3] = total(g_normed)
    for k in range(4):
        small[6 + k : 7 + k] = inner_sums[0:1, k * width : (k + 1) * width]
    for out in (away_x, away_y):
        out[:own, :width] = g_low
        out[own:, :width] = low(small[...])
        out[own:, width:] = jnp.zeros((LINES, half), BF)


def resplit(made):
    lines = made.shape[0]
    loss = made[10:11] + made[11:12]
    return low(jnp.concatenate([made[:10], full(low(loss)), loss - full(low(loss)), made[12:lines]]))


def halve_out(axis, keep, came, next_keep, next_send):
    mine = spot()[axis]
    part = next_keep.shape[0] - LINES
    for k in range(2):
        rows = slice(k * part, (k + 1) * part)
        piece = low(full(keep[rows]) + full(came[rows]))

        @pl.when(mine == k)
        def _():
            next_keep[:part] = piece

        @pl.when(mine != k)
        def _():
            next_send[:part] = piece

    small = resplit(full(keep[2 * part :]) + full(came[2 * part :]))
    next_keep[part:] = small
    next_send[part:] = small


def eight(parts):
    made = full(parts[0])
    for k in range(1, parts.shape[0]):
        made = made + full(parts[k])
    return made


def weight_feed(*refs):
    pieces, (inner_vec, w_inner, i_x, i_y, w_outer, o_x, out) = refs[:8], refs[8:15]
    held_inner, held_outer, states, grads, active, g_inner, sem = refs[15:]
    at_b, at_c, at_y, _ = spot()
    half, width = w_inner.shape[0], states.shape[1]
    other, part = (1 - at_b) * half, half // 2
    copies = []
    for k in range(2):
        cols = slice(k * half, (k + 1) * half)
        there = at((2 * k + at_c) * width + at_y * half, half, 128)
        copies.append((w_inner.at[:, there], held_inner.at[at(at_b * half, half, 128), cols]))
        for y, piece in enumerate((i_x, i_y)):
            rows = at(other + (at_y + y) % 2 * part, part, 64)
            from_rows = slice(k * part, (k + 1) * part)
            copies.append((piece.at[from_rows, at(at_y * half, half, 128)], held_inner.at[rows, cols]))
    rows = at((2 * at_c + at_y) * half, half, 128)
    copies.append((w_outer.at[rows], held_outer.at[at(at_b * half, half, 128)]))
    copies.append((o_x, held_outer.at[at(other, half, 128)]))
    copies = start(copies, sem)
    own = pieces[0].shape[0]
    for k, piece in enumerate(pieces):
        states[k * own : (k + 1) * own] = piece[:, :width]
        grads[k * own : (k + 1) * own] = piece[:, width:]
    bias = jnp.concatenate(
        [inner_vec[0:1, at((2 * k + at_c) * width + at_y * half, half, 128)] for k in range(2)], 1
    )
    finish(copies)

    def block(j, carry):
        rows = at(j * BLOCK, BLOCK, BLOCK)
        before = dot(states[rows], held_inner[...]) + bias
        below = 0.5 * (1.0 + lax.erf(before * 0.7071067811865476))
        active[rows] = low(before * below)
        slope = below + before * jnp.exp(before * before * -0.5) * 0.3989422804014327
        g_inner[rows] = low(dot(grads[rows], held_outer[...], 1, 1) * slope)
        return carry

    lax.fori_loop(0, 8 * own // BLOCK, block, 0)
    mine = at(at_b * half, half, 128)
    depth, rows = out.shape[0], out.shape[1] // 2
    made = low(dot(active[:, mine], grads[...], 0, 0))
    for z in range(depth):
        out[z, :rows] = made[z * rows : (z + 1) * rows]
    made = low(dot(states[:, mine], g_inner[...], 0, 0))
    for z in range(depth):
        out[z, rows:] = made[z * rows : (z + 1) * rows]


def weight_out(*refs):
    pieces, (blocks, made) = (refs[:8], (refs[8:12], refs[14]))
    left, right = refs[12:14]
    _, at_c, at_y, at_z = spot()
    width, part = right.shape[1], left.shape[1]
    rows = right.shape[0] // 8
    for k, piece in enumerate(pieces):
        there = slice(k * rows, (k + 1) * rows)
        right[there] = piece[:rows, :width]
        mixed = piece[:rows, width:]
        mixed = jnp.where(at_c == 0, mixed[:, : 2 * part], mixed[:, 2 * part :])
        left[there] = jnp.where(at_y == 0, mixed[:, :part], mixed[:, part:])
    made[...] = dot(left[...], right[...], 0, 0)
    small = resplit(sum(full(piece[rows:, :width]) for piece in pieces))
    part = part // len(blocks)
    for k, block in enumerate(blocks):
        block[:part] = low(made[at((at_z + k) % len(blocks) * part, part, 8)])
        block[part:] = small


def weight_three(g_query, g_mine, came, states, w_three, back, keep, send, g_three):
    _, at_c, _, _ = spot()
    share = g_query.shape[1]
    g_three[:, :share] = g_query[...]
    g_three[:, share:] = low(g_mine[...] + came[...])
    made = low(dot(states[...], g_three[...], 0, 0))
    part = (keep.shape[0] - LINES) // 2
    for k in range(2):
        for c in range(2):
            piece = made[(2 * k + c) * part : (2 * k + c + 1) * part]

            @pl.when(at_c == c)
            def _():
                keep[k * part : (k + 1) * part] = piece

            @pl.when(at_c != c)
            def _():
                send[k * part : (k + 1) * part] = piece

    bias = jnp.broadcast_to(low(total(full(g_three[...]))), (LINES, 3 * share))
    keep[2 * part :] = bias
    send[2 * part :] = bias
    back[...] = low(dot(g_three[...], w_three[...], 1, 1))


def grad_states(parts, g_one, out):
    seqs, rows = out.shape[:2]
    for s in range(seqs):
        made = g_one[s * rows : (s + 1) * rows]
        for z in range(parts.shape[0] // seqs):
            made = made + full(parts[z * seqs + s])
        out[s] = made


def pack(summed, out_0, out_1, out_2, out_3, keep, came, vecs, out, loss, g_b_inner, *vectors):
    at_b, _, _, _ = spot()
    made = eight(summed)
    width, wide = made.shape[1], keep.shape[1]
    rows, share = (out.shape[0] - 8) // 3, width - wide
    part = out_0.shape[0] - LINES
    out[...] = jnp.zeros_like(out)
    out[: 2 * rows] = low(made)
    made = full(out_0[...]) + full(out_1[...]) + full(out_2[...]) + full(out_3[...])
    three = low(full(keep[...]) + full(came[...]))
    out[2 * rows : 3 * rows, :wide] = three[:rows]
    for k in range(width // share):
        piece = made[:part, k * share : (k + 1) * share]
        out[2 * rows + k * part : 2 * rows + (k + 1) * part, wide:] = low(piece)
    out[3 * rows :, :wide] = three[rows : rows + 8]
    small = made[part:]
    half = width // 2
    loss[...] = (small[10:11, :128] + small[11:12, :128]) / (2.0 * vecs[8:9, :128])
    for k, vector in enumerate(vectors):
        row = small[k : k + 1]
        vector[...] = jnp.where(at_b == 0, row[:, :half], row[:, half:]).reshape(half)
    first = jnp.where(at_b == 0, small[6:7], small[8:9])
    second = jnp.where(at_b == 0, small[7:8], small[9:10])
    g_b_inner[...] = jnp.concatenate([first, second], 1).reshape(2 * width)


def each_piece(pieces, steps):
    _, at_c, at_y, at_z = spot()
    depth = 4
    for j, k in enumerate(steps):
        for c in range(2):
            for y in range(2):
                place = (at_c + c) % 2, (at_y + y) % 2, (at_z + depth - k) % depth
                yield pieces[(j * 2 + c) * 2 + y], place


def final(steps, pieces, g_outer, g_inner, g_out, threes, biases, held, held_out, sem):
    depth = 4
    half, width = threes[0].shape
    rows, share = width // 8, width // depth
    part = rows // depth
    copies = []
    for n, (piece, (c, y, z)) in enumerate(each_piece(pieces, steps)):
        place = (c * 2 + y) * depth + z
        own = slice(n * 2 * rows, (n + 1) * 2 * rows)
        held[own] = full(piece[: 2 * rows])
        first = n * 2 * rows
        copies.append((held.at[first : first + rows], g_outer.at[at(place * rows, rows, 32)]))
        for k in range(2):
            cols = at((2 * k + c) * width + y * half, half, 128)
            copies.append(
                (
                    held.at[first + rows : first + 2 * rows, k * half : (k + 1) * half],
                    g_inner.at[at(z * rows, rows, 32), cols],
                )
            )
        for k in range(depth):
            first = 2 * rows + k * part
            held_out[n * part : (n + 1) * part, k * share : (k + 1) * share] = full(
                piece[first : first + part, 3 * share :]
            )
        copies.append((held_out.at[n * part : (n + 1) * part], g_out.at[at(place * part, part, 8)]))
    copies = start(copies, sem)
    for piece, (c, y, z) in each_piece(pieces, steps):
        there = at((c * 2 + y) * rows, rows, 32)
        for k in range(depth):

            @pl.when(z == k)
            def _():
                cols = slice(k * share, (k + 1) * share)
                for j, out in enumerate(threes):
                    out[there, cols] = full(piece[2 * rows : 3 * rows, j * share : (j + 1) * share])
                for j in (0, 2):
                    bias = full(piece[3 * rows :, j * share : (j + 1) * share])
                    biases[j : j + 1, cols] = bias[0:1]

    finish(copies)


def final_first(*refs):
    biases = refs[18]
    biases[...] = jnp.zeros_like(biases)
    final((0, 1, 3), refs[:12], *refs[12:15], refs[15:18], biases, *refs[19:])


def final_last(*refs):
    at_b, _, _, _ = spot()
    for k in range(3):
        refs[11 + 3 + k][...] = refs[7 + k][...]
    biases = refs[19]
    biases[...] = refs[10][...]
    final((2,), refs[:4], *refs[11:14], refs[14:17], biases, *refs[20:])
    for j, out in ((0, refs[17]), (2, refs[18])):
        half = out.shape[0]
        row = biases[j : j + 1]
        out[...] = jnp.where(at_b == 0, row[:, :half], row[:, half:]).reshape(half)


def per_device_heads(
    inputs,
    teacher,
    segments,
    w_query,
    b_query,
    w_key,
    w_value,
    b_value,
    w_out,
    b_out,
    gain_one,
    shift_one,
    w_inner,
    b_inner,
    w_outer,
    b_outer,
    gain_two,
    shift_two,
):
    count = lax.axis_size("ctx")
    depth = count // 4
    place = lax.axis_index("ctx")
    at_c, at_y = place % 2, place // 2 % 2
    seqs, rows, width = inputs.shape
    own = seqs * rows
    half = width // 2
    ff = w_inner.shape[1]
    share = width // depth
    keys = count // 2 * rows
    joint = ("batch", "ctx")
    pairs = [(y, c) for y in range(2) for c in range(2)]
    groups_z = [[z * 4 + r for z in range(depth)] for r in range(4)]
    groups_yz = [[z * 4 + y * 2 + c for z in range(depth) for y in range(2)] for c in range(2)]
    groups_xyc = [[b * count + z * 4 + y * 2 + c for b in range(2) for y, c in pairs] for z in range(depth)]

    def swap_x(values):
        return lax.ppermute(values, "batch", [(0, 1), (1, 0)])

    def swap_y(values):
        return lax.ppermute(values, "ctx", [(i, i ^ 2) for i in range(count)])

    def swap_xy(values):
        return lax.ppermute(values, joint, [(i, (i + count) % (2 * count) ^ 2) for i in range(2 * count)])

    def swap_c(values):
        return lax.ppermute(values, "ctx", [(i, i ^ 1) for i in range(count)])

    def shift_z(values, step):
        return lax.ppermute(values, "ctx", [(i, (i + 4 * step) % count) for i in range(count)])

    def trade(values, groups, axes="ctx"):
        return lax.all_to_all(values, axes, 0, 0, axis_index_groups=groups, tiled=True)

    tie = lax.optimization_barrier
    dma = pltpu.SemaphoreType.DMA

    blocks, first, p_inner, p_outer, p_out = kernel(
        prepare,
        [
            ((depth * seqs, rows, width), BF),
            ((3 * half // 4 + LINES, width), BF),
            ((half, width), BF),
            ((ff // 8, width), BF),
            ((half // 2, width), BF),
        ],
        [inputs, w_query, w_key, w_value, b_query, b_value, b_out, gain_one, shift_one]
        + [b_outer, gain_two, shift_two, b_inner, segments, w_inner, w_outer, w_out],
        hbm=(14, 15, 16),
        pin=range(14),
        scratch=[dma((4,))],
    )
    states = trade(blocks, groups_yz).reshape(keys, width)
    other = swap_x(first)
    x_inner = swap_x(p_inner)
    seg_seq = lax.dynamic_index_in_dim(segments, at_y, 0, keepdims=False).reshape(-1, 2, rows)
    seg_own = lax.dynamic_index_in_dim(seg_seq, at_c, 1, keepdims=False).reshape(-1)
    seg_peer = lax.dynamic_index_in_dim(seg_seq, 1 - at_c, 1, keepdims=False).reshape(-1)
    seg_key = jnp.concatenate([seg_own, seg_peer])[:, None]
    seg_query = seg_own[None, :]
    seg_tokens = lax.dynamic_slice_in_dim(segments, place * rows, rows, 1).reshape(own, 1)
    states, other, p_outer, p_out, seg_key, seg_query, seg_tokens = tie(
        (states, other, p_outer, p_out, seg_key, seg_query, seg_tokens)
    )
    x_outer = swap_x(p_outer)

    query, pair, vecs, inner_vec, w_three = kernel(
        project,
        [
            ((keys, share), BF),
            ((keys, 2 * share), BF),
            ((LINES, width), F32),
            ((8, ff), F32),
            ((width, 3 * share), BF),
        ],
        [states, first, other],
        scratch=[pltpu.VMEM((width, 3 * share), BF)],
    )
    peer = swap_c(pair)
    query, peer, x_inner = tie((query, peer, x_inner))
    y_inner = swap_y(x_inner)
    mixed, logs = kernel(
        attend,
        [((keys, share), BF), ((8, keys), F32)],
        [query, pair, peer, seg_query, seg_key],
        scratch=[pltpu.VMEM((2 * keys, share), BF), pltpu.VMEM((share, 2 * keys), BF)],
    )
    x_outer, mixed, p_out = tie((x_outer, mixed, p_out))
    mixed = trade(mixed.reshape(depth * seqs, rows, share), groups_yz)
    y_outer = swap_y(x_outer)
    x_out = swap_x(p_out)
    c_inner, c_outer = map(swap_c, (x_inner, x_outer))
    mixed, y_outer, x_out, y_inner, c_inner, c_outer = tie(
        (mixed, y_outer, x_out, y_inner, c_inner, c_outer)
    )
    weights = [w_out, x_out, swap_c(x_out)]
    weights += [w_inner, x_inner, y_inner, c_inner, swap_c(y_inner)]
    weights += [w_outer, x_outer, y_outer, c_outer, swap_c(y_outer)]
    held = [pltpu.VMEM((width, width), BF), pltpu.VMEM((width, ff), BF), pltpu.VMEM((ff, width), BF)]
    output, attended, unit, inverse, slope, two, g_hidden, sums = kernel(
        functools.partial(forward, float(own * 2 * count)),
        [
            (inputs.shape, F32),
            ((own, width), BF),
            ((own, width), F32),
            ((own, 128), F32),
            ((own, ff), F32),
            ((own, 2 * width), BF),
            ((own, width), F32),
            ((LINES, width), F32),
        ],
        [mixed, inputs, teacher, seg_tokens, vecs, inner_vec, *weights],
        hbm=range(6, 19),
        pin=(1, 2),
        scratch=[*held, pltpu.VMEM((own, ff), BF), dma((3, 9))],
    )
    fours = [two, swap_x(two), swap_y(two), swap_xy(two)]
    away_x, away_y, g_one, g_mixed = kernel(
        backward,
        [
            ((own + LINES, width + half), BF),
            ((own + LINES, width + half), BF),
            ((own, width), F32),
            ((depth * seqs, rows, share), BF),
        ],
        [two, slope, g_hidden, unit, inverse, vecs, attended, sums, *weights],
        hbm=range(8, 21),
        scratch=[
            *held,
            pltpu.VMEM((own, ff), BF),
            pltpu.VMEM((8, ff), F32),
            pltpu.VMEM((LINES, width), F32),
            dma((3, 9)),
        ],
    )
    away_x, away_y, *fours = tie((away_x, away_y, *fours))
    g_mixed = trade(g_mixed, groups_yz).reshape(keys, share)
    eights = [*fours, *map(swap_c, fours)]
    outer_rows = half // depth
    (feed,) = kernel(
        weight_feed,
        [((depth, 2 * outer_rows, width), BF)],
        [*eights, inner_vec, w_inner, x_inner, y_inner, w_outer, x_outer],
        hbm=range(9, 14),
        scratch=[
            pltpu.VMEM((width, width), BF),
            pltpu.VMEM((width, width), BF),
            pltpu.VMEM((8 * own, width), BF),
            pltpu.VMEM((8 * own, width), BF),
            pltpu.VMEM((8 * own, width), BF),
            pltpu.VMEM((8 * own, width), BF),
            dma((8,)),
        ],
    )
    feed, g_mixed, away_x, away_y = tie((feed, g_mixed, away_x, away_y))
    feed = trade(feed, groups_z)
    fours = [away_y, swap_x(away_x), swap_y(away_y), swap_xy(away_x)]

    g_query, g_mine, g_theirs = kernel(
        attend_back,
        [((keys, share), BF), ((keys, 2 * share), F32), ((keys, 2 * share), F32)],
        [query, pair, peer, seg_query, seg_key, logs, g_mixed],
        pin=range(6),
        scratch=[
            pltpu.VMEM((2 * keys, share), BF),
            pltpu.VMEM((share, 2 * keys), BF),
            pltpu.VMEM((2 * keys, share), BF),
            pltpu.VMEM((2 * keys, 2 * share), F32),
        ],
    )
    g_theirs, *fours = tie((g_theirs, *fours))
    part = half // 4 // depth
    outs = kernel(
        weight_out,
        [((part + LINES, width), BF)] * depth,
        [*fours, *map(swap_c, fours)],
        scratch=[
            pltpu.VMEM((8 * own, half // 4), BF),
            pltpu.VMEM((8 * own, width), BF),
            pltpu.VMEM((half // 4, width), F32),
        ],
    )
    back, three_keep, three_send = kernel(
        weight_three,
        [((keys, width), BF)] + [((half + LINES, 3 * share), BF)] * 2,
        [g_query, g_mine, swap_c(g_theirs), states, w_three],
        pin=(3, 4),
        scratch=[pltpu.VMEM((keys, 3 * share), BF)],
    )
    three_keep, three_send = kernel(
        functools.partial(halve_out, 0),
        [((half // 2 + LINES, 3 * share), BF)] * 2,
        [three_keep, swap_c(three_send)],
    )
    three_x, *outs = tie((swap_x(three_send), *outs))
    outs = [outs[0]] + [shift_z(outs[k], k) for k in range(1, depth)]
    three_keep, three_send = kernel(
        functools.partial(halve_out, 2),
        [((half // 4 + LINES, 3 * share), BF)] * 2,
        [three_keep, three_x],
    )
    three_came = swap_y(three_send)
    packed, loss, g_b_inner, *vectors = kernel(
        pack,
        [((3 * outer_rows + 8, width), BF), ((1, 128), F32), ((ff // 2,), F32)] + [((half,), F32)] * 6,
        [feed, *outs, three_keep, three_came, vecs],
    )
    packed, back = tie((packed, back))
    up, down, by_y = tie((shift_z(packed, 1), shift_z(packed, -1), swap_y(packed)))
    back = trade(back.reshape(depth * seqs, rows, width), groups_yz)
    across, up_y, down_y = tie((shift_z(up, 1), swap_y(up), swap_y(down)))
    pieces = []
    for pair in ((packed, by_y), (up, up_y), (down, down_y)):
        pieces += [*pair, *map(swap_c, pair)]
    large = [((ff // 2, width), F32), ((half, ff), F32), ((half, width), F32)]
    threes = [((half, width), F32)] * 3
    room = 2 * outer_rows

    def buffers(count):
        return [
            pltpu.VMEM((count * room, width), F32),
            pltpu.VMEM((count * part, width), F32),
            dma((4 * count,)),
        ]

    outs = kernel(
        final_first,
        [*large, *threes, ((8, width), F32)],
        pieces,
        outs_hbm=range(3),
        scratch=buffers(12),
    )
    across_y, *outs = tie((swap_y(across), *outs))
    pieces = [across, across_y, swap_c(across), swap_c(across_y)]
    (g_inputs,) = kernel(grad_states, [(inputs.shape, F32)], [back, g_one])
    g_w_outer, g_w_inner, g_w_out, g_w_query, g_w_key, g_w_value, g_b_query, g_b_value = kernel(
        final_last,
        [*large, *threes] + [((half,), F32)] * 2,
        [*pieces, *outs],
        hbm=range(4, 7),
        outs_hbm=range(3),
        aliases={4: 0, 5: 1, 6: 2},
        scratch=[pltpu.VMEM((8, width), F32), *buffers(4)],
    )
    g_b_out, g_gain_one, g_shift_one, g_b_outer, g_gain_two, g_shift_two = vectors
    return (
        output,
        loss[0, 0],
        g_inputs,
        g_w_query,
        g_b_query,
        g_w_key,
        g_w_value,
        g_b_value,
        g_w_out,
        g_b_out,
        g_gain_one,
        g_shift_one,
        g_w_inner,
        g_b_inner,
        g_w_outer,
        g_b_outer,
        g_gain_two,
        g_shift_two,
    )


def per_device(inputs, *others):
    sizes = (lax.axis_size("batch"), lax.axis_size("ctx"), inputs.shape[0])
    if sizes == (2, 16, 2):
        return per_device_heads(inputs, *others)
    return per_device_any(inputs, *others)


def solution(mesh):
    placed = (
        P("batch", "ctx", None),
        P("batch", "ctx", None),
        P("batch", None),
        P("batch", None),
        P("batch"),
        P("batch", None),
        P("batch", None),
        P("batch"),
        P("batch", None),
        P("batch"),
        P("batch"),
        P("batch"),
        P("batch", None),
        P("batch"),
        P("batch", None),
        P("batch"),
        P("batch"),
        P("batch"),
    )
    return jax.shard_map(
        per_device,
        mesh=mesh,
        in_specs=placed,
        out_specs=(
            P("batch", "ctx", None),
            P(),
            P("batch", "ctx", None),
            P("batch", None),
            P("batch"),
            P("batch", None),
            P("batch", None),
            P("batch"),
            P("batch", None),
            P("batch"),
            P("batch"),
            P("batch"),
            P("batch", None),
            P("batch"),
            P("batch", None),
            P("batch"),
            P("batch"),
            P("batch"),
        ),
        check_vma=False,
    )
```

```python
import functools
import math

import jax
import jax.numpy as jnp
from jax import lax
from jax.experimental import pallas as pl
from jax.experimental.pallas import tpu as pltpu
from jax.sharding import PartitionSpec as P

H = 12
HD = 64


NEGATIVE = -1e30
EPSILON = 1e-12


def norm_rows(hidden, gain, shift):
    center = hidden - jnp.mean(hidden, -1, keepdims=True)
    spread = jnp.mean(center * center, -1, keepdims=True)
    return center * lax.rsqrt(spread + EPSILON) * gain + shift


def gelu_exact(values):
    return jax.nn.gelu(values, approximate=False)


def linear(rows_in, weight):
    return jnp.dot(rows_in, weight, preferred_element_type=jnp.float32)


def contract_rows(left, right):
    return lax.dot_general(
        left, right, (((0,), (0,)), ((), ())), preferred_element_type=jnp.float32
    )


def times_transpose(rows_in, weight):
    return lax.dot_general(
        rows_in, weight, (((1,), (1,)), ((), ())), preferred_element_type=jnp.float32
    )


def score_rows(query_one, keys_all, seg_mine, seg_all):
    heads_query = query_one.reshape(query_one.shape[0], H, HD)
    heads_key = keys_all.reshape(keys_all.shape[0], H, HD)
    raw = jnp.einsum(
        "chd,khd->hck", heads_query, heads_key, preferred_element_type=jnp.float32
    ) * HD ** (-0.5)
    allowed = seg_mine[None, :, None] == seg_all[None, None, :]
    return jnp.where(allowed, raw, NEGATIVE)


def per_device_any(
    inputs,
    teacher,
    segments,
    w_query,
    b_query,
    w_key,
    w_value,
    b_value,
    w_out,
    b_out,
    gain_one,
    shift_one,
    w_inner,
    b_inner,
    w_outer,
    b_outer,
    gain_two,
    shift_two,
):
    (
        w_query,
        b_query,
        w_key,
        w_value,
        b_value,
        w_out,
        b_out,
        gain_one,
        shift_one,
        w_inner,
        b_inner,
        w_outer,
        b_outer,
        gain_two,
        shift_two,
    ) = (
        lax.all_gather(w_query, "batch", axis=0, tiled=True),
        lax.all_gather(b_query, "batch", axis=0, tiled=True),
        lax.all_gather(w_key, "batch", axis=0, tiled=True),
        lax.all_gather(w_value, "batch", axis=0, tiled=True),
        lax.all_gather(b_value, "batch", axis=0, tiled=True),
        lax.all_gather(w_out, "batch", axis=0, tiled=True),
        lax.all_gather(b_out, "batch", axis=0, tiled=True),
        lax.all_gather(gain_one, "batch", axis=0, tiled=True),
        lax.all_gather(shift_one, "batch", axis=0, tiled=True),
        lax.all_gather(w_inner, "batch", axis=0, tiled=True),
        lax.all_gather(b_inner, "batch", axis=0, tiled=True),
        lax.all_gather(w_outer, "batch", axis=0, tiled=True),
        lax.all_gather(b_outer, "batch", axis=0, tiled=True),
        lax.all_gather(gain_two, "batch", axis=0, tiled=True),
        lax.all_gather(shift_two, "batch", axis=0, tiled=True),
    )
    scale = HD ** (-0.5)
    seqs_here, ctx_rows, width = inputs.shape
    rows_here = seqs_here * ctx_rows
    tokens_all = rows_here * lax.axis_size("batch") * lax.axis_size("ctx")
    seg_own = lax.dynamic_slice_in_dim(segments, lax.axis_index("ctx") * ctx_rows, ctx_rows, 1)
    inputs_flat = inputs.reshape(rows_here, width)
    inputs_low = inputs_flat.astype(jnp.bfloat16)
    query = (linear(inputs_low, w_query) + b_query.astype(jnp.float32)).astype(jnp.bfloat16)
    key = linear(inputs_low, w_key).astype(jnp.bfloat16)
    value = (linear(inputs_low, w_value) + b_value.astype(jnp.float32)).astype(jnp.bfloat16)
    query_seq = query.reshape(seqs_here, ctx_rows, width)
    key_seq = key.reshape(seqs_here, ctx_rows, width)
    value_seq = value.reshape(seqs_here, ctx_rows, width)

    def attend_forward(items):
        query_one, key_one, value_one, seg_all, seg_mine = items
        keys_all, values_all = (
            lax.all_gather(key_one, "ctx", axis=0, tiled=True),
            lax.all_gather(value_one, "ctx", axis=0, tiled=True),
        )
        scores = score_rows(query_one, keys_all, seg_mine, seg_all)
        highest = jnp.max(scores, -1, keepdims=True)
        expo = jnp.exp(scores - highest)
        totals = jnp.sum(expo, -1, keepdims=True)
        probs = (expo / totals).astype(jnp.bfloat16)
        mixed = jnp.einsum(
            "hck,khd->chd",
            probs,
            values_all.reshape(keys_all.shape[0], H, HD),
            preferred_element_type=jnp.float32,
        )
        return (
            mixed.reshape(ctx_rows, width).astype(jnp.bfloat16),
            (highest + jnp.log(totals))[:, :, 0],
        )

    attended, log_totals = lax.map(
        attend_forward, (query_seq, key_seq, value_seq, segments, seg_own)
    )
    attended_flat = attended.reshape(rows_here, width)
    gain_one_full = gain_one.astype(jnp.float32)
    shift_one_full = shift_one.astype(jnp.float32)
    gain_two_full = gain_two.astype(jnp.float32)
    shift_two_full = shift_two.astype(jnp.float32)
    hidden_one = inputs_flat + linear(attended_flat, w_out) + b_out.astype(jnp.float32)
    normed_one, back_one = jax.vjp(norm_rows, hidden_one, gain_one_full, shift_one_full)
    normed_low = normed_one.astype(jnp.bfloat16)
    inner_pre = linear(normed_low, w_inner) + b_inner.astype(jnp.float32)
    active_full, gelu_back = jax.vjp(gelu_exact, inner_pre)
    active_low = active_full.astype(jnp.bfloat16)
    hidden_two = normed_one + linear(active_low, w_outer) + b_outer.astype(jnp.float32)
    output, back_two = jax.vjp(norm_rows, hidden_two, gain_two_full, shift_two_full)
    valid = (seg_own.reshape(rows_here) != 0).astype(jnp.float32)[:, None]
    error = output - teacher.reshape(rows_here, width)
    loss_total, valid_count = lax.psum(
        (jnp.sum(valid * error * error), jnp.sum(valid)), ("batch", "ctx")
    )
    loss = loss_total / (2.0 * valid_count)
    grad_output = tokens_all / valid_count * valid * error
    grad_hidden_two, grad_gain_two, grad_shift_two = back_two(grad_output)
    grad_branch_two = grad_hidden_two.astype(jnp.bfloat16)
    grad_b_outer = jnp.sum(grad_branch_two.astype(jnp.float32), 0)
    grad_w_outer = contract_rows(active_low, grad_branch_two)
    grad_active = times_transpose(grad_branch_two, w_outer)
    grad_inner = gelu_back(grad_active)[0].astype(jnp.bfloat16)
    grad_b_inner = jnp.sum(grad_inner.astype(jnp.float32), 0)
    grad_w_inner = contract_rows(normed_low, grad_inner)
    grad_normed = grad_hidden_two + times_transpose(grad_inner, w_inner)
    grad_hidden_one, grad_gain_one, grad_shift_one = back_one(grad_normed)
    grad_branch_one = grad_hidden_one.astype(jnp.bfloat16)
    grad_b_out = jnp.sum(grad_branch_one.astype(jnp.float32), 0)
    grad_w_out = contract_rows(attended_flat, grad_branch_one)
    grad_attended = (
        times_transpose(grad_branch_one, w_out)
        .astype(jnp.bfloat16)
        .reshape(seqs_here, ctx_rows, width)
    )

    def attend_backward(items):
        query_one, key_one, value_one, seg_all, seg_mine, log_one, grad_one = items
        keys_all, values_all = (
            lax.all_gather(key_one, "ctx", axis=0, tiled=True),
            lax.all_gather(value_one, "ctx", axis=0, tiled=True),
        )
        key_count = keys_all.shape[0]
        scores = score_rows(query_one, keys_all, seg_mine, seg_all)
        probs = jnp.exp(scores - log_one[:, :, None])
        grad_heads = grad_one.reshape(ctx_rows, H, HD)
        grad_probs = jnp.einsum(
            "chd,khd->hck",
            grad_heads,
            values_all.reshape(key_count, H, HD),
            preferred_element_type=jnp.float32,
        )
        centre = jnp.sum(probs * grad_probs, -1)
        grad_scores = (probs * (grad_probs - centre[:, :, None])).astype(jnp.bfloat16)
        grad_query = (
            jnp.einsum(
                "hck,khd->chd",
                grad_scores,
                keys_all.reshape(key_count, H, HD),
                preferred_element_type=jnp.float32,
            )
            * scale
        )
        grad_query = grad_query.reshape(ctx_rows, width).astype(jnp.bfloat16)
        probs_low = probs.astype(jnp.bfloat16)
        query_heads = query_one.reshape(ctx_rows, H, HD)
        count = ctx_rows * lax.axis_size("ctx")
        grad_key = (
            jnp.einsum("hck,chd->khd", grad_scores, query_heads, preferred_element_type=jnp.float32)
            * scale
        )
        grad_value = jnp.einsum(
            "hck,chd->khd", probs_low, grad_heads, preferred_element_type=jnp.float32
        )
        both = lax.psum_scatter(
            jnp.concatenate([grad_key.reshape(count, width), grad_value.reshape(count, width)], 1),
            "ctx",
            scatter_dimension=0,
            tiled=True,
        )
        return (
            grad_query,
            both[:, :width].astype(jnp.bfloat16),
            both[:, width:].astype(jnp.bfloat16),
        )

    grad_query_seq, grad_key_seq, grad_value_seq = lax.map(
        attend_backward,
        (query_seq, key_seq, value_seq, segments, seg_own, log_totals, grad_attended),
    )
    grad_query_flat = grad_query_seq.reshape(rows_here, width)
    grad_key_flat = grad_key_seq.reshape(rows_here, width)
    grad_value_flat = grad_value_seq.reshape(rows_here, width)
    grad_w_query = contract_rows(inputs_low, grad_query_flat)
    grad_b_query = jnp.sum(grad_query_flat.astype(jnp.float32), 0)
    grad_w_key = contract_rows(inputs_low, grad_key_flat)
    grad_w_value = contract_rows(inputs_low, grad_value_flat)
    grad_b_value = jnp.sum(grad_value_flat.astype(jnp.float32), 0)
    grad_inputs = (
        grad_hidden_one
        + times_transpose(grad_query_flat, w_query)
        + times_transpose(grad_key_flat, w_key)
        + times_transpose(grad_value_flat, w_value)
    )
    (
        grad_w_query,
        grad_b_query,
        grad_w_key,
        grad_w_value,
        grad_b_value,
        grad_w_out,
        grad_b_out,
        grad_gain_one,
        grad_shift_one,
        grad_w_inner,
        grad_b_inner,
        grad_w_outer,
        grad_b_outer,
        grad_gain_two,
        grad_shift_two,
    ) = (
        lax.psum_scatter(
            grad_w_query.astype(jnp.bfloat16), "batch", scatter_dimension=0, tiled=True
        ).astype(jnp.float32),
        lax.psum_scatter(
            grad_b_query.astype(jnp.bfloat16), "batch", scatter_dimension=0, tiled=True
        ).astype(jnp.float32),
        lax.psum_scatter(
            grad_w_key.astype(jnp.bfloat16), "batch", scatter_dimension=0, tiled=True
        ).astype(jnp.float32),
        lax.psum_scatter(
            grad_w_value.astype(jnp.bfloat16), "batch", scatter_dimension=0, tiled=True
        ).astype(jnp.float32),
        lax.psum_scatter(
            grad_b_value.astype(jnp.bfloat16), "batch", scatter_dimension=0, tiled=True
        ).astype(jnp.float32),
        lax.psum_scatter(
            grad_w_out.astype(jnp.bfloat16), "batch", scatter_dimension=0, tiled=True
        ).astype(jnp.float32),
        lax.psum_scatter(
            grad_b_out.astype(jnp.bfloat16), "batch", scatter_dimension=0, tiled=True
        ).astype(jnp.float32),
        lax.psum_scatter(
            grad_gain_one.astype(jnp.bfloat16), "batch", scatter_dimension=0, tiled=True
        ).astype(jnp.float32),
        lax.psum_scatter(
            grad_shift_one.astype(jnp.bfloat16), "batch", scatter_dimension=0, tiled=True
        ).astype(jnp.float32),
        lax.psum_scatter(
            grad_w_inner.astype(jnp.bfloat16), "batch", scatter_dimension=0, tiled=True
        ).astype(jnp.float32),
        lax.psum_scatter(
            grad_b_inner.astype(jnp.bfloat16), "batch", scatter_dimension=0, tiled=True
        ).astype(jnp.float32),
        lax.psum_scatter(
            grad_w_outer.astype(jnp.bfloat16), "batch", scatter_dimension=0, tiled=True
        ).astype(jnp.float32),
        lax.psum_scatter(
            grad_b_outer.astype(jnp.bfloat16), "batch", scatter_dimension=0, tiled=True
        ).astype(jnp.float32),
        lax.psum_scatter(
            grad_gain_two.astype(jnp.bfloat16), "batch", scatter_dimension=0, tiled=True
        ).astype(jnp.float32),
        lax.psum_scatter(
            grad_shift_two.astype(jnp.bfloat16), "batch", scatter_dimension=0, tiled=True
        ).astype(jnp.float32),
    )
    (
        grad_w_query,
        grad_b_query,
        grad_w_key,
        grad_w_value,
        grad_b_value,
        grad_w_out,
        grad_b_out,
        grad_gain_one,
        grad_shift_one,
        grad_w_inner,
        grad_b_inner,
        grad_w_outer,
        grad_b_outer,
        grad_gain_two,
        grad_shift_two,
    ) = lax.psum(
        (
            grad_w_query,
            grad_b_query,
            grad_w_key,
            grad_w_value,
            grad_b_value,
            grad_w_out,
            grad_b_out,
            grad_gain_one,
            grad_shift_one,
            grad_w_inner,
            grad_b_inner,
            grad_w_outer,
            grad_b_outer,
            grad_gain_two,
            grad_shift_two,
        ),
        "ctx",
    )
    return (
        output.reshape(inputs.shape),
        loss,
        grad_inputs.reshape(inputs.shape),
        grad_w_query,
        grad_b_query,
        grad_w_key,
        grad_w_value,
        grad_b_value,
        grad_w_out,
        grad_b_out,
        grad_gain_one,
        grad_shift_one,
        grad_w_inner,
        grad_b_inner,
        grad_w_outer,
        grad_b_outer,
        grad_gain_two,
        grad_shift_two,
    )


BF, F32 = jnp.bfloat16, jnp.float32
LINES = 16
ROOM = 6 << 20


def low(values):
    return values.astype(BF)


def full(values):
    return values.astype(F32)


def dot(left, right, a=1, b=0):
    return lax.dot_general(left, right, (((a,), (b,)), ((), ())), preferred_element_type=F32)


def spot():
    place = lax.axis_index("ctx")
    return lax.axis_index("batch"), place % 2, place // 2 % 2, place // 4


def at(start, size, step):
    return pl.ds(pl.multiple_of(start, step), size)


def kernel(body, outs, args, hbm=(), scratch=(), pin=(), outs_hbm=(), aliases=None):
    name = getattr(body, "func", body).__name__
    where = [pl.BlockSpec(memory_space=pl.ANY if k in hbm else pltpu.VMEM) for k in range(len(args))]
    shapes = [jax.ShapeDtypeStruct(shape, kind) for shape, kind in outs]
    held = [a for k, a in enumerate(args) if k not in hbm]
    held += [a for k, a in enumerate(shapes) if k not in outs_hbm]
    held += [a for a in scratch if a.memory_space == pltpu.VMEM]
    room = sum(math.prod(a.shape) * jnp.dtype(a.dtype).itemsize for a in held) + ROOM
    args = [
        pltpu.with_memory_space_constraint(a, pltpu.HBM) if k in hbm or k in pin else a
        for k, a in enumerate(args)
    ]
    return pl.pallas_call(
        body,
        out_shape=shapes,
        in_specs=where,
        out_specs=[
            pl.BlockSpec(memory_space=pl.ANY if k in outs_hbm else pltpu.VMEM)
            for k in range(len(shapes))
        ],
        input_output_aliases=aliases or {},
        scratch_shapes=list(scratch),
        compiler_params=pltpu.CompilerParams(vmem_limit_bytes=room),
        name=name,
    )(*args)


def norm_forward(hidden, gain, shift):
    center = hidden - jnp.mean(hidden, -1, keepdims=True)
    inverse = lax.rsqrt(jnp.mean(center * center, -1, keepdims=True) + EPSILON)
    unit = center * inverse
    return unit * gain + shift, unit, inverse


def norm_backward(grad, unit, inverse, gain):
    scaled = grad * gain
    along = jnp.mean(scaled * unit, -1, keepdims=True)
    return inverse * (scaled - jnp.mean(scaled, -1, keepdims=True) - unit * along)


def total(values):
    return jnp.sum(values, 0, keepdims=True)


def prepare(*refs):
    inputs, w_three, vectors, b_inner, segments = refs[0], refs[1:4], refs[4:12], refs[12], refs[13]
    w_inner, w_outer, w_out, blocks, out, p_inner, p_outer, p_out, sem = refs[14:]
    half, width = w_three[0].shape
    _, at_c, at_y, at_z = spot()
    part, wide = half // 2, w_inner.shape[1] // 4
    rows_out, rows_outer = p_out.shape[0], p_outer.shape[0]
    copies = [
        (
            w_inner.at[at(at_y * part, part, 64), at((k * 2 + at_c) * wide, wide, 128)],
            p_inner.at[k * part : (k + 1) * part],
        )
        for k in range(2)
    ]
    copies.append((w_outer.at[at((at_c * 2 + at_y) * rows_outer, rows_outer, 128)], p_outer))
    copies.append((w_out.at[at(at_c * rows_out, rows_out, 64)], p_out))
    copies = start(copies, sem)
    seqs = inputs.shape[0]
    for s in range(seqs):
        piece = low(inputs[s])
        for z in range(blocks.shape[0] // seqs):
            blocks[z * seqs + s] = piece
    share, rows = width // 4, half // 4
    for z in range(4):

        @pl.when(at_z == z)
        def _():
            for j in range(3):
                for k in range(4):
                    piece = w_three[j][k * rows : (k + 1) * rows, z * share : (z + 1) * share]
                    out[j * rows : (j + 1) * rows, k * share : (k + 1) * share] = piece

    first = 3 * rows
    out[first : first + LINES] = jnp.zeros((LINES, width), BF)
    for r in range(8):
        out[first + r : first + r + 1, :half] = vectors[r][...].reshape(1, half)
    inner = b_inner[...].reshape(1, -1)
    for r in range(4):
        out[first + 8 + r : first + 9 + r, :half] = inner[:, half * r : half * (r + 1)]
    valid = jnp.sum(jnp.where(segments[...] != 0, 1, 0))
    lane = lax.broadcasted_iota(jnp.int32, (1, half), 1)
    parts = jnp.where(lane < 128, valid // 256, valid % 256)
    out[first + 12 : first + 13, :half] = low(full(parts))
    finish(copies)


def start(copies, sem):
    made = [pltpu.make_async_copy(*copy, sem.at[k]) for k, copy in enumerate(copies)]
    for copy in made:
        copy.start()
    return made


def finish(copies):
    for copy in copies:
        copy.wait()


def both_halves(at_b, mine, other):
    return jnp.where(at_b == 0, mine, other), jnp.where(at_b == 0, other, mine)


def project(states, mine, other, query, pair, vecs, inner_vec, held, w_back):
    at_b, _, _, at_z = spot()
    width, share = states.shape[1], query.shape[1]
    half, rows = width // 2, width // 8
    for j in range(3):
        for k in range(4):
            first = slice(j * rows, (j + 1) * rows)
            cols = slice(k * share, (k + 1) * share)
            pieces = both_halves(at_b, mine[first, cols], other[first, cols])
            for h, piece in enumerate(pieces):
                start_row = h * half + k * rows
                held[start_row : start_row + rows, j * share : (j + 1) * share] = piece
    w_back[...] = held[...]
    made = dot(states[...], held[...])
    lines = slice(3 * rows, 3 * rows + LINES)
    top, bottom = both_halves(at_b, full(mine[lines]), full(other[lines]))

    def bias(r):
        row = jnp.where(at_z < 2, top[r : r + 1], bottom[r : r + 1])
        return jnp.where(at_z % 2 == 0, row[:, :share], row[:, share : 2 * share])

    query[...] = low(full(low(made[:, :share] + bias(0))) * HD ** (-0.5))
    pair[:, :share] = low(made[:, share : 2 * share])
    pair[:, share:] = low(made[:, 2 * share :] + bias(1))
    vecs[...] = jnp.zeros_like(vecs)
    for r in range(2, 8):
        vecs[r - 2 : r - 1, :half] = top[r : r + 1, :half]
        vecs[r - 2 : r - 1, half:] = bottom[r : r + 1, :half]
    counts = top[12:13] + bottom[12:13]
    counts = counts[:, :128] * 256.0 + counts[:, 256:384]
    vecs[8:9, :128] = counts
    inner_vec[...] = jnp.zeros_like(inner_vec)
    for b, rows in enumerate((top, bottom)):
        for r in range(4):
            cols = slice((4 * b + r) * half, (4 * b + r + 1) * half)
            inner_vec[0:1, cols] = rows[8 + r : 9 + r, :half]


STEP = 256


def attend(query, mine, peer, seg_query, seg_key, mixed, logs, keys, values):
    count, share = query.shape
    keys[:count] = mine[:, :share]
    keys[count:] = peer[:, :share]
    values[:, :count] = mine[:, share:].T
    values[:, count:] = peer[:, share:].T
    logs[...] = jnp.zeros_like(logs)

    def block(j, carry):
        rows = at(j * STEP, STEP, STEP)
        allowed = seg_key[...] == seg_query[:, rows]
        for h in range(share // HD):
            cols = slice(h * HD, (h + 1) * HD)
            scores = dot(keys[:, cols], query[rows, cols], 1, 1)
            scores = jnp.where(allowed, scores, NEGATIVE)
            highest = jnp.max(scores, 0, keepdims=True)
            expo = jnp.exp(scores - highest)
            totals = jnp.sum(expo, 0, keepdims=True)
            probs = low(expo * (1.0 / totals))
            mixed[rows, cols] = low(dot(values[cols], probs).T)
            logs[h : h + 1, rows] = highest + jnp.log(totals)
        return carry

    lax.fori_loop(0, count // STEP, block, 0)


def attend_back(
    query, mine, peer, seg_query, seg_key, logs, grad, g_query, g_mine, g_peer, keys, flipped, values, made
):
    count, share = query.shape
    keys[:count] = mine[:, :share]
    keys[count:] = peer[:, :share]
    values[:count] = mine[:, share:]
    values[count:] = peer[:, share:]
    flipped[:, :count] = mine[:, :share].T
    flipped[:, count:] = peer[:, :share].T
    made[...] = jnp.zeros_like(made)

    def block(j, carry):
        rows = at(j * STEP, STEP, STEP)
        allowed = seg_key[...] == seg_query[:, rows]
        for h in range(share // HD):
            cols = slice(h * HD, (h + 1) * HD)
            cols_value = slice(share + h * HD, share + (h + 1) * HD)
            scores = dot(keys[:, cols], query[rows, cols], 1, 1)
            scores = jnp.where(allowed, scores, NEGATIVE)
            probs = jnp.exp(scores - logs[h : h + 1, rows])
            g_probs = dot(values[:, cols], grad[rows, cols], 1, 1)
            centre = jnp.sum(probs * g_probs, 0, keepdims=True)
            g_scores = low(probs * (g_probs - centre))
            g_query[rows, cols] = low((dot(flipped[cols], g_scores) * HD ** (-0.5)).T)
            made[:, cols] += dot(g_scores, query[rows, cols])
            made[:, cols_value] += dot(low(probs), grad[rows, cols])
        return carry

    lax.fori_loop(0, count // STEP, block, 0)
    g_mine[...] = made[:count]
    g_peer[...] = made[count:]


def fetch_out(own, pieces, held, sem):
    at_b, at_c, _, _ = spot()
    half, part = own.shape[0], pieces[0].shape[0]
    copies = [(own, held.at[at(at_b * half, half, 128)])]
    for k, piece in enumerate(pieces):
        first = (1 - at_b) * half + (at_c + k) % 2 * part
        copies.append((piece, held.at[at(first, part, 64)]))
    return start(copies, sem)


def fetch_inner(own, pieces, held, sem):
    at_b, at_c, at_y, _ = spot()
    half, part, wide = own.shape[0], pieces[0].shape[0] // 2, pieces[0].shape[1]
    copies = [(own, held.at[at(at_b * half, half, 128)])]
    for c in range(2):
        for y in range(2):
            rows = at((1 - at_b) * half + (at_y + y) % 2 * part, part, 64)
            for k in range(2):
                cols = at((2 * k + (at_c + c) % 2) * wide, wide, 128)
                piece = pieces[2 * c + y].at[k * part : (k + 1) * part]
                copies.append((piece, held.at[rows, cols]))
    return start(copies, sem)


def fetch_outer(own, pieces, held, sem):
    at_b, at_c, at_y, _ = spot()
    half, part = own.shape[0], pieces[0].shape[0]
    copies = [(own, held.at[at(at_b * half, half, 128)])]
    for c in range(2):
        for y in range(2):
            first = (1 - at_b) * half + ((at_c + c) % 2 * 2 + (at_y + y) % 2) * part
            copies.append((pieces[2 * c + y], held.at[at(first, part, 128)]))
    return start(copies, sem)


BLOCK = 256


def forward(tokens_all, *refs):
    mixed, inputs, teacher, seg, vecs, inner_vec = refs[:6]
    weights, (output, attended, unit, inverse, slope, two, g_hidden, sums) = refs[6:19], refs[19:27]
    held_out, held_inner, held_outer, active, sem = refs[27:]
    copies_out = fetch_out(weights[0], weights[1:3], held_out, sem.at[0])
    copies_inner = fetch_inner(weights[3], weights[4:8], held_inner, sem.at[1])
    copies_outer = fetch_outer(weights[8], weights[9:13], held_outer, sem.at[2])
    rows, share = mixed.shape[1:]
    seqs = inputs.shape[0]
    own, width = attended.shape
    ff = slope.shape[1]
    for s in range(seqs):
        for z in range(mixed.shape[0] // seqs):
            attended[s * rows : (s + 1) * rows, z * share : (z + 1) * share] = mixed[z * seqs + s]
    finish(copies_out)
    hidden = inputs[...].reshape(own, width) + dot(attended[...], held_out[...]) + vecs[0:1]
    normed, made_unit, made_inverse = norm_forward(hidden, vecs[1:2], vecs[2:3])
    unit[...] = made_unit
    inverse[...] = jnp.broadcast_to(made_inverse, inverse.shape)
    two[:, :width] = low(normed)
    finish(copies_inner)

    def block(j, carry):
        cols = at(j * BLOCK, BLOCK, BLOCK)
        before = dot(two[:, :width], held_inner[:, cols]) + inner_vec[0:1, cols]
        below = 0.5 * (1.0 + lax.erf(before * 0.7071067811865476))
        active[:, cols] = low(before * below)
        slope[:, cols] = below + before * jnp.exp(before * before * -0.5) * 0.3989422804014327
        return carry

    lax.fori_loop(0, ff // BLOCK, block, 0)
    finish(copies_outer)
    hidden = normed + dot(active[...], held_outer[...]) + vecs[3:4]
    made, unit_two, inverse_two = norm_forward(hidden, vecs[4:5], vecs[5:6])
    output[...] = made.reshape(output.shape)
    valid = jnp.where(seg[...] != 0, 1.0, 0.0)
    error = (made - teacher[...].reshape(own, width)) * valid
    grad = error * (tokens_all / vecs[8:9, 0:1])
    made = norm_backward(grad, unit_two, inverse_two, vecs[4:5])
    g_hidden[...] = made
    g_low = low(made)
    two[:, width:] = g_low
    sums[...] = jnp.zeros_like(sums)
    sums[3:4] = total(full(g_low))
    sums[4:5] = total(grad * unit_two)
    sums[5:6] = total(grad)
    loss = jnp.broadcast_to(jnp.sum(total(error * error), 1, keepdims=True), (1, width))
    sums[10:11] = full(low(loss))
    sums[11:12] = loss - full(low(loss))


def backward(*refs):
    two, slope, g_hidden, unit, inverse, vecs, attended, sums = refs[:8]
    weights, (away_x, away_y, g_one, g_mixed) = refs[8:21], refs[21:25]
    held_out, held_inner, held_outer, g_inner, inner_sums, small, sem = refs[25:]
    at_b, _, _, _ = spot()
    copies_outer = fetch_outer(weights[8], weights[9:13], held_outer, sem.at[2])
    copies_inner = fetch_inner(weights[3], weights[4:8], held_inner, sem.at[1])
    copies_out = fetch_out(weights[0], weights[1:3], held_out, sem.at[0])
    (own, width), ff = unit.shape, slope.shape[1]
    half = width // 2
    away_y[:own, width:] = jnp.where(at_b == 0, attended[:, :half], attended[:, half:])
    away_x[:own, width:] = jnp.where(at_b == 0, attended[:, half:], attended[:, :half])
    finish(copies_outer)

    def block(j, carry):
        cols = at(j * BLOCK, BLOCK, BLOCK)
        grad = low(dot(two[:, width:], held_outer[cols, :], 1, 1) * slope[:, cols])
        g_inner[:, cols] = grad
        inner_sums[0:1, cols] = total(full(grad))
        return carry

    lax.fori_loop(0, ff // BLOCK, block, 0)
    finish(copies_inner)
    g_normed = g_hidden[...] + dot(g_inner[...], held_inner[...], 1, 1)
    made = norm_backward(g_normed, unit[...], inverse[:, 0:1], vecs[1:2])
    g_one[...] = made
    g_low = low(made)
    finish(copies_out)
    g_attended = low(dot(g_low, held_out[...], 1, 1))
    rows, share = g_mixed.shape[1], g_mixed.shape[2] // 2
    seqs = own // rows
    g_mixed[:, :, share:] = jnp.zeros((g_mixed.shape[0], rows, share), BF)
    for s in range(seqs):
        for z in range(g_mixed.shape[0] // seqs):
            g_mixed[z * seqs + s, :, :share] = g_attended[s * rows : (s + 1) * rows, z * share : (z + 1) * share]
    small[...] = sums[...]
    small[0:1] = total(full(g_low))
    small[1:2] = total(g_normed * unit[...])
    small[2:3] = total(g_normed)
    for k in range(4):
        small[6 + k : 7 + k] = inner_sums[0:1, k * width : (k + 1) * width]
    for out in (away_x, away_y):
        out[:own, :width] = g_low
        out[own:, :width] = low(small[...])
        out[own:, width:] = jnp.zeros((LINES, half), BF)


def resplit(made):
    lines = made.shape[0]
    loss = made[10:11] + made[11:12]
    return low(jnp.concatenate([made[:10], full(low(loss)), loss - full(low(loss)), made[12:lines]]))


def halve_out(axis, keep, came, next_keep, next_send):
    mine = spot()[axis]
    part = next_keep.shape[0] - LINES
    for k in range(2):
        rows = slice(k * part, (k + 1) * part)
        piece = low(full(keep[rows]) + full(came[rows]))

        @pl.when(mine == k)
        def _():
            next_keep[:part] = piece

        @pl.when(mine != k)
        def _():
            next_send[:part] = piece

    small = resplit(full(keep[2 * part :]) + full(came[2 * part :]))
    next_keep[part:] = small
    next_send[part:] = small


def eight(parts):
    made = full(parts[0])
    for k in range(1, parts.shape[0]):
        made = made + full(parts[k])
    return made


def weight_feed(*refs):
    pieces, (inner_vec, w_inner, i_x, i_y, w_outer, o_x, out) = refs[:8], refs[8:15]
    held_inner, held_outer, states, grads, active, g_inner, sem = refs[15:]
    at_b, at_c, at_y, _ = spot()
    half, width = w_inner.shape[0], states.shape[1]
    other, part = (1 - at_b) * half, half // 2
    copies = []
    for k in range(2):
        cols = slice(k * half, (k + 1) * half)
        there = at((2 * k + at_c) * width + at_y * half, half, 128)
        copies.append((w_inner.at[:, there], held_inner.at[at(at_b * half, half, 128), cols]))
        for y, piece in enumerate((i_x, i_y)):
            rows = at(other + (at_y + y) % 2 * part, part, 64)
            from_rows = slice(k * part, (k + 1) * part)
            copies.append((piece.at[from_rows, at(at_y * half, half, 128)], held_inner.at[rows, cols]))
    rows = at((2 * at_c + at_y) * half, half, 128)
    copies.append((w_outer.at[rows], held_outer.at[at(at_b * half, half, 128)]))
    copies.append((o_x, held_outer.at[at(other, half, 128)]))
    copies = start(copies, sem)
    own = pieces[0].shape[0]
    for k, piece in enumerate(pieces):
        states[k * own : (k + 1) * own] = piece[:, :width]
        grads[k * own : (k + 1) * own] = piece[:, width:]
    bias = jnp.concatenate(
        [inner_vec[0:1, at((2 * k + at_c) * width + at_y * half, half, 128)] for k in range(2)], 1
    )
    finish(copies)

    def block(j, carry):
        rows = at(j * BLOCK, BLOCK, BLOCK)
        before = dot(states[rows], held_inner[...]) + bias
        below = 0.5 * (1.0 + lax.erf(before * 0.7071067811865476))
        active[rows] = low(before * below)
        slope = below + before * jnp.exp(before * before * -0.5) * 0.3989422804014327
        g_inner[rows] = low(dot(grads[rows], held_outer[...], 1, 1) * slope)
        return carry

    lax.fori_loop(0, 8 * own // BLOCK, block, 0)
    mine = at(at_b * half, half, 128)
    depth, rows = out.shape[0], out.shape[1] // 2
    made = low(dot(active[:, mine], grads[...], 0, 0))
    for z in range(depth):
        out[z, :rows] = made[z * rows : (z + 1) * rows]
    made = low(dot(states[:, mine], g_inner[...], 0, 0))
    for z in range(depth):
        out[z, rows:] = made[z * rows : (z + 1) * rows]


def weight_out(*refs):
    pieces, (blocks, made) = (refs[:8], (refs[8:12], refs[14]))
    left, right = refs[12:14]
    _, at_c, at_y, at_z = spot()
    width, part = right.shape[1], left.shape[1]
    rows = right.shape[0] // 8
    for k, piece in enumerate(pieces):
        there = slice(k * rows, (k + 1) * rows)
        right[there] = piece[:rows, :width]
        mixed = piece[:rows, width:]
        mixed = jnp.where(at_c == 0, mixed[:, : 2 * part], mixed[:, 2 * part :])
        left[there] = jnp.where(at_y == 0, mixed[:, :part], mixed[:, part:])
    made[...] = dot(left[...], right[...], 0, 0)
    small = resplit(sum(full(piece[rows:, :width]) for piece in pieces))
    part = part // len(blocks)
    for k, block in enumerate(blocks):
        block[:part] = low(made[at((at_z + k) % len(blocks) * part, part, 8)])
        block[part:] = small


def weight_three(g_query, g_mine, came, states, w_three, back, keep, send, g_three):
    _, at_c, _, _ = spot()
    share = g_query.shape[1]
    g_three[:, :share] = g_query[...]
    g_three[:, share:] = low(g_mine[...] + came[...])
    made = low(dot(states[...], g_three[...], 0, 0))
    part = (keep.shape[0] - LINES) // 2
    for k in range(2):
        for c in range(2):
            piece = made[(2 * k + c) * part : (2 * k + c + 1) * part]

            @pl.when(at_c == c)
            def _():
                keep[k * part : (k + 1) * part] = piece

            @pl.when(at_c != c)
            def _():
                send[k * part : (k + 1) * part] = piece

    bias = jnp.broadcast_to(low(total(full(g_three[...]))), (LINES, 3 * share))
    keep[2 * part :] = bias
    send[2 * part :] = bias
    back[...] = low(dot(g_three[...], w_three[...], 1, 1))


def grad_states(parts, g_one, out):
    seqs, rows = out.shape[:2]
    for s in range(seqs):
        made = g_one[s * rows : (s + 1) * rows]
        for z in range(parts.shape[0] // seqs):
            made = made + full(parts[z * seqs + s])
        out[s] = made


def pack(summed, out_0, out_1, out_2, out_3, keep, came, vecs, out, loss, g_b_inner, *vectors):
    at_b, _, _, _ = spot()
    made = eight(summed)
    width, wide = made.shape[1], keep.shape[1]
    rows, share = (out.shape[0] - 8) // 3, width - wide
    part = out_0.shape[0] - LINES
    out[...] = jnp.zeros_like(out)
    out[: 2 * rows] = low(made)
    made = full(out_0[...]) + full(out_1[...]) + full(out_2[...]) + full(out_3[...])
    three = low(full(keep[...]) + full(came[...]))
    out[2 * rows : 3 * rows, :wide] = three[:rows]
    for k in range(width // share):
        piece = made[:part, k * share : (k + 1) * share]
        out[2 * rows + k * part : 2 * rows + (k + 1) * part, wide:] = low(piece)
    out[3 * rows :, :wide] = three[rows : rows + 8]
    small = made[part:]
    half = width // 2
    loss[...] = (small[10:11, :128] + small[11:12, :128]) / (2.0 * vecs[8:9, :128])
    for k, vector in enumerate(vectors):
        row = small[k : k + 1]
        vector[...] = jnp.where(at_b == 0, row[:, :half], row[:, half:]).reshape(half)
    first = jnp.where(at_b == 0, small[6:7], small[8:9])
    second = jnp.where(at_b == 0, small[7:8], small[9:10])
    g_b_inner[...] = jnp.concatenate([first, second], 1).reshape(2 * width)


def each_piece(pieces, steps):
    _, at_c, at_y, at_z = spot()
    depth = 4
    for j, k in enumerate(steps):
        for c in range(2):
            for y in range(2):
                place = (at_c + c) % 2, (at_y + y) % 2, (at_z + depth - k) % depth
                yield pieces[(j * 2 + c) * 2 + y], place


def final(steps, pieces, g_outer, g_inner, g_out, threes, biases, held, held_out, sem):
    depth = 4
    half, width = threes[0].shape
    rows, share = width // 8, width // depth
    part = rows // depth
    copies = []
    for n, (piece, (c, y, z)) in enumerate(each_piece(pieces, steps)):
        place = (c * 2 + y) * depth + z
        own = slice(n * 2 * rows, (n + 1) * 2 * rows)
        held[own] = full(piece[: 2 * rows])
        first = n * 2 * rows
        copies.append((held.at[first : first + rows], g_outer.at[at(place * rows, rows, 32)]))
        for k in range(2):
            cols = at((2 * k + c) * width + y * half, half, 128)
            copies.append(
                (
                    held.at[first + rows : first + 2 * rows, k * half : (k + 1) * half],
                    g_inner.at[at(z * rows, rows, 32), cols],
                )
            )
        for k in range(depth):
            first = 2 * rows + k * part
            held_out[n * part : (n + 1) * part, k * share : (k + 1) * share] = full(
                piece[first : first + part, 3 * share :]
            )
        copies.append((held_out.at[n * part : (n + 1) * part], g_out.at[at(place * part, part, 8)]))
    copies = start(copies, sem)
    for piece, (c, y, z) in each_piece(pieces, steps):
        there = at((c * 2 + y) * rows, rows, 32)
        for k in range(depth):

            @pl.when(z == k)
            def _():
                cols = slice(k * share, (k + 1) * share)
                for j, out in enumerate(threes):
                    out[there, cols] = full(piece[2 * rows : 3 * rows, j * share : (j + 1) * share])
                for j in (0, 2):
                    bias = full(piece[3 * rows :, j * share : (j + 1) * share])
                    biases[j : j + 1, cols] = bias[0:1]

    finish(copies)


def final_first(*refs):
    biases = refs[18]
    biases[...] = jnp.zeros_like(biases)
    final((0, 1, 3), refs[:12], *refs[12:15], refs[15:18], biases, *refs[19:])


def final_last(*refs):
    at_b, _, _, _ = spot()
    for k in range(3):
        refs[11 + 3 + k][...] = refs[7 + k][...]
    biases = refs[19]
    biases[...] = refs[10][...]
    final((2,), refs[:4], *refs[11:14], refs[14:17], biases, *refs[20:])
    for j, out in ((0, refs[17]), (2, refs[18])):
        half = out.shape[0]
        row = biases[j : j + 1]
        out[...] = jnp.where(at_b == 0, row[:, :half], row[:, half:]).reshape(half)


def per_device_heads(
    inputs,
    teacher,
    segments,
    w_query,
    b_query,
    w_key,
    w_value,
    b_value,
    w_out,
    b_out,
    gain_one,
    shift_one,
    w_inner,
    b_inner,
    w_outer,
    b_outer,
    gain_two,
    shift_two,
):
    count = lax.axis_size("ctx")
    depth = count // 4
    place = lax.axis_index("ctx")
    at_c, at_y = place % 2, place // 2 % 2
    seqs, rows, width = inputs.shape
    own = seqs * rows
    half = width // 2
    ff = w_inner.shape[1]
    share = width // depth
    keys = count // 2 * rows
    joint = ("batch", "ctx")
    pairs = [(y, c) for y in range(2) for c in range(2)]
    groups_z = [[z * 4 + r for z in range(depth)] for r in range(4)]
    groups_yz = [[z * 4 + y * 2 + c for z in range(depth) for y in range(2)] for c in range(2)]
    groups_xyc = [[b * count + z * 4 + y * 2 + c for b in range(2) for y, c in pairs] for z in range(depth)]

    def swap_x(values):
        return lax.ppermute(values, "batch", [(0, 1), (1, 0)])

    def swap_y(values):
        return lax.ppermute(values, "ctx", [(i, i ^ 2) for i in range(count)])

    def swap_xy(values):
        return lax.ppermute(values, joint, [(i, (i + count) % (2 * count) ^ 2) for i in range(2 * count)])

    def swap_c(values):
        return lax.ppermute(values, "ctx", [(i, i ^ 1) for i in range(count)])

    def shift_z(values, step):
        return lax.ppermute(values, "ctx", [(i, (i + 4 * step) % count) for i in range(count)])

    def trade(values, groups, axes="ctx"):
        return lax.all_to_all(values, axes, 0, 0, axis_index_groups=groups, tiled=True)

    tie = lax.optimization_barrier
    dma = pltpu.SemaphoreType.DMA

    blocks, first, p_inner, p_outer, p_out = kernel(
        prepare,
        [
            ((depth * seqs, rows, width), BF),
            ((3 * half // 4 + LINES, width), BF),
            ((half, width), BF),
            ((ff // 8, width), BF),
            ((half // 2, width), BF),
        ],
        [inputs, w_query, w_key, w_value, b_query, b_value, b_out, gain_one, shift_one]
        + [b_outer, gain_two, shift_two, b_inner, segments, w_inner, w_outer, w_out],
        hbm=(14, 15, 16),
        pin=range(14),
        scratch=[dma((4,))],
    )
    states = trade(blocks, groups_yz).reshape(keys, width)
    other = swap_x(first)
    x_inner = swap_x(p_inner)
    seg_seq = lax.dynamic_index_in_dim(segments, at_y, 0, keepdims=False).reshape(-1, 2, rows)
    seg_own = lax.dynamic_index_in_dim(seg_seq, at_c, 1, keepdims=False).reshape(-1)
    seg_peer = lax.dynamic_index_in_dim(seg_seq, 1 - at_c, 1, keepdims=False).reshape(-1)
    seg_key = jnp.concatenate([seg_own, seg_peer])[:, None]
    seg_query = seg_own[None, :]
    seg_tokens = lax.dynamic_slice_in_dim(segments, place * rows, rows, 1).reshape(own, 1)
    states, other, p_outer, p_out, seg_key, seg_query, seg_tokens = tie(
        (states, other, p_outer, p_out, seg_key, seg_query, seg_tokens)
    )
    x_outer = swap_x(p_outer)

    query, pair, vecs, inner_vec, w_three = kernel(
        project,
        [
            ((keys, share), BF),
            ((keys, 2 * share), BF),
            ((LINES, width), F32),
            ((8, ff), F32),
            ((width, 3 * share), BF),
        ],
        [states, first, other],
        scratch=[pltpu.VMEM((width, 3 * share), BF)],
    )
    peer = swap_c(pair)
    query, peer, x_inner = tie((query, peer, x_inner))
    y_inner = swap_y(x_inner)
    mixed, logs = kernel(
        attend,
        [((keys, share), BF), ((8, keys), F32)],
        [query, pair, peer, seg_query, seg_key],
        scratch=[pltpu.VMEM((2 * keys, share), BF), pltpu.VMEM((share, 2 * keys), BF)],
    )
    x_outer, mixed, p_out = tie((x_outer, mixed, p_out))
    mixed = trade(mixed.reshape(depth * seqs, rows, share), groups_yz)
    y_outer = swap_y(x_outer)
    x_out = swap_x(p_out)
    c_inner, c_outer = map(swap_c, (x_inner, x_outer))
    mixed, y_outer, x_out, y_inner, c_inner, c_outer = tie(
        (mixed, y_outer, x_out, y_inner, c_inner, c_outer)
    )
    weights = [w_out, x_out, swap_c(x_out)]
    weights += [w_inner, x_inner, y_inner, c_inner, swap_c(y_inner)]
    weights += [w_outer, x_outer, y_outer, c_outer, swap_c(y_outer)]
    held = [pltpu.VMEM((width, width), BF), pltpu.VMEM((width, ff), BF), pltpu.VMEM((ff, width), BF)]
    output, attended, unit, inverse, slope, two, g_hidden, sums = kernel(
        functools.partial(forward, float(own * 2 * count)),
        [
            (inputs.shape, F32),
            ((own, width), BF),
            ((own, width), F32),
            ((own, 128), F32),
            ((own, ff), F32),
            ((own, 2 * width), BF),
            ((own, width), F32),
            ((LINES, width), F32),
        ],
        [mixed, inputs, teacher, seg_tokens, vecs, inner_vec, *weights],
        hbm=range(6, 19),
        pin=(1, 2),
        scratch=[*held, pltpu.VMEM((own, ff), BF), dma((3, 9))],
    )
    fours = [two, swap_x(two), swap_y(two), swap_xy(two)]
    away_x, away_y, g_one, g_mixed = kernel(
        backward,
        [
            ((own + LINES, width + half), BF),
            ((own + LINES, width + half), BF),
            ((own, width), F32),
            ((depth * seqs, rows, 2 * share), BF),
        ],
        [two, slope, g_hidden, unit, inverse, vecs, attended, sums, *weights],
        hbm=range(8, 21),
        scratch=[
            *held,
            pltpu.VMEM((own, ff), BF),
            pltpu.VMEM((8, ff), F32),
            pltpu.VMEM((LINES, width), F32),
            dma((3, 9)),
        ],
    )
    away_x, away_y, *fours = tie((away_x, away_y, *fours))
    g_mixed = trade(g_mixed, groups_yz).reshape(keys, 2 * share)
    eights = [*fours, *map(swap_c, fours)]
    outer_rows = half // depth
    (feed,) = kernel(
        weight_feed,
        [((depth, 2 * outer_rows, width), BF)],
        [*eights, inner_vec, w_inner, x_inner, y_inner, w_outer, x_outer],
        hbm=range(9, 14),
        scratch=[
            pltpu.VMEM((width, width), BF),
            pltpu.VMEM((width, width), BF),
            pltpu.VMEM((8 * own, width), BF),
            pltpu.VMEM((8 * own, width), BF),
            pltpu.VMEM((8 * own, width), BF),
            pltpu.VMEM((8 * own, width), BF),
            dma((8,)),
        ],
    )
    feed, g_mixed, away_x, away_y = tie((feed, g_mixed, away_x, away_y))
    feed = trade(feed, groups_z)
    fours = [away_y, swap_x(away_x), swap_y(away_y), swap_xy(away_x)]

    g_query, g_mine, g_theirs = kernel(
        attend_back,
        [((keys, share), BF), ((keys, 2 * share), F32), ((keys, 2 * share), F32)],
        [query, pair, peer, seg_query, seg_key, logs, g_mixed],
        pin=range(6),
        scratch=[
            pltpu.VMEM((2 * keys, share), BF),
            pltpu.VMEM((share, 2 * keys), BF),
            pltpu.VMEM((2 * keys, share), BF),
            pltpu.VMEM((2 * keys, 2 * share), F32),
        ],
    )
    g_theirs, *fours = tie((g_theirs, *fours))
    part = half // 4 // depth
    outs = kernel(
        weight_out,
        [((part + LINES, width), BF)] * depth,
        [*fours, *map(swap_c, fours)],
        scratch=[
            pltpu.VMEM((8 * own, half // 4), BF),
            pltpu.VMEM((8 * own, width), BF),
            pltpu.VMEM((half // 4, width), F32),
        ],
    )
    back, three_keep, three_send = kernel(
        weight_three,
        [((keys, width), BF)] + [((half + LINES, 3 * share), BF)] * 2,
        [g_query, g_mine, swap_c(g_theirs), states, w_three],
        pin=(3, 4),
        scratch=[pltpu.VMEM((keys, 3 * share), BF)],
    )
    three_keep, three_send = kernel(
        functools.partial(halve_out, 0),
        [((half // 2 + LINES, 3 * share), BF)] * 2,
        [three_keep, swap_c(three_send)],
    )
    three_x, *outs = tie((swap_x(three_send), *outs))
    outs = [outs[0]] + [shift_z(outs[k], k) for k in range(1, depth)]
    three_keep, three_send = kernel(
        functools.partial(halve_out, 2),
        [((half // 4 + LINES, 3 * share), BF)] * 2,
        [three_keep, three_x],
    )
    three_came = swap_y(three_send)
    packed, loss, g_b_inner, *vectors = kernel(
        pack,
        [((3 * outer_rows + 8, width), BF), ((1, 128), F32), ((ff // 2,), F32)] + [((half,), F32)] * 6,
        [feed, *outs, three_keep, three_came, vecs],
    )
    packed, back = tie((packed, back))
    up, down, by_y = tie((shift_z(packed, 1), shift_z(packed, -1), swap_y(packed)))
    back = trade(back.reshape(depth * seqs, rows, width), groups_yz)
    across, up_y, down_y = tie((shift_z(up, 1), swap_y(up), swap_y(down)))
    pieces = []
    for pair in ((packed, by_y), (up, up_y), (down, down_y)):
        pieces += [*pair, *map(swap_c, pair)]
    large = [((ff // 2, width), F32), ((half, ff), F32), ((half, width), F32)]
    threes = [((half, width), F32)] * 3
    room = 2 * outer_rows

    def buffers(count):
        return [
            pltpu.VMEM((count * room, width), F32),
            pltpu.VMEM((count * part, width), F32),
            dma((4 * count,)),
        ]

    outs = kernel(
        final_first,
        [*large, *threes, ((8, width), F32)],
        pieces,
        outs_hbm=range(3),
        scratch=buffers(12),
    )
    across_y, *outs = tie((swap_y(across), *outs))
    pieces = [across, across_y, swap_c(across), swap_c(across_y)]
    (g_inputs,) = kernel(grad_states, [(inputs.shape, F32)], [back, g_one])
    g_w_outer, g_w_inner, g_w_out, g_w_query, g_w_key, g_w_value, g_b_query, g_b_value = kernel(
        final_last,
        [*large, *threes] + [((half,), F32)] * 2,
        [*pieces, *outs],
        hbm=range(4, 7),
        outs_hbm=range(3),
        aliases={4: 0, 5: 1, 6: 2},
        scratch=[pltpu.VMEM((8, width), F32), *buffers(4)],
    )
    g_b_out, g_gain_one, g_shift_one, g_b_outer, g_gain_two, g_shift_two = vectors
    return (
        output,
        loss[0, 0],
        g_inputs,
        g_w_query,
        g_b_query,
        g_w_key,
        g_w_value,
        g_b_value,
        g_w_out,
        g_b_out,
        g_gain_one,
        g_shift_one,
        g_w_inner,
        g_b_inner,
        g_w_outer,
        g_b_outer,
        g_gain_two,
        g_shift_two,
    )


def per_device(inputs, *others):
    sizes = (lax.axis_size("batch"), lax.axis_size("ctx"), inputs.shape[0])
    if sizes == (2, 16, 2):
        return per_device_heads(inputs, *others)
    return per_device_any(inputs, *others)


def solution(mesh):
    placed = (
        P("batch", "ctx", None),
        P("batch", "ctx", None),
        P("batch", None),
        P("batch", None),
        P("batch"),
        P("batch", None),
        P("batch", None),
        P("batch"),
        P("batch", None),
        P("batch"),
        P("batch"),
        P("batch"),
        P("batch", None),
        P("batch"),
        P("batch", None),
        P("batch"),
        P("batch"),
        P("batch"),
    )
    return jax.shard_map(
        per_device,
        mesh=mesh,
        in_specs=placed,
        out_specs=(
            P("batch", "ctx", None),
            P(),
            P("batch", "ctx", None),
            P("batch", None),
            P("batch"),
            P("batch", None),
            P("batch", None),
            P("batch"),
            P("batch", None),
            P("batch"),
            P("batch"),
            P("batch"),
            P("batch", None),
            P("batch"),
            P("batch", None),
            P("batch"),
            P("batch"),
            P("batch"),
        ),
        check_vma=False,
    )
```

```python
import functools
import math

import jax
import jax.numpy as jnp
from jax import lax
from jax.experimental import pallas as pl
from jax.experimental.pallas import tpu as pltpu
from jax.sharding import PartitionSpec as P

H = 12
HD = 64


NEGATIVE = -1e30
EPSILON = 1e-12


def norm_rows(hidden, gain, shift):
    center = hidden - jnp.mean(hidden, -1, keepdims=True)
    spread = jnp.mean(center * center, -1, keepdims=True)
    return center * lax.rsqrt(spread + EPSILON) * gain + shift


def gelu_exact(values):
    return jax.nn.gelu(values, approximate=False)


def linear(rows_in, weight):
    return jnp.dot(rows_in, weight, preferred_element_type=jnp.float32)


def contract_rows(left, right):
    return lax.dot_general(
        left, right, (((0,), (0,)), ((), ())), preferred_element_type=jnp.float32
    )


def times_transpose(rows_in, weight):
    return lax.dot_general(
        rows_in, weight, (((1,), (1,)), ((), ())), preferred_element_type=jnp.float32
    )


def score_rows(query_one, keys_all, seg_mine, seg_all):
    heads_query = query_one.reshape(query_one.shape[0], H, HD)
    heads_key = keys_all.reshape(keys_all.shape[0], H, HD)
    raw = jnp.einsum(
        "chd,khd->hck", heads_query, heads_key, preferred_element_type=jnp.float32
    ) * HD ** (-0.5)
    allowed = seg_mine[None, :, None] == seg_all[None, None, :]
    return jnp.where(allowed, raw, NEGATIVE)


def per_device_any(
    inputs,
    teacher,
    segments,
    w_query,
    b_query,
    w_key,
    w_value,
    b_value,
    w_out,
    b_out,
    gain_one,
    shift_one,
    w_inner,
    b_inner,
    w_outer,
    b_outer,
    gain_two,
    shift_two,
):
    (
        w_query,
        b_query,
        w_key,
        w_value,
        b_value,
        w_out,
        b_out,
        gain_one,
        shift_one,
        w_inner,
        b_inner,
        w_outer,
        b_outer,
        gain_two,
        shift_two,
    ) = (
        lax.all_gather(w_query, "batch", axis=0, tiled=True),
        lax.all_gather(b_query, "batch", axis=0, tiled=True),
        lax.all_gather(w_key, "batch", axis=0, tiled=True),
        lax.all_gather(w_value, "batch", axis=0, tiled=True),
        lax.all_gather(b_value, "batch", axis=0, tiled=True),
        lax.all_gather(w_out, "batch", axis=0, tiled=True),
        lax.all_gather(b_out, "batch", axis=0, tiled=True),
        lax.all_gather(gain_one, "batch", axis=0, tiled=True),
        lax.all_gather(shift_one, "batch", axis=0, tiled=True),
        lax.all_gather(w_inner, "batch", axis=0, tiled=True),
        lax.all_gather(b_inner, "batch", axis=0, tiled=True),
        lax.all_gather(w_outer, "batch", axis=0, tiled=True),
        lax.all_gather(b_outer, "batch", axis=0, tiled=True),
        lax.all_gather(gain_two, "batch", axis=0, tiled=True),
        lax.all_gather(shift_two, "batch", axis=0, tiled=True),
    )
    scale = HD ** (-0.5)
    seqs_here, ctx_rows, width = inputs.shape
    rows_here = seqs_here * ctx_rows
    tokens_all = rows_here * lax.axis_size("batch") * lax.axis_size("ctx")
    seg_own = lax.dynamic_slice_in_dim(segments, lax.axis_index("ctx") * ctx_rows, ctx_rows, 1)
    inputs_flat = inputs.reshape(rows_here, width)
    inputs_low = inputs_flat.astype(jnp.bfloat16)
    query = (linear(inputs_low, w_query) + b_query.astype(jnp.float32)).astype(jnp.bfloat16)
    key = linear(inputs_low, w_key).astype(jnp.bfloat16)
    value = (linear(inputs_low, w_value) + b_value.astype(jnp.float32)).astype(jnp.bfloat16)
    query_seq = query.reshape(seqs_here, ctx_rows, width)
    key_seq = key.reshape(seqs_here, ctx_rows, width)
    value_seq = value.reshape(seqs_here, ctx_rows, width)

    def attend_forward(items):
        query_one, key_one, value_one, seg_all, seg_mine = items
        keys_all, values_all = (
            lax.all_gather(key_one, "ctx", axis=0, tiled=True),
            lax.all_gather(value_one, "ctx", axis=0, tiled=True),
        )
        scores = score_rows(query_one, keys_all, seg_mine, seg_all)
        highest = jnp.max(scores, -1, keepdims=True)
        expo = jnp.exp(scores - highest)
        totals = jnp.sum(expo, -1, keepdims=True)
        probs = (expo / totals).astype(jnp.bfloat16)
        mixed = jnp.einsum(
            "hck,khd->chd",
            probs,
            values_all.reshape(keys_all.shape[0], H, HD),
            preferred_element_type=jnp.float32,
        )
        return (
            mixed.reshape(ctx_rows, width).astype(jnp.bfloat16),
            (highest + jnp.log(totals))[:, :, 0],
        )

    attended, log_totals = lax.map(
        attend_forward, (query_seq, key_seq, value_seq, segments, seg_own)
    )
    attended_flat = attended.reshape(rows_here, width)
    gain_one_full = gain_one.astype(jnp.float32)
    shift_one_full = shift_one.astype(jnp.float32)
    gain_two_full = gain_two.astype(jnp.float32)
    shift_two_full = shift_two.astype(jnp.float32)
    hidden_one = inputs_flat + linear(attended_flat, w_out) + b_out.astype(jnp.float32)
    normed_one, back_one = jax.vjp(norm_rows, hidden_one, gain_one_full, shift_one_full)
    normed_low = normed_one.astype(jnp.bfloat16)
    inner_pre = linear(normed_low, w_inner) + b_inner.astype(jnp.float32)
    active_full, gelu_back = jax.vjp(gelu_exact, inner_pre)
    active_low = active_full.astype(jnp.bfloat16)
    hidden_two = normed_one + linear(active_low, w_outer) + b_outer.astype(jnp.float32)
    output, back_two = jax.vjp(norm_rows, hidden_two, gain_two_full, shift_two_full)
    valid = (seg_own.reshape(rows_here) != 0).astype(jnp.float32)[:, None]
    error = output - teacher.reshape(rows_here, width)
    loss_total, valid_count = lax.psum(
        (jnp.sum(valid * error * error), jnp.sum(valid)), ("batch", "ctx")
    )
    loss = loss_total / (2.0 * valid_count)
    grad_output = tokens_all / valid_count * valid * error
    grad_hidden_two, grad_gain_two, grad_shift_two = back_two(grad_output)
    grad_branch_two = grad_hidden_two.astype(jnp.bfloat16)
    grad_b_outer = jnp.sum(grad_branch_two.astype(jnp.float32), 0)
    grad_w_outer = contract_rows(active_low, grad_branch_two)
    grad_active = times_transpose(grad_branch_two, w_outer)
    grad_inner = gelu_back(grad_active)[0].astype(jnp.bfloat16)
    grad_b_inner = jnp.sum(grad_inner.astype(jnp.float32), 0)
    grad_w_inner = contract_rows(normed_low, grad_inner)
    grad_normed = grad_hidden_two + times_transpose(grad_inner, w_inner)
    grad_hidden_one, grad_gain_one, grad_shift_one = back_one(grad_normed)
    grad_branch_one = grad_hidden_one.astype(jnp.bfloat16)
    grad_b_out = jnp.sum(grad_branch_one.astype(jnp.float32), 0)
    grad_w_out = contract_rows(attended_flat, grad_branch_one)
    grad_attended = (
        times_transpose(grad_branch_one, w_out)
        .astype(jnp.bfloat16)
        .reshape(seqs_here, ctx_rows, width)
    )

    def attend_backward(items):
        query_one, key_one, value_one, seg_all, seg_mine, log_one, grad_one = items
        keys_all, values_all = (
            lax.all_gather(key_one, "ctx", axis=0, tiled=True),
            lax.all_gather(value_one, "ctx", axis=0, tiled=True),
        )
        key_count = keys_all.shape[0]
        scores = score_rows(query_one, keys_all, seg_mine, seg_all)
        probs = jnp.exp(scores - log_one[:, :, None])
        grad_heads = grad_one.reshape(ctx_rows, H, HD)
        grad_probs = jnp.einsum(
            "chd,khd->hck",
            grad_heads,
            values_all.reshape(key_count, H, HD),
            preferred_element_type=jnp.float32,
        )
        centre = jnp.sum(probs * grad_probs, -1)
        grad_scores = (probs * (grad_probs - centre[:, :, None])).astype(jnp.bfloat16)
        grad_query = (
            jnp.einsum(
                "hck,khd->chd",
                grad_scores,
                keys_all.reshape(key_count, H, HD),
                preferred_element_type=jnp.float32,
            )
            * scale
        )
        grad_query = grad_query.reshape(ctx_rows, width).astype(jnp.bfloat16)
        probs_low = probs.astype(jnp.bfloat16)
        query_heads = query_one.reshape(ctx_rows, H, HD)
        count = ctx_rows * lax.axis_size("ctx")
        grad_key = (
            jnp.einsum("hck,chd->khd", grad_scores, query_heads, preferred_element_type=jnp.float32)
            * scale
        )
        grad_value = jnp.einsum(
            "hck,chd->khd", probs_low, grad_heads, preferred_element_type=jnp.float32
        )
        both = lax.psum_scatter(
            jnp.concatenate([grad_key.reshape(count, width), grad_value.reshape(count, width)], 1),
            "ctx",
            scatter_dimension=0,
            tiled=True,
        )
        return (
            grad_query,
            both[:, :width].astype(jnp.bfloat16),
            both[:, width:].astype(jnp.bfloat16),
        )

    grad_query_seq, grad_key_seq, grad_value_seq = lax.map(
        attend_backward,
        (query_seq, key_seq, value_seq, segments, seg_own, log_totals, grad_attended),
    )
    grad_query_flat = grad_query_seq.reshape(rows_here, width)
    grad_key_flat = grad_key_seq.reshape(rows_here, width)
    grad_value_flat = grad_value_seq.reshape(rows_here, width)
    grad_w_query = contract_rows(inputs_low, grad_query_flat)
    grad_b_query = jnp.sum(grad_query_flat.astype(jnp.float32), 0)
    grad_w_key = contract_rows(inputs_low, grad_key_flat)
    grad_w_value = contract_rows(inputs_low, grad_value_flat)
    grad_b_value = jnp.sum(grad_value_flat.astype(jnp.float32), 0)
    grad_inputs = (
        grad_hidden_one
        + times_transpose(grad_query_flat, w_query)
        + times_transpose(grad_key_flat, w_key)
        + times_transpose(grad_value_flat, w_value)
    )
    (
        grad_w_query,
        grad_b_query,
        grad_w_key,
        grad_w_value,
        grad_b_value,
        grad_w_out,
        grad_b_out,
        grad_gain_one,
        grad_shift_one,
        grad_w_inner,
        grad_b_inner,
        grad_w_outer,
        grad_b_outer,
        grad_gain_two,
        grad_shift_two,
    ) = (
        lax.psum_scatter(
            grad_w_query.astype(jnp.bfloat16), "batch", scatter_dimension=0, tiled=True
        ).astype(jnp.float32),
        lax.psum_scatter(
            grad_b_query.astype(jnp.bfloat16), "batch", scatter_dimension=0, tiled=True
        ).astype(jnp.float32),
        lax.psum_scatter(
            grad_w_key.astype(jnp.bfloat16), "batch", scatter_dimension=0, tiled=True
        ).astype(jnp.float32),
        lax.psum_scatter(
            grad_w_value.astype(jnp.bfloat16), "batch", scatter_dimension=0, tiled=True
        ).astype(jnp.float32),
        lax.psum_scatter(
            grad_b_value.astype(jnp.bfloat16), "batch", scatter_dimension=0, tiled=True
        ).astype(jnp.float32),
        lax.psum_scatter(
            grad_w_out.astype(jnp.bfloat16), "batch", scatter_dimension=0, tiled=True
        ).astype(jnp.float32),
        lax.psum_scatter(
            grad_b_out.astype(jnp.bfloat16), "batch", scatter_dimension=0, tiled=True
        ).astype(jnp.float32),
        lax.psum_scatter(
            grad_gain_one.astype(jnp.bfloat16), "batch", scatter_dimension=0, tiled=True
        ).astype(jnp.float32),
        lax.psum_scatter(
            grad_shift_one.astype(jnp.bfloat16), "batch", scatter_dimension=0, tiled=True
        ).astype(jnp.float32),
        lax.psum_scatter(
            grad_w_inner.astype(jnp.bfloat16), "batch", scatter_dimension=0, tiled=True
        ).astype(jnp.float32),
        lax.psum_scatter(
            grad_b_inner.astype(jnp.bfloat16), "batch", scatter_dimension=0, tiled=True
        ).astype(jnp.float32),
        lax.psum_scatter(
            grad_w_outer.astype(jnp.bfloat16), "batch", scatter_dimension=0, tiled=True
        ).astype(jnp.float32),
        lax.psum_scatter(
            grad_b_outer.astype(jnp.bfloat16), "batch", scatter_dimension=0, tiled=True
        ).astype(jnp.float32),
        lax.psum_scatter(
            grad_gain_two.astype(jnp.bfloat16), "batch", scatter_dimension=0, tiled=True
        ).astype(jnp.float32),
        lax.psum_scatter(
            grad_shift_two.astype(jnp.bfloat16), "batch", scatter_dimension=0, tiled=True
        ).astype(jnp.float32),
    )
    (
        grad_w_query,
        grad_b_query,
        grad_w_key,
        grad_w_value,
        grad_b_value,
        grad_w_out,
        grad_b_out,
        grad_gain_one,
        grad_shift_one,
        grad_w_inner,
        grad_b_inner,
        grad_w_outer,
        grad_b_outer,
        grad_gain_two,
        grad_shift_two,
    ) = lax.psum(
        (
            grad_w_query,
            grad_b_query,
            grad_w_key,
            grad_w_value,
            grad_b_value,
            grad_w_out,
            grad_b_out,
            grad_gain_one,
            grad_shift_one,
            grad_w_inner,
            grad_b_inner,
            grad_w_outer,
            grad_b_outer,
            grad_gain_two,
            grad_shift_two,
        ),
        "ctx",
    )
    return (
        output.reshape(inputs.shape),
        loss,
        grad_inputs.reshape(inputs.shape),
        grad_w_query,
        grad_b_query,
        grad_w_key,
        grad_w_value,
        grad_b_value,
        grad_w_out,
        grad_b_out,
        grad_gain_one,
        grad_shift_one,
        grad_w_inner,
        grad_b_inner,
        grad_w_outer,
        grad_b_outer,
        grad_gain_two,
        grad_shift_two,
    )


BF, F32 = jnp.bfloat16, jnp.float32
LINES = 16
ROOM = 6 << 20


def low(values):
    return values.astype(BF)


def full(values):
    return values.astype(F32)


def dot(left, right, a=1, b=0):
    return lax.dot_general(left, right, (((a,), (b,)), ((), ())), preferred_element_type=F32)


def spot():
    place = lax.axis_index("ctx")
    return lax.axis_index("batch"), place % 2, place // 2 % 2, place // 4


def at(start, size, step):
    return pl.ds(pl.multiple_of(start, step), size)


def kernel(body, outs, args, hbm=(), scratch=(), pin=(), outs_hbm=(), aliases=None):
    name = getattr(body, "func", body).__name__
    where = [pl.BlockSpec(memory_space=pl.ANY if k in hbm else pltpu.VMEM) for k in range(len(args))]
    shapes = [jax.ShapeDtypeStruct(shape, kind) for shape, kind in outs]
    held = [a for k, a in enumerate(args) if k not in hbm]
    held += [a for k, a in enumerate(shapes) if k not in outs_hbm]
    held += [a for a in scratch if a.memory_space == pltpu.VMEM]
    room = sum(math.prod(a.shape) * jnp.dtype(a.dtype).itemsize for a in held) + ROOM
    args = [
        pltpu.with_memory_space_constraint(a, pltpu.HBM) if k in hbm or k in pin else a
        for k, a in enumerate(args)
    ]
    return pl.pallas_call(
        body,
        out_shape=shapes,
        in_specs=where,
        out_specs=[
            pl.BlockSpec(memory_space=pl.ANY if k in outs_hbm else pltpu.VMEM)
            for k in range(len(shapes))
        ],
        input_output_aliases=aliases or {},
        scratch_shapes=list(scratch),
        compiler_params=pltpu.CompilerParams(vmem_limit_bytes=room),
        name=name,
    )(*args)


def norm_forward(hidden, gain, shift):
    center = hidden - jnp.mean(hidden, -1, keepdims=True)
    inverse = lax.rsqrt(jnp.mean(center * center, -1, keepdims=True) + EPSILON)
    unit = center * inverse
    return unit * gain + shift, unit, inverse


def norm_backward(grad, unit, inverse, gain):
    scaled = grad * gain
    along = jnp.mean(scaled * unit, -1, keepdims=True)
    return inverse * (scaled - jnp.mean(scaled, -1, keepdims=True) - unit * along)


def total(values):
    return jnp.sum(values, 0, keepdims=True)


def prepare(*refs):
    inputs, w_three, vectors, b_inner, segments = refs[0], refs[1:4], refs[4:12], refs[12], refs[13]
    w_inner, w_outer, w_out, blocks, out, p_inner, p_outer, p_out, sem = refs[14:]
    half, width = w_three[0].shape
    _, at_c, at_y, at_z = spot()
    part, wide = half // 2, w_inner.shape[1] // 4
    rows_out, rows_outer = p_out.shape[0], p_outer.shape[0]
    copies = [
        (
            w_inner.at[at(at_y * part, part, 64), at((k * 2 + at_c) * wide, wide, 128)],
            p_inner.at[k * part : (k + 1) * part],
        )
        for k in range(2)
    ]
    copies.append((w_outer.at[at((at_c * 2 + at_y) * rows_outer, rows_outer, 128)], p_outer))
    copies.append((w_out.at[at(at_c * rows_out, rows_out, 64)], p_out))
    copies = start(copies, sem)
    seqs = inputs.shape[0]
    for s in range(seqs):
        piece = low(inputs[s])
        for z in range(blocks.shape[0] // seqs):
            blocks[z * seqs + s] = piece
    share, rows = width // 4, half // 4
    for z in range(4):

        @pl.when(at_z == z)
        def _():
            for j in range(3):
                for k in range(4):
                    piece = w_three[j][k * rows : (k + 1) * rows, z * share : (z + 1) * share]
                    out[j * rows : (j + 1) * rows, k * share : (k + 1) * share] = piece

    first = 3 * rows
    out[first : first + LINES] = jnp.zeros((LINES, width), BF)
    for r in range(8):
        out[first + r : first + r + 1, :half] = vectors[r][...].reshape(1, half)
    inner = b_inner[...].reshape(1, -1)
    for r in range(4):
        out[first + 8 + r : first + 9 + r, :half] = inner[:, half * r : half * (r + 1)]
    valid = jnp.sum(jnp.where(segments[...] != 0, 1, 0))
    lane = lax.broadcasted_iota(jnp.int32, (1, half), 1)
    parts = jnp.where(lane < 128, valid // 256, valid % 256)
    out[first + 12 : first + 13, :half] = low(full(parts))
    finish(copies)


def start(copies, sem):
    made = [pltpu.make_async_copy(*copy, sem.at[k]) for k, copy in enumerate(copies)]
    for copy in made:
        copy.start()
    return made


def finish(copies):
    for copy in copies:
        copy.wait()


def both_halves(at_b, mine, other):
    return jnp.where(at_b == 0, mine, other), jnp.where(at_b == 0, other, mine)


def project(states, mine, other, query, pair, vecs, inner_vec, held, w_back):
    at_b, _, _, at_z = spot()
    width, share = states.shape[1], query.shape[1]
    half, rows = width // 2, width // 8
    for j in range(3):
        for k in range(4):
            first = slice(j * rows, (j + 1) * rows)
            cols = slice(k * share, (k + 1) * share)
            pieces = both_halves(at_b, mine[first, cols], other[first, cols])
            for h, piece in enumerate(pieces):
                start_row = h * half + k * rows
                held[start_row : start_row + rows, j * share : (j + 1) * share] = piece
    w_back[...] = held[...]
    made = dot(states[...], held[...])
    lines = slice(3 * rows, 3 * rows + LINES)
    top, bottom = both_halves(at_b, full(mine[lines]), full(other[lines]))

    def bias(r):
        row = jnp.where(at_z < 2, top[r : r + 1], bottom[r : r + 1])
        return jnp.where(at_z % 2 == 0, row[:, :share], row[:, share : 2 * share])

    query[...] = low(full(low(made[:, :share] + bias(0))) * HD ** (-0.5))
    pair[:, :share] = low(made[:, share : 2 * share])
    pair[:, share:] = low(made[:, 2 * share :] + bias(1))
    vecs[...] = jnp.zeros_like(vecs)
    for r in range(2, 8):
        vecs[r - 2 : r - 1, :half] = top[r : r + 1, :half]
        vecs[r - 2 : r - 1, half:] = bottom[r : r + 1, :half]
    counts = top[12:13] + bottom[12:13]
    counts = counts[:, :128] * 256.0 + counts[:, 256:384]
    vecs[8:9, :128] = counts
    inner_vec[...] = jnp.zeros_like(inner_vec)
    for b, rows in enumerate((top, bottom)):
        for r in range(4):
            cols = slice((4 * b + r) * half, (4 * b + r + 1) * half)
            inner_vec[0:1, cols] = rows[8 + r : 9 + r, :half]


STEP = 256


def attend(query, mine, peer, seg_query, seg_key, mixed, logs, keys, values):
    count, share = query.shape
    keys[:count] = mine[:, :share]
    keys[count:] = peer[:, :share]
    values[:, :count] = mine[:, share:].T
    values[:, count:] = peer[:, share:].T
    logs[...] = jnp.zeros_like(logs)

    def block(j, carry):
        rows = at(j * STEP, STEP, STEP)
        allowed = seg_key[...] == seg_query[:, rows]
        for h in range(share // HD):
            cols = slice(h * HD, (h + 1) * HD)
            scores = dot(keys[:, cols], query[rows, cols], 1, 1)
            scores = jnp.where(allowed, scores, NEGATIVE)
            highest = jnp.max(scores, 0, keepdims=True)
            expo = jnp.exp(scores - highest)
            totals = jnp.sum(expo, 0, keepdims=True)
            probs = low(expo * (1.0 / totals))
            mixed[rows, cols] = low(dot(values[cols], probs).T)
            logs[h : h + 1, rows] = highest + jnp.log(totals)
        return carry

    lax.fori_loop(0, count // STEP, block, 0)


def attend_back(
    query, mine, peer, seg_query, seg_key, logs, grad, g_query, g_mine, g_peer, keys, flipped, values, made
):
    count, share = query.shape
    keys[:count] = mine[:, :share]
    keys[count:] = peer[:, :share]
    values[:count] = mine[:, share:]
    values[count:] = peer[:, share:]
    flipped[:, :count] = mine[:, :share].T
    flipped[:, count:] = peer[:, :share].T
    made[...] = jnp.zeros_like(made)

    def block(j, carry):
        rows = at(j * STEP, STEP, STEP)
        allowed = seg_key[...] == seg_query[:, rows]
        for h in range(share // HD):
            cols = slice(h * HD, (h + 1) * HD)
            cols_value = slice(share + h * HD, share + (h + 1) * HD)
            scores = dot(keys[:, cols], query[rows, cols], 1, 1)
            scores = jnp.where(allowed, scores, NEGATIVE)
            probs = jnp.exp(scores - logs[h : h + 1, rows])
            g_probs = dot(values[:, cols], grad[rows, cols], 1, 1)
            centre = jnp.sum(probs * g_probs, 0, keepdims=True)
            g_scores = low(probs * (g_probs - centre))
            g_query[rows, cols] = low((dot(flipped[cols], g_scores) * HD ** (-0.5)).T)
            made[:, cols] += dot(g_scores, query[rows, cols])
            made[:, cols_value] += dot(low(probs), grad[rows, cols])
        return carry

    lax.fori_loop(0, count // STEP, block, 0)
    g_mine[...] = made[:count]
    g_peer[...] = made[count:]


def fetch_out(own, pieces, held, sem):
    at_b, at_c, _, _ = spot()
    half, part = own.shape[0], pieces[0].shape[0]
    copies = [(own, held.at[at(at_b * half, half, 128)])]
    for k, piece in enumerate(pieces):
        first = (1 - at_b) * half + (at_c + k) % 2 * part
        copies.append((piece, held.at[at(first, part, 64)]))
    return start(copies, sem)


def fetch_inner(own, pieces, held, sem):
    at_b, at_c, at_y, _ = spot()
    half, part, wide = own.shape[0], pieces[0].shape[0] // 2, pieces[0].shape[1]
    copies = [(own, held.at[at(at_b * half, half, 128)])]
    for c in range(2):
        for y in range(2):
            rows = at((1 - at_b) * half + (at_y + y) % 2 * part, part, 64)
            for k in range(2):
                cols = at((2 * k + (at_c + c) % 2) * wide, wide, 128)
                piece = pieces[2 * c + y].at[k * part : (k + 1) * part]
                copies.append((piece, held.at[rows, cols]))
    return start(copies, sem)


def fetch_outer(own, pieces, held, sem):
    at_b, at_c, at_y, _ = spot()
    half, part = own.shape[0], pieces[0].shape[0]
    copies = [(own, held.at[at(at_b * half, half, 128)])]
    for c in range(2):
        for y in range(2):
            first = (1 - at_b) * half + ((at_c + c) % 2 * 2 + (at_y + y) % 2) * part
            copies.append((pieces[2 * c + y], held.at[at(first, part, 128)]))
    return start(copies, sem)


BLOCK = 256


def forward(tokens_all, *refs):
    mixed, inputs, teacher, seg, vecs, inner_vec = refs[:6]
    weights, (output, attended, unit, inverse, slope, two, g_hidden, sums) = refs[6:19], refs[19:27]
    held_out, held_inner, held_outer, active, sem = refs[27:]
    copies_out = fetch_out(weights[0], weights[1:3], held_out, sem.at[0])
    copies_inner = fetch_inner(weights[3], weights[4:8], held_inner, sem.at[1])
    copies_outer = fetch_outer(weights[8], weights[9:13], held_outer, sem.at[2])
    rows, share = mixed.shape[1:]
    seqs = inputs.shape[0]
    own, width = attended.shape
    ff = slope.shape[1]
    for s in range(seqs):
        for z in range(mixed.shape[0] // seqs):
            attended[s * rows : (s + 1) * rows, z * share : (z + 1) * share] = mixed[z * seqs + s]
    finish(copies_out)
    hidden = inputs[...].reshape(own, width) + dot(attended[...], held_out[...]) + vecs[0:1]
    normed, made_unit, made_inverse = norm_forward(hidden, vecs[1:2], vecs[2:3])
    unit[...] = made_unit
    inverse[...] = jnp.broadcast_to(made_inverse, inverse.shape)
    two[:, :width] = low(normed)
    finish(copies_inner)

    def block(j, carry):
        cols = at(j * BLOCK, BLOCK, BLOCK)
        before = dot(two[:, :width], held_inner[:, cols]) + inner_vec[0:1, cols]
        below = 0.5 * (1.0 + lax.erf(before * 0.7071067811865476))
        active[:, cols] = low(before * below)
        slope[:, cols] = below + before * jnp.exp(before * before * -0.5) * 0.3989422804014327
        return carry

    lax.fori_loop(0, ff // BLOCK, block, 0)
    finish(copies_outer)
    hidden = normed + dot(active[...], held_outer[...]) + vecs[3:4]
    made, unit_two, inverse_two = norm_forward(hidden, vecs[4:5], vecs[5:6])
    output[...] = made.reshape(output.shape)
    valid = jnp.where(seg[...] != 0, 1.0, 0.0)
    error = (made - teacher[...].reshape(own, width)) * valid
    grad = error * (tokens_all / vecs[8:9, 0:1])
    made = norm_backward(grad, unit_two, inverse_two, vecs[4:5])
    g_hidden[...] = made
    g_low = low(made)
    two[:, width:] = g_low
    sums[...] = jnp.zeros_like(sums)
    sums[3:4] = total(full(g_low))
    sums[4:5] = total(grad * unit_two)
    sums[5:6] = total(grad)
    loss = jnp.broadcast_to(jnp.sum(total(error * error), 1, keepdims=True), (1, width))
    sums[10:11] = full(low(loss))
    sums[11:12] = loss - full(low(loss))


def backward(*refs):
    two, slope, g_hidden, unit, inverse, vecs, attended, sums = refs[:8]
    weights, (away_x, away_y, g_one, g_mixed) = refs[8:21], refs[21:25]
    held_out, held_inner, held_outer, g_inner, inner_sums, small, sem = refs[25:]
    at_b, _, _, _ = spot()
    copies_outer = fetch_outer(weights[8], weights[9:13], held_outer, sem.at[2])
    copies_inner = fetch_inner(weights[3], weights[4:8], held_inner, sem.at[1])
    copies_out = fetch_out(weights[0], weights[1:3], held_out, sem.at[0])
    (own, width), ff = unit.shape, slope.shape[1]
    half = width // 2
    away_y[:own, width:] = jnp.where(at_b == 0, attended[:, :half], attended[:, half:])
    away_x[:own, width:] = jnp.where(at_b == 0, attended[:, half:], attended[:, :half])
    finish(copies_outer)

    def block(j, carry):
        cols = at(j * BLOCK, BLOCK, BLOCK)
        grad = low(dot(two[:, width:], held_outer[cols, :], 1, 1) * slope[:, cols])
        g_inner[:, cols] = grad
        inner_sums[0:1, cols] = total(full(grad))
        return carry

    lax.fori_loop(0, ff // BLOCK, block, 0)
    finish(copies_inner)
    g_normed = g_hidden[...] + dot(g_inner[...], held_inner[...], 1, 1)
    made = norm_backward(g_normed, unit[...], inverse[:, 0:1], vecs[1:2])
    g_one[...] = made
    g_low = low(made)
    finish(copies_out)
    g_attended = low(dot(g_low, held_out[...], 1, 1))
    rows, share = g_mixed.shape[1], g_mixed.shape[2] // 2
    seqs = own // rows
    g_mixed[:, :, share:] = jnp.zeros((g_mixed.shape[0], rows, share), BF)
    for s in range(seqs):
        for z in range(g_mixed.shape[0] // seqs):
            g_mixed[z * seqs + s, :, :share] = g_attended[s * rows : (s + 1) * rows, z * share : (z + 1) * share]
    small[...] = sums[...]
    small[0:1] = total(full(g_low))
    small[1:2] = total(g_normed * unit[...])
    small[2:3] = total(g_normed)
    for k in range(4):
        small[6 + k : 7 + k] = inner_sums[0:1, k * width : (k + 1) * width]
    for out in (away_x, away_y):
        out[:own, :width] = g_low
        out[own:, :width] = low(small[...])
        out[own:, width:] = jnp.zeros((LINES, half), BF)


def resplit(made):
    lines = made.shape[0]
    loss = made[10:11] + made[11:12]
    return low(jnp.concatenate([made[:10], full(low(loss)), loss - full(low(loss)), made[12:lines]]))


def halve_out(axis, keep, came, next_keep, next_send):
    mine = spot()[axis]
    part = next_keep.shape[0] - LINES
    for k in range(2):
        rows = slice(k * part, (k + 1) * part)
        piece = low(full(keep[rows]) + full(came[rows]))

        @pl.when(mine == k)
        def _():
            next_keep[:part] = piece

        @pl.when(mine != k)
        def _():
            next_send[:part] = piece

    small = resplit(full(keep[2 * part :]) + full(came[2 * part :]))
    next_keep[part:] = small
    next_send[part:] = small


def eight(parts):
    made = full(parts[0])
    for k in range(1, parts.shape[0]):
        made = made + full(parts[k])
    return made


def weight_feed(*refs):
    pieces, (inner_vec, w_inner, i_x, i_y, w_outer, o_x, out) = refs[:8], refs[8:15]
    held_inner, held_outer, states, grads, active, g_inner, sem = refs[15:]
    at_b, at_c, at_y, _ = spot()
    half, width = w_inner.shape[0], states.shape[1]
    other, part = (1 - at_b) * half, half // 2
    copies = []
    for k in range(2):
        cols = slice(k * half, (k + 1) * half)
        there = at((2 * k + at_c) * width + at_y * half, half, 128)
        copies.append((w_inner.at[:, there], held_inner.at[at(at_b * half, half, 128), cols]))
        for y, piece in enumerate((i_x, i_y)):
            rows = at(other + (at_y + y) % 2 * part, part, 64)
            from_rows = slice(k * part, (k + 1) * part)
            copies.append((piece.at[from_rows, at(at_y * half, half, 128)], held_inner.at[rows, cols]))
    rows = at((2 * at_c + at_y) * half, half, 128)
    copies.append((w_outer.at[rows], held_outer.at[at(at_b * half, half, 128)]))
    copies.append((o_x, held_outer.at[at(other, half, 128)]))
    copies = start(copies, sem)
    own = pieces[0].shape[0]
    for k, piece in enumerate(pieces):
        states[k * own : (k + 1) * own] = piece[:, :width]
        grads[k * own : (k + 1) * own] = piece[:, width:]
    bias = jnp.concatenate(
        [inner_vec[0:1, at((2 * k + at_c) * width + at_y * half, half, 128)] for k in range(2)], 1
    )
    finish(copies)

    def block(j, carry):
        rows = at(j * BLOCK, BLOCK, BLOCK)
        before = dot(states[rows], held_inner[...]) + bias
        below = 0.5 * (1.0 + lax.erf(before * 0.7071067811865476))
        active[rows] = low(before * below)
        slope = below + before * jnp.exp(before * before * -0.5) * 0.3989422804014327
        g_inner[rows] = low(dot(grads[rows], held_outer[...], 1, 1) * slope)
        return carry

    lax.fori_loop(0, 8 * own // BLOCK, block, 0)
    mine = at(at_b * half, half, 128)
    depth, rows = out.shape[0], out.shape[1] // 2
    made = low(dot(active[:, mine], grads[...], 0, 0))
    for z in range(depth):
        out[z, :rows] = made[z * rows : (z + 1) * rows]
    made = low(dot(states[:, mine], g_inner[...], 0, 0))
    for z in range(depth):
        out[z, rows:] = made[z * rows : (z + 1) * rows]


def weight_out(*refs):
    pieces, (blocks, made) = (refs[:8], (refs[8:12], refs[14]))
    left, right = refs[12:14]
    _, at_c, at_y, at_z = spot()
    width, part = right.shape[1], left.shape[1]
    rows = right.shape[0] // 8
    for k, piece in enumerate(pieces):
        there = slice(k * rows, (k + 1) * rows)
        right[there] = piece[:rows, :width]
        mixed = piece[:rows, width:]
        mixed = jnp.where(at_c == 0, mixed[:, : 2 * part], mixed[:, 2 * part :])
        left[there] = jnp.where(at_y == 0, mixed[:, :part], mixed[:, part:])
    made[...] = dot(left[...], right[...], 0, 0)
    small = resplit(sum(full(piece[rows:, :width]) for piece in pieces))
    part = part // len(blocks)
    for k, block in enumerate(blocks):
        block[:part] = low(made[at((at_z + k) % len(blocks) * part, part, 8)])
        block[part:] = small


def weight_three(g_query, g_mine, came, states, w_three, back, keep, send, g_three):
    _, at_c, _, _ = spot()
    share = g_query.shape[1]
    g_three[:, :share] = g_query[...]
    g_three[:, share:] = low(g_mine[...] + came[...])
    made = low(dot(states[...], g_three[...], 0, 0))
    part = (keep.shape[0] - LINES) // 2
    for k in range(2):
        for c in range(2):
            piece = made[(2 * k + c) * part : (2 * k + c + 1) * part]

            @pl.when(at_c == c)
            def _():
                keep[k * part : (k + 1) * part] = piece

            @pl.when(at_c != c)
            def _():
                send[k * part : (k + 1) * part] = piece

    bias = jnp.broadcast_to(low(total(full(g_three[...]))), (LINES, 3 * share))
    keep[2 * part :] = bias
    send[2 * part :] = bias
    back[...] = low(dot(g_three[...], w_three[...], 1, 1))


def grad_states(parts, g_one, out):
    seqs, rows = out.shape[:2]
    for s in range(seqs):
        made = g_one[s * rows : (s + 1) * rows]
        for z in range(parts.shape[0] // seqs):
            made = made + full(parts[z * seqs + s])
        out[s] = made


def pack(summed, out_0, out_1, out_2, out_3, keep, came, vecs, out, loss, g_b_inner, *vectors):
    at_b, _, _, _ = spot()
    made = eight(summed)
    width, wide = made.shape[1], keep.shape[1]
    rows, share = (out.shape[0] - 8) // 3, width - wide
    part = out_0.shape[0] - LINES
    out[...] = jnp.zeros_like(out)
    out[: 2 * rows] = low(made)
    made = full(out_0[...]) + full(out_1[...]) + full(out_2[...]) + full(out_3[...])
    three = low(full(keep[...]) + full(came[...]))
    out[2 * rows : 3 * rows, :wide] = three[:rows]
    for k in range(width // share):
        piece = made[:part, k * share : (k + 1) * share]
        out[2 * rows + k * part : 2 * rows + (k + 1) * part, wide:] = low(piece)
    out[3 * rows :, :wide] = three[rows : rows + 8]
    small = made[part:]
    half = width // 2
    loss[...] = (small[10:11, :128] + small[11:12, :128]) / (2.0 * vecs[8:9, :128])
    for k, vector in enumerate(vectors):
        row = small[k : k + 1]
        vector[...] = jnp.where(at_b == 0, row[:, :half], row[:, half:]).reshape(half)
    first = jnp.where(at_b == 0, small[6:7], small[8:9])
    second = jnp.where(at_b == 0, small[7:8], small[9:10])
    g_b_inner[...] = jnp.concatenate([first, second], 1).reshape(2 * width)


def each_piece(pieces, steps):
    _, at_c, at_y, at_z = spot()
    depth = 4
    for j, k in enumerate(steps):
        for c in range(2):
            for y in range(2):
                place = (at_c + c) % 2, (at_y + y) % 2, (at_z + depth - k) % depth
                yield pieces[(j * 2 + c) * 2 + y], place


def final(steps, pieces, g_outer, g_inner, g_out, threes, biases, held, held_out, sem):
    depth = 4
    half, width = threes[0].shape
    rows, share = width // 8, width // depth
    part = rows // depth
    copies = []
    for n, (piece, (c, y, z)) in enumerate(each_piece(pieces, steps)):
        place = (c * 2 + y) * depth + z
        own = slice(n * 2 * rows, (n + 1) * 2 * rows)
        held[own] = full(piece[: 2 * rows])
        first = n * 2 * rows
        copies.append((held.at[first : first + rows], g_outer.at[at(place * rows, rows, 32)]))
        for k in range(2):
            cols = at((2 * k + c) * width + y * half, half, 128)
            copies.append(
                (
                    held.at[first + rows : first + 2 * rows, k * half : (k + 1) * half],
                    g_inner.at[at(z * rows, rows, 32), cols],
                )
            )
        for k in range(depth):
            first = 2 * rows + k * part
            held_out[n * part : (n + 1) * part, k * share : (k + 1) * share] = full(
                piece[first : first + part, 3 * share :]
            )
        copies.append((held_out.at[n * part : (n + 1) * part], g_out.at[at(place * part, part, 8)]))
    copies = start(copies, sem)
    for piece, (c, y, z) in each_piece(pieces, steps):
        there = at((c * 2 + y) * rows, rows, 32)
        for k in range(depth):

            @pl.when(z == k)
            def _():
                cols = slice(k * share, (k + 1) * share)
                for j, out in enumerate(threes):
                    out[there, cols] = full(piece[2 * rows : 3 * rows, j * share : (j + 1) * share])
                for j in (0, 2):
                    bias = full(piece[3 * rows :, j * share : (j + 1) * share])
                    biases[j : j + 1, cols] = bias[0:1]

    finish(copies)


def final_first(*refs):
    biases = refs[18]
    biases[...] = jnp.zeros_like(biases)
    final((0, 1, 3), refs[:12], *refs[12:15], refs[15:18], biases, *refs[19:])


def final_last(*refs):
    at_b, _, _, _ = spot()
    for k in range(3):
        refs[11 + 3 + k][...] = refs[7 + k][...]
    biases = refs[19]
    biases[...] = refs[10][...]
    final((2,), refs[:4], *refs[11:14], refs[14:17], biases, *refs[20:])
    for j, out in ((0, refs[17]), (2, refs[18])):
        half = out.shape[0]
        row = biases[j : j + 1]
        out[...] = jnp.where(at_b == 0, row[:, :half], row[:, half:]).reshape(half)


def per_device_heads(
    inputs,
    teacher,
    segments,
    w_query,
    b_query,
    w_key,
    w_value,
    b_value,
    w_out,
    b_out,
    gain_one,
    shift_one,
    w_inner,
    b_inner,
    w_outer,
    b_outer,
    gain_two,
    shift_two,
):
    count = lax.axis_size("ctx")
    depth = count // 4
    place = lax.axis_index("ctx")
    at_c, at_y = place % 2, place // 2 % 2
    seqs, rows, width = inputs.shape
    own = seqs * rows
    half = width // 2
    ff = w_inner.shape[1]
    share = width // depth
    keys = count // 2 * rows
    joint = ("batch", "ctx")
    pairs = [(y, c) for y in range(2) for c in range(2)]
    groups_z = [[z * 4 + r for z in range(depth)] for r in range(4)]
    groups_yz = [[z * 4 + y * 2 + c for z in range(depth) for y in range(2)] for c in range(2)]
    groups_xyc = [[b * count + z * 4 + y * 2 + c for b in range(2) for y, c in pairs] for z in range(depth)]

    def swap_x(values):
        return lax.ppermute(values, "batch", [(0, 1), (1, 0)])

    def swap_y(values):
        return lax.ppermute(values, "ctx", [(i, i ^ 2) for i in range(count)])

    def swap_xy(values):
        return lax.ppermute(values, joint, [(i, (i + count) % (2 * count) ^ 2) for i in range(2 * count)])

    def swap_c(values):
        return lax.ppermute(values, "ctx", [(i, i ^ 1) for i in range(count)])

    def shift_z(values, step):
        return lax.ppermute(values, "ctx", [(i, (i + 4 * step) % count) for i in range(count)])

    def trade(values, groups, axes="ctx"):
        return lax.all_to_all(values, axes, 0, 0, axis_index_groups=groups, tiled=True)

    tie = lax.optimization_barrier
    dma = pltpu.SemaphoreType.DMA

    blocks, first, p_inner, p_outer, p_out = kernel(
        prepare,
        [
            ((depth * seqs, rows, width), BF),
            ((3 * half // 4 + LINES, width), BF),
            ((half, width), BF),
            ((ff // 8, width), BF),
            ((half // 2, width), BF),
        ],
        [inputs, w_query, w_key, w_value, b_query, b_value, b_out, gain_one, shift_one]
        + [b_outer, gain_two, shift_two, b_inner, segments, w_inner, w_outer, w_out],
        hbm=(14, 15, 16),
        pin=range(14),
        scratch=[dma((4,))],
    )
    states = trade(blocks, groups_yz).reshape(keys, width)
    other = swap_x(first)
    x_inner = swap_x(p_inner)
    seg_seq = lax.dynamic_index_in_dim(segments, at_y, 0, keepdims=False).reshape(-1, 2, rows)
    seg_own = lax.dynamic_index_in_dim(seg_seq, at_c, 1, keepdims=False).reshape(-1)
    seg_peer = lax.dynamic_index_in_dim(seg_seq, 1 - at_c, 1, keepdims=False).reshape(-1)
    seg_key = jnp.concatenate([seg_own, seg_peer])[:, None]
    seg_query = seg_own[None, :]
    seg_tokens = lax.dynamic_slice_in_dim(segments, place * rows, rows, 1).reshape(own, 1)
    states, other, p_outer, p_out, seg_key, seg_query, seg_tokens = tie(
        (states, other, p_outer, p_out, seg_key, seg_query, seg_tokens)
    )
    x_outer = swap_x(p_outer)

    query, pair, vecs, inner_vec, w_three = kernel(
        project,
        [
            ((keys, share), BF),
            ((keys, 2 * share), BF),
            ((LINES, width), F32),
            ((8, ff), F32),
            ((width, 3 * share), BF),
        ],
        [states, first, other],
        scratch=[pltpu.VMEM((width, 3 * share), BF)],
    )
    peer = swap_c(pair)
    query, peer, x_inner = tie((query, peer, x_inner))
    y_inner = swap_y(x_inner)
    mixed, logs = kernel(
        attend,
        [((keys, share), BF), ((8, keys), F32)],
        [query, pair, peer, seg_query, seg_key],
        scratch=[pltpu.VMEM((2 * keys, share), BF), pltpu.VMEM((share, 2 * keys), BF)],
    )
    x_outer, mixed, p_out = tie((x_outer, mixed, p_out))
    mixed = trade(mixed.reshape(depth * seqs, rows, share), groups_yz)
    y_outer = swap_y(x_outer)
    x_out = swap_x(p_out)
    c_inner, c_outer = map(swap_c, (x_inner, x_outer))
    c_out, yc_inner = swap_c(x_out), swap_c(y_inner)
    mixed, y_outer, c_out, yc_inner, c_inner, c_outer = tie(
        (mixed, y_outer, c_out, yc_inner, c_inner, c_outer)
    )
    weights = [w_out, x_out, c_out]
    weights += [w_inner, x_inner, y_inner, c_inner, yc_inner]
    weights += [w_outer, x_outer, y_outer, c_outer, swap_c(y_outer)]
    held = [pltpu.VMEM((width, width), BF), pltpu.VMEM((width, ff), BF), pltpu.VMEM((ff, width), BF)]
    output, attended, unit, inverse, slope, two, g_hidden, sums = kernel(
        functools.partial(forward, float(own * 2 * count)),
        [
            (inputs.shape, F32),
            ((own, width), BF),
            ((own, width), F32),
            ((own, 128), F32),
            ((own, ff), F32),
            ((own, 2 * width), BF),
            ((own, width), F32),
            ((LINES, width), F32),
        ],
        [mixed, inputs, teacher, seg_tokens, vecs, inner_vec, *weights],
        hbm=range(6, 19),
        pin=(1, 2),
        scratch=[*held, pltpu.VMEM((own, ff), BF), dma((3, 9))],
    )
    fours = [two, swap_x(two), swap_y(two), swap_xy(two)]
    away_x, away_y, g_one, g_mixed = kernel(
        backward,
        [
            ((own + LINES, width + half), BF),
            ((own + LINES, width + half), BF),
            ((own, width), F32),
            ((depth * seqs, rows, 2 * share), BF),
        ],
        [two, slope, g_hidden, unit, inverse, vecs, attended, sums, *weights],
        hbm=range(8, 21),
        scratch=[
            *held,
            pltpu.VMEM((own, ff), BF),
            pltpu.VMEM((8, ff), F32),
            pltpu.VMEM((LINES, width), F32),
            dma((3, 9)),
        ],
    )
    away_x, away_y, *fours = tie((away_x, away_y, *fours))
    g_mixed = trade(g_mixed, groups_yz).reshape(keys, 2 * share)
    eights = [*fours, *map(swap_c, fours)]
    outer_rows = half // depth
    (feed,) = kernel(
        weight_feed,
        [((depth, 2 * outer_rows, width), BF)],
        [*eights, inner_vec, w_inner, x_inner, y_inner, w_outer, x_outer],
        hbm=range(9, 14),
        scratch=[
            pltpu.VMEM((width, width), BF),
            pltpu.VMEM((width, width), BF),
            pltpu.VMEM((8 * own, width), BF),
            pltpu.VMEM((8 * own, width), BF),
            pltpu.VMEM((8 * own, width), BF),
            pltpu.VMEM((8 * own, width), BF),
            dma((8,)),
        ],
    )
    feed, g_mixed, away_x, away_y = tie((feed, g_mixed, away_x, away_y))
    feed = trade(feed, groups_z)
    fours = [away_y, swap_x(away_x), swap_y(away_y), swap_xy(away_x)]

    g_query, g_mine, g_theirs = kernel(
        attend_back,
        [((keys, share), BF), ((keys, 2 * share), F32), ((keys, 2 * share), F32)],
        [query, pair, peer, seg_query, seg_key, logs, g_mixed],
        pin=range(6),
        scratch=[
            pltpu.VMEM((2 * keys, share), BF),
            pltpu.VMEM((share, 2 * keys), BF),
            pltpu.VMEM((2 * keys, share), BF),
            pltpu.VMEM((2 * keys, 2 * share), F32),
        ],
    )
    g_theirs, *fours = tie((g_theirs, *fours))
    part = half // 4 // depth
    outs = kernel(
        weight_out,
        [((part + LINES, width), BF)] * depth,
        [*fours, *map(swap_c, fours)],
        scratch=[
            pltpu.VMEM((8 * own, half // 4), BF),
            pltpu.VMEM((8 * own, width), BF),
            pltpu.VMEM((half // 4, width), F32),
        ],
    )
    back, three_keep, three_send = kernel(
        weight_three,
        [((keys, width), BF)] + [((half + LINES, 3 * share), BF)] * 2,
        [g_query, g_mine, swap_c(g_theirs), states, w_three],
        pin=(3, 4),
        scratch=[pltpu.VMEM((keys, 3 * share), BF)],
    )
    three_keep, three_send = kernel(
        functools.partial(halve_out, 0),
        [((half // 2 + LINES, 3 * share), BF)] * 2,
        [three_keep, swap_c(three_send)],
    )
    outs = [outs[0]] + [shift_z(outs[k], k) for k in range(1, depth)]
    three_x, outs[1], outs[2] = tie((swap_x(three_send), outs[1], outs[2]))
    three_keep, three_send = kernel(
        functools.partial(halve_out, 2),
        [((half // 4 + LINES, 3 * share), BF)] * 2,
        [three_keep, three_x],
    )
    three_came = swap_y(three_send)
    packed, loss, g_b_inner, *vectors = kernel(
        pack,
        [((3 * outer_rows + 8, width), BF), ((1, 128), F32), ((ff // 2,), F32)] + [((half,), F32)] * 6,
        [feed, *outs, three_keep, three_came, vecs],
    )
    packed, back = tie((packed, back))
    up, down, by_y = tie((shift_z(packed, 1), shift_z(packed, -1), swap_y(packed)))
    back = trade(back.reshape(depth * seqs, rows, width), groups_yz)
    across, up_y, down_y = tie((shift_z(up, 1), swap_y(up), swap_y(down)))
    pieces = []
    for pair in ((packed, by_y), (up, up_y), (down, down_y)):
        pieces += [*pair, *map(swap_c, pair)]
    large = [((ff // 2, width), F32), ((half, ff), F32), ((half, width), F32)]
    threes = [((half, width), F32)] * 3
    room = 2 * outer_rows

    def buffers(count):
        return [
            pltpu.VMEM((count * room, width), F32),
            pltpu.VMEM((count * part, width), F32),
            dma((4 * count,)),
        ]

    outs = kernel(
        final_first,
        [*large, *threes, ((8, width), F32)],
        pieces,
        outs_hbm=range(3),
        scratch=buffers(12),
    )
    across_y, *outs = tie((swap_y(across), *outs))
    pieces = [across, across_y, swap_c(across), swap_c(across_y)]
    (g_inputs,) = kernel(grad_states, [(inputs.shape, F32)], [back, g_one])
    g_w_outer, g_w_inner, g_w_out, g_w_query, g_w_key, g_w_value, g_b_query, g_b_value = kernel(
        final_last,
        [*large, *threes] + [((half,), F32)] * 2,
        [*pieces, *outs],
        hbm=range(4, 7),
        outs_hbm=range(3),
        aliases={4: 0, 5: 1, 6: 2},
        scratch=[pltpu.VMEM((8, width), F32), *buffers(4)],
    )
    g_b_out, g_gain_one, g_shift_one, g_b_outer, g_gain_two, g_shift_two = vectors
    return (
        output,
        loss[0, 0],
        g_inputs,
        g_w_query,
        g_b_query,
        g_w_key,
        g_w_value,
        g_b_value,
        g_w_out,
        g_b_out,
        g_gain_one,
        g_shift_one,
        g_w_inner,
        g_b_inner,
        g_w_outer,
        g_b_outer,
        g_gain_two,
        g_shift_two,
    )


def per_device(inputs, *others):
    sizes = (lax.axis_size("batch"), lax.axis_size("ctx"), inputs.shape[0])
    if sizes == (2, 16, 2):
        return per_device_heads(inputs, *others)
    return per_device_any(inputs, *others)


def solution(mesh):
    placed = (
        P("batch", "ctx", None),
        P("batch", "ctx", None),
        P("batch", None),
        P("batch", None),
        P("batch"),
        P("batch", None),
        P("batch", None),
        P("batch"),
        P("batch", None),
        P("batch"),
        P("batch"),
        P("batch"),
        P("batch", None),
        P("batch"),
        P("batch", None),
        P("batch"),
        P("batch"),
        P("batch"),
    )
    return jax.shard_map(
        per_device,
        mesh=mesh,
        in_specs=placed,
        out_specs=(
            P("batch", "ctx", None),
            P(),
            P("batch", "ctx", None),
            P("batch", None),
            P("batch"),
            P("batch", None),
            P("batch", None),
            P("batch"),
            P("batch", None),
            P("batch"),
            P("batch"),
            P("batch"),
            P("batch", None),
            P("batch"),
            P("batch", None),
            P("batch"),
            P("batch"),
            P("batch"),
        ),
        check_vma=False,
    )
```

```python
import functools
import math

import jax
import jax.numpy as jnp
from jax import lax
from jax.experimental import pallas as pl
from jax.experimental.pallas import tpu as pltpu
from jax.sharding import PartitionSpec as P

H = 12
HD = 64


NEGATIVE = -1e30
EPSILON = 1e-12


def norm_rows(hidden, gain, shift):
    center = hidden - jnp.mean(hidden, -1, keepdims=True)
    spread = jnp.mean(center * center, -1, keepdims=True)
    return center * lax.rsqrt(spread + EPSILON) * gain + shift


def gelu_exact(values):
    return jax.nn.gelu(values, approximate=False)


def linear(rows_in, weight):
    return jnp.dot(rows_in, weight, preferred_element_type=jnp.float32)


def contract_rows(left, right):
    return lax.dot_general(
        left, right, (((0,), (0,)), ((), ())), preferred_element_type=jnp.float32
    )


def times_transpose(rows_in, weight):
    return lax.dot_general(
        rows_in, weight, (((1,), (1,)), ((), ())), preferred_element_type=jnp.float32
    )


def score_rows(query_one, keys_all, seg_mine, seg_all):
    heads_query = query_one.reshape(query_one.shape[0], H, HD)
    heads_key = keys_all.reshape(keys_all.shape[0], H, HD)
    raw = jnp.einsum(
        "chd,khd->hck", heads_query, heads_key, preferred_element_type=jnp.float32
    ) * HD ** (-0.5)
    allowed = seg_mine[None, :, None] == seg_all[None, None, :]
    return jnp.where(allowed, raw, NEGATIVE)


def per_device_any(
    inputs,
    teacher,
    segments,
    w_query,
    b_query,
    w_key,
    w_value,
    b_value,
    w_out,
    b_out,
    gain_one,
    shift_one,
    w_inner,
    b_inner,
    w_outer,
    b_outer,
    gain_two,
    shift_two,
):
    (
        w_query,
        b_query,
        w_key,
        w_value,
        b_value,
        w_out,
        b_out,
        gain_one,
        shift_one,
        w_inner,
        b_inner,
        w_outer,
        b_outer,
        gain_two,
        shift_two,
    ) = (
        lax.all_gather(w_query, "batch", axis=0, tiled=True),
        lax.all_gather(b_query, "batch", axis=0, tiled=True),
        lax.all_gather(w_key, "batch", axis=0, tiled=True),
        lax.all_gather(w_value, "batch", axis=0, tiled=True),
        lax.all_gather(b_value, "batch", axis=0, tiled=True),
        lax.all_gather(w_out, "batch", axis=0, tiled=True),
        lax.all_gather(b_out, "batch", axis=0, tiled=True),
        lax.all_gather(gain_one, "batch", axis=0, tiled=True),
        lax.all_gather(shift_one, "batch", axis=0, tiled=True),
        lax.all_gather(w_inner, "batch", axis=0, tiled=True),
        lax.all_gather(b_inner, "batch", axis=0, tiled=True),
        lax.all_gather(w_outer, "batch", axis=0, tiled=True),
        lax.all_gather(b_outer, "batch", axis=0, tiled=True),
        lax.all_gather(gain_two, "batch", axis=0, tiled=True),
        lax.all_gather(shift_two, "batch", axis=0, tiled=True),
    )
    scale = HD ** (-0.5)
    seqs_here, ctx_rows, width = inputs.shape
    rows_here = seqs_here * ctx_rows
    tokens_all = rows_here * lax.axis_size("batch") * lax.axis_size("ctx")
    seg_own = lax.dynamic_slice_in_dim(segments, lax.axis_index("ctx") * ctx_rows, ctx_rows, 1)
    inputs_flat = inputs.reshape(rows_here, width)
    inputs_low = inputs_flat.astype(jnp.bfloat16)
    query = (linear(inputs_low, w_query) + b_query.astype(jnp.float32)).astype(jnp.bfloat16)
    key = linear(inputs_low, w_key).astype(jnp.bfloat16)
    value = (linear(inputs_low, w_value) + b_value.astype(jnp.float32)).astype(jnp.bfloat16)
    query_seq = query.reshape(seqs_here, ctx_rows, width)
    key_seq = key.reshape(seqs_here, ctx_rows, width)
    value_seq = value.reshape(seqs_here, ctx_rows, width)

    def attend_forward(items):
        query_one, key_one, value_one, seg_all, seg_mine = items
        keys_all, values_all = (
            lax.all_gather(key_one, "ctx", axis=0, tiled=True),
            lax.all_gather(value_one, "ctx", axis=0, tiled=True),
        )
        scores = score_rows(query_one, keys_all, seg_mine, seg_all)
        highest = jnp.max(scores, -1, keepdims=True)
        expo = jnp.exp(scores - highest)
        totals = jnp.sum(expo, -1, keepdims=True)
        probs = (expo / totals).astype(jnp.bfloat16)
        mixed = jnp.einsum(
            "hck,khd->chd",
            probs,
            values_all.reshape(keys_all.shape[0], H, HD),
            preferred_element_type=jnp.float32,
        )
        return (
            mixed.reshape(ctx_rows, width).astype(jnp.bfloat16),
            (highest + jnp.log(totals))[:, :, 0],
        )

    attended, log_totals = lax.map(
        attend_forward, (query_seq, key_seq, value_seq, segments, seg_own)
    )
    attended_flat = attended.reshape(rows_here, width)
    gain_one_full = gain_one.astype(jnp.float32)
    shift_one_full = shift_one.astype(jnp.float32)
    gain_two_full = gain_two.astype(jnp.float32)
    shift_two_full = shift_two.astype(jnp.float32)
    hidden_one = inputs_flat + linear(attended_flat, w_out) + b_out.astype(jnp.float32)
    normed_one, back_one = jax.vjp(norm_rows, hidden_one, gain_one_full, shift_one_full)
    normed_low = normed_one.astype(jnp.bfloat16)
    inner_pre = linear(normed_low, w_inner) + b_inner.astype(jnp.float32)
    active_full, gelu_back = jax.vjp(gelu_exact, inner_pre)
    active_low = active_full.astype(jnp.bfloat16)
    hidden_two = normed_one + linear(active_low, w_outer) + b_outer.astype(jnp.float32)
    output, back_two = jax.vjp(norm_rows, hidden_two, gain_two_full, shift_two_full)
    valid = (seg_own.reshape(rows_here) != 0).astype(jnp.float32)[:, None]
    error = output - teacher.reshape(rows_here, width)
    loss_total, valid_count = lax.psum(
        (jnp.sum(valid * error * error), jnp.sum(valid)), ("batch", "ctx")
    )
    loss = loss_total / (2.0 * valid_count)
    grad_output = tokens_all / valid_count * valid * error
    grad_hidden_two, grad_gain_two, grad_shift_two = back_two(grad_output)
    grad_branch_two = grad_hidden_two.astype(jnp.bfloat16)
    grad_b_outer = jnp.sum(grad_branch_two.astype(jnp.float32), 0)
    grad_w_outer = contract_rows(active_low, grad_branch_two)
    grad_active = times_transpose(grad_branch_two, w_outer)
    grad_inner = gelu_back(grad_active)[0].astype(jnp.bfloat16)
    grad_b_inner = jnp.sum(grad_inner.astype(jnp.float32), 0)
    grad_w_inner = contract_rows(normed_low, grad_inner)
    grad_normed = grad_hidden_two + times_transpose(grad_inner, w_inner)
    grad_hidden_one, grad_gain_one, grad_shift_one = back_one(grad_normed)
    grad_branch_one = grad_hidden_one.astype(jnp.bfloat16)
    grad_b_out = jnp.sum(grad_branch_one.astype(jnp.float32), 0)
    grad_w_out = contract_rows(attended_flat, grad_branch_one)
    grad_attended = (
        times_transpose(grad_branch_one, w_out)
        .astype(jnp.bfloat16)
        .reshape(seqs_here, ctx_rows, width)
    )

    def attend_backward(items):
        query_one, key_one, value_one, seg_all, seg_mine, log_one, grad_one = items
        keys_all, values_all = (
            lax.all_gather(key_one, "ctx", axis=0, tiled=True),
            lax.all_gather(value_one, "ctx", axis=0, tiled=True),
        )
        key_count = keys_all.shape[0]
        scores = score_rows(query_one, keys_all, seg_mine, seg_all)
        probs = jnp.exp(scores - log_one[:, :, None])
        grad_heads = grad_one.reshape(ctx_rows, H, HD)
        grad_probs = jnp.einsum(
            "chd,khd->hck",
            grad_heads,
            values_all.reshape(key_count, H, HD),
            preferred_element_type=jnp.float32,
        )
        centre = jnp.sum(probs * grad_probs, -1)
        grad_scores = (probs * (grad_probs - centre[:, :, None])).astype(jnp.bfloat16)
        grad_query = (
            jnp.einsum(
                "hck,khd->chd",
                grad_scores,
                keys_all.reshape(key_count, H, HD),
                preferred_element_type=jnp.float32,
            )
            * scale
        )
        grad_query = grad_query.reshape(ctx_rows, width).astype(jnp.bfloat16)
        probs_low = probs.astype(jnp.bfloat16)
        query_heads = query_one.reshape(ctx_rows, H, HD)
        count = ctx_rows * lax.axis_size("ctx")
        grad_key = (
            jnp.einsum("hck,chd->khd", grad_scores, query_heads, preferred_element_type=jnp.float32)
            * scale
        )
        grad_value = jnp.einsum(
            "hck,chd->khd", probs_low, grad_heads, preferred_element_type=jnp.float32
        )
        both = lax.psum_scatter(
            jnp.concatenate([grad_key.reshape(count, width), grad_value.reshape(count, width)], 1),
            "ctx",
            scatter_dimension=0,
            tiled=True,
        )
        return (
            grad_query,
            both[:, :width].astype(jnp.bfloat16),
            both[:, width:].astype(jnp.bfloat16),
        )

    grad_query_seq, grad_key_seq, grad_value_seq = lax.map(
        attend_backward,
        (query_seq, key_seq, value_seq, segments, seg_own, log_totals, grad_attended),
    )
    grad_query_flat = grad_query_seq.reshape(rows_here, width)
    grad_key_flat = grad_key_seq.reshape(rows_here, width)
    grad_value_flat = grad_value_seq.reshape(rows_here, width)
    grad_w_query = contract_rows(inputs_low, grad_query_flat)
    grad_b_query = jnp.sum(grad_query_flat.astype(jnp.float32), 0)
    grad_w_key = contract_rows(inputs_low, grad_key_flat)
    grad_w_value = contract_rows(inputs_low, grad_value_flat)
    grad_b_value = jnp.sum(grad_value_flat.astype(jnp.float32), 0)
    grad_inputs = (
        grad_hidden_one
        + times_transpose(grad_query_flat, w_query)
        + times_transpose(grad_key_flat, w_key)
        + times_transpose(grad_value_flat, w_value)
    )
    (
        grad_w_query,
        grad_b_query,
        grad_w_key,
        grad_w_value,
        grad_b_value,
        grad_w_out,
        grad_b_out,
        grad_gain_one,
        grad_shift_one,
        grad_w_inner,
        grad_b_inner,
        grad_w_outer,
        grad_b_outer,
        grad_gain_two,
        grad_shift_two,
    ) = (
        lax.psum_scatter(
            grad_w_query.astype(jnp.bfloat16), "batch", scatter_dimension=0, tiled=True
        ).astype(jnp.float32),
        lax.psum_scatter(
            grad_b_query.astype(jnp.bfloat16), "batch", scatter_dimension=0, tiled=True
        ).astype(jnp.float32),
        lax.psum_scatter(
            grad_w_key.astype(jnp.bfloat16), "batch", scatter_dimension=0, tiled=True
        ).astype(jnp.float32),
        lax.psum_scatter(
            grad_w_value.astype(jnp.bfloat16), "batch", scatter_dimension=0, tiled=True
        ).astype(jnp.float32),
        lax.psum_scatter(
            grad_b_value.astype(jnp.bfloat16), "batch", scatter_dimension=0, tiled=True
        ).astype(jnp.float32),
        lax.psum_scatter(
            grad_w_out.astype(jnp.bfloat16), "batch", scatter_dimension=0, tiled=True
        ).astype(jnp.float32),
        lax.psum_scatter(
            grad_b_out.astype(jnp.bfloat16), "batch", scatter_dimension=0, tiled=True
        ).astype(jnp.float32),
        lax.psum_scatter(
            grad_gain_one.astype(jnp.bfloat16), "batch", scatter_dimension=0, tiled=True
        ).astype(jnp.float32),
        lax.psum_scatter(
            grad_shift_one.astype(jnp.bfloat16), "batch", scatter_dimension=0, tiled=True
        ).astype(jnp.float32),
        lax.psum_scatter(
            grad_w_inner.astype(jnp.bfloat16), "batch", scatter_dimension=0, tiled=True
        ).astype(jnp.float32),
        lax.psum_scatter(
            grad_b_inner.astype(jnp.bfloat16), "batch", scatter_dimension=0, tiled=True
        ).astype(jnp.float32),
        lax.psum_scatter(
            grad_w_outer.astype(jnp.bfloat16), "batch", scatter_dimension=0, tiled=True
        ).astype(jnp.float32),
        lax.psum_scatter(
            grad_b_outer.astype(jnp.bfloat16), "batch", scatter_dimension=0, tiled=True
        ).astype(jnp.float32),
        lax.psum_scatter(
            grad_gain_two.astype(jnp.bfloat16), "batch", scatter_dimension=0, tiled=True
        ).astype(jnp.float32),
        lax.psum_scatter(
            grad_shift_two.astype(jnp.bfloat16), "batch", scatter_dimension=0, tiled=True
        ).astype(jnp.float32),
    )
    (
        grad_w_query,
        grad_b_query,
        grad_w_key,
        grad_w_value,
        grad_b_value,
        grad_w_out,
        grad_b_out,
        grad_gain_one,
        grad_shift_one,
        grad_w_inner,
        grad_b_inner,
        grad_w_outer,
        grad_b_outer,
        grad_gain_two,
        grad_shift_two,
    ) = lax.psum(
        (
            grad_w_query,
            grad_b_query,
            grad_w_key,
            grad_w_value,
            grad_b_value,
            grad_w_out,
            grad_b_out,
            grad_gain_one,
            grad_shift_one,
            grad_w_inner,
            grad_b_inner,
            grad_w_outer,
            grad_b_outer,
            grad_gain_two,
            grad_shift_two,
        ),
        "ctx",
    )
    return (
        output.reshape(inputs.shape),
        loss,
        grad_inputs.reshape(inputs.shape),
        grad_w_query,
        grad_b_query,
        grad_w_key,
        grad_w_value,
        grad_b_value,
        grad_w_out,
        grad_b_out,
        grad_gain_one,
        grad_shift_one,
        grad_w_inner,
        grad_b_inner,
        grad_w_outer,
        grad_b_outer,
        grad_gain_two,
        grad_shift_two,
    )


BF, F32 = jnp.bfloat16, jnp.float32
LINES = 16
ROOM = 6 << 20


def low(values):
    return values.astype(BF)


def full(values):
    return values.astype(F32)


def dot(left, right, a=1, b=0):
    return lax.dot_general(left, right, (((a,), (b,)), ((), ())), preferred_element_type=F32)


def spot():
    place = lax.axis_index("ctx")
    return lax.axis_index("batch"), place % 2, place // 2 % 2, place // 4


def at(start, size, step):
    return pl.ds(pl.multiple_of(start, step), size)


def kernel(body, outs, args, hbm=(), scratch=(), pin=(), outs_hbm=(), aliases=None):
    name = getattr(body, "func", body).__name__
    where = [pl.BlockSpec(memory_space=pl.ANY if k in hbm else pltpu.VMEM) for k in range(len(args))]
    shapes = [jax.ShapeDtypeStruct(shape, kind) for shape, kind in outs]
    held = [a for k, a in enumerate(args) if k not in hbm]
    held += [a for k, a in enumerate(shapes) if k not in outs_hbm]
    held += [a for a in scratch if a.memory_space == pltpu.VMEM]
    room = sum(math.prod(a.shape) * jnp.dtype(a.dtype).itemsize for a in held) + ROOM
    args = [
        pltpu.with_memory_space_constraint(a, pltpu.HBM) if k in hbm or k in pin else a
        for k, a in enumerate(args)
    ]
    return pl.pallas_call(
        body,
        out_shape=shapes,
        in_specs=where,
        out_specs=[
            pl.BlockSpec(memory_space=pl.ANY if k in outs_hbm else pltpu.VMEM)
            for k in range(len(shapes))
        ],
        input_output_aliases=aliases or {},
        scratch_shapes=list(scratch),
        compiler_params=pltpu.CompilerParams(vmem_limit_bytes=room),
        name=name,
    )(*args)


def norm_forward(hidden, gain, shift):
    center = hidden - jnp.mean(hidden, -1, keepdims=True)
    inverse = lax.rsqrt(jnp.mean(center * center, -1, keepdims=True) + EPSILON)
    unit = center * inverse
    return unit * gain + shift, unit, inverse


def norm_backward(grad, unit, inverse, gain):
    scaled = grad * gain
    along = jnp.mean(scaled * unit, -1, keepdims=True)
    return inverse * (scaled - jnp.mean(scaled, -1, keepdims=True) - unit * along)


def total(values):
    return jnp.sum(values, 0, keepdims=True)


def prepare(*refs):
    inputs, w_three, vectors, b_inner, segments = refs[0], refs[1:4], refs[4:12], refs[12], refs[13]
    w_inner, w_outer, w_out, blocks, out, p_inner, p_outer, p_out, sem = refs[14:]
    half, width = w_three[0].shape
    _, at_c, at_y, at_z = spot()
    part, wide = half // 2, w_inner.shape[1] // 4
    rows_out, rows_outer = p_out.shape[0], p_outer.shape[0]
    copies = [
        (
            w_inner.at[at(at_y * part, part, 64), at((k * 2 + at_c) * wide, wide, 128)],
            p_inner.at[k * part : (k + 1) * part],
        )
        for k in range(2)
    ]
    copies.append((w_outer.at[at((at_c * 2 + at_y) * rows_outer, rows_outer, 128)], p_outer))
    copies.append((w_out.at[at(at_c * rows_out, rows_out, 64)], p_out))
    copies = start(copies, sem)
    seqs = inputs.shape[0]
    for s in range(seqs):
        piece = low(inputs[s])
        for z in range(blocks.shape[0] // seqs):
            blocks[z * seqs + s] = piece
    share, rows = width // 4, half // 4
    for z in range(4):

        @pl.when(at_z == z)
        def _():
            for j in range(3):
                for k in range(4):
                    piece = w_three[j][k * rows : (k + 1) * rows, z * share : (z + 1) * share]
                    out[j * rows : (j + 1) * rows, k * share : (k + 1) * share] = piece

    first = 3 * rows
    out[first : first + LINES] = jnp.zeros((LINES, width), BF)
    for r in range(8):
        out[first + r : first + r + 1, :half] = vectors[r][...].reshape(1, half)
    inner = b_inner[...].reshape(1, -1)
    for r in range(4):
        out[first + 8 + r : first + 9 + r, :half] = inner[:, half * r : half * (r + 1)]
    valid = jnp.sum(jnp.where(segments[...] != 0, 1, 0))
    lane = lax.broadcasted_iota(jnp.int32, (1, half), 1)
    parts = jnp.where(lane < 128, valid // 256, valid % 256)
    out[first + 12 : first + 13, :half] = low(full(parts))
    finish(copies)


def start(copies, sem):
    made = [pltpu.make_async_copy(*copy, sem.at[k]) for k, copy in enumerate(copies)]
    for copy in made:
        copy.start()
    return made


def finish(copies):
    for copy in copies:
        copy.wait()


def both_halves(at_b, mine, other):
    return jnp.where(at_b == 0, mine, other), jnp.where(at_b == 0, other, mine)


def project(states, mine, other, query, pair, vecs, inner_vec, held, w_back):
    at_b, _, _, at_z = spot()
    width, share = states.shape[1], query.shape[1]
    half, rows = width // 2, width // 8
    for j in range(3):
        for k in range(4):
            first = slice(j * rows, (j + 1) * rows)
            cols = slice(k * share, (k + 1) * share)
            pieces = both_halves(at_b, mine[first, cols], other[first, cols])
            for h, piece in enumerate(pieces):
                start_row = h * half + k * rows
                held[start_row : start_row + rows, j * share : (j + 1) * share] = piece
    w_back[...] = held[...]
    made = dot(states[...], held[...])
    lines = slice(3 * rows, 3 * rows + LINES)
    top, bottom = both_halves(at_b, full(mine[lines]), full(other[lines]))

    def bias(r):
        row = jnp.where(at_z < 2, top[r : r + 1], bottom[r : r + 1])
        return jnp.where(at_z % 2 == 0, row[:, :share], row[:, share : 2 * share])

    query[...] = low(full(low(made[:, :share] + bias(0))) * HD ** (-0.5))
    pair[:, :share] = low(made[:, share : 2 * share])
    pair[:, share:] = low(made[:, 2 * share :] + bias(1))
    vecs[...] = jnp.zeros_like(vecs)
    for r in range(2, 8):
        vecs[r - 2 : r - 1, :half] = top[r : r + 1, :half]
        vecs[r - 2 : r - 1, half:] = bottom[r : r + 1, :half]
    counts = top[12:13] + bottom[12:13]
    counts = counts[:, :128] * 256.0 + counts[:, 256:384]
    vecs[8:9, :128] = counts
    inner_vec[...] = jnp.zeros_like(inner_vec)
    for b, rows in enumerate((top, bottom)):
        for r in range(4):
            cols = slice((4 * b + r) * half, (4 * b + r + 1) * half)
            inner_vec[0:1, cols] = rows[8 + r : 9 + r, :half]


STEP = 256


def attend(query, mine, peer, seg_query, seg_key, mixed, logs, keys, values):
    count, share = query.shape
    keys[:count] = mine[:, :share]
    keys[count:] = peer[:, :share]
    values[:, :count] = mine[:, share:].T
    values[:, count:] = peer[:, share:].T
    logs[...] = jnp.zeros_like(logs)

    def block(j, carry):
        rows = at(j * STEP, STEP, STEP)
        allowed = seg_key[...] == seg_query[:, rows]
        for h in range(share // HD):
            cols = slice(h * HD, (h + 1) * HD)
            scores = dot(keys[:, cols], query[rows, cols], 1, 1)
            scores = jnp.where(allowed, scores, NEGATIVE)
            highest = jnp.max(scores, 0, keepdims=True)
            expo = jnp.exp(scores - highest)
            totals = jnp.sum(expo, 0, keepdims=True)
            probs = low(expo * (1.0 / totals))
            mixed[rows, cols] = low(dot(values[cols], probs).T)
            logs[h : h + 1, rows] = highest + jnp.log(totals)
        return carry

    lax.fori_loop(0, count // STEP, block, 0)


def attend_back(
    query, mine, peer, seg_query, seg_key, logs, grad, g_query, g_mine, g_peer, keys, flipped, values, made
):
    count, share = query.shape
    keys[:count] = mine[:, :share]
    keys[count:] = peer[:, :share]
    values[:count] = mine[:, share:]
    values[count:] = peer[:, share:]
    flipped[:, :count] = mine[:, :share].T
    flipped[:, count:] = peer[:, :share].T
    made[...] = jnp.zeros_like(made)

    def block(j, carry):
        rows = at(j * STEP, STEP, STEP)
        allowed = seg_key[...] == seg_query[:, rows]
        for h in range(share // HD):
            cols = slice(h * HD, (h + 1) * HD)
            cols_value = slice(share + h * HD, share + (h + 1) * HD)
            scores = dot(keys[:, cols], query[rows, cols], 1, 1)
            scores = jnp.where(allowed, scores, NEGATIVE)
            probs = jnp.exp(scores - logs[h : h + 1, rows])
            g_probs = dot(values[:, cols], grad[rows, cols], 1, 1)
            centre = jnp.sum(probs * g_probs, 0, keepdims=True)
            g_scores = low(probs * (g_probs - centre))
            g_query[rows, cols] = low((dot(flipped[cols], g_scores) * HD ** (-0.5)).T)
            made[:, cols] += dot(g_scores, query[rows, cols])
            made[:, cols_value] += dot(low(probs), grad[rows, cols])
        return carry

    lax.fori_loop(0, count // STEP, block, 0)
    g_mine[...] = made[:count]
    g_peer[...] = made[count:]


def fetch_out(own, pieces, held, sem):
    at_b, at_c, _, _ = spot()
    half, part = own.shape[0], pieces[0].shape[0]
    copies = [(own, held.at[at(at_b * half, half, 128)])]
    for k, piece in enumerate(pieces):
        first = (1 - at_b) * half + (at_c + k) % 2 * part
        copies.append((piece, held.at[at(first, part, 64)]))
    return start(copies, sem)


def fetch_inner(own, pieces, held, sem):
    at_b, at_c, at_y, _ = spot()
    half, part, wide = own.shape[0], pieces[0].shape[0] // 2, pieces[0].shape[1]
    copies = [(own, held.at[at(at_b * half, half, 128)])]
    for c in range(2):
        for y in range(2):
            rows = at((1 - at_b) * half + (at_y + y) % 2 * part, part, 64)
            for k in range(2):
                cols = at((2 * k + (at_c + c) % 2) * wide, wide, 128)
                piece = pieces[2 * c + y].at[k * part : (k + 1) * part]
                copies.append((piece, held.at[rows, cols]))
    return start(copies, sem)


def fetch_outer(own, pieces, held, sem):
    at_b, at_c, at_y, _ = spot()
    half, part = own.shape[0], pieces[0].shape[0]
    copies = [(own, held.at[at(at_b * half, half, 128)])]
    for c in range(2):
        for y in range(2):
            first = (1 - at_b) * half + ((at_c + c) % 2 * 2 + (at_y + y) % 2) * part
            copies.append((pieces[2 * c + y], held.at[at(first, part, 128)]))
    return start(copies, sem)


BLOCK = 256


def forward(tokens_all, *refs):
    mixed, inputs, teacher, seg, vecs, inner_vec = refs[:6]
    weights, (output, attended, unit, inverse, slope, two, g_hidden, sums) = refs[6:19], refs[19:27]
    held_out, held_inner, held_outer, active, sem = refs[27:]
    copies_out = fetch_out(weights[0], weights[1:3], held_out, sem.at[0])
    copies_inner = fetch_inner(weights[3], weights[4:8], held_inner, sem.at[1])
    copies_outer = fetch_outer(weights[8], weights[9:13], held_outer, sem.at[2])
    rows, share = mixed.shape[1:]
    seqs = inputs.shape[0]
    own, width = attended.shape
    ff = slope.shape[1]
    for s in range(seqs):
        for z in range(mixed.shape[0] // seqs):
            attended[s * rows : (s + 1) * rows, z * share : (z + 1) * share] = mixed[z * seqs + s]
    finish(copies_out)
    hidden = inputs[...].reshape(own, width) + dot(attended[...], held_out[...]) + vecs[0:1]
    normed, made_unit, made_inverse = norm_forward(hidden, vecs[1:2], vecs[2:3])
    unit[...] = made_unit
    inverse[...] = jnp.broadcast_to(made_inverse, inverse.shape)
    two[:, :width] = low(normed)
    finish(copies_inner)

    def block(j, carry):
        cols = at(j * BLOCK, BLOCK, BLOCK)
        before = dot(two[:, :width], held_inner[:, cols]) + inner_vec[0:1, cols]
        below = 0.5 * (1.0 + lax.erf(before * 0.7071067811865476))
        active[:, cols] = low(before * below)
        slope[:, cols] = below + before * jnp.exp(before * before * -0.5) * 0.3989422804014327
        return carry

    lax.fori_loop(0, ff // BLOCK, block, 0)
    finish(copies_outer)
    hidden = normed + dot(active[...], held_outer[...]) + vecs[3:4]
    made, unit_two, inverse_two = norm_forward(hidden, vecs[4:5], vecs[5:6])
    output[...] = made.reshape(output.shape)
    valid = jnp.where(seg[...] != 0, 1.0, 0.0)
    error = (made - teacher[...].reshape(own, width)) * valid
    grad = error * (tokens_all / vecs[8:9, 0:1])
    made = norm_backward(grad, unit_two, inverse_two, vecs[4:5])
    g_hidden[...] = made
    g_low = low(made)
    two[:, width:] = g_low
    sums[...] = jnp.zeros_like(sums)
    sums[3:4] = total(full(g_low))
    sums[4:5] = total(grad * unit_two)
    sums[5:6] = total(grad)
    loss = jnp.broadcast_to(jnp.sum(total(error * error), 1, keepdims=True), (1, width))
    sums[10:11] = full(low(loss))
    sums[11:12] = loss - full(low(loss))


def backward(*refs):
    two, slope, g_hidden, unit, inverse, vecs, attended, sums = refs[:8]
    weights, (away_x, away_y, g_one, g_mixed) = refs[8:21], refs[21:25]
    held_out, held_inner, held_outer, g_inner, inner_sums, small, sem = refs[25:]
    at_b, _, _, _ = spot()
    copies_outer = fetch_outer(weights[8], weights[9:13], held_outer, sem.at[2])
    copies_inner = fetch_inner(weights[3], weights[4:8], held_inner, sem.at[1])
    copies_out = fetch_out(weights[0], weights[1:3], held_out, sem.at[0])
    (own, width), ff = unit.shape, slope.shape[1]
    half = width // 2
    away_y[:own, width:] = jnp.where(at_b == 0, attended[:, :half], attended[:, half:])
    away_x[:own, width:] = jnp.where(at_b == 0, attended[:, half:], attended[:, :half])
    finish(copies_outer)

    def block(j, carry):
        cols = at(j * BLOCK, BLOCK, BLOCK)
        grad = low(dot(two[:, width:], held_outer[cols, :], 1, 1) * slope[:, cols])
        g_inner[:, cols] = grad
        inner_sums[0:1, cols] = total(full(grad))
        return carry

    lax.fori_loop(0, ff // BLOCK, block, 0)
    finish(copies_inner)
    g_normed = g_hidden[...] + dot(g_inner[...], held_inner[...], 1, 1)
    made = norm_backward(g_normed, unit[...], inverse[:, 0:1], vecs[1:2])
    g_one[...] = made
    g_low = low(made)
    finish(copies_out)
    g_attended = low(dot(g_low, held_out[...], 1, 1))
    rows, share = g_mixed.shape[1], g_mixed.shape[2] // 2
    seqs = own // rows
    g_mixed[:, :, share:] = jnp.zeros((g_mixed.shape[0], rows, share), BF)
    for s in range(seqs):
        for z in range(g_mixed.shape[0] // seqs):
            g_mixed[z * seqs + s, :, :share] = g_attended[s * rows : (s + 1) * rows, z * share : (z + 1) * share]
    small[...] = sums[...]
    small[0:1] = total(full(g_low))
    small[1:2] = total(g_normed * unit[...])
    small[2:3] = total(g_normed)
    for k in range(4):
        small[6 + k : 7 + k] = inner_sums[0:1, k * width : (k + 1) * width]
    for out in (away_x, away_y):
        out[:own, :width] = g_low
        out[own:, :width] = low(small[...])
        out[own:, width:] = jnp.zeros((LINES, half), BF)


def resplit(made):
    lines = made.shape[0]
    loss = made[10:11] + made[11:12]
    return low(jnp.concatenate([made[:10], full(low(loss)), loss - full(low(loss)), made[12:lines]]))


def halve_out(axis, keep, came, next_keep, next_send):
    mine = spot()[axis]
    part = next_keep.shape[0] - LINES
    for k in range(2):
        rows = slice(k * part, (k + 1) * part)
        piece = low(full(keep[rows]) + full(came[rows]))

        @pl.when(mine == k)
        def _():
            next_keep[:part] = piece

        @pl.when(mine != k)
        def _():
            next_send[:part] = piece

    small = resplit(full(keep[2 * part :]) + full(came[2 * part :]))
    next_keep[part:] = small
    next_send[part:] = small


def eight(parts):
    made = full(parts[0])
    for k in range(1, parts.shape[0]):
        made = made + full(parts[k])
    return made


def weight_feed(*refs):
    pieces, (inner_vec, w_inner, i_x, i_y, w_outer, o_x, out) = refs[:8], refs[8:15]
    held_inner, held_outer, states, grads, active, g_inner, sem = refs[15:]
    at_b, at_c, at_y, _ = spot()
    half, width = w_inner.shape[0], states.shape[1]
    other, part = (1 - at_b) * half, half // 2
    copies = []
    for k in range(2):
        cols = slice(k * half, (k + 1) * half)
        there = at((2 * k + at_c) * width + at_y * half, half, 128)
        copies.append((w_inner.at[:, there], held_inner.at[at(at_b * half, half, 128), cols]))
        for y, piece in enumerate((i_x, i_y)):
            rows = at(other + (at_y + y) % 2 * part, part, 64)
            from_rows = slice(k * part, (k + 1) * part)
            copies.append((piece.at[from_rows, at(at_y * half, half, 128)], held_inner.at[rows, cols]))
    rows = at((2 * at_c + at_y) * half, half, 128)
    copies.append((w_outer.at[rows], held_outer.at[at(at_b * half, half, 128)]))
    copies.append((o_x, held_outer.at[at(other, half, 128)]))
    copies = start(copies, sem)
    own = pieces[0].shape[0]
    for k, piece in enumerate(pieces):
        states[k * own : (k + 1) * own] = piece[:, :width]
        grads[k * own : (k + 1) * own] = piece[:, width:]
    bias = jnp.concatenate(
        [inner_vec[0:1, at((2 * k + at_c) * width + at_y * half, half, 128)] for k in range(2)], 1
    )
    finish(copies)

    def block(j, carry):
        rows = at(j * BLOCK, BLOCK, BLOCK)
        before = dot(states[rows], held_inner[...]) + bias
        below = 0.5 * (1.0 + lax.erf(before * 0.7071067811865476))
        active[rows] = low(before * below)
        slope = below + before * jnp.exp(before * before * -0.5) * 0.3989422804014327
        g_inner[rows] = low(dot(grads[rows], held_outer[...], 1, 1) * slope)
        return carry

    lax.fori_loop(0, 8 * own // BLOCK, block, 0)
    mine = at(at_b * half, half, 128)
    depth, rows = out.shape[0], out.shape[1] // 2
    made = low(dot(active[:, mine], grads[...], 0, 0))
    for z in range(depth):
        out[z, :rows] = made[z * rows : (z + 1) * rows]
    made = low(dot(states[:, mine], g_inner[...], 0, 0))
    for z in range(depth):
        out[z, rows:] = made[z * rows : (z + 1) * rows]


def weight_out(*refs):
    pieces, (blocks, made) = (refs[:8], (refs[8:12], refs[14]))
    left, right = refs[12:14]
    _, at_c, at_y, at_z = spot()
    width, part = right.shape[1], left.shape[1]
    rows = right.shape[0] // 8
    for k, piece in enumerate(pieces):
        there = slice(k * rows, (k + 1) * rows)
        right[there] = piece[:rows, :width]
        mixed = piece[:rows, width:]
        mixed = jnp.where(at_c == 0, mixed[:, : 2 * part], mixed[:, 2 * part :])
        left[there] = jnp.where(at_y == 0, mixed[:, :part], mixed[:, part:])
    made[...] = dot(left[...], right[...], 0, 0)
    small = resplit(sum(full(piece[rows:, :width]) for piece in pieces))
    part = part // len(blocks)
    for k, block in enumerate(blocks):
        block[:part] = low(made[at((at_z + k) % len(blocks) * part, part, 8)])
        block[part:] = small


def weight_three(g_query, g_mine, came, states, w_three, back, keep, send, g_three):
    _, at_c, _, _ = spot()
    share = g_query.shape[1]
    g_three[:, :share] = g_query[...]
    g_three[:, share:] = low(g_mine[...] + came[...])
    made = low(dot(states[...], g_three[...], 0, 0))
    part = (keep.shape[0] - LINES) // 2
    for k in range(2):
        for c in range(2):
            piece = made[(2 * k + c) * part : (2 * k + c + 1) * part]

            @pl.when(at_c == c)
            def _():
                keep[k * part : (k + 1) * part] = piece

            @pl.when(at_c != c)
            def _():
                send[k * part : (k + 1) * part] = piece

    bias = jnp.broadcast_to(low(total(full(g_three[...]))), (LINES, 3 * share))
    keep[2 * part :] = bias
    send[2 * part :] = bias
    back[...] = low(dot(g_three[...], w_three[...], 1, 1))


def grad_states(parts, g_one, out):
    seqs, rows = out.shape[:2]
    for s in range(seqs):
        made = g_one[s * rows : (s + 1) * rows]
        for z in range(parts.shape[0] // seqs):
            made = made + full(parts[z * seqs + s])
        out[s] = made


def pack(summed, out_0, out_1, out_2, out_3, keep, came, vecs, out, loss, g_b_inner, *vectors):
    at_b, _, _, _ = spot()
    made = eight(summed)
    width, wide = made.shape[1], keep.shape[1]
    rows, share = (out.shape[0] - 8) // 3, width - wide
    part = out_0.shape[0] - LINES
    out[...] = jnp.zeros_like(out)
    out[: 2 * rows] = low(made)
    made = full(out_0[...]) + full(out_1[...]) + full(out_2[...]) + full(out_3[...])
    three = low(full(keep[...]) + full(came[...]))
    out[2 * rows : 3 * rows, :wide] = three[:rows]
    for k in range(width // share):
        piece = made[:part, k * share : (k + 1) * share]
        out[2 * rows + k * part : 2 * rows + (k + 1) * part, wide:] = low(piece)
    out[3 * rows :, :wide] = three[rows : rows + 8]
    small = made[part:]
    half = width // 2
    loss[...] = (small[10:11, :128] + small[11:12, :128]) / (2.0 * vecs[8:9, :128])
    for k, vector in enumerate(vectors):
        row = small[k : k + 1]
        vector[...] = jnp.where(at_b == 0, row[:, :half], row[:, half:]).reshape(half)
    first = jnp.where(at_b == 0, small[6:7], small[8:9])
    second = jnp.where(at_b == 0, small[7:8], small[9:10])
    g_b_inner[...] = jnp.concatenate([first, second], 1).reshape(2 * width)


def each_piece(pieces, steps):
    _, at_c, at_y, at_z = spot()
    depth = 4
    for j, k in enumerate(steps):
        for c in range(2):
            for y in range(2):
                place = (at_c + c) % 2, (at_y + y) % 2, (at_z + depth - k) % depth
                yield pieces[(j * 2 + c) * 2 + y], place


def final(steps, pieces, g_outer, g_inner, g_out, threes, biases, held, held_out, sem):
    depth = 4
    half, width = threes[0].shape
    rows, share = width // 8, width // depth
    part = rows // depth
    copies = []
    for n, (piece, (c, y, z)) in enumerate(each_piece(pieces, steps)):
        place = (c * 2 + y) * depth + z
        own = slice(n * 2 * rows, (n + 1) * 2 * rows)
        held[own] = full(piece[: 2 * rows])
        first = n * 2 * rows
        copies.append((held.at[first : first + rows], g_outer.at[at(place * rows, rows, 32)]))
        for k in range(2):
            cols = at((2 * k + c) * width + y * half, half, 128)
            copies.append(
                (
                    held.at[first + rows : first + 2 * rows, k * half : (k + 1) * half],
                    g_inner.at[at(z * rows, rows, 32), cols],
                )
            )
        for k in range(depth):
            first = 2 * rows + k * part
            held_out[n * part : (n + 1) * part, k * share : (k + 1) * share] = full(
                piece[first : first + part, 3 * share :]
            )
        copies.append((held_out.at[n * part : (n + 1) * part], g_out.at[at(place * part, part, 8)]))
    copies = start(copies, sem)
    for piece, (c, y, z) in each_piece(pieces, steps):
        there = at((c * 2 + y) * rows, rows, 32)
        for k in range(depth):

            @pl.when(z == k)
            def _():
                cols = slice(k * share, (k + 1) * share)
                for j, out in enumerate(threes):
                    out[there, cols] = full(piece[2 * rows : 3 * rows, j * share : (j + 1) * share])
                for j in (0, 2):
                    bias = full(piece[3 * rows :, j * share : (j + 1) * share])
                    biases[j : j + 1, cols] = bias[0:1]

    finish(copies)


def final_first(*refs):
    biases = refs[18]
    biases[...] = jnp.zeros_like(biases)
    final((0, 1, 3), refs[:12], *refs[12:15], refs[15:18], biases, *refs[19:])


def final_last(*refs):
    at_b, _, _, _ = spot()
    for k in range(3):
        refs[11 + 3 + k][...] = refs[7 + k][...]
    biases = refs[19]
    biases[...] = refs[10][...]
    final((2,), refs[:4], *refs[11:14], refs[14:17], biases, *refs[20:])
    for j, out in ((0, refs[17]), (2, refs[18])):
        half = out.shape[0]
        row = biases[j : j + 1]
        out[...] = jnp.where(at_b == 0, row[:, :half], row[:, half:]).reshape(half)


def per_device_heads(
    inputs,
    teacher,
    segments,
    w_query,
    b_query,
    w_key,
    w_value,
    b_value,
    w_out,
    b_out,
    gain_one,
    shift_one,
    w_inner,
    b_inner,
    w_outer,
    b_outer,
    gain_two,
    shift_two,
):
    count = lax.axis_size("ctx")
    depth = count // 4
    place = lax.axis_index("ctx")
    at_c, at_y = place % 2, place // 2 % 2
    seqs, rows, width = inputs.shape
    own = seqs * rows
    half = width // 2
    ff = w_inner.shape[1]
    share = width // depth
    keys = count // 2 * rows
    joint = ("batch", "ctx")
    pairs = [(y, c) for y in range(2) for c in range(2)]
    groups_z = [[z * 4 + r for z in range(depth)] for r in range(4)]
    groups_yz = [[z * 4 + y * 2 + c for z in range(depth) for y in range(2)] for c in range(2)]
    groups_xyc = [[b * count + z * 4 + y * 2 + c for b in range(2) for y, c in pairs] for z in range(depth)]

    def swap_x(values):
        return lax.ppermute(values, "batch", [(0, 1), (1, 0)])

    def swap_y(values):
        return lax.ppermute(values, "ctx", [(i, i ^ 2) for i in range(count)])

    def swap_xy(values):
        return lax.ppermute(values, joint, [(i, (i + count) % (2 * count) ^ 2) for i in range(2 * count)])

    def swap_c(values):
        return lax.ppermute(values, "ctx", [(i, i ^ 1) for i in range(count)])

    def shift_z(values, step):
        return lax.ppermute(values, "ctx", [(i, (i + 4 * step) % count) for i in range(count)])

    def trade(values, groups, axes="ctx"):
        return lax.all_to_all(values, axes, 0, 0, axis_index_groups=groups, tiled=True)

    tie = lax.optimization_barrier
    dma = pltpu.SemaphoreType.DMA

    blocks, first, p_inner, p_outer, p_out = kernel(
        prepare,
        [
            ((depth * seqs, rows, width), BF),
            ((3 * half // 4 + LINES, width), BF),
            ((half, width), BF),
            ((ff // 8, width), BF),
            ((half // 2, width), BF),
        ],
        [inputs, w_query, w_key, w_value, b_query, b_value, b_out, gain_one, shift_one]
        + [b_outer, gain_two, shift_two, b_inner, segments, w_inner, w_outer, w_out],
        hbm=(14, 15, 16),
        pin=range(14),
        scratch=[dma((4,))],
    )
    states = trade(blocks, groups_yz).reshape(keys, width)
    other = swap_x(first)
    x_inner = swap_x(p_inner)
    seg_seq = lax.dynamic_index_in_dim(segments, at_y, 0, keepdims=False).reshape(-1, 2, rows)
    seg_own = lax.dynamic_index_in_dim(seg_seq, at_c, 1, keepdims=False).reshape(-1)
    seg_peer = lax.dynamic_index_in_dim(seg_seq, 1 - at_c, 1, keepdims=False).reshape(-1)
    seg_key = jnp.concatenate([seg_own, seg_peer])[:, None]
    seg_query = seg_own[None, :]
    seg_tokens = lax.dynamic_slice_in_dim(segments, place * rows, rows, 1).reshape(own, 1)
    states, other, p_outer, p_out, seg_key, seg_query, seg_tokens = tie(
        (states, other, p_outer, p_out, seg_key, seg_query, seg_tokens)
    )
    x_outer = swap_x(p_outer)

    query, pair, vecs, inner_vec, w_three = kernel(
        project,
        [
            ((keys, share), BF),
            ((keys, 2 * share), BF),
            ((LINES, width), F32),
            ((8, ff), F32),
            ((width, 3 * share), BF),
        ],
        [states, first, other],
        scratch=[pltpu.VMEM((width, 3 * share), BF)],
    )
    peer = swap_c(pair)
    query, peer, x_inner = tie((query, peer, x_inner))
    y_inner = swap_y(x_inner)
    mixed, logs = kernel(
        attend,
        [((keys, share), BF), ((8, keys), F32)],
        [query, pair, peer, seg_query, seg_key],
        scratch=[pltpu.VMEM((2 * keys, share), BF), pltpu.VMEM((share, 2 * keys), BF)],
    )
    x_outer, mixed, p_out = tie((x_outer, mixed, p_out))
    mixed = trade(mixed.reshape(depth * seqs, rows, share), groups_yz)
    y_outer = swap_y(x_outer)
    x_out = swap_x(p_out)
    c_inner, c_outer = map(swap_c, (x_inner, x_outer))
    c_out, yc_inner = swap_c(x_out), swap_c(y_inner)
    mixed, y_outer, c_out, yc_inner, c_inner, c_outer = tie(
        (mixed, y_outer, c_out, yc_inner, c_inner, c_outer)
    )
    weights = [w_out, x_out, c_out]
    weights += [w_inner, x_inner, y_inner, c_inner, yc_inner]
    weights += [w_outer, x_outer, y_outer, c_outer, swap_c(y_outer)]
    held = [pltpu.VMEM((width, width), BF), pltpu.VMEM((width, ff), BF), pltpu.VMEM((ff, width), BF)]
    output, attended, unit, inverse, slope, two, g_hidden, sums = kernel(
        functools.partial(forward, float(own * 2 * count)),
        [
            (inputs.shape, F32),
            ((own, width), BF),
            ((own, width), F32),
            ((own, 128), F32),
            ((own, ff), F32),
            ((own, 2 * width), BF),
            ((own, width), F32),
            ((LINES, width), F32),
        ],
        [mixed, inputs, teacher, seg_tokens, vecs, inner_vec, *weights],
        hbm=range(6, 19),
        pin=(1, 2),
        scratch=[*held, pltpu.VMEM((own, ff), BF), dma((3, 9))],
    )
    fours = [two, swap_x(two), swap_y(two), swap_xy(two)]
    away_x, away_y, g_one, g_mixed = kernel(
        backward,
        [
            ((own + LINES, width + half), BF),
            ((own + LINES, width + half), BF),
            ((own, width), F32),
            ((depth * seqs, rows, 2 * share), BF),
        ],
        [two, slope, g_hidden, unit, inverse, vecs, attended, sums, *weights],
        hbm=range(8, 21),
        scratch=[
            *held,
            pltpu.VMEM((own, ff), BF),
            pltpu.VMEM((8, ff), F32),
            pltpu.VMEM((LINES, width), F32),
            dma((3, 9)),
        ],
    )
    away_x, away_y, *fours = tie((away_x, away_y, *fours))
    g_mixed = trade(g_mixed, groups_yz).reshape(keys, 2 * share)
    eights = [*fours, *map(swap_c, fours)]
    outer_rows = half // depth
    (feed,) = kernel(
        weight_feed,
        [((depth, 2 * outer_rows, width), BF)],
        [*eights, inner_vec, w_inner, x_inner, y_inner, w_outer, x_outer],
        hbm=range(9, 14),
        scratch=[
            pltpu.VMEM((width, width), BF),
            pltpu.VMEM((width, width), BF),
            pltpu.VMEM((8 * own, width), BF),
            pltpu.VMEM((8 * own, width), BF),
            pltpu.VMEM((8 * own, width), BF),
            pltpu.VMEM((8 * own, width), BF),
            dma((8,)),
        ],
    )
    feed, g_mixed, away_x, away_y = tie((feed, g_mixed, away_x, away_y))
    feed = trade(feed, groups_z)
    fours = [away_y, swap_x(away_x), swap_y(away_y), swap_xy(away_x)]

    g_query, g_mine, g_theirs = kernel(
        attend_back,
        [((keys, share), BF), ((keys, 2 * share), F32), ((keys, 2 * share), F32)],
        [query, pair, peer, seg_query, seg_key, logs, g_mixed],
        pin=range(6),
        scratch=[
            pltpu.VMEM((2 * keys, share), BF),
            pltpu.VMEM((share, 2 * keys), BF),
            pltpu.VMEM((2 * keys, share), BF),
            pltpu.VMEM((2 * keys, 2 * share), F32),
        ],
    )
    g_theirs, *fours = tie((g_theirs, *fours))
    part = half // 4 // depth
    outs = kernel(
        weight_out,
        [((part + LINES, width), BF)] * depth,
        [*fours, *map(swap_c, fours)],
        scratch=[
            pltpu.VMEM((8 * own, half // 4), BF),
            pltpu.VMEM((8 * own, width), BF),
            pltpu.VMEM((half // 4, width), F32),
        ],
    )
    back, three_keep, three_send = kernel(
        weight_three,
        [((keys, width), BF)] + [((half + LINES, 3 * share), BF)] * 2,
        [g_query, g_mine, swap_c(g_theirs), states, w_three],
        pin=(3, 4),
        scratch=[pltpu.VMEM((keys, 3 * share), BF)],
    )
    three_keep, three_send = kernel(
        functools.partial(halve_out, 0),
        [((half // 2 + LINES, 3 * share), BF)] * 2,
        [three_keep, swap_c(three_send)],
    )
    outs = [outs[0]] + [shift_z(outs[k], k) for k in range(1, depth)]
    three_x, outs[1], outs[2] = tie((swap_x(three_send), outs[1], outs[2]))
    three_keep, three_send = kernel(
        functools.partial(halve_out, 2),
        [((half // 4 + LINES, 3 * share), BF)] * 2,
        [three_keep, three_x],
    )
    three_came = swap_y(three_send)
    packed, loss, g_b_inner, *vectors = kernel(
        pack,
        [((3 * outer_rows + 8, width), BF), ((1, 128), F32), ((ff // 2,), F32)] + [((half,), F32)] * 6,
        [feed, *outs, three_keep, three_came, vecs],
    )
    packed, back = tie((packed, back))
    up, down, by_y = tie((shift_z(packed, 1), shift_z(packed, -1), swap_y(packed)))
    back = trade(back.reshape(depth * seqs, rows, width), groups_yz)
    across, up_y, down_y = tie((shift_z(up, 1), swap_y(up), swap_y(down)))
    pieces = []
    for pair in ((packed, by_y), (up, up_y), (down, down_y)):
        pieces += [*pair, *map(swap_c, pair)]
    large = [((ff // 2, width), F32), ((half, ff), F32), ((half, width), F32)]
    threes = [((half, width), F32)] * 3
    room = 2 * outer_rows

    def buffers(count):
        return [
            pltpu.VMEM((count * room, width), F32),
            pltpu.VMEM((count * part, width), F32),
            dma((4 * count,)),
        ]

    outs = kernel(
        final_first,
        [*large, *threes, ((8, width), F32)],
        pieces,
        pin=range(12),
        outs_hbm=range(3),
        scratch=buffers(12),
    )
    across_y, *outs = tie((swap_y(across), *outs))
    pieces = [across, across_y, swap_c(across), swap_c(across_y)]
    (g_inputs,) = kernel(grad_states, [(inputs.shape, F32)], [back, g_one])
    g_w_outer, g_w_inner, g_w_out, g_w_query, g_w_key, g_w_value, g_b_query, g_b_value = kernel(
        final_last,
        [*large, *threes] + [((half,), F32)] * 2,
        [*pieces, *outs],
        hbm=range(4, 7),
        outs_hbm=range(3),
        aliases={4: 0, 5: 1, 6: 2},
        scratch=[pltpu.VMEM((8, width), F32), *buffers(4)],
    )
    g_b_out, g_gain_one, g_shift_one, g_b_outer, g_gain_two, g_shift_two = vectors
    return (
        output,
        loss[0, 0],
        g_inputs,
        g_w_query,
        g_b_query,
        g_w_key,
        g_w_value,
        g_b_value,
        g_w_out,
        g_b_out,
        g_gain_one,
        g_shift_one,
        g_w_inner,
        g_b_inner,
        g_w_outer,
        g_b_outer,
        g_gain_two,
        g_shift_two,
    )


def per_device(inputs, *others):
    sizes = (lax.axis_size("batch"), lax.axis_size("ctx"), inputs.shape[0])
    if sizes == (2, 16, 2):
        return per_device_heads(inputs, *others)
    return per_device_any(inputs, *others)


def solution(mesh):
    placed = (
        P("batch", "ctx", None),
        P("batch", "ctx", None),
        P("batch", None),
        P("batch", None),
        P("batch"),
        P("batch", None),
        P("batch", None),
        P("batch"),
        P("batch", None),
        P("batch"),
        P("batch"),
        P("batch"),
        P("batch", None),
        P("batch"),
        P("batch", None),
        P("batch"),
        P("batch"),
        P("batch"),
    )
    return jax.shard_map(
        per_device,
        mesh=mesh,
        in_specs=placed,
        out_specs=(
            P("batch", "ctx", None),
            P(),
            P("batch", "ctx", None),
            P("batch", None),
            P("batch"),
            P("batch", None),
            P("batch", None),
            P("batch"),
            P("batch", None),
            P("batch"),
            P("batch"),
            P("batch"),
            P("batch", None),
            P("batch"),
            P("batch", None),
            P("batch"),
            P("batch"),
            P("batch"),
        ),
        check_vma=False,
    )
```
